32 devices in a mesh: dp: 16 (over z, y, x), mp: 2 (over core).
Axes of the slice: x: 2, y: 2, z: 4, core: 2. Of those that a mesh axis runs over, the one named last changes fastest.
Arguments:
- tokens: bfloat16 [16384, 768], P(('dp', 'mp')), may hold values from -8 to 8
- segment_ids: int32 [16, 1024], P('dp'), may hold values from 0 to 16, never falling along the last dimension, each value on 1 to 512 neighbouring positions
- query_weight: bfloat16 [768, 768], P(None, 'mp'), may hold values from -0.21875 to 0.21875
- key_weight: bfloat16 [768, 768], P(None, 'mp'), may hold values from -0.21875 to 0.21875
- value_weight: bfloat16 [768, 768], P(None, 'mp'), may hold values from -0.21875 to 0.21875
- output_weight: bfloat16 [768, 768], P('mp'), may hold values from -0.875 to 0.875
- inner_weight: bfloat16 [768, 3072], P(None, 'mp'), may hold values from -0.21875 to 0.21875
- outer_weight: bfloat16 [3072, 768], P('mp'), may hold values from -0.109375 to 0.109375
- mixer_down: bfloat16 [768, 64], replicated, may hold values from -0.21875 to 0.21875
- mixer_down_bias: bfloat16 [64], replicated, may hold values from -3 to 3
- mixer_up: bfloat16 [64, 768], replicated, may hold values from -0.75 to 0.75
- mixer_up_bias: bfloat16 [768], replicated, may hold values from -3 to 3
- dense_down: bfloat16 [768, 64], replicated, may hold values from -0.21875 to 0.21875
- dense_down_bias: bfloat16 [64], replicated, may hold values from -3 to 3
- dense_up: bfloat16 [64, 768], replicated, may hold values from -0.75 to 0.75
- dense_up_bias: bfloat16 [768], replicated, may hold values from -3 to 3
- first_gain: bfloat16 [768], replicated, may hold values from 0.5 to 1.5
- first_shift: bfloat16 [768], replicated, may hold values from -3 to 3
- second_gain: bfloat16 [768], replicated, may hold values from 0.5 to 1.5
- second_shift: bfloat16 [768], replicated, may hold values from -3 to 3
- output_grad: bfloat16 [16384, 768], P(('dp', 'mp')), may hold values from -6 to 6
Outputs:
- activations: bfloat16 [16384, 768], P(('dp', 'mp'))
- input_grad: bfloat16 [16384, 768], P(('dp', 'mp'))
- mixer_down_grad: float32 [768, 64], replicated
- mixer_down_bias_grad: float32 [64], replicated
- mixer_up_grad: float32 [64, 768], replicated
- mixer_up_bias_grad: float32 [768], replicated
- dense_down_grad: float32 [768, 64], replicated
- dense_down_bias_grad: float32 [64], replicated
- dense_up_grad: float32 [64, 768], replicated
- dense_up_bias_grad: float32 [768], replicated
- first_gain_grad: float32 [768], replicated
- first_shift_grad: float32 [768], replicated
- second_gain_grad: float32 [768], replicated
- second_shift_grad: float32 [768], replicated
- norm_ratios: float32 [2], replicated
The draws below stay inside these ranges and needn't reach their ends.
Inputs may be any that keep to these rules, and one draw needn't show every extreme that they name: `segment_ids`: each row numbers the items of one packed batch from 0, never falling.
All inputs are finite; a program needn't handle non-finite values.
Results may differ from the reference program's by a relative error of at most 0.019.
Values may be sent and summed in bfloat16 or wider, within the bound.
No kernel may reach another device: no remote copies, remote signals or barrier semaphores. Data moves between devices by JAX's collectives and lax.ppermute only.
A program may use at most 128 MiB of HBM per device.

```python
import math
import jax
import jax.numpy as jnp
import numpy as np
from jax import lax

D = 768
HEADS = 12
HEAD_DIM = 64
FF = 3072
ADAPT = 64
TOK_DEV = 1024
LONG = 512
ITEMS = 17
GROUPS = 16
TOKENS = 16384


def draw_tokens(key, part):
    group = (jnp.arange(TOKENS) // TOK_DEV).astype(jnp.float32)
    level = 0.7 * 2.0 ** (group / max(GROUPS - 1, 1))
    values = jax.random.normal(key, (TOKENS, D), jnp.float32) * level[:, None]
    return jnp.clip(values, -8.0, 8.0).astype(jnp.bfloat16)


def levels(stream_key, dims, pieces, smallest, high):
    level = 1.0
    for position, blocks in pieces:
        draws = jax.random.uniform(jax.random.fold_in(jax.random.fold_in(stream_key, 6), position), (blocks,), jnp.float32, smallest / len(pieces), high / len(pieces))
        level = level * jnp.repeat(jnp.exp(draws), dims[position] // blocks).reshape((-1,) + (1,) * (len(dims) - 1 - position))
    return level


def split_up(amount, total, bound, slope):
    loads = [(1 << 20) // math.isqrt(grade ** slope) + 1 for grade in range(2, amount + 1)]
    surplus, given = total - bound - (amount - 1), [1] * (amount - 1)
    while surplus > 0:
        movable = [i for i in range(amount - 1) if given[i] < bound]
        whole, remaining = sum([loads[i] for i in movable]), surplus
        for i in movable:
            extra = min(bound - given[i], max(1, remaining * loads[i] // whole), surplus)
            given[i] = given[i] + extra
            surplus = surplus - extra
    return np.array([bound] + given)


def ragged_sizes(key, amount, total, bound, lean):
    if amount == 2:
        one = jax.random.randint(key, (), max(1, total - bound), min(bound, total - 1) + 1)
        return jnp.stack([one, total - one])
    sizes = jnp.asarray(split_up(amount, total, bound, lean), jnp.int32)
    twos = (amount - 1) // 2
    donor, sink = sizes[1:1 + 2 * twos:2], sizes[2:2 + 2 * twos:2]
    slack = jnp.minimum(donor - 1, bound - sink)
    shifted = jax.random.randint(jax.random.fold_in(key, 1), (twos,), 0, 1 << 20) % (slack + 1)
    sizes = sizes.at[1:1 + 2 * twos:2].set(donor - shifted).at[2:2 + 2 * twos:2].set(sink + shifted)
    return sizes[jax.random.permutation(jax.random.fold_in(key, 2), amount)]


def normal_values(rng, extent, scale, most, cuts=(), held_as=jnp.bfloat16):
    factor_of = levels(rng, extent, cuts, -0.22, 0.18) if cuts else 1.0
    entries = jax.random.normal(rng, extent, jnp.float32) * scale * factor_of
    return jnp.minimum(jnp.maximum(entries, -most), most).astype(held_as)


def setup_inputs(seed: int = 0) -> dict:
    key_of = jax.random.split(jax.random.key(seed), 22)
    tokens = draw_tokens(jax.random.fold_in(key_of[21], 71), 0)
    segment_ids = jax.vmap(lambda own: jnp.searchsorted(jnp.cumsum(ragged_sizes(own, ITEMS, TOK_DEV, LONG, 1)), jnp.arange(TOK_DEV), side="right"))(jax.random.split(key_of[1], GROUPS)).reshape((GROUPS, TOK_DEV)).astype(jnp.int32)
    query_weight = normal_values(key_of[2], (D, D), D ** -0.5, 0.21875, ((1, 2),))
    key_weight = normal_values(key_of[3], (D, D), D ** -0.5, 0.21875, ((1, 2),))
    value_weight = normal_values(key_of[4], (D, D), D ** -0.5, 0.21875, ((1, 2),))
    output_weight = normal_values(key_of[5], (D, D), (D // 16) ** -0.5, 0.875, ((0, 2),))
    inner_weight = normal_values(key_of[6], (D, FF), D ** -0.5, 0.21875, ((1, 2),))
    outer_weight = normal_values(key_of[7], (FF, D), FF ** -0.5, 0.109375, ((0, 2),))
    mixer_down = normal_values(key_of[8], (D, ADAPT), D ** -0.5, 0.21875)
    mixer_down_bias = normal_values(key_of[9], (ADAPT,), 0.5, 3.0)
    mixer_up = normal_values(key_of[10], (ADAPT, D), ADAPT ** -0.5, 0.75)
    mixer_up_bias = normal_values(key_of[11], (D,), 0.3, 3.0)
    dense_down = normal_values(key_of[12], (D, ADAPT), D ** -0.5, 0.21875)
    dense_down_bias = normal_values(key_of[13], (ADAPT,), 0.5, 3.0)
    dense_up = normal_values(key_of[14], (ADAPT, D), ADAPT ** -0.5, 0.75)
    dense_up_bias = normal_values(key_of[15], (D,), 0.3, 3.0)
    first_gain = jnp.clip(1.0 + 0.1 * jax.random.normal(key_of[16], (D,), jnp.float32), 0.5, 1.5).astype(jnp.bfloat16)
    first_shift = normal_values(key_of[17], (D,), 0.3, 3.0)
    second_gain = jnp.clip(1.0 + 0.1 * jax.random.normal(key_of[18], (D,), jnp.float32), 0.5, 1.5).astype(jnp.bfloat16)
    second_shift = normal_values(key_of[19], (D,), 0.3, 3.0)
    output_grad = normal_values(key_of[20], (TOKENS, D), 1.0, 6.0, ((0, 32),))
    return {"tokens": tokens, "segment_ids": segment_ids, "query_weight": query_weight, "key_weight": key_weight, "value_weight": value_weight, "output_weight": output_weight, "inner_weight": inner_weight, "outer_weight": outer_weight, "mixer_down": mixer_down, "mixer_down_bias": mixer_down_bias, "mixer_up": mixer_up, "mixer_up_bias": mixer_up_bias, "dense_down": dense_down, "dense_down_bias": dense_down_bias, "dense_up": dense_up, "dense_up_bias": dense_up_bias, "first_gain": first_gain, "first_shift": first_shift, "second_gain": second_gain, "second_shift": second_shift, "output_grad": output_grad}


@jax.custom_vjp
def low(v):
    return lax.optimization_barrier(v.astype(jnp.bfloat16)).astype(jnp.float32)

@jax.custom_vjp
def low_back(v):
    return v

def low_keep(v):
    return (low(v), None)

def low_pass(kept, grad):
    return (grad,)

def back_keep(v):
    return (v, None)

def back_low(kept, grad):
    return (low(grad),)
low.defvjp(low_keep, low_pass)
low_back.defvjp(back_keep, back_low)
EPS = 1e-12
highest = lax.Precision.HIGHEST

def product(left, right):
    return jnp.dot(left, right, precision=highest)

def gelu_value(values):
    return jax.nn.gelu(values, approximate=False)

def layer_norm(values, gain, shift):
    mean = lax.optimization_barrier(jnp.mean(values, -1, keepdims=True))
    centred = values - mean
    variance = lax.optimization_barrier(jnp.mean(centred * centred, -1, keepdims=True))
    return centred * lax.rsqrt(variance + EPS) * gain + shift

def adapter(values, down, down_bias, up, up_bias):
    inner = low_back(product(low(values), down) + down_bias)
    return low_back(product(low(gelu_value(inner)), up) + up_bias)

def group_layer(frozen, trained, inputs, seg_row):
    query_weight, key_weight, value_weight, output_weight, inner_weight, outer_weight = frozen
    mixer_down, mixer_down_bias, mixer_up, mixer_up_bias, dense_down, dense_down_bias, dense_up, dense_up_bias, first_gain, first_shift, second_gain, second_shift = trained
    rows = inputs.shape[0]
    queries = low_back(low(product(inputs, query_weight))).reshape(rows, HEADS, HEAD_DIM)
    keys = low_back(low(product(inputs, key_weight))).reshape(rows, HEADS, HEAD_DIM)
    values = low_back(low(product(inputs, value_weight))).reshape(rows, HEADS, HEAD_DIM)
    scores = low_back(jnp.einsum('qhd,khd->hqk', queries, keys, precision=highest) * HEAD_DIM ** (-0.5))
    same = seg_row[:, None] == seg_row[None, :]
    scores = jnp.where(same[None], scores, -1e+30)
    peak = lax.optimization_barrier(jnp.max(scores, -1, keepdims=True))
    exponent = jnp.exp(scores - peak)
    shares = exponent / lax.optimization_barrier(jnp.sum(exponent, -1, keepdims=True))
    mixed = jnp.einsum('hqk,khd->qhd', low(shares), values, precision=highest).reshape(rows, D)
    mixed = low_back(low(mixed))
    attended = low_back(product(mixed, output_weight))
    mixer_out = adapter(attended, mixer_down, mixer_down_bias, mixer_up, mixer_up_bias)
    hidden = layer_norm(inputs + attended + mixer_out, first_gain, first_shift)
    inner = low_back(product(low(hidden), inner_weight))
    dense_in = low_back(product(low(gelu_value(inner)), outer_weight))
    dense_out = adapter(dense_in, dense_down, dense_down_bias, dense_up, dense_up_bias)
    result = layer_norm(hidden + dense_in + dense_out, second_gain, second_shift)
    sums = jnp.stack([jnp.sum(mixer_out * mixer_out), jnp.sum(dense_out * dense_out), jnp.sum(inputs * inputs)])
    return (result, sums)

def reference(tokens, segment_ids, query_weight, key_weight, value_weight, output_weight, inner_weight, outer_weight, mixer_down, mixer_down_bias, mixer_up, mixer_up_bias, dense_down, dense_down_bias, dense_up, dense_up_bias, first_gain, first_shift, second_gain, second_shift, output_grad):
    frozen = tuple((weight.astype(jnp.float32) for weight in (query_weight, key_weight, value_weight, output_weight, inner_weight, outer_weight)))
    trained = tuple((weight.astype(jnp.float32) for weight in (mixer_down, mixer_down_bias, mixer_up, mixer_up_bias, dense_down, dense_down_bias, dense_up, dense_up_bias, first_gain, first_shift, second_gain, second_shift)))
    inputs = tokens.astype(jnp.float32).reshape(GROUPS, TOK_DEV, D)

    def forward(values, params):

        def one_group(item_pair):
            return group_layer(frozen, params, item_pair[0], item_pair[1])
        return lax.map(jax.checkpoint(one_group), (values, segment_ids))
    (results, sums), pullback = jax.vjp(forward, inputs, trained)
    cotangent = output_grad.astype(jnp.float32).reshape(GROUPS, TOK_DEV, D)
    grad_inputs, grads = pullback((cotangent, jnp.zeros_like(sums)))
    totals = lax.optimization_barrier(jnp.sum(sums, 0))
    ratios = jnp.sqrt(totals[0:2] / totals[2])
    return (results.reshape(TOKENS, D).astype(jnp.bfloat16), grad_inputs.reshape(TOKENS, D).astype(jnp.bfloat16), grads[0], grads[1], grads[2], grads[3], grads[4], grads[5], grads[6], grads[7], grads[8], grads[9], grads[10], grads[11], ratios)
```

```python
import functools

import jax
import jax.numpy as jnp
from jax import lax
from jax.experimental import pallas as pl
from jax.experimental.pallas import tpu as pltpu
from jax.sharding import PartitionSpec as P

F32 = jnp.float32
BF16 = jnp.bfloat16
HEAD_DIM = 64
PAIR = 2 * HEAD_DIM
EPS = 1e-12
LOG2E = 1.4426950408889634
LN2 = 0.6931471805599453
ROOT_HALF = 0.7071067811865476
ROOT_TWO_PI = 0.3989422804014327
MASKED = -1e30
BLOCK = 256
MIB = 1 << 20

VM = pl.BlockSpec(memory_space=pltpu.VMEM)
SM = pl.BlockSpec(memory_space=pltpu.SMEM)


def dot(left, right):
    return jnp.dot(left, right, preferred_element_type=F32)


def dot_nt(left, right):
    return lax.dot_general(left, right, (((1,), (1,)), ((), ())), preferred_element_type=F32)


def dot_tn(left, right):
    return lax.dot_general(left, right, (((0,), (0,)), ((), ())), preferred_element_type=F32)


def aligned(index, size):
    return pl.ds(pl.multiple_of(index * size, size), size)


def split_pair(pair):
    lane = lax.broadcasted_iota(jnp.int32, pair.shape, 1)
    zero = jnp.zeros_like(pair)
    return jnp.where(lane < HEAD_DIM, pair, zero), jnp.where(lane < HEAD_DIM, zero, pair)


def stack_heads(source, target, block):
    first, second = split_pair(source)
    for t in range(source.shape[0] // block):
        target[pl.ds(2 * t * block, block), :] = first[t * block : (t + 1) * block]
        target[pl.ds((2 * t + 1) * block, block), :] = second[t * block : (t + 1) * block]


def fill_columns(row_ref, column_ref):
    for t in range(row_ref.shape[1] // 128):
        span = slice(t * 128, (t + 1) * 128)
        column_ref[span, :] = jnp.broadcast_to(row_ref[0:1, span], (128, 128)).T


def block_ranges(seg_row, block):
    ids = seg_row.reshape(-1)
    first = ids[::block]
    last = ids[block - 1 :: block]
    low = jnp.sum((ids[None, :] < first[:, None]).astype(jnp.int32), 1) // block
    high = (jnp.sum((ids[None, :] <= last[:, None]).astype(jnp.int32), 1) + block - 1) // block
    return jnp.stack([low, high])


def project_kernel(x_ref, wq_ref, wk_ref, wv_ref, out_ref):
    width = wq_ref.shape[1]
    x = x_ref[...]
    out_ref[:, :width] = (dot(x, wq_ref[...]) * (HEAD_DIM**-0.5 * LOG2E)).astype(BF16)
    out_ref[:, width : 2 * width] = dot(x, wk_ref[...]).astype(BF16)
    out_ref[:, 2 * width :] = dot(x, wv_ref[...]).astype(BF16)


def project(x, wq, wk, wv):
    rows, width = x.shape[0], wq.shape[1]
    return pl.pallas_call(
        project_kernel,
        out_shape=jax.ShapeDtypeStruct((rows, 3 * width), BF16),
        in_specs=[VM] * 4,
        out_specs=VM,
        compiler_params=pltpu.CompilerParams(vmem_limit_bytes=16 * MIB),
        cost_estimate=pl.CostEstimate(flops=2 * rows * x.shape[1] * 3 * width, bytes_accessed=5 * MIB, transcendentals=0),
        name="project",
    )(x, wq, wk, wv)


def attention_kernel(
    rng_ref, half_ref, seg_ref, own_ref, x_ref, wq_ref, wk_ref, wv_ref,
    qkv_ref, keep_ref, send_ref, lse_ref,
    seg_col, keys, values, scores, peaks, totals, mix,
):
    half = own_ref.shape[0]
    count, width = qkv_ref.shape[0], wq_ref.shape[1]
    pairs, heads, block = width // PAIR, width // HEAD_DIM, BLOCK
    here, there = half_ref[0], 1 - half_ref[0]
    fill_columns(seg_ref, seg_col)
    qkv_ref[aligned(here, half), :] = own_ref[...]
    project_kernel(x_ref, wq_ref, wk_ref, wv_ref, qkv_ref.at[aligned(there, half), :])
    for p in range(pairs):
        first, second = split_pair(qkv_ref[:, width + p * PAIR : width + (p + 1) * PAIR])
        keys[2 * p], keys[2 * p + 1] = first, second
        stack_heads(qkv_ref[:, 2 * width + p * PAIR : 2 * width + (p + 1) * PAIR], values.at[p], block)

    def query_block(g, carry):
        rows = aligned(g, block)
        low, high = rng_ref[0, g], rng_ref[1, g]
        peaks[...] = jnp.full(peaks.shape, MASKED, F32)
        totals[...] = jnp.zeros(totals.shape, F32)
        mix[...] = jnp.zeros(mix.shape, F32)

        def score_pass(j, c):
            cols = aligned(j, block)
            same = seg_col[rows, 0:1] == seg_ref[0:1, cols]
            for h in range(heads):
                p = h // 2
                s = dot_nt(qkv_ref[rows, p * PAIR : (p + 1) * PAIR], keys[h, cols, :])
                s = jnp.where(same, s, MASKED)
                scores[h, :, cols] = s
                top = peaks[h]
                for t in range(block // 128):
                    top = jnp.maximum(top, s[:, t * 128 : (t + 1) * 128])
                peaks[h] = top
            return c

        lax.fori_loop(low, high, score_pass, 0)
        for h in range(heads):
            peaks[h] = jnp.broadcast_to(jnp.max(peaks[h], -1, keepdims=True), (block, 128))

        def mix_pass(j, c):
            cols = aligned(j, block)
            for p in range(pairs):
                parts = []
                for h in (2 * p, 2 * p + 1):
                    peak = jnp.concatenate([peaks[h]] * (block // 128), 1)
                    e = jnp.exp2(scores[h, :, cols] - peak)
                    total = totals[h]
                    for t in range(block // 128):
                        total = total + e[:, t * 128 : (t + 1) * 128]
                    totals[h] = total
                    parts.append(e.astype(BF16))
                mix[:, p * PAIR : (p + 1) * PAIR] += dot(jnp.concatenate(parts, 1), values[p, aligned(j, 2 * block), :])
            return c

        lax.fori_loop(low, high, mix_pass, 0)
        lane = lax.broadcasted_iota(jnp.int32, (block, 128), 1)
        lse = jnp.zeros((block, 128), F32)
        outs = []
        for p in range(pairs):
            sums = [jnp.sum(totals[h], -1, keepdims=True) for h in (2 * p, 2 * p + 1)]
            for a in range(2):
                lse = jnp.where(lane == 2 * p + a, peaks[2 * p + a] + jnp.log2(sums[a]), lse)
            scale = jnp.where(lane < HEAD_DIM, 1.0 / sums[0], 1.0 / sums[1])
            outs.append((mix[:, p * PAIR : (p + 1) * PAIR] * scale).astype(BF16))
        lse_ref[:, rows] = lse.T[0:8, :]
        result = jnp.concatenate(outs, 1)
        per_half = half // block

        @pl.when(g // per_half == here)
        def _():
            keep_ref[aligned(g % per_half, block), :] = result

        @pl.when(g // per_half != here)
        def _():
            send_ref[aligned(g % per_half, block), :] = result

        return carry

    lax.fori_loop(0, count // block, query_block, 0)


def attention(rng, half_index, seg, own, x, wq, wk, wv):
    half, width = own.shape[0], wq.shape[1]
    count, pairs = 2 * half, width // PAIR
    return pl.pallas_call(
        attention_kernel,
        out_shape=(
            jax.ShapeDtypeStruct((count, 3 * width), BF16),
            jax.ShapeDtypeStruct((half, width), BF16),
            jax.ShapeDtypeStruct((half, width), BF16),
            jax.ShapeDtypeStruct((8, count), F32),
        ),
        in_specs=[SM, SM] + [VM] * 6,
        out_specs=(VM,) * 4,
        scratch_shapes=[
            pltpu.VMEM((count, 128), F32),
            pltpu.VMEM((2 * pairs, count, PAIR), BF16),
            pltpu.VMEM((pairs, 2 * count, PAIR), BF16),
            pltpu.VMEM((2 * pairs, BLOCK, count), F32),
            pltpu.VMEM((2 * pairs, BLOCK, 128), F32),
            pltpu.VMEM((2 * pairs, BLOCK, 128), F32),
            pltpu.VMEM((BLOCK, width), F32),
        ],
        compiler_params=pltpu.CompilerParams(vmem_limit_bytes=32 * MIB),
        cost_estimate=pl.CostEstimate(flops=10**10, bytes_accessed=8 * MIB, transcendentals=10**6),
        name="attention",
    )(rng, half_index, seg, own, x, wq, wk, wv)


def attention_grad_kernel(
    rng_ref, half_ref, seg_ref, qkv_ref, keep_ref, send_ref, own_ref, other_ref, lse_ref, wq_ref, wk_ref, wv_ref, first_ref,
    away_ref, home_ref,
    seg_col, keys, values, queries, grads, grad, delta, dq, dk, dv, dqkv,
):
    half = own_ref.shape[0]
    count, width = qkv_ref.shape[0], wq_ref.shape[1]
    pairs, block = width // PAIR, BLOCK
    here, there = half_ref[0], 1 - half_ref[0]
    fill_columns(seg_ref, seg_col)
    grad[aligned(here, half), :] = own_ref[...]
    grad[aligned(there, half), :] = other_ref[...]
    row = lax.broadcasted_iota(jnp.int32, (8, width), 0)
    column = lax.broadcasted_iota(jnp.int32, (8, width), 1)
    pick = jnp.where(column // HEAD_DIM == row, 1.0, 0.0).astype(BF16)
    for which, mixed_ref, up_ref in ((here, keep_ref, own_ref), (there, send_ref, other_ref)):
        product = mixed_ref[...].astype(F32) * up_ref[...].astype(F32)
        high = product.astype(BF16)
        low = (product - high.astype(F32)).astype(BF16)
        delta[:, aligned(which, half)] = dot_nt(pick, high) + dot_nt(pick, low)
    for p in range(pairs):
        cols = slice(p * PAIR, (p + 1) * PAIR)
        stack_heads(qkv_ref[:, cols], queries.at[p], block)
        stack_heads(qkv_ref[:, width + p * PAIR : width + (p + 1) * PAIR], keys.at[p], block)
        stack_heads(qkv_ref[:, 2 * width + p * PAIR : 2 * width + (p + 1) * PAIR], values.at[p], block)
        stack_heads(grad[:, cols], grads.at[p], block)
    dk[...] = jnp.zeros(dk.shape, F32)
    dv[...] = jnp.zeros(dv.shape, F32)

    def query_block(g, carry):
        rows = aligned(g, block)
        low, high = rng_ref[0, g], rng_ref[1, g]
        dq[...] = jnp.zeros(dq.shape, F32)

        def key_block(j, c):
            span = aligned(j, block)
            same = seg_col[span, 0:1] == seg_ref[0:1, rows]
            for p in range(pairs):
                cols = slice(p * PAIR, (p + 1) * PAIR)
                s2 = dot_nt(keys[p, aligned(j, 2 * block), :], qkv_ref[rows, cols])
                d2 = dot_nt(values[p, aligned(j, 2 * block), :], grad[rows, cols])
                shares, slopes = [], []
                for a in range(2):
                    h = 2 * p + a
                    s = jnp.where(same, s2[a * block : (a + 1) * block] - lse_ref[h : h + 1, rows], MASKED)
                    e = jnp.exp2(s)
                    d = e * (d2[a * block : (a + 1) * block] - delta[h : h + 1, rows])
                    shares.append(e.astype(BF16))
                    slopes.append(d.astype(BF16))
                dv[span, cols] += dot(jnp.concatenate(shares, 1), grads[p, aligned(g, 2 * block), :])
                dk[span, cols] += dot(jnp.concatenate(slopes, 1), queries[p, aligned(g, 2 * block), :])
                dq[:, cols] += dot_tn(jnp.concatenate(slopes, 0), keys[p, aligned(j, 2 * block), :])
            return c

        lax.fori_loop(low, high, key_block, 0)
        dqkv[rows, :width] = (dq[...] * HEAD_DIM**-0.5).astype(BF16)
        return carry

    lax.fori_loop(0, count // block, query_block, 0)
    dqkv[:, width : 2 * width] = (dk[...] * LN2).astype(BF16)
    dqkv[:, 2 * width :] = dv[...].astype(BF16)

    def input_part(which):
        rows = aligned(which, half)
        return (
            dot_nt(dqkv[rows, :width], wq_ref[...])
            + dot_nt(dqkv[rows, width : 2 * width], wk_ref[...])
            + dot_nt(dqkv[rows, 2 * width :], wv_ref[...])
        )

    away_ref[...] = input_part(there).astype(BF16)
    home_ref[...] = input_part(here) + first_ref[...]


def attention_grad(rng, half_index, seg, qkv, keep, send, own, other, lse, wq, wk, wv, first_grad):
    half, width = own.shape
    count, pairs, features = 2 * half, width // PAIR, wq.shape[0]
    return pl.pallas_call(
        attention_grad_kernel,
        out_shape=(
            jax.ShapeDtypeStruct((half, features), BF16),
            jax.ShapeDtypeStruct((half, features), F32),
        ),
        in_specs=[SM, SM] + [VM] * 11,
        out_specs=(VM,) * 2,
        scratch_shapes=[pltpu.VMEM((count, 128), F32)]
        + [pltpu.VMEM((pairs, 2 * count, PAIR), BF16)] * 4
        + [
            pltpu.VMEM((count, width), BF16),
            pltpu.VMEM((8, count), F32),
            pltpu.VMEM((BLOCK, width), F32),
            pltpu.VMEM((count, width), F32),
            pltpu.VMEM((count, width), F32),
            pltpu.VMEM((count, 3 * width), BF16),
        ],
        compiler_params=pltpu.CompilerParams(vmem_limit_bytes=40 * MIB),
        cost_estimate=pl.CostEstimate(flops=2 * 10**10, bytes_accessed=10 * MIB, transcendentals=10**6),
        name="attention_grad",
    )(rng, half_index, seg, qkv, keep, send, own, other, lse, wq, wk, wv, first_grad)


def gelu_both(v):
    part = 0.5 + 0.5 * lax.erf(v * ROOT_HALF)
    return v * part, part + v * jnp.exp(-0.5 * v * v) * ROOT_TWO_PI


def norm(values, gain, shift):
    mean = jnp.mean(values, -1, keepdims=True)
    centred = values - mean
    reciprocal = lax.rsqrt(jnp.mean(centred * centred, -1, keepdims=True) + EPS)
    normed = centred * reciprocal
    return normed * gain + shift, normed, reciprocal


def norm_grad(upstream, normed, reciprocal, gain):
    scaled = upstream * gain
    return reciprocal * (
        scaled - jnp.mean(scaled, -1, keepdims=True) - normed * jnp.mean(scaled * normed, -1, keepdims=True)
    )


def column_sum(values):
    return jnp.sum(values, 0, keepdims=True)


def middle_kernel(
    x_ref, keep_ref, got_ref, wo_ref, wo2_ref, w1_ref, w12_ref, w2_ref, w22_ref,
    md_ref, mdb_ref, mu_ref, mub_ref, dd_ref, ddb_ref, du_ref, dub_ref,
    fg_ref, fs_ref, sg_ref, ss_ref, up_ref,
    act_ref, first_ref, own_ref, away_ref, big_ref, small_ref,
    slope_ref, hidden_ref, normed_ref,
):
    rows, features = x_ref.shape
    adapt = md_ref.shape[1]
    x = x_ref[...].astype(F32)
    attended = dot(keep_ref[...], wo_ref[...]) + dot(got_ref[...], wo2_ref[...])
    attended_low = attended.astype(BF16)
    mixer_active, mixer_slope = gelu_both(dot(attended_low, md_ref[...]) + mdb_ref[...].astype(F32))
    mixer_active = mixer_active.astype(BF16)
    mixer_out = dot(mixer_active, mu_ref[...]) + mub_ref[...].astype(F32)
    hidden, normed_one, reciprocal_one = norm(x + attended + mixer_out, fg_ref[...].astype(F32), fs_ref[...].astype(F32))
    normed_ref[...] = normed_one
    hidden_ref[...] = hidden
    mixer_square = jnp.sum(column_sum(mixer_out * mixer_out), -1, keepdims=True)
    input_square = jnp.sum(column_sum(x * x), -1, keepdims=True)
    hidden_low = hidden.astype(BF16)
    chunk = 512
    units = w1_ref.shape[1]
    dense_in = jnp.zeros((rows, features), F32)
    for s, (win, wout) in enumerate(((w1_ref, w2_ref), (w12_ref, w22_ref))):
        for c in range(units // chunk):
            span = slice(c * chunk, (c + 1) * chunk)
            value, slope = gelu_both(dot(hidden_low, win[:, span]))
            slope_ref[:, s * units + c * chunk : s * units + (c + 1) * chunk] = slope.astype(BF16)
            dense_in = dense_in + dot(value.astype(BF16), wout[span, :])
    dense_low = dense_in.astype(BF16)
    dense_active, dense_slope = gelu_both(dot(dense_low, dd_ref[...]) + ddb_ref[...].astype(F32))
    dense_active = dense_active.astype(BF16)
    dense_out = dot(dense_active, du_ref[...]) + dub_ref[...].astype(F32)
    second_gain = sg_ref[...].astype(F32)
    result, normed_two, reciprocal_two = norm(hidden_ref[...] + dense_in + dense_out, second_gain, ss_ref[...].astype(F32))
    act_ref[...] = result.astype(BF16)
    dense_square = jnp.sum(column_sum(dense_out * dense_out), -1, keepdims=True)

    upstream = up_ref[...].astype(F32)
    small_ref[4:5, :] = column_sum(upstream * normed_two)
    small_ref[5:6, :] = column_sum(upstream)
    second_grad = norm_grad(upstream, normed_two, reciprocal_two, second_gain)
    dense_top = second_grad.astype(BF16)
    big_ref[3 * adapt : 4 * adapt, :] = dot_tn(dense_active, dense_top).astype(BF16)
    small_ref[1:2, :] = column_sum(dense_top.astype(F32))
    dense_mid = (dot_nt(dense_top, du_ref[...]) * dense_slope).astype(BF16)
    big_ref[2 * adapt : 3 * adapt, :] = dot_tn(dense_mid, dense_low).astype(BF16)
    dense_mid_sum = column_sum(dense_mid.astype(F32))
    dense_in_grad = (second_grad + dot_nt(dense_mid, dd_ref[...])).astype(BF16)
    hidden_grad = second_grad
    for s, (win, wout) in enumerate(((w1_ref, w2_ref), (w12_ref, w22_ref))):
        for c in range(units // chunk):
            span = slice(c * chunk, (c + 1) * chunk)
            slope = slope_ref[:, s * units + c * chunk : s * units + (c + 1) * chunk].astype(F32)
            inner_grad = (dot_nt(dense_in_grad, wout[span, :]) * slope).astype(BF16)
            hidden_grad = hidden_grad + dot_nt(inner_grad, win[:, span])
    normed_one = normed_ref[...]
    small_ref[2:3, :] = column_sum(hidden_grad * normed_one)
    small_ref[3:4, :] = column_sum(hidden_grad)
    first_grad = norm_grad(hidden_grad, normed_one, reciprocal_one, fg_ref[...].astype(F32))
    first_ref[...] = first_grad
    mixer_top = first_grad.astype(BF16)
    big_ref[adapt : 2 * adapt, :] = dot_tn(mixer_active, mixer_top).astype(BF16)
    small_ref[0:1, :] = column_sum(mixer_top.astype(F32))
    mixer_mid = (dot_nt(mixer_top, mu_ref[...]) * mixer_slope).astype(BF16)
    big_ref[0:adapt, :] = dot_tn(mixer_mid, attended_low).astype(BF16)
    mixer_mid_sum = column_sum(mixer_mid.astype(F32))
    attended_grad = (first_grad + dot_nt(mixer_mid, md_ref[...])).astype(BF16)
    own_ref[...] = dot_nt(attended_grad, wo_ref[...]).astype(BF16)
    away_ref[...] = dot_nt(attended_grad, wo2_ref[...]).astype(BF16)
    lane = lax.broadcasted_iota(jnp.int32, (1, 128), 1)
    squares = jnp.where(lane == 0, mixer_square, jnp.where(lane == 1, dense_square, jnp.where(lane == 2, input_square, 0.0)))
    small_ref[6:7, :] = jnp.concatenate(
        [mixer_mid_sum, dense_mid_sum, squares, jnp.zeros((1, features - 2 * adapt - 128), F32)], 1
    )
    small_ref[7:8, :] = jnp.zeros((1, features), F32)


def middle(x, keep, got, weights, adapters, up):
    rows, features = x.shape
    width = keep.shape[1]
    adapt = adapters[0].shape[1]
    units = weights[2].shape[1]
    return pl.pallas_call(
        middle_kernel,
        out_shape=(
            jax.ShapeDtypeStruct((rows, features), BF16),
            jax.ShapeDtypeStruct((rows, features), F32),
            jax.ShapeDtypeStruct((rows, width), BF16),
            jax.ShapeDtypeStruct((rows, width), BF16),
            jax.ShapeDtypeStruct((4 * adapt, features), BF16),
            jax.ShapeDtypeStruct((8, features), F32),
        ),
        in_specs=[VM] * 22,
        out_specs=(VM,) * 6,
        scratch_shapes=[
            pltpu.VMEM((rows, 2 * units), BF16),
            pltpu.VMEM((rows, features), F32),
            pltpu.VMEM((rows, features), F32),
        ],
        compiler_params=pltpu.CompilerParams(vmem_limit_bytes=56 * MIB),
        cost_estimate=pl.CostEstimate(flops=2 * 10**10, bytes_accessed=16 * MIB, transcendentals=10**6),
        name="middle",
    )(x, keep, got, *weights, *adapters, up)


def swap_cores(value):
    return lax.ppermute(value, "mp", [(0, 1), (1, 0)])


def high_low(value):
    high = value.astype(BF16)
    return high, (value - high.astype(F32)).astype(BF16)


def reduce_gradients(big, small, half_index):
    rows = big.shape[0] // 2
    high, low = high_low(small)
    mine = lax.dynamic_slice_in_dim(big, half_index * rows, rows, 0)
    theirs = lax.dynamic_slice_in_dim(big, (1 - half_index) * rows, rows, 0)
    tail = jnp.concatenate([high, low], 0)
    got = swap_cores(jnp.concatenate([theirs, tail], 0))

    def combine(held_big, held_tail, received):
        total = held_big.astype(F32) + received[:rows].astype(F32)
        held = held_tail.astype(F32)
        arrived = received[rows:].astype(F32)
        vector = (held[:8] + held[8:]) + (arrived[:8] + arrived[8:])
        return total, vector

    total, vector = combine(mine, tail, got)
    devices = lax.axis_size("dp")
    step = 1
    while step < devices:
        packed = jnp.concatenate([total.astype(BF16), *high_low(vector)], 0)
        got = lax.ppermute(packed, "dp", [(i, i ^ step) for i in range(devices)])
        total, vector = combine(packed[:rows], packed[rows:], got)
        step *= 2
    other = swap_cores(total.astype(BF16)).astype(F32)
    mine = total.astype(BF16).astype(F32)
    lower = jnp.where(half_index == 0, mine, other)
    upper = jnp.where(half_index == 0, other, mine)
    return lower, upper, vector


def per_device(
    tokens, segment_ids, query_weight, key_weight, value_weight, output_weight, inner_weight, outer_weight,
    mixer_down, mixer_down_bias, mixer_up, mixer_up_bias, dense_down, dense_down_bias, dense_up, dense_up_bias,
    first_gain, first_shift, second_gain, second_shift, output_grad,
):
    half_index = lax.axis_index("mp")
    position = half_index.astype(jnp.int32).reshape(1)
    other_tokens = swap_cores(tokens)
    other_output = swap_cores(output_weight)
    other_inner = swap_cores(inner_weight)
    other_outer = swap_cores(outer_weight)
    rng = block_ranges(segment_ids, BLOCK)
    seg = segment_ids.astype(F32)
    own = project(tokens, query_weight, key_weight, value_weight)
    qkv, keep, send, lse = attention(rng, position, seg, own, other_tokens, query_weight, key_weight, value_weight)
    got = swap_cores(send)
    row = lambda v: v.reshape(1, -1)
    adapters = (
        mixer_down, row(mixer_down_bias), mixer_up, row(mixer_up_bias),
        dense_down, row(dense_down_bias), dense_up, row(dense_up_bias),
        row(first_gain), row(first_shift), row(second_gain), row(second_shift),
    )
    weights = (output_weight, other_output, inner_weight, other_inner, outer_weight, other_outer)
    result, first_grad, own_grad, away_grad, big, small = middle(tokens, keep, got, weights, adapters, output_grad)
    got_grad = swap_cores(away_grad)
    lower, upper, vector = reduce_gradients(big, small, half_index)
    away, home = attention_grad(
        rng, position, seg, qkv, keep, send, own_grad, got_grad, lse, query_weight, key_weight, value_weight, first_grad
    )
    input_grad = (home + swap_cores(away).astype(F32)).astype(BF16)
    adapt = mixer_down.shape[1]
    return (
        result,
        input_grad,
        lower[:adapt].T,
        vector[6, :adapt],
        lower[adapt:],
        vector[0],
        upper[:adapt].T,
        vector[6, adapt : 2 * adapt],
        upper[adapt:],
        vector[1],
        vector[2],
        vector[3],
        vector[4],
        vector[5],
        jnp.sqrt(vector[6, 2 * adapt : 2 * adapt + 2] / vector[6, 2 * adapt + 2]),
    )


def solution(mesh):
    tokens = P(("dp", "mp"), None)
    columns, rows, whole = P(None, "mp"), P("mp", None), P()
    return jax.shard_map(
        per_device,
        mesh=mesh,
        in_specs=(tokens, P("dp", None), columns, columns, columns, rows, columns, rows) + (whole,) * 12 + (tokens,),
        out_specs=(tokens, tokens) + (whole,) * 13,
        check_vma=False,
    )
```

```python
import functools

import jax
import jax.numpy as jnp
from jax import lax
from jax.experimental import pallas as pl
from jax.experimental.pallas import tpu as pltpu
from jax.sharding import PartitionSpec as P

F32 = jnp.float32
BF16 = jnp.bfloat16
HEAD_DIM = 64
PAIR = 2 * HEAD_DIM
EPS = 1e-12
LOG2E = 1.4426950408889634
LN2 = 0.6931471805599453
ROOT_HALF = 0.7071067811865476
ROOT_TWO_PI = 0.3989422804014327
MASKED = -1e30
BLOCK = 256
MIB = 1 << 20

VM = pl.BlockSpec(memory_space=pltpu.VMEM)
SM = pl.BlockSpec(memory_space=pltpu.SMEM)
HB = pl.BlockSpec(memory_space=pltpu.HBM)


def dot(left, right):
    return jnp.dot(left, right, preferred_element_type=F32)


def dot_nt(left, right):
    return lax.dot_general(left, right, (((1,), (1,)), ((), ())), preferred_element_type=F32)


def dot_tn(left, right):
    return lax.dot_general(left, right, (((0,), (0,)), ((), ())), preferred_element_type=F32)


def aligned(index, size):
    return pl.ds(pl.multiple_of(index * size, size), size)


def split_pair(pair):
    lane = lax.broadcasted_iota(jnp.int32, pair.shape, 1)
    zero = jnp.zeros_like(pair)
    return jnp.where(lane < HEAD_DIM, pair, zero), jnp.where(lane < HEAD_DIM, zero, pair)


def stack_heads(source, target, block):
    first, second = split_pair(source)
    for t in range(source.shape[0] // block):
        target[pl.ds(2 * t * block, block), :] = first[t * block : (t + 1) * block]
        target[pl.ds((2 * t + 1) * block, block), :] = second[t * block : (t + 1) * block]


def fill_columns(row_ref, column_ref):
    for t in range(row_ref.shape[1] // 128):
        span = slice(t * 128, (t + 1) * 128)
        column_ref[span, :] = jnp.broadcast_to(row_ref[0:1, span], (128, 128)).T


def start_all(sources, buffers, sems):
    copies = [pltpu.make_async_copy(src, dst, sems.at[i]) for i, (src, dst) in enumerate(zip(sources, buffers))]
    for copy in copies:
        copy.start()
    return copies


def write_projection(x, weights, copies, out_ref):
    width = weights[0].shape[1]
    for i, weight in enumerate(weights):
        if copies:
            copies[i].wait()
        part = dot(x, weight[...])
        if i == 0:
            part = part * (HEAD_DIM**-0.5 * LOG2E)
        out_ref[:, i * width : (i + 1) * width] = part.astype(BF16)


def project_kernel(x_ref, wq_ref, wk_ref, wv_ref, out_ref, x_buf, wq, wk, wv, sems):
    copies = start_all((x_ref, wq_ref, wk_ref, wv_ref), (x_buf, wq, wk, wv), sems)
    copies[0].wait()
    write_projection(x_buf[...], (wq, wk, wv), copies[1:], out_ref)


def project(x, wq, wk, wv):
    rows, width = x.shape[0], wq.shape[1]
    return pl.pallas_call(
        project_kernel,
        out_shape=jax.ShapeDtypeStruct((rows, 3 * width), BF16),
        in_specs=[HB] * 4,
        out_specs=VM,
        scratch_shapes=[pltpu.VMEM(v.shape, BF16) for v in (x, wq, wk, wv)] + [pltpu.SemaphoreType.DMA((4,))],
        compiler_params=pltpu.CompilerParams(vmem_limit_bytes=12 * MIB),
        cost_estimate=pl.CostEstimate(flops=2 * rows * x.shape[1] * 3 * width, bytes_accessed=5 * MIB, transcendentals=0),
        name="project",
    )(x, wq, wk, wv)


def attention_kernel(
    half_ref, ids_ref, seg_ref, own_ref, x_ref, wq_ref, wk_ref, wv_ref,
    qkv_ref, keep_ref, send_ref, inverse_ref, rng_ref, *rest,
):
    half = own_ref.shape[0]
    count, width = qkv_ref.shape[0], wq_ref.shape[1]
    pairs, heads, block = width // PAIR, width // HEAD_DIM, BLOCK
    share_refs = rest[:pairs]
    seg_row, seg_col, keys, values, scores, peaks, totals, mix, wq, wk, wv, sems = rest[pairs:]
    here, there = half_ref[0], 1 - half_ref[0]
    copies = start_all((wq_ref, wk_ref, wv_ref), (wq, wk, wv), sems)
    seg_row[...] = seg_ref[...].astype(F32)
    fill_columns(seg_row, seg_col)
    ids = seg_row[...]
    for g in range(count // block):
        first = ids_ref[0, g * block].astype(F32)
        last = ids_ref[0, (g + 1) * block - 1].astype(F32)
        rng_ref[0, g] = jnp.sum(jnp.where(ids < first, 1.0, 0.0)).astype(jnp.int32) // block
        rng_ref[1, g] = (jnp.sum(jnp.where(ids <= last, 1.0, 0.0)).astype(jnp.int32) + block - 1) // block
    qkv_ref[aligned(here, half), :] = own_ref[...]
    write_projection(x_ref[...], (wq, wk, wv), copies, qkv_ref.at[aligned(there, half), :])
    for p in range(pairs):
        stack_heads(qkv_ref[:, width + p * PAIR : width + (p + 1) * PAIR], keys.at[p], block)
        stack_heads(qkv_ref[:, 2 * width + p * PAIR : 2 * width + (p + 1) * PAIR], values.at[p], block)

    def query_block(g, carry):
        rows = aligned(g, block)
        low, high = rng_ref[0, g], rng_ref[1, g]
        peaks[...] = jnp.full(peaks.shape, MASKED, F32)
        totals[...] = jnp.zeros(totals.shape, F32)
        mix[...] = jnp.zeros(mix.shape, F32)

        def score_pass(j, c):
            both = aligned(j, 2 * block)
            same = seg_col[rows, 0:1] == seg_row[0:1, aligned(j, block)]
            for p in range(pairs):
                s2 = dot_nt(qkv_ref[rows, p * PAIR : (p + 1) * PAIR], keys[p, both, :])
                for a in range(2):
                    s = jnp.where(same, s2[:, a * block : (a + 1) * block], MASKED)
                    scores[p, :, aligned(2 * j + a, block)] = s
                    top = peaks[2 * p + a]
                    for t in range(block // 128):
                        top = jnp.maximum(top, s[:, t * 128 : (t + 1) * 128])
                    peaks[2 * p + a] = top
            return c

        lax.fori_loop(low, high, score_pass, 0)
        for h in range(heads):
            peaks[h] = jnp.broadcast_to(jnp.max(peaks[h], -1, keepdims=True), (block, 128))

        def mix_pass(j, c):
            both = aligned(j, 2 * block)
            for p in range(pairs):
                parts = []
                for a in range(2):
                    peak = jnp.concatenate([peaks[2 * p + a]] * (block // 128), 1)
                    e = jnp.exp2(scores[p, :, aligned(2 * j + a, block)] - peak)
                    total = totals[2 * p + a]
                    for t in range(block // 128):
                        total = total + e[:, t * 128 : (t + 1) * 128]
                    totals[2 * p + a] = total
                    parts.append(e.astype(BF16))
                shares = jnp.concatenate(parts, 1)
                share_refs[p][rows, both] = shares
                mix[:, p * PAIR : (p + 1) * PAIR] += dot(shares, values[p, both, :])
            return c

        lax.fori_loop(low, high, mix_pass, 0)
        lane = lax.broadcasted_iota(jnp.int32, (block, 128), 1)
        outs = []
        for p in range(pairs):
            sums = [jnp.sum(totals[h], -1, keepdims=True) for h in (2 * p, 2 * p + 1)]
            scale = jnp.where(lane < HEAD_DIM, 1.0 / sums[0], 1.0 / sums[1])
            inverse_ref[rows, p * PAIR : (p + 1) * PAIR] = scale
            outs.append((mix[:, p * PAIR : (p + 1) * PAIR] * scale).astype(BF16))
        result = jnp.concatenate(outs, 1)
        per_half = half // block

        @pl.when(g // per_half == here)
        def _():
            keep_ref[aligned(g % per_half, block), :] = result

        @pl.when(g // per_half != here)
        def _():
            send_ref[aligned(g % per_half, block), :] = result

        return carry

    lax.fori_loop(0, count // block, query_block, 0)


def attention(half_index, seg, own, x, wq, wk, wv):
    half, width = own.shape[0], wq.shape[1]
    count, pairs = 2 * half, width // PAIR
    return pl.pallas_call(
        attention_kernel,
        out_shape=(
            jax.ShapeDtypeStruct((count, 3 * width), BF16),
            jax.ShapeDtypeStruct((half, width), BF16),
            jax.ShapeDtypeStruct((half, width), BF16),
            jax.ShapeDtypeStruct((count, width), F32),
            jax.ShapeDtypeStruct((2, count // BLOCK), jnp.int32),
        )
        + (jax.ShapeDtypeStruct((count, 2 * count), BF16),) * pairs,
        in_specs=[SM, SM] + [VM] * 3 + [HB] * 3,
        out_specs=(VM,) * 4 + (SM,) + (VM,) * pairs,
        scratch_shapes=[
            pltpu.VMEM((1, count), F32),
            pltpu.VMEM((count, 128), F32),
            pltpu.VMEM((pairs, 2 * count, PAIR), BF16),
            pltpu.VMEM((pairs, 2 * count, PAIR), BF16),
            pltpu.VMEM((pairs, BLOCK, 2 * count), F32),
            pltpu.VMEM((2 * pairs, BLOCK, 128), F32),
            pltpu.VMEM((2 * pairs, BLOCK, 128), F32),
            pltpu.VMEM((BLOCK, width), F32),
        ]
        + [pltpu.VMEM(wq.shape, BF16)] * 3
        + [pltpu.SemaphoreType.DMA((3,))],
        compiler_params=pltpu.CompilerParams(vmem_limit_bytes=40 * MIB),
        cost_estimate=pl.CostEstimate(flops=10**10, bytes_accessed=8 * MIB, transcendentals=10**6),
        name="attention",
    )(half_index, seg, seg, own, x, wq, wk, wv)


def pair_grad_kernel(
    p, half_ref, rng_ref, qkv_ref, keep_ref, send_ref, own_ref, other_ref, inverse_ref, share_ref,
    dq_ref, dk_ref, dv_ref,
    keys, values, grad, turned_grad, turned_query, delta, dq, dk, dv,
):
    half = own_ref.shape[0]
    count, block = qkv_ref.shape[0], BLOCK
    width = keep_ref.shape[1]
    cols = slice(p * PAIR, (p + 1) * PAIR)
    here, there = half_ref[0], 1 - half_ref[0]
    lane = lax.broadcasted_iota(jnp.int32, (half, PAIR), 1)
    for which, mixed_ref, up_ref in ((here, keep_ref, own_ref), (there, send_ref, other_ref)):
        rows = aligned(which, half)
        scaled = (up_ref[:, cols].astype(F32) * inverse_ref[rows, cols]).astype(BF16)
        grad[rows, :] = scaled
        product = mixed_ref[:, cols].astype(F32) * scaled.astype(F32)
        for a in range(2):
            side = jnp.where(lane // HEAD_DIM == a, product, 0.0)
            delta[a, rows, :] = jnp.broadcast_to(jnp.sum(side, -1, keepdims=True), (half, PAIR))
    stack_heads(qkv_ref[:, width + p * PAIR : width + (p + 1) * PAIR], keys, block)
    stack_heads(qkv_ref[:, 2 * width + p * PAIR : 2 * width + (p + 1) * PAIR], values, block)
    turned_grad[...] = grad[...].T
    turned_query[...] = qkv_ref[:, cols].T
    dk[...] = jnp.zeros(dk.shape, F32)
    dv[...] = jnp.zeros(dv.shape, F32)

    def query_block(g, carry):
        rows = aligned(g, block)
        low, high = rng_ref[0, g], rng_ref[1, g]
        dq[...] = jnp.zeros(dq.shape, F32)

        def key_block(j, c):
            both = aligned(j, 2 * block)
            span = aligned(j, block)
            d2 = dot_nt(grad[rows, :], values[both, :])
            shares = share_ref[rows, both]
            slopes = []
            for a in range(2):
                side = slice(a * block, (a + 1) * block)
                level = jnp.concatenate([delta[a, rows, :]] * (block // 128), 1)
                slopes.append((shares[:, side].astype(F32) * (d2[:, side] - level)).astype(BF16))
            dq[...] += dot(jnp.concatenate(slopes, 1), keys[both, :])
            for a in range(2):
                head = slice(a * HEAD_DIM, (a + 1) * HEAD_DIM)
                dv[head, span] += dot(turned_grad[head, rows], shares[:, a * block : (a + 1) * block])
                dk[head, span] += dot(turned_query[head, rows], slopes[a])
            return c

        lax.fori_loop(low, high, key_block, 0)
        dq_ref[rows, :] = (dq[...] * HEAD_DIM**-0.5).astype(BF16)
        return carry

    lax.fori_loop(0, count // block, query_block, 0)
    dk_ref[...] = (dk[...] * LN2).T.astype(BF16)
    dv_ref[...] = dv[...].T.astype(BF16)


def pair_grad(p, half_index, rng, qkv, keep, send, own, other, inverse, shares):
    half = own.shape[0]
    count = 2 * half
    return pl.pallas_call(
        functools.partial(pair_grad_kernel, p),
        out_shape=(jax.ShapeDtypeStruct((count, PAIR), BF16),) * 3,
        in_specs=[SM, SM] + [VM] * 7,
        out_specs=(VM,) * 3,
        scratch_shapes=[pltpu.VMEM((2 * count, PAIR), BF16)] * 2
        + [
            pltpu.VMEM((count, PAIR), BF16),
            pltpu.VMEM((PAIR, count), BF16),
            pltpu.VMEM((PAIR, count), BF16),
            pltpu.VMEM((2, count, PAIR), F32),
            pltpu.VMEM((BLOCK, PAIR), F32),
            pltpu.VMEM((PAIR, count), F32),
            pltpu.VMEM((PAIR, count), F32),
        ],
        compiler_params=pltpu.CompilerParams(vmem_limit_bytes=16 * MIB),
        cost_estimate=pl.CostEstimate(flops=4 * 10**9, bytes_accessed=8 * MIB, transcendentals=0),
        name=f"pair_grad_{p}",
    )(half_index, rng, qkv, keep, send, own, other, inverse, shares)


def input_part(half_ref, flip, pieces, weights, half):
    which = 1 - half_ref[0] if flip else half_ref[0]
    rows = aligned(which, half)
    left = jnp.concatenate([piece[rows, :] for piece in pieces], 1)
    right = jnp.concatenate([weight[...] for weight in weights], 1)
    return dot_nt(left, right)


def away_kernel(half_ref, *refs):
    out_ref = refs[-1]
    out_ref[...] = input_part(half_ref, True, refs[:-4], refs[-4:-1], out_ref.shape[0]).astype(BF16)


def home_kernel(half_ref, first_ref, got_ref, *refs):
    out_ref = refs[-1]
    part = input_part(half_ref, False, refs[:-4], refs[-4:-1], out_ref.shape[0])
    out_ref[...] = (part + first_ref[...] + got_ref[...].astype(F32)).astype(BF16)


def input_call(kernel, half_index, extra, pieces, weights, name):
    half, features = pieces[0].shape[0] // 2, weights[0].shape[0]
    return pl.pallas_call(
        kernel,
        out_shape=jax.ShapeDtypeStruct((half, features), BF16),
        in_specs=[SM] + [VM] * (len(extra) + len(pieces) + len(weights)),
        out_specs=VM,
        compiler_params=pltpu.CompilerParams(vmem_limit_bytes=16 * MIB),
        cost_estimate=pl.CostEstimate(flops=10**9, bytes_accessed=6 * MIB, transcendentals=0),
        name=name,
    )(half_index, *extra, *pieces, *weights)


def gelu_both(v):
    part = 0.5 + 0.5 * lax.erf(v * ROOT_HALF)
    return v * part, part + v * jnp.exp(-0.5 * v * v) * ROOT_TWO_PI


def norm(values, gain, shift):
    mean = jnp.mean(values, -1, keepdims=True)
    centred = values - mean
    reciprocal = lax.rsqrt(jnp.mean(centred * centred, -1, keepdims=True) + EPS)
    normed = centred * reciprocal
    return normed * gain + shift, normed, reciprocal


def norm_grad(upstream, normed, reciprocal, gain):
    scaled = upstream * gain
    return reciprocal * (
        scaled - jnp.mean(scaled, -1, keepdims=True) - normed * jnp.mean(scaled * normed, -1, keepdims=True)
    )


def column_sum(values):
    return jnp.sum(values, 0, keepdims=True)


def middle_kernel(
    half_ref, x_ref, keep_ref, got_ref, up_ref,
    mdb_ref, mub_ref, ddb_ref, dub_ref, fg_ref, fs_ref, sg_ref, ss_ref,
    wo_hbm, wo2_hbm, md_hbm, mu_hbm, w1_hbm, w12_hbm, w2_hbm, w22_hbm, dd_hbm, du_hbm,
    act_hbm, first_ref, own_ref, away_ref, mine_ref, theirs_ref,
    wo_ref, wo2_ref, md_ref, mu_ref, w1_ref, w12_ref, w2_ref, w22_ref, dd_ref, du_ref,
    slope_ref, hidden_ref, normed_ref, act_ref, big_ref, small_ref, sems, act_sem,
):
    rows, features = x_ref.shape
    adapt = md_ref.shape[0]
    names = ("wo", "wo2", "md", "mu", "w1", "w2", "w12", "w22", "dd", "du")
    waits = dict(
        zip(
            names,
            start_all(
                (wo_hbm, wo2_hbm, md_hbm, mu_hbm, w1_hbm, w2_hbm, w12_hbm, w22_hbm, dd_hbm, du_hbm),
                (wo_ref, wo2_ref, md_ref, mu_ref, w1_ref, w2_ref, w12_ref, w22_ref, dd_ref, du_ref),
                sems,
            ),
        )
    )

    def vector(ref):
        return ref[...].astype(F32).reshape(1, -1)

    x = x_ref[...].astype(F32)
    waits["wo"].wait()
    attended = dot(keep_ref[...], wo_ref[...])
    waits["wo2"].wait()
    attended = attended + dot(got_ref[...], wo2_ref[...])
    attended_low = attended.astype(BF16)
    waits["md"].wait()
    waits["mu"].wait()
    mixer_active, mixer_slope = gelu_both(dot_nt(attended_low, md_ref[...]) + vector(mdb_ref))
    mixer_active = mixer_active.astype(BF16)
    mixer_out = dot(mixer_active, mu_ref[...]) + vector(mub_ref)
    hidden, normed_one, reciprocal_one = norm(x + attended + mixer_out, vector(fg_ref), vector(fs_ref))
    normed_ref[...] = normed_one
    hidden_ref[...] = hidden
    mixer_square = jnp.sum(column_sum(mixer_out * mixer_out), -1, keepdims=True)
    input_square = jnp.sum(column_sum(x * x), -1, keepdims=True)
    hidden_low = hidden.astype(BF16)
    chunk = 512
    units = w1_ref.shape[1]
    sides = ((w1_ref, w2_ref, "w1", "w2"), (w12_ref, w22_ref, "w12", "w22"))
    dense_in = jnp.zeros((rows, features), F32)
    for s, (win, wout, first, second) in enumerate(sides):
        waits[first].wait()
        waits[second].wait()
        for c in range(units // chunk):
            span = slice(c * chunk, (c + 1) * chunk)
            value, slope = gelu_both(dot(hidden_low, win[:, span]))
            slope_ref[:, s * units + c * chunk : s * units + (c + 1) * chunk] = slope.astype(BF16)
            dense_in = dense_in + dot(value.astype(BF16), wout[span, :])
    dense_low = dense_in.astype(BF16)
    waits["dd"].wait()
    waits["du"].wait()
    dense_active, dense_slope = gelu_both(dot_nt(dense_low, dd_ref[...]) + vector(ddb_ref))
    dense_active = dense_active.astype(BF16)
    dense_out = dot(dense_active, du_ref[...]) + vector(dub_ref)
    second_gain = vector(sg_ref)
    result, normed_two, reciprocal_two = norm(hidden_ref[...] + dense_in + dense_out, second_gain, vector(ss_ref))
    act_ref[...] = result.astype(BF16)
    act_copy = pltpu.make_async_copy(act_ref, act_hbm, act_sem)
    act_copy.start()
    dense_square = jnp.sum(column_sum(dense_out * dense_out), -1, keepdims=True)

    upstream = up_ref[...].astype(F32)
    small_ref[4:5, :] = column_sum(upstream * normed_two)
    small_ref[5:6, :] = column_sum(upstream)
    second_grad = norm_grad(upstream, normed_two, reciprocal_two, second_gain)
    dense_top = second_grad.astype(BF16)
    big_ref[3 * adapt : 4 * adapt, :] = dot_tn(dense_active, dense_top).astype(BF16)
    small_ref[1:2, :] = column_sum(dense_top.astype(F32))
    dense_mid = (dot_nt(dense_top, du_ref[...]) * dense_slope).astype(BF16)
    big_ref[2 * adapt : 3 * adapt, :] = dot_tn(dense_mid, dense_low).astype(BF16)
    dense_mid_sum = column_sum(dense_mid.astype(F32))
    dense_in_grad = (second_grad + dot(dense_mid, dd_ref[...])).astype(BF16)
    hidden_grad = second_grad
    for s, (win, wout, _, _) in enumerate(sides):
        for c in range(units // chunk):
            span = slice(c * chunk, (c + 1) * chunk)
            slope = slope_ref[:, s * units + c * chunk : s * units + (c + 1) * chunk].astype(F32)
            inner_grad = (dot_nt(dense_in_grad, wout[span, :]) * slope).astype(BF16)
            hidden_grad = hidden_grad + dot_nt(inner_grad, win[:, span])
    normed_one = normed_ref[...]
    small_ref[2:3, :] = column_sum(hidden_grad * normed_one)
    small_ref[3:4, :] = column_sum(hidden_grad)
    first_grad = norm_grad(hidden_grad, normed_one, reciprocal_one, vector(fg_ref))
    first_ref[...] = first_grad
    mixer_top = first_grad.astype(BF16)
    big_ref[adapt : 2 * adapt, :] = dot_tn(mixer_active, mixer_top).astype(BF16)
    small_ref[0:1, :] = column_sum(mixer_top.astype(F32))
    mixer_mid = (dot_nt(mixer_top, mu_ref[...]) * mixer_slope).astype(BF16)
    big_ref[0:adapt, :] = dot_tn(mixer_mid, attended_low).astype(BF16)
    mixer_mid_sum = column_sum(mixer_mid.astype(F32))
    attended_grad = (first_grad + dot(mixer_mid, md_ref[...])).astype(BF16)
    own_ref[...] = dot_nt(attended_grad, wo_ref[...]).astype(BF16)
    away_ref[...] = dot_nt(attended_grad, wo2_ref[...]).astype(BF16)
    lane = lax.broadcasted_iota(jnp.int32, (1, 128), 1)
    squares = jnp.where(lane == 0, mixer_square, jnp.where(lane == 1, dense_square, jnp.where(lane == 2, input_square, 0.0)))
    small_ref[6:7, :] = jnp.concatenate(
        [mixer_mid_sum, dense_mid_sum, squares, jnp.zeros((1, features - 2 * adapt - 128), F32)], 1
    )
    small_ref[7:8, :] = jnp.zeros((1, features), F32)
    tail = tail_of(small_ref[...])
    share = 2 * adapt
    for out_ref, which in ((mine_ref, half_ref[0]), (theirs_ref, 1 - half_ref[0])):
        out_ref[:share, :] = big_ref[aligned(which, share), :]
        out_ref[share:, :] = tail
    act_copy.wait()


def tail_of(vectors):
    high = vectors.astype(BF16)
    return jnp.concatenate([high, (vectors - high.astype(F32)).astype(BF16)], 0)


def vectors_of(tail):
    wide = tail.astype(F32)
    return wide[:8] + wide[8:]


def middle(half_index, x, keep, got, up, vectors, matrices):
    rows, features = x.shape
    width = keep.shape[1]
    adapt = matrices[2].shape[0]
    units = matrices[4].shape[1]
    packed = jax.ShapeDtypeStruct((2 * adapt + 16, features), BF16)
    return pl.pallas_call(
        middle_kernel,
        out_shape=(
            jax.ShapeDtypeStruct((rows, features), BF16),
            jax.ShapeDtypeStruct((rows, features), F32),
            jax.ShapeDtypeStruct((rows, width), BF16),
            jax.ShapeDtypeStruct((rows, width), BF16),
            packed,
            packed,
        ),
        in_specs=[SM] + [VM] * 12 + [HB] * 10,
        out_specs=(HB,) + (VM,) * 5,
        scratch_shapes=[pltpu.VMEM(m.shape, BF16) for m in matrices]
        + [
            pltpu.VMEM((rows, 2 * units), BF16),
            pltpu.VMEM((rows, features), F32),
            pltpu.VMEM((rows, features), F32),
            pltpu.VMEM((rows, features), BF16),
            pltpu.VMEM((4 * adapt, features), BF16),
            pltpu.VMEM((8, features), F32),
            pltpu.SemaphoreType.DMA((10,)),
            pltpu.SemaphoreType.DMA,
        ],
        compiler_params=pltpu.CompilerParams(vmem_limit_bytes=40 * MIB),
        cost_estimate=pl.CostEstimate(flops=2 * 10**10, bytes_accessed=16 * MIB, transcendentals=10**6),
        name="middle",
    )(half_index, x, keep, got, up, *vectors, *matrices)


def combine_kernel(held_ref, got_ref, out_ref):
    rows = held_ref.shape[0] - 16
    out_ref[:rows, :] = (held_ref[:rows, :].astype(F32) + got_ref[:rows, :].astype(F32)).astype(BF16)
    out_ref[rows:, :] = tail_of(vectors_of(held_ref[rows:, :]) + vectors_of(got_ref[rows:, :]))


def combine(held, got):
    return pl.pallas_call(
        combine_kernel,
        out_shape=jax.ShapeDtypeStruct(held.shape, BF16),
        in_specs=[VM] * 2,
        out_specs=VM,
        compiler_params=pltpu.CompilerParams(vmem_limit_bytes=4 * MIB),
        cost_estimate=pl.CostEstimate(flops=10**5, bytes_accessed=MIB, transcendentals=0),
        name="combine",
    )(held, got)


def finish_kernel(half_ref, held_ref, got_ref, md_ref, mu_ref, dd_ref, du_ref, vec_ref, bias_ref, ratio_ref):
    adapt = md_ref.shape[0]

    def write(first_ref, second_ref):
        md_ref[...] = first_ref[:adapt, :].astype(F32)
        mu_ref[...] = first_ref[adapt : 2 * adapt, :].astype(F32)
        dd_ref[...] = second_ref[:adapt, :].astype(F32)
        du_ref[...] = second_ref[adapt : 2 * adapt, :].astype(F32)

    @pl.when(half_ref[0] == 0)
    def _():
        write(held_ref, got_ref)

    @pl.when(half_ref[0] != 0)
    def _():
        write(got_ref, held_ref)

    vectors = vectors_of(held_ref[2 * adapt :, :])
    vec_ref[...] = vectors
    last = vectors[6:7, :]
    bias_ref[0:1, :] = last[:, :adapt]
    bias_ref[1:2, :] = last[:, adapt : 2 * adapt]
    squares = last[:, 2 * adapt : 2 * adapt + 128]
    lane = lax.broadcasted_iota(jnp.int32, (1, 128), 1)
    base = jnp.sum(jnp.where(lane == 2, squares, 0.0), -1, keepdims=True)
    ratio_ref[...] = jnp.sqrt(squares / base)


def finish(half_index, held, got, adapt):
    features = held.shape[1]
    matrix = jax.ShapeDtypeStruct((adapt, features), F32)
    return pl.pallas_call(
        finish_kernel,
        out_shape=(matrix,) * 4
        + (
            jax.ShapeDtypeStruct((8, features), F32),
            jax.ShapeDtypeStruct((2, adapt), F32),
            jax.ShapeDtypeStruct((1, 128), F32),
        ),
        in_specs=[SM, VM, VM],
        out_specs=(VM,) * 7,
        compiler_params=pltpu.CompilerParams(vmem_limit_bytes=4 * MIB),
        name="finish",
    )(half_index, held, got)


def swap_cores(value):
    return lax.ppermute(value, "mp", [(0, 1), (1, 0)])


def tie(*values):
    return lax.optimization_barrier(values)


def per_device(
    tokens, segment_ids, query_weight, key_weight, value_weight, output_weight, inner_weight, outer_weight,
    mixer_down, mixer_down_bias, mixer_up, mixer_up_bias, dense_down, dense_down_bias, dense_up, dense_up_bias,
    first_gain, first_shift, second_gain, second_shift, output_grad,
):
    half_index = lax.axis_index("mp").astype(jnp.int32).reshape(1)
    devices = lax.axis_size("dp")
    adapt = mixer_down.shape[1]
    other_tokens = swap_cores(tokens)
    own = project(tokens, query_weight, key_weight, value_weight)
    other_tokens, output_late, inner_late, outer_late = tie(other_tokens, output_weight, inner_weight, outer_weight)
    other_output = swap_cores(output_late)
    other_inner = swap_cores(inner_late)
    other_outer = swap_cores(outer_late)
    qkv, keep, send, inverse, rng, *shares = attention(
        half_index, segment_ids, own, other_tokens, query_weight, key_weight, value_weight
    )
    got = swap_cores(send)
    vectors = (
        mixer_down_bias, mixer_up_bias, dense_down_bias, dense_up_bias, first_gain, first_shift, second_gain, second_shift,
    )
    matrices = (
        output_weight, other_output, mixer_down.T, mixer_up,
        inner_weight, other_inner, outer_weight, other_outer, dense_down.T, dense_up,
    )
    result, first_grad, own_grad, away_grad, mine, theirs = middle(
        half_index, tokens, keep, got, output_grad, vectors, matrices
    )
    got_grad = swap_cores(away_grad)
    packed = combine(mine, swap_cores(theirs))

    steps = []
    while 2 ** len(steps) < devices:
        steps.append(2 ** len(steps))
    steps.reverse()
    pairs = len(shares)
    grads = []
    away = None
    weights = (query_weight, key_weight, value_weight)
    for n, step in enumerate(steps):
        arriving = lax.ppermute(packed, "dp", [(i, i ^ step) for i in range(devices)])
        if n < pairs:
            got_grad, packed = tie(got_grad, packed)
            parts = pair_grad(n, half_index, rng, qkv, keep, send, own_grad, got_grad, inverse, shares[n])
            arriving, *parts = tie(arriving, *parts)
            grads.append(parts)
        elif n == pairs:
            pieces = [grads[p][i] for i in range(3) for p in range(pairs)]
            away = swap_cores(input_call(away_kernel, half_index, (), pieces, weights, "away"))
            input_grad = input_call(home_kernel, half_index, (first_grad, away), pieces, weights, "home")
            arriving, input_grad = tie(arriving, input_grad)
        packed = combine(packed, arriving)
    md, mu, dd, du, vec, bias, ratio = finish(half_index, packed, swap_cores(packed), adapt)
    return (
        result, input_grad, md.T, bias[0], mu, vec[0], dd.T, bias[1], du, vec[1], vec[2], vec[3], vec[4], vec[5], ratio[0, :2],
    )


def solution(mesh):
    tokens = P(("dp", "mp"), None)
    columns, rows, whole = P(None, "mp"), P("mp", None), P()
    return jax.shard_map(
        per_device,
        mesh=mesh,
        in_specs=(tokens, P("dp", None), columns, columns, columns, rows, columns, rows) + (whole,) * 12 + (tokens,),
        out_specs=(tokens, tokens) + (whole,) * 13,
        check_vma=False,
    )
```

```python
import functools

import jax
import jax.numpy as jnp
from jax import lax
from jax.experimental import pallas as pl
from jax.experimental.pallas import tpu as pltpu
from jax.sharding import PartitionSpec as P

F32 = jnp.float32
BF16 = jnp.bfloat16
HEAD_DIM = 64
PAIR = 2 * HEAD_DIM
EPS = 1e-12
LOG2E = 1.4426950408889634
LN2 = 0.6931471805599453
ROOT_HALF = 0.7071067811865476
ROOT_TWO_PI = 0.3989422804014327
MASKED = -1e30
BLOCK = 256
MIB = 1 << 20

VM = pl.BlockSpec(memory_space=pltpu.VMEM)
SM = pl.BlockSpec(memory_space=pltpu.SMEM)
HB = pl.BlockSpec(memory_space=pltpu.HBM)


def dot(left, right):
    return jnp.dot(left, right, preferred_element_type=F32)


def dot_nt(left, right):
    return lax.dot_general(left, right, (((1,), (1,)), ((), ())), preferred_element_type=F32)


def dot_tn(left, right):
    return lax.dot_general(left, right, (((0,), (0,)), ((), ())), preferred_element_type=F32)


def aligned(index, size):
    return pl.ds(pl.multiple_of(index * size, size), size)


def split_pair(pair):
    lane = lax.broadcasted_iota(jnp.int32, pair.shape, 1)
    zero = jnp.zeros_like(pair)
    return jnp.where(lane < HEAD_DIM, pair, zero), jnp.where(lane < HEAD_DIM, zero, pair)


def stack_heads(source, target, block):
    first, second = split_pair(source)
    for t in range(source.shape[0] // block):
        target[pl.ds(2 * t * block, block), :] = first[t * block : (t + 1) * block]
        target[pl.ds((2 * t + 1) * block, block), :] = second[t * block : (t + 1) * block]


def fill_columns(row_ref, column_ref):
    for t in range(row_ref.shape[1] // 128):
        span = slice(t * 128, (t + 1) * 128)
        column_ref[span, :] = jnp.broadcast_to(row_ref[0:1, span], (128, 128)).T


def start_all(sources, buffers, sems):
    copies = [pltpu.make_async_copy(src, dst, sems.at[i]) for i, (src, dst) in enumerate(zip(sources, buffers))]
    for copy in copies:
        copy.start()
    return copies


def write_projection(x, weights, copies, out_ref):
    width = weights[0].shape[1]
    for i, weight in enumerate(weights):
        if copies:
            copies[i].wait()
        part = dot(x, weight[...])
        if i == 0:
            part = part * (HEAD_DIM**-0.5 * LOG2E)
        out_ref[:, i * width : (i + 1) * width] = part.astype(BF16)


def project_kernel(x_ref, wq_ref, wk_ref, wv_ref, out_ref, x_buf, wq, wk, wv, sems):
    copies = start_all((x_ref, wq_ref, wk_ref, wv_ref), (x_buf, wq, wk, wv), sems)
    copies[0].wait()
    write_projection(x_buf[...], (wq, wk, wv), copies[1:], out_ref)


def project(x, wq, wk, wv):
    rows, width = x.shape[0], wq.shape[1]
    return pl.pallas_call(
        project_kernel,
        out_shape=jax.ShapeDtypeStruct((rows, 3 * width), BF16),
        in_specs=[HB] * 4,
        out_specs=VM,
        scratch_shapes=[pltpu.VMEM(v.shape, BF16) for v in (x, wq, wk, wv)] + [pltpu.SemaphoreType.DMA((4,))],
        compiler_params=pltpu.CompilerParams(vmem_limit_bytes=12 * MIB),
        cost_estimate=pl.CostEstimate(flops=2 * rows * x.shape[1] * 3 * width, bytes_accessed=5 * MIB, transcendentals=0),
        name="project",
    )(x, wq, wk, wv)


def attention_kernel(
    half_ref, ids_ref, seg_ref, own_ref, x_ref, wq_ref, wk_ref, wv_ref,
    kv_ref, queries_ref, keep_ref, send_ref, factor_ref, rng_ref, *rest,
):
    half = own_ref.shape[0]
    count, width = kv_ref.shape[0], wq_ref.shape[1]
    pairs, block = width // PAIR, BLOCK
    share_refs = rest[:pairs]
    seg_row, seg_col, fresh, turned, bias, peaks, totals, mix, wq, wk, wv, sems = rest[pairs:]
    here, there = half_ref[0], 1 - half_ref[0]
    copies = start_all((wq_ref, wk_ref, wv_ref), (wq, wk, wv), sems)
    seg_row[...] = seg_ref[...].astype(F32)
    fill_columns(seg_row, seg_col)
    ids = seg_row[...]
    for g in range(count // block):
        first = ids_ref[0, g * block].astype(F32)
        last = ids_ref[0, (g + 1) * block - 1].astype(F32)
        rng_ref[0, g] = jnp.sum(jnp.where(ids < first, 1.0, 0.0)).astype(jnp.int32) // block
        rng_ref[1, g] = (jnp.sum(jnp.where(ids <= last, 1.0, 0.0)).astype(jnp.int32) + block - 1) // block
    write_projection(x_ref[...], (wq, wk, wv), copies, fresh)
    for source, which in ((own_ref, here), (fresh, there)):
        kv_ref[aligned(which, half), :] = source[:, width:]
        for p in range(pairs):
            cols = slice(p * PAIR, (p + 1) * PAIR)
            stack_heads(source[:, cols], queries_ref.at[p, aligned(which, 2 * half), :], block)
            turned[cols, aligned(which, half)] = source[:, 2 * width + p * PAIR : 2 * width + (p + 1) * PAIR].T

    def query_block(g, carry):
        rows, both = aligned(g, block), aligned(g, 2 * block)
        peaks[...] = jnp.full(peaks.shape, MASKED, F32)
        totals[...] = jnp.zeros(totals.shape, F32)
        mix[...] = jnp.zeros(mix.shape, F32)
        factor_ref[:, :, both] = jnp.full((pairs, 8, 2 * block), MASKED, F32)

        def key_block(j, c):
            span = aligned(j, block)
            bias[...] = jnp.where(seg_col[span, 0:1] == seg_row[0:1, rows], 0.0, MASKED)
            for p in range(pairs):
                s = dot_nt(kv_ref[span, p * PAIR : (p + 1) * PAIR], queries_ref[p, both, :])
                hide = bias[...]
                s = s + jnp.concatenate([hide, hide], 1)
                old = peaks[p]
                top = jnp.maximum(old, jnp.max(s, 0, keepdims=True))
                e = jnp.exp2(s - top)
                drop = jnp.exp2(old - top)
                peaks[p] = top
                totals[p] = totals[p] * drop + jnp.sum(e, 0, keepdims=True)
                factor_ref[p, pl.ds(j, 1), both] = top
                e = e.astype(BF16)
                share_refs[p][span, both] = e
                for a in range(2):
                    side = slice(a * block, (a + 1) * block)
                    head = slice(p * PAIR + a * HEAD_DIM, p * PAIR + (a + 1) * HEAD_DIM)
                    mix[head, :] = mix[head, :] * drop[:, side] + dot(turned[head, span], e[:, side])
            return c

        lax.fori_loop(rng_ref[0, g], rng_ref[1, g], key_block, 0)
        outs = []
        for p in range(pairs):
            inverse = 1.0 / totals[p]
            factor_ref[p, :, both] = jnp.exp2(factor_ref[p, :, both] - peaks[p]) * inverse
            for a in range(2):
                head = slice(p * PAIR + a * HEAD_DIM, p * PAIR + (a + 1) * HEAD_DIM)
                outs.append((mix[head, :] * inverse[:, a * block : (a + 1) * block]).astype(BF16))
        result = jnp.concatenate(outs, 0).T
        per_half = half // block

        @pl.when(g // per_half == here)
        def _():
            keep_ref[aligned(g % per_half, block), :] = result

        @pl.when(g // per_half != here)
        def _():
            send_ref[aligned(g % per_half, block), :] = result

        return carry

    lax.fori_loop(0, count // block, query_block, 0)


def attention(half_index, seg, own, x, wq, wk, wv):
    half, width = own.shape[0], wq.shape[1]
    count, pairs = 2 * half, width // PAIR
    return pl.pallas_call(
        attention_kernel,
        out_shape=(
            jax.ShapeDtypeStruct((count, 2 * width), BF16),
            jax.ShapeDtypeStruct((pairs, 2 * count, PAIR), BF16),
            jax.ShapeDtypeStruct((half, width), BF16),
            jax.ShapeDtypeStruct((half, width), BF16),
            jax.ShapeDtypeStruct((pairs, 8, 2 * count), F32),
            jax.ShapeDtypeStruct((2, count // BLOCK), jnp.int32),
        )
        + (jax.ShapeDtypeStruct((count, 2 * count), BF16),) * pairs,
        in_specs=[SM, SM] + [VM] * 3 + [HB] * 3,
        out_specs=(VM,) * 5 + (SM,) + (VM,) * pairs,
        scratch_shapes=[
            pltpu.VMEM((1, count), F32),
            pltpu.VMEM((count, 128), F32),
            pltpu.VMEM((half, 3 * width), BF16),
            pltpu.VMEM((width, count), BF16),
            pltpu.VMEM((BLOCK, BLOCK), F32),
            pltpu.VMEM((pairs, 1, 2 * BLOCK), F32),
            pltpu.VMEM((pairs, 1, 2 * BLOCK), F32),
            pltpu.VMEM((width, BLOCK), F32),
        ]
        + [pltpu.VMEM(wq.shape, BF16)] * 3
        + [pltpu.SemaphoreType.DMA((3,))],
        compiler_params=pltpu.CompilerParams(vmem_limit_bytes=16 * MIB),
        cost_estimate=pl.CostEstimate(flops=10**10, bytes_accessed=8 * MIB, transcendentals=10**6),
        name="attention",
    )(half_index, seg, seg, own, x, wq, wk, wv)


def pair_grad_kernel(
    p, half_ref, rng_ref, kv_ref, queries_ref, keep_ref, send_ref, own_ref, other_ref, factor_ref, share_ref,
    dq_ref, dk_ref, dv_ref,
    grads, turned, delta, dq, dk, dv,
):
    half, width = keep_ref.shape
    count, block = kv_ref.shape[0], BLOCK
    cols = slice(p * PAIR, (p + 1) * PAIR)
    here, there = half_ref[0], 1 - half_ref[0]
    row = lax.broadcasted_iota(jnp.int32, (8, PAIR), 0)
    column = lax.broadcasted_iota(jnp.int32, (8, PAIR), 1)
    pick = jnp.where(column // HEAD_DIM == row, 1.0, 0.0).astype(BF16)
    for which, mixed_ref, up_ref in ((here, keep_ref, own_ref), (there, send_ref, other_ref)):
        product = mixed_ref[:, cols].astype(F32) * up_ref[:, cols].astype(F32)
        high = product.astype(BF16)
        low = (product - high.astype(F32)).astype(BF16)
        delta[:, aligned(which, half)] = dot_nt(pick, high) + dot_nt(pick, low)
        stack_heads(up_ref[:, cols], grads.at[aligned(which, 2 * half), :], block)
    turned[...] = kv_ref[:, cols].T
    dk[...] = jnp.zeros(dk.shape, F32)
    dv[...] = jnp.zeros(dv.shape, F32)

    def query_block(g, carry):
        rows, both = aligned(g, block), aligned(g, 2 * block)
        dq[...] = jnp.zeros(dq.shape, F32)

        def key_block(j, c):
            span = aligned(j, block)
            d = dot_nt(kv_ref[span, width + p * PAIR : width + (p + 1) * PAIR], grads[both, :])
            shares = share_ref[span, both].astype(F32) * factor_ref[p, pl.ds(j, 1), both]
            level = jnp.concatenate([delta[0:1, rows], delta[1:2, rows]], 1)
            slopes = (shares * (d - level)).astype(BF16)
            dv[span, :] += dot(shares.astype(BF16), grads[both, :])
            dk[span, :] += dot(slopes, queries_ref[p, both, :])
            for a in range(2):
                head = slice(a * HEAD_DIM, (a + 1) * HEAD_DIM)
                dq[head, :] += dot(turned[head, span], slopes[:, a * block : (a + 1) * block])
            return c

        lax.fori_loop(rng_ref[0, g], rng_ref[1, g], key_block, 0)
        dq_ref[rows, :] = (dq[...] * HEAD_DIM**-0.5).astype(BF16).T
        return carry

    lax.fori_loop(0, count // block, query_block, 0)
    dk_ref[...] = (dk[...] * LN2).astype(BF16)
    dv_ref[...] = dv[...].astype(BF16)


def pair_grad(p, half_index, rng, kv, queries, keep, send, own, other, factor, shares):
    count = kv.shape[0]
    return pl.pallas_call(
        functools.partial(pair_grad_kernel, p),
        out_shape=(jax.ShapeDtypeStruct((count, PAIR), BF16),) * 3,
        in_specs=[SM, SM] + [VM] * 8,
        out_specs=(VM,) * 3,
        scratch_shapes=[
            pltpu.VMEM((2 * count, PAIR), BF16),
            pltpu.VMEM((PAIR, count), BF16),
            pltpu.VMEM((8, count), F32),
            pltpu.VMEM((PAIR, BLOCK), F32),
            pltpu.VMEM((count, PAIR), F32),
            pltpu.VMEM((count, PAIR), F32),
        ],
        compiler_params=pltpu.CompilerParams(vmem_limit_bytes=12 * MIB),
        cost_estimate=pl.CostEstimate(flops=4 * 10**9, bytes_accessed=8 * MIB, transcendentals=0),
        name=f"pair_grad_{p}",
    )(half_index, rng, kv, queries, keep, send, own, other, factor, shares)


def input_part(half_ref, flip, pieces, weights, half):
    which = 1 - half_ref[0] if flip else half_ref[0]
    rows = aligned(which, half)
    left = jnp.concatenate([piece[rows, :] for piece in pieces], 1)
    right = jnp.concatenate([weight[...] for weight in weights], 1)
    return dot_nt(left, right)


def away_kernel(half_ref, *refs):
    out_ref = refs[-1]
    out_ref[...] = input_part(half_ref, True, refs[:-4], refs[-4:-1], out_ref.shape[0]).astype(BF16)


def home_kernel(half_ref, first_ref, got_ref, *refs):
    out_ref = refs[-1]
    part = input_part(half_ref, False, refs[:-4], refs[-4:-1], out_ref.shape[0])
    out_ref[...] = (part + first_ref[...] + got_ref[...].astype(F32)).astype(BF16)


def input_call(kernel, half_index, extra, pieces, weights, name):
    half, features = pieces[0].shape[0] // 2, weights[0].shape[0]
    return pl.pallas_call(
        kernel,
        out_shape=jax.ShapeDtypeStruct((half, features), BF16),
        in_specs=[SM] + [VM] * (len(extra) + len(pieces) + len(weights)),
        out_specs=VM,
        compiler_params=pltpu.CompilerParams(vmem_limit_bytes=16 * MIB),
        cost_estimate=pl.CostEstimate(flops=10**9, bytes_accessed=6 * MIB, transcendentals=0),
        name=name,
    )(half_index, *extra, *pieces, *weights)


def gelu_both(v):
    part = 0.5 + 0.5 * lax.erf(v * ROOT_HALF)
    return v * part, part + v * jnp.exp(-0.5 * v * v) * ROOT_TWO_PI


def norm(values, gain, shift):
    mean = jnp.mean(values, -1, keepdims=True)
    centred = values - mean
    reciprocal = lax.rsqrt(jnp.mean(centred * centred, -1, keepdims=True) + EPS)
    normed = centred * reciprocal
    return normed * gain + shift, normed, reciprocal


def norm_grad(upstream, normed, reciprocal, gain):
    scaled = upstream * gain
    return reciprocal * (
        scaled - jnp.mean(scaled, -1, keepdims=True) - normed * jnp.mean(scaled * normed, -1, keepdims=True)
    )


def column_sum(values):
    return jnp.sum(values, 0, keepdims=True)


def middle_kernel(
    half_ref, x_ref, keep_ref, got_ref, up_ref,
    mdb_ref, mub_ref, ddb_ref, dub_ref, fg_ref, fs_ref, sg_ref, ss_ref,
    wo_hbm, wo2_hbm, md_hbm, mu_hbm, w1_hbm, w12_hbm, w2_hbm, w22_hbm, dd_hbm, du_hbm,
    act_hbm, first_ref, own_ref, away_ref, mine_ref, theirs_ref,
    wo_ref, wo2_ref, md_ref, mu_ref, w1_ref, w12_ref, w2_ref, w22_ref, dd_ref, du_ref,
    slope_ref, hidden_ref, normed_ref, act_ref, big_ref, small_ref, sems, act_sem,
):
    rows, features = x_ref.shape
    adapt = md_ref.shape[0]
    names = ("wo", "wo2", "md", "mu", "w1", "w2", "w12", "w22", "dd", "du")
    waits = dict(
        zip(
            names,
            start_all(
                (wo_hbm, wo2_hbm, md_hbm, mu_hbm, w1_hbm, w2_hbm, w12_hbm, w22_hbm, dd_hbm, du_hbm),
                (wo_ref, wo2_ref, md_ref, mu_ref, w1_ref, w2_ref, w12_ref, w22_ref, dd_ref, du_ref),
                sems,
            ),
        )
    )

    def vector(ref):
        return ref[...].astype(F32).reshape(1, -1)

    x = x_ref[...].astype(F32)
    waits["wo"].wait()
    attended = dot(keep_ref[...], wo_ref[...])
    waits["wo2"].wait()
    attended = attended + dot(got_ref[...], wo2_ref[...])
    attended_low = attended.astype(BF16)
    waits["md"].wait()
    waits["mu"].wait()
    mixer_active, mixer_slope = gelu_both(dot_nt(attended_low, md_ref[...]) + vector(mdb_ref))
    mixer_active = mixer_active.astype(BF16)
    mixer_out = dot(mixer_active, mu_ref[...]) + vector(mub_ref)
    hidden, normed_one, reciprocal_one = norm(x + attended + mixer_out, vector(fg_ref), vector(fs_ref))
    normed_ref[...] = normed_one
    hidden_ref[...] = hidden
    mixer_square = jnp.sum(column_sum(mixer_out * mixer_out), -1, keepdims=True)
    input_square = jnp.sum(column_sum(x * x), -1, keepdims=True)
    hidden_low = hidden.astype(BF16)
    chunk = 512
    units = w1_ref.shape[1]
    sides = ((w1_ref, w2_ref, "w1", "w2"), (w12_ref, w22_ref, "w12", "w22"))
    dense_in = jnp.zeros((rows, features), F32)
    for s, (win, wout, first, second) in enumerate(sides):
        waits[first].wait()
        waits[second].wait()
        for c in range(units // chunk):
            span = slice(c * chunk, (c + 1) * chunk)
            value, slope = gelu_both(dot(hidden_low, win[:, span]))
            slope_ref[:, s * units + c * chunk : s * units + (c + 1) * chunk] = slope.astype(BF16)
            dense_in = dense_in + dot(value.astype(BF16), wout[span, :])
    dense_low = dense_in.astype(BF16)
    waits["dd"].wait()
    waits["du"].wait()
    dense_active, dense_slope = gelu_both(dot_nt(dense_low, dd_ref[...]) + vector(ddb_ref))
    dense_active = dense_active.astype(BF16)
    dense_out = dot(dense_active, du_ref[...]) + vector(dub_ref)
    second_gain = vector(sg_ref)
    result, normed_two, reciprocal_two = norm(hidden_ref[...] + dense_in + dense_out, second_gain, vector(ss_ref))
    act_ref[...] = result.astype(BF16)
    act_copy = pltpu.make_async_copy(act_ref, act_hbm, act_sem)
    act_copy.start()
    dense_square = jnp.sum(column_sum(dense_out * dense_out), -1, keepdims=True)

    upstream = up_ref[...].astype(F32)
    small_ref[4:5, :] = column_sum(upstream * normed_two)
    small_ref[5:6, :] = column_sum(upstream)
    second_grad = norm_grad(upstream, normed_two, reciprocal_two, second_gain)
    dense_top = second_grad.astype(BF16)
    big_ref[3 * adapt : 4 * adapt, :] = dot_tn(dense_active, dense_top).astype(BF16)
    small_ref[1:2, :] = column_sum(dense_top.astype(F32))
    dense_mid = (dot_nt(dense_top, du_ref[...]) * dense_slope).astype(BF16)
    big_ref[2 * adapt : 3 * adapt, :] = dot_tn(dense_mid, dense_low).astype(BF16)
    dense_mid_sum = column_sum(dense_mid.astype(F32))
    dense_in_grad = (second_grad + dot(dense_mid, dd_ref[...])).astype(BF16)
    hidden_grad = second_grad
    for s, (win, wout, _, _) in enumerate(sides):
        for c in range(units // chunk):
            span = slice(c * chunk, (c + 1) * chunk)
            slope = slope_ref[:, s * units + c * chunk : s * units + (c + 1) * chunk].astype(F32)
            inner_grad = (dot_nt(dense_in_grad, wout[span, :]) * slope).astype(BF16)
            hidden_grad = hidden_grad + dot_nt(inner_grad, win[:, span])
    normed_one = normed_ref[...]
    small_ref[2:3, :] = column_sum(hidden_grad * normed_one)
    small_ref[3:4, :] = column_sum(hidden_grad)
    first_grad = norm_grad(hidden_grad, normed_one, reciprocal_one, vector(fg_ref))
    first_ref[...] = first_grad
    mixer_top = first_grad.astype(BF16)
    big_ref[adapt : 2 * adapt, :] = dot_tn(mixer_active, mixer_top).astype(BF16)
    small_ref[0:1, :] = column_sum(mixer_top.astype(F32))
    mixer_mid = (dot_nt(mixer_top, mu_ref[...]) * mixer_slope).astype(BF16)
    big_ref[0:adapt, :] = dot_tn(mixer_mid, attended_low).astype(BF16)
    mixer_mid_sum = column_sum(mixer_mid.astype(F32))
    attended_grad = (first_grad + dot(mixer_mid, md_ref[...])).astype(BF16)
    own_ref[...] = dot_nt(attended_grad, wo_ref[...]).astype(BF16)
    away_ref[...] = dot_nt(attended_grad, wo2_ref[...]).astype(BF16)
    lane = lax.broadcasted_iota(jnp.int32, (1, 128), 1)
    squares = jnp.where(lane == 0, mixer_square, jnp.where(lane == 1, dense_square, jnp.where(lane == 2, input_square, 0.0)))
    small_ref[6:7, :] = jnp.concatenate(
        [mixer_mid_sum, dense_mid_sum, squares, jnp.zeros((1, features - 2 * adapt - 128), F32)], 1
    )
    small_ref[7:8, :] = jnp.zeros((1, features), F32)
    tail = tail_of(small_ref[...])
    share = 2 * adapt
    for out_ref, which in ((mine_ref, half_ref[0]), (theirs_ref, 1 - half_ref[0])):
        out_ref[:share, :] = big_ref[aligned(which, share), :]
        out_ref[share:, :] = tail
    act_copy.wait()


def tail_of(vectors):
    high = vectors.astype(BF16)
    return jnp.concatenate([high, (vectors - high.astype(F32)).astype(BF16)], 0)


def vectors_of(tail):
    wide = tail.astype(F32)
    return wide[:8] + wide[8:]


def middle(half_index, x, keep, got, up, vectors, matrices):
    rows, features = x.shape
    width = keep.shape[1]
    adapt = matrices[2].shape[0]
    units = matrices[4].shape[1]
    packed = jax.ShapeDtypeStruct((2 * adapt + 16, features), BF16)
    return pl.pallas_call(
        middle_kernel,
        out_shape=(
            jax.ShapeDtypeStruct((rows, features), BF16),
            jax.ShapeDtypeStruct((rows, features), F32),
            jax.ShapeDtypeStruct((rows, width), BF16),
            jax.ShapeDtypeStruct((rows, width), BF16),
            packed,
            packed,
        ),
        in_specs=[SM] + [VM] * 12 + [HB] * 10,
        out_specs=(HB,) + (VM,) * 5,
        scratch_shapes=[pltpu.VMEM(m.shape, BF16) for m in matrices]
        + [
            pltpu.VMEM((rows, 2 * units), BF16),
            pltpu.VMEM((rows, features), F32),
            pltpu.VMEM((rows, features), F32),
            pltpu.VMEM((rows, features), BF16),
            pltpu.VMEM((4 * adapt, features), BF16),
            pltpu.VMEM((8, features), F32),
            pltpu.SemaphoreType.DMA((10,)),
            pltpu.SemaphoreType.DMA,
        ],
        compiler_params=pltpu.CompilerParams(vmem_limit_bytes=40 * MIB),
        cost_estimate=pl.CostEstimate(flops=2 * 10**10, bytes_accessed=16 * MIB, transcendentals=10**6),
        name="middle",
    )(half_index, x, keep, got, up, *vectors, *matrices)


def combine_kernel(held_ref, got_ref, out_ref):
    rows = held_ref.shape[0] - 16
    out_ref[:rows, :] = (held_ref[:rows, :].astype(F32) + got_ref[:rows, :].astype(F32)).astype(BF16)
    out_ref[rows:, :] = tail_of(vectors_of(held_ref[rows:, :]) + vectors_of(got_ref[rows:, :]))


def combine(held, got):
    return pl.pallas_call(
        combine_kernel,
        out_shape=jax.ShapeDtypeStruct(held.shape, BF16),
        in_specs=[VM] * 2,
        out_specs=VM,
        compiler_params=pltpu.CompilerParams(vmem_limit_bytes=4 * MIB),
        cost_estimate=pl.CostEstimate(flops=10**5, bytes_accessed=MIB, transcendentals=0),
        name="combine",
    )(held, got)


def finish_kernel(half_ref, held_ref, got_ref, md_ref, mu_ref, dd_ref, du_ref, vec_ref, bias_ref, ratio_ref):
    adapt = md_ref.shape[0]

    def write(first_ref, second_ref):
        md_ref[...] = first_ref[:adapt, :].astype(F32)
        mu_ref[...] = first_ref[adapt : 2 * adapt, :].astype(F32)
        dd_ref[...] = second_ref[:adapt, :].astype(F32)
        du_ref[...] = second_ref[adapt : 2 * adapt, :].astype(F32)

    @pl.when(half_ref[0] == 0)
    def _():
        write(held_ref, got_ref)

    @pl.when(half_ref[0] != 0)
    def _():
        write(got_ref, held_ref)

    vectors = vectors_of(held_ref[2 * adapt :, :])
    vec_ref[...] = vectors
    last = vectors[6:7, :]
    bias_ref[0:1, :] = last[:, :adapt]
    bias_ref[1:2, :] = last[:, adapt : 2 * adapt]
    squares = last[:, 2 * adapt : 2 * adapt + 128]
    lane = lax.broadcasted_iota(jnp.int32, (1, 128), 1)
    base = jnp.sum(jnp.where(lane == 2, squares, 0.0), -1, keepdims=True)
    ratio_ref[...] = jnp.sqrt(squares / base)


def finish(half_index, held, got, adapt):
    features = held.shape[1]
    matrix = jax.ShapeDtypeStruct((adapt, features), F32)
    return pl.pallas_call(
        finish_kernel,
        out_shape=(matrix,) * 4
        + (
            jax.ShapeDtypeStruct((8, features), F32),
            jax.ShapeDtypeStruct((2, adapt), F32),
            jax.ShapeDtypeStruct((1, 128), F32),
        ),
        in_specs=[SM, VM, VM],
        out_specs=(VM,) * 7,
        compiler_params=pltpu.CompilerParams(vmem_limit_bytes=4 * MIB),
        name="finish",
    )(half_index, held, got)


def swap_cores(value):
    return lax.ppermute(value, "mp", [(0, 1), (1, 0)])


def tie(*values):
    return lax.optimization_barrier(values)


def per_device(
    tokens, segment_ids, query_weight, key_weight, value_weight, output_weight, inner_weight, outer_weight,
    mixer_down, mixer_down_bias, mixer_up, mixer_up_bias, dense_down, dense_down_bias, dense_up, dense_up_bias,
    first_gain, first_shift, second_gain, second_shift, output_grad,
):
    half_index = lax.axis_index("mp").astype(jnp.int32).reshape(1)
    devices = lax.axis_size("dp")
    adapt = mixer_down.shape[1]
    other_tokens = swap_cores(tokens)
    own = project(tokens, query_weight, key_weight, value_weight)
    other_tokens, output_late, inner_late, outer_late = tie(other_tokens, output_weight, inner_weight, outer_weight)
    other_output = swap_cores(output_late)
    other_inner = swap_cores(inner_late)
    other_outer = swap_cores(outer_late)
    kv, queries, keep, send, factor, rng, *shares = attention(
        half_index, segment_ids, own, other_tokens, query_weight, key_weight, value_weight
    )
    got = swap_cores(send)
    vectors = (
        mixer_down_bias, mixer_up_bias, dense_down_bias, dense_up_bias, first_gain, first_shift, second_gain, second_shift,
    )
    matrices = (
        output_weight, other_output, mixer_down.T, mixer_up,
        inner_weight, other_inner, outer_weight, other_outer, dense_down.T, dense_up,
    )
    result, first_grad, own_grad, away_grad, mine, theirs = middle(
        half_index, tokens, keep, got, output_grad, vectors, matrices
    )
    got_grad = swap_cores(away_grad)
    packed = combine(mine, swap_cores(theirs))

    steps = []
    while 2 ** len(steps) < devices:
        steps.append(2 ** len(steps))
    steps.reverse()
    pairs = len(shares)
    grads = []
    away = None
    weights = (query_weight, key_weight, value_weight)
    for n, step in enumerate(steps):
        arriving = lax.ppermute(packed, "dp", [(i, i ^ step) for i in range(devices)])
        if n < pairs:
            got_grad, packed = tie(got_grad, packed)
            parts = pair_grad(n, half_index, rng, kv, queries, keep, send, own_grad, got_grad, factor, shares[n])
            arriving, *parts = tie(arriving, *parts)
            grads.append(parts)
        elif n == pairs:
            pieces = [grads[p][i] for i in range(3) for p in range(pairs)]
            away = swap_cores(input_call(away_kernel, half_index, (), pieces, weights, "away"))
            input_grad = input_call(home_kernel, half_index, (first_grad, away), pieces, weights, "home")
            arriving, input_grad = tie(arriving, input_grad)
        packed = combine(packed, arriving)
    md, mu, dd, du, vec, bias, ratio = finish(half_index, packed, swap_cores(packed), adapt)
    return (
        result, input_grad, md.T, bias[0], mu, vec[0], dd.T, bias[1], du, vec[1], vec[2], vec[3], vec[4], vec[5], ratio[0, :2],
    )


def solution(mesh):
    tokens = P(("dp", "mp"), None)
    columns, rows, whole = P(None, "mp"), P("mp", None), P()
    return jax.shard_map(
        per_device,
        mesh=mesh,
        in_specs=(tokens, P("dp", None), columns, columns, columns, rows, columns, rows) + (whole,) * 12 + (tokens,),
        out_specs=(tokens, tokens) + (whole,) * 13,
        check_vma=False,
    )
```

```python
import functools

import jax
import jax.numpy as jnp
from jax import lax
from jax.experimental import pallas as pl
from jax.experimental.pallas import tpu as pltpu
from jax.sharding import PartitionSpec as P

F32 = jnp.float32
BF16 = jnp.bfloat16
HEAD_DIM = 64
PAIR = 2 * HEAD_DIM
EPS = 1e-12
LOG2E = 1.4426950408889634
LN2 = 0.6931471805599453
ROOT_HALF = 0.7071067811865476
ROOT_TWO_PI = 0.3989422804014327
MASKED = -(2.0**100)
LARGEST = 2.0**100
SMALLEST = 2.0**-60
TURNED = 80
BLOCK = 256
MIB = 1 << 20

VM = pl.BlockSpec(memory_space=pltpu.VMEM)
SM = pl.BlockSpec(memory_space=pltpu.SMEM)
HB = pl.BlockSpec(memory_space=pltpu.HBM)


def dot(left, right):
    return jnp.dot(left, right, preferred_element_type=F32)


def dot_nt(left, right):
    return lax.dot_general(left, right, (((1,), (1,)), ((), ())), preferred_element_type=F32)


def dot_tn(left, right):
    return lax.dot_general(left, right, (((0,), (0,)), ((), ())), preferred_element_type=F32)


def aligned(index, size):
    return pl.ds(pl.multiple_of(index * size, size), size)


def split_pair(pair):
    lane = lax.broadcasted_iota(jnp.int32, pair.shape, 1)
    zero = jnp.zeros_like(pair)
    return jnp.where(lane < HEAD_DIM, pair, zero), jnp.where(lane < HEAD_DIM, zero, pair)


def stack_heads(source, target, block):
    first, second = split_pair(source)
    for t in range(source.shape[0] // block):
        target[pl.ds(2 * t * block, block), :] = first[t * block : (t + 1) * block]
        target[pl.ds((2 * t + 1) * block, block), :] = second[t * block : (t + 1) * block]


def stack_heads_across(source, target, block):
    row = lax.broadcasted_iota(jnp.int32, source.shape, 0)
    zero = jnp.zeros_like(source)
    first = jnp.where(row < HEAD_DIM, source, zero)
    second = jnp.where(row < HEAD_DIM, zero, source)
    for t in range(source.shape[1] // block):
        target[:, 2 * t * block : (2 * t + 1) * block] = first[:, t * block : (t + 1) * block]
        target[:, (2 * t + 1) * block : (2 * t + 2) * block] = second[:, t * block : (t + 1) * block]


def in_hbm(value):
    return pltpu.with_memory_space_constraint(value, pltpu.HBM)


def start_all(sources, buffers, sems):
    copies = [pltpu.make_async_copy(src, dst, sems.at[i]) for i, (src, dst) in enumerate(zip(sources, buffers))]
    for copy in copies:
        copy.start()
    return copies


def write_projection(which, x, weights, copies, kv_ref, queries_ref, across_ref, turned_ref):
    rows, width = x.shape[0], weights[0].shape[1]
    pairs = width // PAIR
    if copies:
        copies[0].wait()
    queries = (dot(x, weights[0][...]) * (HEAD_DIM**-0.5 * LOG2E)).astype(BF16)
    for p in range(pairs):
        pair = queries[:, p * PAIR : (p + 1) * PAIR]
        stack_heads(pair, queries_ref.at[p, aligned(which, 2 * rows), :], BLOCK)
        stack_heads_across(pair.T, across_ref.at[p, :, aligned(which, 2 * rows)], BLOCK)
    if copies:
        copies[1].wait()
    kv_ref[aligned(which, rows), :width] = dot(x, weights[1][...]).astype(BF16)
    if copies:
        copies[2].wait()
    values = dot(x, weights[2][...]).astype(BF16)
    kv_ref[aligned(which, rows), width:] = values
    ones = jnp.ones((TURNED - HEAD_DIM, rows), BF16)
    for p in range(pairs):
        turned = values[:, p * PAIR : (p + 1) * PAIR].T
        for a in range(2):
            base = (2 * p + a) * TURNED
            turned_ref[base : base + HEAD_DIM, aligned(which, rows)] = turned[a * HEAD_DIM : (a + 1) * HEAD_DIM]
            turned_ref[base + HEAD_DIM : base + TURNED, aligned(which, rows)] = ones


def is_shift(lane):
    return (lane == 63) | (lane == 95) | (lane == 127)


def project_kernel(
    half_ref, ids_ref, seg_ref, x_ref, wq_ref, wk_ref, wv_ref,
    kv_ref, queries_ref, across_ref, turned_ref, item_ref, hide_ref, rng_ref,
    x_buf, wq, wk, wv, sems,
):
    copies = start_all((x_ref, wq_ref, wk_ref, wv_ref), (x_buf, wq, wk, wv), sems)
    count, block = kv_ref.shape[0], BLOCK
    ids = seg_ref[...].astype(F32)
    for g in range(count // block):
        first = ids_ref[0, g * block].astype(F32)
        last = ids_ref[0, (g + 1) * block - 1].astype(F32)
        rng_ref[0, g] = jnp.sum(jnp.where(ids < first, 1.0, 0.0)).astype(jnp.int32) // block
        rng_ref[1, g] = (jnp.sum(jnp.where(ids <= last, 1.0, 0.0)).astype(jnp.int32) + block - 1) // block
    lane = lax.broadcasted_iota(jnp.int32, (128, 128), 1)
    for t in range(count // 128):
        same = jnp.broadcast_to(ids[:, t * 128 : (t + 1) * 128], (128, 128)).T == lane.astype(F32)
        item_ref[t * 128 : (t + 1) * 128, :] = jnp.where(same | is_shift(lane), 1.0, 0.0).astype(BF16)
    row = lax.broadcasted_iota(jnp.int32, (128, block), 0)
    for t in range(count // block):
        same = row.astype(F32) == ids[:, t * block : (t + 1) * block]
        hide = jnp.where(same | is_shift(row), 0.0, MASKED).astype(BF16)
        for a in range(2):
            hide_ref[:, (2 * t + a) * block : (2 * t + a + 1) * block] = hide
    copies[0].wait()
    write_projection(half_ref[0], x_buf[...], (wq, wk, wv), copies[1:], kv_ref, queries_ref, across_ref, turned_ref)


def project(half_index, seg, x, wq, wk, wv):
    rows, width = x.shape[0], wq.shape[1]
    count, pairs = 2 * rows, width // PAIR
    return pl.pallas_call(
        project_kernel,
        out_shape=(
            jax.ShapeDtypeStruct((count, 2 * width), BF16),
            jax.ShapeDtypeStruct((pairs, 2 * count, PAIR), BF16),
            jax.ShapeDtypeStruct((pairs, PAIR, 2 * count), BF16),
            jax.ShapeDtypeStruct((2 * pairs * TURNED, count), BF16),
            jax.ShapeDtypeStruct((count, 128), BF16),
            jax.ShapeDtypeStruct((128, 2 * count), BF16),
            jax.ShapeDtypeStruct((2, count // BLOCK), jnp.int32),
        ),
        in_specs=[SM, SM, VM] + [HB] * 4,
        out_specs=(VM,) * 6 + (SM,),
        scratch_shapes=[pltpu.VMEM(v.shape, BF16) for v in (x, wq, wk, wv)] + [pltpu.SemaphoreType.DMA((4,))],
        compiler_params=pltpu.CompilerParams(vmem_limit_bytes=16 * MIB),
        cost_estimate=pl.CostEstimate(flops=2 * rows * x.shape[1] * 3 * width, bytes_accessed=5 * MIB, transcendentals=0),
        name="project",
    )(half_index, seg, seg, *map(in_hbm, (x, wq, wk, wv)))


def attention_kernel(
    half_ref, rng_ref, x_ref, item_ref, hide_ref, wq_ref, wk_ref, wv_ref, kv_in, queries_in, across_in, turned_in,
    kv_ref, queries_ref, keep_ref, send_ref, inverse_ref, *rest,
):
    half = x_ref.shape[0]
    count, width = kv_ref.shape[0], wq_ref.shape[1]
    pairs, block = width // PAIR, BLOCK
    share_refs = rest[:pairs]
    across, turned, mix, shifted, peaks = rest[pairs:]
    here, there = half_ref[0], 1 - half_ref[0]
    turned[:, aligned(here, half)] = turned_in[:, aligned(here, half)]
    across[:, :, aligned(here, 2 * half)] = across_in[:, :, aligned(here, 2 * half)]
    kv_ref[aligned(here, half), :] = kv_in[aligned(here, half), :]
    queries_ref[:, aligned(here, 2 * half), :] = queries_in[:, aligned(here, 2 * half), :]
    write_projection(there, x_ref[...], (wq_ref, wk_ref, wv_ref), (), kv_ref, queries_ref, across, turned)

    def scores(p, span, both, hide):
        keys = jnp.concatenate([kv_ref[span, p * PAIR : (p + 1) * PAIR], item_ref[span, :]], 1)
        return dot(keys, jnp.concatenate([across[p, :, both], hide], 0))

    def query_block(g, carry):
        rows, both = aligned(g, block), aligned(g, 2 * block)
        low, high = rng_ref[0, g], rng_ref[1, g]

        def mix_all(hide_of):
            mix[...] = jnp.zeros(mix.shape, F32)

            def key_block(j, c):
                span = aligned(j, block)
                for p in range(pairs):
                    e = jnp.exp2(scores(p, span, both, hide_of(p))).astype(BF16)
                    share_refs[p][span, both] = e
                    for a in range(2):
                        head = slice((2 * p + a) * TURNED, (2 * p + a + 1) * TURNED)
                        mix[head, :] += dot(turned[head, span], e[:, a * block : (a + 1) * block])
                return c

            lax.fori_loop(low, high, key_block, 0)

        mix_all(lambda p: hide_ref[:, both])
        total_rows = [h * TURNED + HEAD_DIM for h in range(2 * pairs)]
        sums = jnp.concatenate([mix[r : r + 8, :] for r in total_rows], 0)
        fine = jnp.where((sums <= LARGEST) & (sums >= SMALLEST), 0.0, 1.0)

        @pl.when(jnp.max(fine) > 0.0)
        def _():
            peaks[...] = jnp.full(peaks.shape, MASKED, F32)

            def peak_block(j, c):
                for p in range(pairs):
                    s = scores(p, aligned(j, block), both, hide_ref[:, both])
                    peaks[p] = jnp.maximum(peaks[p], jnp.max(s, 0, keepdims=True))
                return c

            lax.fori_loop(low, high, peak_block, 0)
            row = lax.broadcasted_iota(jnp.int32, (128, 2 * block), 0)
            hide = hide_ref[:, both].astype(F32)
            for p in range(pairs):
                peak = peaks[p]
                first = peak.astype(BF16).astype(F32)
                second = (peak - first).astype(BF16).astype(F32)
                third = peak - first - second
                parts = jnp.where(row < 64, first, jnp.where(row < 96, second, third))
                shifted[p] = jnp.where(is_shift(row), -parts, hide).astype(BF16)
            mix_all(lambda p: shifted[p])

        outs = []
        for p in range(pairs):
            scales = []
            for a in range(2):
                base = (2 * p + a) * TURNED
                scale = jnp.broadcast_to(1.0 / mix[base + HEAD_DIM : base + HEAD_DIM + 1, :], (HEAD_DIM, block))
                outs.append((mix[base : base + HEAD_DIM, :] * scale).astype(BF16))
                scales.append(scale)
            inverse_ref[rows, p * PAIR : (p + 1) * PAIR] = jnp.concatenate(scales, 0).T
        result = jnp.concatenate(outs, 0).T
        per_half = half // block

        @pl.when(g // per_half == here)
        def _():
            keep_ref[aligned(g % per_half, block), :] = result

        @pl.when(g // per_half != here)
        def _():
            send_ref[aligned(g % per_half, block), :] = result

        return carry

    lax.fori_loop(0, count // block, query_block, 0)


def attention(half_index, rng, x, item, hide, wq, wk, wv, kv, queries, across, turned):
    half, width = x.shape[0], wq.shape[1]
    count, pairs = 2 * half, width // PAIR
    like = lambda v: jax.ShapeDtypeStruct(v.shape, v.dtype)
    return pl.pallas_call(
        attention_kernel,
        out_shape=(
            like(kv),
            like(queries),
            jax.ShapeDtypeStruct((half, width), BF16),
            jax.ShapeDtypeStruct((half, width), BF16),
            jax.ShapeDtypeStruct((count, width), F32),
        )
        + (jax.ShapeDtypeStruct((count, 2 * count), BF16),) * pairs,
        in_specs=[SM, SM] + [VM] * 10,
        out_specs=(VM,) * (5 + pairs),
        scratch_shapes=[
            pltpu.VMEM(across.shape, BF16),
            pltpu.VMEM(turned.shape, BF16),
            pltpu.VMEM((2 * pairs * TURNED, BLOCK), F32),
            pltpu.VMEM((pairs, 128, 2 * BLOCK), BF16),
            pltpu.VMEM((pairs, 1, 2 * BLOCK), F32),
        ],
        compiler_params=pltpu.CompilerParams(vmem_limit_bytes=12 * MIB),
        cost_estimate=pl.CostEstimate(flops=10**10, bytes_accessed=8 * MIB, transcendentals=10**6),
        name="attention",
    )(half_index, rng, x, item, hide, wq, wk, wv, kv, queries, across, turned)


def pair_grad_kernel(
    p, half_ref, rng_ref, kv_ref, queries_ref, keep_ref, send_ref, own_ref, other_ref, inverse_ref, share_ref,
    dq_ref, dk_ref, dv_ref,
    grads, across, turned, delta, dq, dk, dv,
):
    half, width = keep_ref.shape
    count, block = kv_ref.shape[0], BLOCK
    cols = slice(p * PAIR, (p + 1) * PAIR)
    here, there = half_ref[0], 1 - half_ref[0]
    row = lax.broadcasted_iota(jnp.int32, (8, PAIR), 0)
    column = lax.broadcasted_iota(jnp.int32, (8, PAIR), 1)
    pick = jnp.where(column // HEAD_DIM == row, 1.0, 0.0).astype(BF16)
    for which, mixed_ref, up_ref in ((here, keep_ref, own_ref), (there, send_ref, other_ref)):
        scaled = (up_ref[:, cols].astype(F32) * inverse_ref[aligned(which, half), cols]).astype(BF16)
        product = mixed_ref[:, cols].astype(F32) * scaled.astype(F32)
        high = product.astype(BF16)
        low = (product - high.astype(F32)).astype(BF16)
        delta[:, aligned(which, half)] = dot_nt(pick, high) + dot_nt(pick, low)
        stack_heads(scaled, grads.at[aligned(which, 2 * half), :], block)
        stack_heads_across(scaled.T, across.at[:, aligned(which, 2 * half)], block)
    turned[...] = kv_ref[:, cols].T
    dk[...] = jnp.zeros(dk.shape, F32)
    dv[...] = jnp.zeros(dv.shape, F32)

    def query_block(g, carry):
        rows, both = aligned(g, block), aligned(g, 2 * block)
        dq[...] = jnp.zeros(dq.shape, F32)
        level = jnp.concatenate([delta[0:1, rows], delta[1:2, rows]], 1)

        def key_block(j, c):
            span = aligned(j, block)
            d = dot(kv_ref[span, width + p * PAIR : width + (p + 1) * PAIR], across[:, both])
            shares = share_ref[span, both]
            slopes = (shares.astype(F32) * (d - level)).astype(BF16)
            dv[span, :] += dot(shares, grads[both, :])
            dk[span, :] += dot(slopes, queries_ref[p, both, :])
            for a in range(2):
                head = slice(a * HEAD_DIM, (a + 1) * HEAD_DIM)
                dq[head, :] += dot(turned[head, span], slopes[:, a * block : (a + 1) * block])
            return c

        lax.fori_loop(rng_ref[0, g], rng_ref[1, g], key_block, 0)
        dq_ref[rows, :] = (dq[...] * HEAD_DIM**-0.5).astype(BF16).T
        return carry

    lax.fori_loop(0, count // block, query_block, 0)
    dk_ref[...] = (dk[...] * LN2).astype(BF16)
    dv_ref[...] = dv[...].astype(BF16)


def pair_grad(p, half_index, rng, kv, queries, keep, send, own, other, inverse, shares):
    count = kv.shape[0]
    return pl.pallas_call(
        functools.partial(pair_grad_kernel, p),
        out_shape=(jax.ShapeDtypeStruct((count, PAIR), BF16),) * 3,
        in_specs=[SM, SM] + [VM] * 8,
        out_specs=(VM,) * 3,
        scratch_shapes=[
            pltpu.VMEM((2 * count, PAIR), BF16),
            pltpu.VMEM((PAIR, 2 * count), BF16),
            pltpu.VMEM((PAIR, count), BF16),
            pltpu.VMEM((8, count), F32),
            pltpu.VMEM((PAIR, BLOCK), F32),
            pltpu.VMEM((count, PAIR), F32),
            pltpu.VMEM((count, PAIR), F32),
        ],
        compiler_params=pltpu.CompilerParams(vmem_limit_bytes=12 * MIB),
        cost_estimate=pl.CostEstimate(flops=4 * 10**9, bytes_accessed=8 * MIB, transcendentals=0),
        name=f"pair_grad_{p}",
    )(half_index, rng, kv, queries, keep, send, own, other, inverse, shares)


def input_part(half_ref, flip, pieces, weights, half):
    which = 1 - half_ref[0] if flip else half_ref[0]
    rows = aligned(which, half)
    left = jnp.concatenate([piece[rows, :] for piece in pieces], 1)
    right = jnp.concatenate([weight[...] for weight in weights], 1)
    return dot_nt(left, right)


def away_kernel(half_ref, *refs):
    out_ref = refs[-1]
    out_ref[...] = input_part(half_ref, True, refs[:-4], refs[-4:-1], out_ref.shape[0]).astype(BF16)


def home_kernel(half_ref, first_ref, got_ref, *refs):
    out_ref = refs[-1]
    part = input_part(half_ref, False, refs[:-4], refs[-4:-1], out_ref.shape[0])
    out_ref[...] = (part + first_ref[...] + got_ref[...].astype(F32)).astype(BF16)


def input_call(kernel, half_index, extra, pieces, weights, name):
    half, features = pieces[0].shape[0] // 2, weights[0].shape[0]
    return pl.pallas_call(
        kernel,
        out_shape=jax.ShapeDtypeStruct((half, features), BF16),
        in_specs=[SM] + [VM] * (len(extra) + len(pieces) + len(weights)),
        out_specs=VM,
        compiler_params=pltpu.CompilerParams(vmem_limit_bytes=16 * MIB),
        cost_estimate=pl.CostEstimate(flops=10**9, bytes_accessed=6 * MIB, transcendentals=0),
        name=name,
    )(half_index, *extra, *pieces, *weights)


def gelu_both(v):
    part = 0.5 + 0.5 * lax.erf(v * ROOT_HALF)
    return v * part, part + v * jnp.exp(-0.5 * v * v) * ROOT_TWO_PI


def norm(values, gain, shift):
    mean = jnp.mean(values, -1, keepdims=True)
    centred = values - mean
    reciprocal = lax.rsqrt(jnp.mean(centred * centred, -1, keepdims=True) + EPS)
    normed = centred * reciprocal
    return normed * gain + shift, normed, reciprocal


def norm_grad(upstream, normed, reciprocal, gain):
    scaled = upstream * gain
    return reciprocal * (
        scaled - jnp.mean(scaled, -1, keepdims=True) - normed * jnp.mean(scaled * normed, -1, keepdims=True)
    )


def column_sum(values):
    return jnp.sum(values, 0, keepdims=True)


def middle_kernel(
    half_ref, x_ref, keep_ref, got_ref, up_ref,
    mdb_ref, mub_ref, ddb_ref, dub_ref, fg_ref, fs_ref, sg_ref, ss_ref,
    wo_hbm, wo2_hbm, md_hbm, mu_hbm, w1_hbm, w12_hbm, w2_hbm, w22_hbm, dd_hbm, du_hbm,
    act_hbm, first_ref, own_ref, away_ref, mine_ref, theirs_ref,
    wo_ref, wo2_ref, md_ref, mu_ref, w1_ref, w12_ref, w2_ref, w22_ref, dd_ref, du_ref,
    slope_ref, hidden_ref, normed_ref, act_ref, big_ref, small_ref, sems, act_sem,
):
    rows, features = x_ref.shape
    adapt = md_ref.shape[0]
    names = ("wo", "wo2", "md", "mu", "w1", "w2", "w12", "w22", "dd", "du")
    waits = dict(
        zip(
            names,
            start_all(
                (wo_hbm, wo2_hbm, md_hbm, mu_hbm, w1_hbm, w2_hbm, w12_hbm, w22_hbm, dd_hbm, du_hbm),
                (wo_ref, wo2_ref, md_ref, mu_ref, w1_ref, w2_ref, w12_ref, w22_ref, dd_ref, du_ref),
                sems,
            ),
        )
    )

    def vector(ref):
        return ref[...].astype(F32).reshape(1, -1)

    x = x_ref[...].astype(F32)
    waits["wo"].wait()
    attended = dot(keep_ref[...], wo_ref[...])
    waits["wo2"].wait()
    attended = attended + dot(got_ref[...], wo2_ref[...])
    attended_low = attended.astype(BF16)
    waits["md"].wait()
    waits["mu"].wait()
    mixer_active, mixer_slope = gelu_both(dot_nt(attended_low, md_ref[...]) + vector(mdb_ref))
    mixer_active = mixer_active.astype(BF16)
    mixer_out = dot(mixer_active, mu_ref[...]) + vector(mub_ref)
    hidden, normed_one, reciprocal_one = norm(x + attended + mixer_out, vector(fg_ref), vector(fs_ref))
    normed_ref[...] = normed_one
    hidden_ref[...] = hidden
    mixer_square = jnp.sum(column_sum(mixer_out * mixer_out), -1, keepdims=True)
    input_square = jnp.sum(column_sum(x * x), -1, keepdims=True)
    hidden_low = hidden.astype(BF16)
    chunk = 512
    units = w1_ref.shape[1]
    sides = ((w1_ref, w2_ref, "w1", "w2"), (w12_ref, w22_ref, "w12", "w22"))
    dense_in = jnp.zeros((rows, features), F32)
    for s, (win, wout, first, second) in enumerate(sides):
        waits[first].wait()
        waits[second].wait()
        for c in range(units // chunk):
            span = slice(c * chunk, (c + 1) * chunk)
            value, slope = gelu_both(dot(hidden_low, win[:, span]))
            slope_ref[:, s * units + c * chunk : s * units + (c + 1) * chunk] = slope.astype(BF16)
            dense_in = dense_in + dot(value.astype(BF16), wout[span, :])
    dense_low = dense_in.astype(BF16)
    waits["dd"].wait()
    waits["du"].wait()
    dense_active, dense_slope = gelu_both(dot_nt(dense_low, dd_ref[...]) + vector(ddb_ref))
    dense_active = dense_active.astype(BF16)
    dense_out = dot(dense_active, du_ref[...]) + vector(dub_ref)
    second_gain = vector(sg_ref)
    result, normed_two, reciprocal_two = norm(hidden_ref[...] + dense_in + dense_out, second_gain, vector(ss_ref))
    act_ref[...] = result.astype(BF16)
    act_copy = pltpu.make_async_copy(act_ref, act_hbm, act_sem)
    act_copy.start()
    dense_square = jnp.sum(column_sum(dense_out * dense_out), -1, keepdims=True)

    upstream = up_ref[...].astype(F32)
    small_ref[4:5, :] = column_sum(upstream * normed_two)
    small_ref[5:6, :] = column_sum(upstream)
    second_grad = norm_grad(upstream, normed_two, reciprocal_two, second_gain)
    dense_top = second_grad.astype(BF16)
    big_ref[3 * adapt : 4 * adapt, :] = dot_tn(dense_active, dense_top).astype(BF16)
    small_ref[1:2, :] = column_sum(dense_top.astype(F32))
    dense_mid = (dot_nt(dense_top, du_ref[...]) * dense_slope).astype(BF16)
    big_ref[2 * adapt : 3 * adapt, :] = dot_tn(dense_mid, dense_low).astype(BF16)
    dense_mid_sum = column_sum(dense_mid.astype(F32))
    dense_in_grad = (second_grad + dot(dense_mid, dd_ref[...])).astype(BF16)
    hidden_grad = second_grad
    for s, (win, wout, _, _) in enumerate(sides):
        for c in range(units // chunk):
            span = slice(c * chunk, (c + 1) * chunk)
            slope = slope_ref[:, s * units + c * chunk : s * units + (c + 1) * chunk].astype(F32)
            inner_grad = (dot_nt(dense_in_grad, wout[span, :]) * slope).astype(BF16)
            hidden_grad = hidden_grad + dot_nt(inner_grad, win[:, span])
    normed_one = normed_ref[...]
    small_ref[2:3, :] = column_sum(hidden_grad * normed_one)
    small_ref[3:4, :] = column_sum(hidden_grad)
    first_grad = norm_grad(hidden_grad, normed_one, reciprocal_one, vector(fg_ref))
    first_ref[...] = first_grad
    mixer_top = first_grad.astype(BF16)
    big_ref[adapt : 2 * adapt, :] = dot_tn(mixer_active, mixer_top).astype(BF16)
    small_ref[0:1, :] = column_sum(mixer_top.astype(F32))
    mixer_mid = (dot_nt(mixer_top, mu_ref[...]) * mixer_slope).astype(BF16)
    big_ref[0:adapt, :] = dot_tn(mixer_mid, attended_low).astype(BF16)
    mixer_mid_sum = column_sum(mixer_mid.astype(F32))
    attended_grad = (first_grad + dot(mixer_mid, md_ref[...])).astype(BF16)
    own_ref[...] = dot_nt(attended_grad, wo_ref[...]).astype(BF16)
    away_ref[...] = dot_nt(attended_grad, wo2_ref[...]).astype(BF16)
    lane = lax.broadcasted_iota(jnp.int32, (1, 128), 1)
    squares = jnp.where(lane == 0, mixer_square, jnp.where(lane == 1, dense_square, jnp.where(lane == 2, input_square, 0.0)))
    small_ref[6:7, :] = jnp.concatenate(
        [mixer_mid_sum, dense_mid_sum, squares, jnp.zeros((1, features - 2 * adapt - 128), F32)], 1
    )
    small_ref[7:8, :] = jnp.zeros((1, features), F32)
    tail = tail_of(small_ref[...])
    share = 2 * adapt
    for out_ref, which in ((mine_ref, half_ref[0]), (theirs_ref, 1 - half_ref[0])):
        out_ref[:share, :] = big_ref[aligned(which, share), :]
        out_ref[share:, :] = tail
    act_copy.wait()


def tail_of(vectors):
    high = vectors.astype(BF16)
    return jnp.concatenate([high, (vectors - high.astype(F32)).astype(BF16)], 0)


def vectors_of(tail):
    wide = tail.astype(F32)
    return wide[:8] + wide[8:]


def middle(half_index, x, keep, got, up, vectors, matrices):
    rows, features = x.shape
    width = keep.shape[1]
    adapt = matrices[2].shape[0]
    units = matrices[4].shape[1]
    packed = jax.ShapeDtypeStruct((2 * adapt + 16, features), BF16)
    return pl.pallas_call(
        middle_kernel,
        out_shape=(
            jax.ShapeDtypeStruct((rows, features), BF16),
            jax.ShapeDtypeStruct((rows, features), F32),
            jax.ShapeDtypeStruct((rows, width), BF16),
            jax.ShapeDtypeStruct((rows, width), BF16),
            packed,
            packed,
        ),
        in_specs=[SM] + [VM] * 12 + [HB] * 10,
        out_specs=(HB,) + (VM,) * 5,
        scratch_shapes=[pltpu.VMEM(m.shape, BF16) for m in matrices]
        + [
            pltpu.VMEM((rows, 2 * units), BF16),
            pltpu.VMEM((rows, features), F32),
            pltpu.VMEM((rows, features), F32),
            pltpu.VMEM((rows, features), BF16),
            pltpu.VMEM((4 * adapt, features), BF16),
            pltpu.VMEM((8, features), F32),
            pltpu.SemaphoreType.DMA((10,)),
            pltpu.SemaphoreType.DMA,
        ],
        compiler_params=pltpu.CompilerParams(vmem_limit_bytes=36 * MIB),
        cost_estimate=pl.CostEstimate(flops=2 * 10**10, bytes_accessed=16 * MIB, transcendentals=10**6),
        name="middle",
    )(half_index, x, keep, got, up, *vectors, *map(in_hbm, matrices))


def combine_kernel(held_ref, got_ref, out_ref):
    rows = held_ref.shape[0] - 16
    out_ref[:rows, :] = (held_ref[:rows, :].astype(F32) + got_ref[:rows, :].astype(F32)).astype(BF16)
    out_ref[rows:, :] = tail_of(vectors_of(held_ref[rows:, :]) + vectors_of(got_ref[rows:, :]))


def combine(held, got):
    return pl.pallas_call(
        combine_kernel,
        out_shape=jax.ShapeDtypeStruct(held.shape, BF16),
        in_specs=[VM] * 2,
        out_specs=VM,
        compiler_params=pltpu.CompilerParams(vmem_limit_bytes=4 * MIB),
        cost_estimate=pl.CostEstimate(flops=10**5, bytes_accessed=MIB, transcendentals=0),
        name="combine",
    )(held, got)


def finish_kernel(half_ref, held_ref, got_ref, md_ref, mu_ref, dd_ref, du_ref, vec_ref, bias_ref, ratio_ref):
    adapt = md_ref.shape[0]

    def write(first_ref, second_ref):
        md_ref[...] = first_ref[:adapt, :].astype(F32)
        mu_ref[...] = first_ref[adapt : 2 * adapt, :].astype(F32)
        dd_ref[...] = second_ref[:adapt, :].astype(F32)
        du_ref[...] = second_ref[adapt : 2 * adapt, :].astype(F32)

    @pl.when(half_ref[0] == 0)
    def _():
        write(held_ref, got_ref)

    @pl.when(half_ref[0] != 0)
    def _():
        write(got_ref, held_ref)

    vectors = vectors_of(held_ref[2 * adapt :, :])
    vec_ref[...] = vectors
    last = vectors[6:7, :]
    bias_ref[0:1, :] = last[:, :adapt]
    bias_ref[1:2, :] = last[:, adapt : 2 * adapt]
    squares = last[:, 2 * adapt : 2 * adapt + 128]
    lane = lax.broadcasted_iota(jnp.int32, (1, 128), 1)
    base = jnp.sum(jnp.where(lane == 2, squares, 0.0), -1, keepdims=True)
    ratio_ref[...] = jnp.sqrt(squares / base)


def finish(half_index, held, got, adapt):
    features = held.shape[1]
    matrix = jax.ShapeDtypeStruct((adapt, features), F32)
    return pl.pallas_call(
        finish_kernel,
        out_shape=(matrix,) * 4
        + (
            jax.ShapeDtypeStruct((8, features), F32),
            jax.ShapeDtypeStruct((2, adapt), F32),
            jax.ShapeDtypeStruct((1, 128), F32),
        ),
        in_specs=[SM, VM, VM],
        out_specs=(VM,) * 7,
        compiler_params=pltpu.CompilerParams(vmem_limit_bytes=4 * MIB),
        name="finish",
    )(half_index, held, got)


def swap_cores(value):
    return lax.ppermute(value, "mp", [(0, 1), (1, 0)])


def tie(*values):
    return lax.optimization_barrier(values)


def per_device(
    tokens, segment_ids, query_weight, key_weight, value_weight, output_weight, inner_weight, outer_weight,
    mixer_down, mixer_down_bias, mixer_up, mixer_up_bias, dense_down, dense_down_bias, dense_up, dense_up_bias,
    first_gain, first_shift, second_gain, second_shift, output_grad,
):
    half_index = lax.axis_index("mp").astype(jnp.int32).reshape(1)
    devices = lax.axis_size("dp")
    adapt = mixer_down.shape[1]
    other_tokens = swap_cores(tokens)
    kv, queries, across, turned, item, hide, rng = project(
        half_index, segment_ids, tokens, query_weight, key_weight, value_weight
    )
    other_tokens, output_late, inner_late, outer_late = tie(other_tokens, output_weight, inner_weight, outer_weight)
    other_output = swap_cores(output_late)
    other_inner = swap_cores(inner_late)
    other_outer = swap_cores(outer_late)
    kv, queries, keep, send, inverse, *shares = attention(
        half_index, rng, other_tokens, item, hide, query_weight, key_weight, value_weight, kv, queries, across, turned
    )
    got = swap_cores(send)
    vectors = (
        mixer_down_bias, mixer_up_bias, dense_down_bias, dense_up_bias, first_gain, first_shift, second_gain, second_shift,
    )
    matrices = (
        output_weight, other_output, mixer_down.T, mixer_up,
        inner_weight, other_inner, outer_weight, other_outer, dense_down.T, dense_up,
    )
    result, first_grad, own_grad, away_grad, mine, theirs = middle(
        half_index, tokens, keep, got, output_grad, vectors, matrices
    )
    got_grad = swap_cores(away_grad)
    packed = combine(mine, swap_cores(theirs))

    steps = []
    while 2 ** len(steps) < devices:
        steps.append(2 ** len(steps))
    steps.reverse()
    pairs = len(shares)
    grads = []
    away = None
    weights = (query_weight, key_weight, value_weight)
    for n, step in enumerate(steps):
        arriving = lax.ppermute(packed, "dp", [(i, i ^ step) for i in range(devices)])
        if n < pairs:
            got_grad, packed = tie(got_grad, packed)
            parts = pair_grad(n, half_index, rng, kv, queries, keep, send, own_grad, got_grad, inverse, shares[n])
            arriving, *parts = tie(arriving, *parts)
            grads.append(parts)
        elif n == pairs:
            pieces = [grads[p][i] for i in range(3) for p in range(pairs)]
            away = swap_cores(input_call(away_kernel, half_index, (), pieces, weights, "away"))
            input_grad = input_call(home_kernel, half_index, (first_grad, away), pieces, weights, "home")
            arriving, input_grad = tie(arriving, input_grad)
        packed = combine(packed, arriving)
    md, mu, dd, du, vec, bias, ratio = finish(half_index, packed, swap_cores(packed), adapt)
    return (
        result, input_grad, md.T, bias[0], mu, vec[0], dd.T, bias[1], du, vec[1], vec[2], vec[3], vec[4], vec[5], ratio[0, :2],
    )


def solution(mesh):
    tokens = P(("dp", "mp"), None)
    columns, rows, whole = P(None, "mp"), P("mp", None), P()
    return jax.shard_map(
        per_device,
        mesh=mesh,
        in_specs=(tokens, P("dp", None), columns, columns, columns, rows, columns, rows) + (whole,) * 12 + (tokens,),
        out_specs=(tokens, tokens) + (whole,) * 13,
        check_vma=False,
    )
```

```python
import functools

import jax
import jax.numpy as jnp
from jax import lax
from jax.experimental import pallas as pl
from jax.experimental.pallas import tpu as pltpu
from jax.sharding import PartitionSpec as P

F32 = jnp.float32
BF16 = jnp.bfloat16
HEAD_DIM = 64
PAIR = 2 * HEAD_DIM
EPS = 1e-12
LOG2E = 1.4426950408889634
LN2 = 0.6931471805599453
ROOT_HALF = 0.7071067811865476
ROOT_TWO_PI = 0.3989422804014327
MASKED = -(2.0**100)
LARGEST = 2.0**100
SMALLEST = 2.0**-60
TURNED = 80
BLOCK = 256
MIB = 1 << 20

VM = pl.BlockSpec(memory_space=pltpu.VMEM)
SM = pl.BlockSpec(memory_space=pltpu.SMEM)
HB = pl.BlockSpec(memory_space=pltpu.HBM)


def dot(left, right):
    return jnp.dot(left, right, preferred_element_type=F32)


def dot_nt(left, right):
    return lax.dot_general(left, right, (((1,), (1,)), ((), ())), preferred_element_type=F32)


def dot_tn(left, right):
    return lax.dot_general(left, right, (((0,), (0,)), ((), ())), preferred_element_type=F32)


def aligned(index, size):
    return pl.ds(pl.multiple_of(index * size, size), size)


def split_pair(pair):
    lane = lax.broadcasted_iota(jnp.int32, pair.shape, 1)
    zero = jnp.zeros_like(pair)
    return jnp.where(lane < HEAD_DIM, pair, zero), jnp.where(lane < HEAD_DIM, zero, pair)


def stack_heads(source, target, block):
    first, second = split_pair(source)
    for t in range(source.shape[0] // block):
        target[pl.ds(2 * t * block, block), :] = first[t * block : (t + 1) * block]
        target[pl.ds((2 * t + 1) * block, block), :] = second[t * block : (t + 1) * block]


def stack_heads_across(source, target, block):
    row = lax.broadcasted_iota(jnp.int32, source.shape, 0)
    zero = jnp.zeros_like(source)
    first = jnp.where(row < HEAD_DIM, source, zero)
    second = jnp.where(row < HEAD_DIM, zero, source)
    for t in range(source.shape[1] // block):
        target[:, 2 * t * block : (2 * t + 1) * block] = first[:, t * block : (t + 1) * block]
        target[:, (2 * t + 1) * block : (2 * t + 2) * block] = second[:, t * block : (t + 1) * block]


def in_hbm(value):
    return pltpu.with_memory_space_constraint(value, pltpu.HBM)


def start_all(sources, buffers, sems):
    copies = [pltpu.make_async_copy(src, dst, sems.at[i]) for i, (src, dst) in enumerate(zip(sources, buffers))]
    for copy in copies:
        copy.start()
    return copies


def write_projection(which, x, weights, copies, kv_ref, queries_ref, across_ref, turned_ref):
    rows, width = x.shape[0], weights[0].shape[1]
    pairs = width // PAIR
    if copies:
        copies[0].wait()
    queries = (dot(x, weights[0][...]) * (HEAD_DIM**-0.5 * LOG2E)).astype(BF16)
    for p in range(pairs):
        pair = queries[:, p * PAIR : (p + 1) * PAIR]
        stack_heads(pair, queries_ref.at[p, aligned(which, 2 * rows), :], BLOCK)
        stack_heads_across(pair.T, across_ref.at[p, :, aligned(which, 2 * rows)], BLOCK)
    if copies:
        copies[1].wait()
    kv_ref[aligned(which, rows), :width] = dot(x, weights[1][...]).astype(BF16)
    if copies:
        copies[2].wait()
    values = dot(x, weights[2][...]).astype(BF16)
    kv_ref[aligned(which, rows), width:] = values
    ones = jnp.ones((TURNED - HEAD_DIM, rows), BF16)
    for p in range(pairs):
        turned = values[:, p * PAIR : (p + 1) * PAIR].T
        for a in range(2):
            base = (2 * p + a) * TURNED
            turned_ref[base : base + HEAD_DIM, aligned(which, rows)] = turned[a * HEAD_DIM : (a + 1) * HEAD_DIM]
            turned_ref[base + HEAD_DIM : base + TURNED, aligned(which, rows)] = ones


def is_shift(lane):
    return (lane == 63) | (lane == 95) | (lane == 127)


def project_kernel(
    half_ref, ids_ref, seg_ref, x_ref, wq_ref, wk_ref, wv_ref,
    kv_ref, queries_ref, across_ref, turned_ref, item_ref, hide_ref, rng_ref,
    x_buf, wq, wk, wv, sems,
):
    copies = start_all((x_ref, wq_ref, wk_ref, wv_ref), (x_buf, wq, wk, wv), sems)
    count, block = kv_ref.shape[0], BLOCK
    ids = seg_ref[...].astype(F32)
    for g in range(count // block):
        first = ids_ref[0, g * block].astype(F32)
        last = ids_ref[0, (g + 1) * block - 1].astype(F32)
        rng_ref[0, g] = jnp.sum(jnp.where(ids < first, 1.0, 0.0)).astype(jnp.int32) // block
        rng_ref[1, g] = (jnp.sum(jnp.where(ids <= last, 1.0, 0.0)).astype(jnp.int32) + block - 1) // block
    lane = lax.broadcasted_iota(jnp.int32, (128, 128), 1)
    for t in range(count // 128):
        same = jnp.broadcast_to(ids[:, t * 128 : (t + 1) * 128], (128, 128)).T == lane.astype(F32)
        item_ref[t * 128 : (t + 1) * 128, :] = jnp.where(same | is_shift(lane), 1.0, 0.0).astype(BF16)
    row = lax.broadcasted_iota(jnp.int32, (128, block), 0)
    for t in range(count // block):
        same = row.astype(F32) == ids[:, t * block : (t + 1) * block]
        hide = jnp.where(same | is_shift(row), 0.0, MASKED).astype(BF16)
        for a in range(2):
            hide_ref[:, (2 * t + a) * block : (2 * t + a + 1) * block] = hide
    copies[0].wait()
    write_projection(half_ref[0], x_buf[...], (wq, wk, wv), copies[1:], kv_ref, queries_ref, across_ref, turned_ref)


def project(half_index, seg, x, wq, wk, wv):
    rows, width = x.shape[0], wq.shape[1]
    count, pairs = 2 * rows, width // PAIR
    return pl.pallas_call(
        project_kernel,
        out_shape=(
            jax.ShapeDtypeStruct((count, 2 * width), BF16),
            jax.ShapeDtypeStruct((pairs, 2 * count, PAIR), BF16),
            jax.ShapeDtypeStruct((pairs, PAIR, 2 * count), BF16),
            jax.ShapeDtypeStruct((2 * pairs * TURNED, count), BF16),
            jax.ShapeDtypeStruct((count, 128), BF16),
            jax.ShapeDtypeStruct((128, 2 * count), BF16),
            jax.ShapeDtypeStruct((2, count // BLOCK), jnp.int32),
        ),
        in_specs=[SM, SM, VM] + [HB] * 4,
        out_specs=(VM,) * 6 + (SM,),
        scratch_shapes=[pltpu.VMEM(v.shape, BF16) for v in (x, wq, wk, wv)] + [pltpu.SemaphoreType.DMA((4,))],
        compiler_params=pltpu.CompilerParams(vmem_limit_bytes=16 * MIB),
        cost_estimate=pl.CostEstimate(flops=2 * rows * x.shape[1] * 3 * width, bytes_accessed=5 * MIB, transcendentals=0),
        name="project",
    )(half_index, seg, seg, *map(in_hbm, (x, wq, wk, wv)))


def attention_kernel(
    half_ref, rng_ref, x_ref, item_ref, hide_ref, wq_ref, wk_ref, wv_ref, kv_in, queries_in, across_in, turned_in,
    kv_ref, queries_ref, keep_ref, send_ref, inverse_ref, *rest,
):
    half = x_ref.shape[0]
    count, width = kv_ref.shape[0], wq_ref.shape[1]
    pairs, block = width // PAIR, BLOCK
    share_refs = rest[:pairs]
    across, turned, mix, shifted, peaks = rest[pairs:]
    here, there = half_ref[0], 1 - half_ref[0]
    turned[:, aligned(here, half)] = turned_in[:, aligned(here, half)]
    across[:, :, aligned(here, 2 * half)] = across_in[:, :, aligned(here, 2 * half)]
    kv_ref[aligned(here, half), :] = kv_in[aligned(here, half), :]
    queries_ref[:, aligned(here, 2 * half), :] = queries_in[:, aligned(here, 2 * half), :]
    write_projection(there, x_ref[...], (wq_ref, wk_ref, wv_ref), (), kv_ref, queries_ref, across, turned)

    def scores(p, span, both, hide):
        keys = jnp.concatenate([kv_ref[span, p * PAIR : (p + 1) * PAIR], item_ref[span, :]], 1)
        return dot(keys, jnp.concatenate([across[p, :, both], hide], 0))

    def query_block(g, carry):
        rows, both = aligned(g, block), aligned(g, 2 * block)
        low, high = rng_ref[0, g], rng_ref[1, g]

        def mix_all(hide_of):
            mix[...] = jnp.zeros(mix.shape, F32)

            def key_block(j, c):
                span = aligned(j, block)
                ahead = scores(0, span, both, hide_of(0))
                for p in range(pairs):
                    s = ahead
                    if p + 1 < pairs:
                        ahead = scores(p + 1, span, both, hide_of(p + 1))
                    e = jnp.exp2(s).astype(BF16)
                    share_refs[p][span, both] = e
                    for a in range(2):
                        head = slice((2 * p + a) * TURNED, (2 * p + a + 1) * TURNED)
                        mix[head, :] += dot(turned[head, span], e[:, a * block : (a + 1) * block])
                return c

            lax.fori_loop(low, high, key_block, 0)

        mix_all(lambda p: hide_ref[:, both])
        total_rows = [h * TURNED + HEAD_DIM for h in range(2 * pairs)]
        sums = jnp.concatenate([mix[r : r + 8, :] for r in total_rows], 0)
        fine = jnp.where((sums <= LARGEST) & (sums >= SMALLEST), 0.0, 1.0)

        @pl.when(jnp.max(fine) > 0.0)
        def _():
            peaks[...] = jnp.full(peaks.shape, MASKED, F32)

            def peak_block(j, c):
                for p in range(pairs):
                    s = scores(p, aligned(j, block), both, hide_ref[:, both])
                    peaks[p] = jnp.maximum(peaks[p], jnp.max(s, 0, keepdims=True))
                return c

            lax.fori_loop(low, high, peak_block, 0)
            row = lax.broadcasted_iota(jnp.int32, (128, 2 * block), 0)
            hide = hide_ref[:, both].astype(F32)
            for p in range(pairs):
                peak = peaks[p]
                first = peak.astype(BF16).astype(F32)
                second = (peak - first).astype(BF16).astype(F32)
                third = peak - first - second
                parts = jnp.where(row < 64, first, jnp.where(row < 96, second, third))
                shifted[p] = jnp.where(is_shift(row), -parts, hide).astype(BF16)
            mix_all(lambda p: shifted[p])

        outs = []
        for p in range(pairs):
            scales = []
            for a in range(2):
                base = (2 * p + a) * TURNED
                scale = jnp.broadcast_to(1.0 / mix[base + HEAD_DIM : base + HEAD_DIM + 1, :], (HEAD_DIM, block))
                outs.append((mix[base : base + HEAD_DIM, :] * scale).astype(BF16))
                scales.append(scale)
            inverse_ref[rows, p * PAIR : (p + 1) * PAIR] = jnp.concatenate(scales, 0).T
        result = jnp.concatenate(outs, 0).T
        per_half = half // block

        @pl.when(g // per_half == here)
        def _():
            keep_ref[aligned(g % per_half, block), :] = result

        @pl.when(g // per_half != here)
        def _():
            send_ref[aligned(g % per_half, block), :] = result

        return carry

    lax.fori_loop(0, count // block, query_block, 0)


def attention(half_index, rng, x, item, hide, wq, wk, wv, kv, queries, across, turned):
    half, width = x.shape[0], wq.shape[1]
    count, pairs = 2 * half, width // PAIR
    like = lambda v: jax.ShapeDtypeStruct(v.shape, v.dtype)
    return pl.pallas_call(
        attention_kernel,
        out_shape=(
            like(kv),
            like(queries),
            jax.ShapeDtypeStruct((half, width), BF16),
            jax.ShapeDtypeStruct((half, width), BF16),
            jax.ShapeDtypeStruct((count, width), F32),
        )
        + (jax.ShapeDtypeStruct((count, 2 * count), BF16),) * pairs,
        in_specs=[SM, SM] + [VM] * 10,
        out_specs=(VM,) * (5 + pairs),
        scratch_shapes=[
            pltpu.VMEM(across.shape, BF16),
            pltpu.VMEM(turned.shape, BF16),
            pltpu.VMEM((2 * pairs * TURNED, BLOCK), F32),
            pltpu.VMEM((pairs, 128, 2 * BLOCK), BF16),
            pltpu.VMEM((pairs, 1, 2 * BLOCK), F32),
        ],
        compiler_params=pltpu.CompilerParams(vmem_limit_bytes=12 * MIB),
        cost_estimate=pl.CostEstimate(flops=10**10, bytes_accessed=8 * MIB, transcendentals=10**6),
        name="attention",
    )(half_index, rng, x, item, hide, wq, wk, wv, kv, queries, across, turned)


def pair_grad_kernel(
    p, half_ref, rng_ref, kv_ref, queries_ref, keep_ref, send_ref, own_ref, other_ref, inverse_ref, share_ref,
    dq_ref, dk_ref, dv_ref,
    grads, across, turned, delta, dq, dk, dv,
):
    half, width = keep_ref.shape
    count, block = kv_ref.shape[0], BLOCK
    cols = slice(p * PAIR, (p + 1) * PAIR)
    here, there = half_ref[0], 1 - half_ref[0]
    row = lax.broadcasted_iota(jnp.int32, (8, PAIR), 0)
    column = lax.broadcasted_iota(jnp.int32, (8, PAIR), 1)
    pick = jnp.where(column // HEAD_DIM == row, 1.0, 0.0).astype(BF16)
    for which, mixed_ref, up_ref in ((here, keep_ref, own_ref), (there, send_ref, other_ref)):
        scaled = (up_ref[:, cols].astype(F32) * inverse_ref[aligned(which, half), cols]).astype(BF16)
        product = mixed_ref[:, cols].astype(F32) * scaled.astype(F32)
        high = product.astype(BF16)
        low = (product - high.astype(F32)).astype(BF16)
        delta[:, aligned(which, half)] = dot_nt(pick, high) + dot_nt(pick, low)
        stack_heads(scaled, grads.at[aligned(which, 2 * half), :], block)
        stack_heads_across(scaled.T, across.at[:, aligned(which, 2 * half)], block)
    turned[...] = kv_ref[:, cols].T
    dk[...] = jnp.zeros(dk.shape, F32)
    dv[...] = jnp.zeros(dv.shape, F32)

    def query_block(g, carry):
        rows, both = aligned(g, block), aligned(g, 2 * block)
        dq[...] = jnp.zeros(dq.shape, F32)
        level = jnp.concatenate([delta[0:1, rows], delta[1:2, rows]], 1)

        def key_block(j, c):
            span = aligned(j, block)
            d = dot(kv_ref[span, width + p * PAIR : width + (p + 1) * PAIR], across[:, both])
            shares = share_ref[span, both]
            slopes = (shares.astype(F32) * (d - level)).astype(BF16)
            dv[span, :] += dot(shares, grads[both, :])
            dk[span, :] += dot(slopes, queries_ref[p, both, :])
            for a in range(2):
                head = slice(a * HEAD_DIM, (a + 1) * HEAD_DIM)
                dq[head, :] += dot(turned[head, span], slopes[:, a * block : (a + 1) * block])
            return c

        lax.fori_loop(rng_ref[0, g], rng_ref[1, g], key_block, 0)
        dq_ref[rows, :] = (dq[...] * HEAD_DIM**-0.5).astype(BF16).T
        return carry

    lax.fori_loop(0, count // block, query_block, 0)
    dk_ref[...] = (dk[...] * LN2).astype(BF16)
    dv_ref[...] = dv[...].astype(BF16)


def pair_grad(p, half_index, rng, kv, queries, keep, send, own, other, inverse, shares):
    count = kv.shape[0]
    return pl.pallas_call(
        functools.partial(pair_grad_kernel, p),
        out_shape=(jax.ShapeDtypeStruct((count, PAIR), BF16),) * 3,
        in_specs=[SM, SM] + [VM] * 8,
        out_specs=(VM,) * 3,
        scratch_shapes=[
            pltpu.VMEM((2 * count, PAIR), BF16),
            pltpu.VMEM((PAIR, 2 * count), BF16),
            pltpu.VMEM((PAIR, count), BF16),
            pltpu.VMEM((8, count), F32),
            pltpu.VMEM((PAIR, BLOCK), F32),
            pltpu.VMEM((count, PAIR), F32),
            pltpu.VMEM((count, PAIR), F32),
        ],
        compiler_params=pltpu.CompilerParams(vmem_limit_bytes=12 * MIB),
        cost_estimate=pl.CostEstimate(flops=4 * 10**9, bytes_accessed=8 * MIB, transcendentals=0),
        name=f"pair_grad_{p}",
    )(half_index, rng, kv, queries, keep, send, own, other, inverse, shares)


def input_part(half_ref, flip, pieces, weights, half):
    which = 1 - half_ref[0] if flip else half_ref[0]
    rows = aligned(which, half)
    left = jnp.concatenate([piece[rows, :] for piece in pieces], 1)
    right = jnp.concatenate([weight[...] for weight in weights], 1)
    return dot_nt(left, right)


def away_kernel(half_ref, *refs):
    out_ref = refs[-1]
    out_ref[...] = input_part(half_ref, True, refs[:-4], refs[-4:-1], out_ref.shape[0]).astype(BF16)


def home_kernel(half_ref, first_ref, got_ref, *refs):
    out_ref = refs[-1]
    part = input_part(half_ref, False, refs[:-4], refs[-4:-1], out_ref.shape[0])
    out_ref[...] = (part + first_ref[...] + got_ref[...].astype(F32)).astype(BF16)


def input_call(kernel, half_index, extra, pieces, weights, name):
    half, features = pieces[0].shape[0] // 2, weights[0].shape[0]
    return pl.pallas_call(
        kernel,
        out_shape=jax.ShapeDtypeStruct((half, features), BF16),
        in_specs=[SM] + [VM] * (len(extra) + len(pieces) + len(weights)),
        out_specs=VM,
        compiler_params=pltpu.CompilerParams(vmem_limit_bytes=16 * MIB),
        cost_estimate=pl.CostEstimate(flops=10**9, bytes_accessed=6 * MIB, transcendentals=0),
        name=name,
    )(half_index, *extra, *pieces, *weights)


def gelu_both(v):
    part = 0.5 + 0.5 * lax.erf(v * ROOT_HALF)
    return v * part, part + v * jnp.exp(-0.5 * v * v) * ROOT_TWO_PI


def norm(values, gain, shift):
    mean = jnp.mean(values, -1, keepdims=True)
    centred = values - mean
    reciprocal = lax.rsqrt(jnp.mean(centred * centred, -1, keepdims=True) + EPS)
    normed = centred * reciprocal
    return normed * gain + shift, normed, reciprocal


def norm_grad(upstream, normed, reciprocal, gain):
    scaled = upstream * gain
    return reciprocal * (
        scaled - jnp.mean(scaled, -1, keepdims=True) - normed * jnp.mean(scaled * normed, -1, keepdims=True)
    )


def column_sum(values):
    return jnp.sum(values, 0, keepdims=True)


def middle_kernel(
    half_ref, x_ref, keep_ref, got_ref, up_ref,
    mdb_ref, mub_ref, ddb_ref, dub_ref, fg_ref, fs_ref, sg_ref, ss_ref,
    wo_hbm, wo2_hbm, md_hbm, mu_hbm, w1_hbm, w12_hbm, w2_hbm, w22_hbm, dd_hbm, du_hbm,
    act_hbm, first_ref, own_ref, away_ref, mine_ref, theirs_ref,
    wo_ref, wo2_ref, md_ref, mu_ref, w1_ref, w12_ref, w2_ref, w22_ref, dd_ref, du_ref,
    slope_ref, hidden_ref, normed_ref, act_ref, big_ref, small_ref, sems, act_sem,
):
    rows, features = x_ref.shape
    adapt = md_ref.shape[0]
    names = ("wo", "wo2", "md", "mu", "w1", "w2", "w12", "w22", "dd", "du")
    waits = dict(
        zip(
            names,
            start_all(
                (wo_hbm, wo2_hbm, md_hbm, mu_hbm, w1_hbm, w2_hbm, w12_hbm, w22_hbm, dd_hbm, du_hbm),
                (wo_ref, wo2_ref, md_ref, mu_ref, w1_ref, w2_ref, w12_ref, w22_ref, dd_ref, du_ref),
                sems,
            ),
        )
    )

    def vector(ref):
        return ref[...].astype(F32).reshape(1, -1)

    x = x_ref[...].astype(F32)
    waits["wo"].wait()
    attended = dot(keep_ref[...], wo_ref[...])
    waits["wo2"].wait()
    attended = attended + dot(got_ref[...], wo2_ref[...])
    attended_low = attended.astype(BF16)
    waits["md"].wait()
    waits["mu"].wait()
    mixer_active, mixer_slope = gelu_both(dot_nt(attended_low, md_ref[...]) + vector(mdb_ref))
    mixer_active = mixer_active.astype(BF16)
    mixer_out = dot(mixer_active, mu_ref[...]) + vector(mub_ref)
    hidden, normed_one, reciprocal_one = norm(x + attended + mixer_out, vector(fg_ref), vector(fs_ref))
    normed_ref[...] = normed_one
    hidden_ref[...] = hidden
    mixer_square = jnp.sum(column_sum(mixer_out * mixer_out), -1, keepdims=True)
    input_square = jnp.sum(column_sum(x * x), -1, keepdims=True)
    hidden_low = hidden.astype(BF16)
    chunk = 512
    units = w1_ref.shape[1]
    sides = ((w1_ref, w2_ref, "w1", "w2"), (w12_ref, w22_ref, "w12", "w22"))
    dense_in = jnp.zeros((rows, features), F32)
    for s, (win, wout, first, second) in enumerate(sides):
        waits[first].wait()
        waits[second].wait()
        for c in range(units // chunk):
            span = slice(c * chunk, (c + 1) * chunk)
            value, slope = gelu_both(dot(hidden_low, win[:, span]))
            slope_ref[:, s * units + c * chunk : s * units + (c + 1) * chunk] = slope.astype(BF16)
            dense_in = dense_in + dot(value.astype(BF16), wout[span, :])
    dense_low = dense_in.astype(BF16)
    waits["dd"].wait()
    waits["du"].wait()
    dense_active, dense_slope = gelu_both(dot_nt(dense_low, dd_ref[...]) + vector(ddb_ref))
    dense_active = dense_active.astype(BF16)
    dense_out = dot(dense_active, du_ref[...]) + vector(dub_ref)
    second_gain = vector(sg_ref)
    result, normed_two, reciprocal_two = norm(hidden_ref[...] + dense_in + dense_out, second_gain, vector(ss_ref))
    act_ref[...] = result.astype(BF16)
    act_copy = pltpu.make_async_copy(act_ref, act_hbm, act_sem)
    act_copy.start()
    dense_square = jnp.sum(column_sum(dense_out * dense_out), -1, keepdims=True)

    upstream = up_ref[...].astype(F32)
    small_ref[4:5, :] = column_sum(upstream * normed_two)
    small_ref[5:6, :] = column_sum(upstream)
    second_grad = norm_grad(upstream, normed_two, reciprocal_two, second_gain)
    dense_top = second_grad.astype(BF16)
    big_ref[3 * adapt : 4 * adapt, :] = dot_tn(dense_active, dense_top).astype(BF16)
    small_ref[1:2, :] = column_sum(dense_top.astype(F32))
    dense_mid = (dot_nt(dense_top, du_ref[...]) * dense_slope).astype(BF16)
    big_ref[2 * adapt : 3 * adapt, :] = dot_tn(dense_mid, dense_low).astype(BF16)
    dense_mid_sum = column_sum(dense_mid.astype(F32))
    dense_in_grad = (second_grad + dot(dense_mid, dd_ref[...])).astype(BF16)
    hidden_grad = second_grad
    for s, (win, wout, _, _) in enumerate(sides):
        for c in range(units // chunk):
            span = slice(c * chunk, (c + 1) * chunk)
            slope = slope_ref[:, s * units + c * chunk : s * units + (c + 1) * chunk].astype(F32)
            inner_grad = (dot_nt(dense_in_grad, wout[span, :]) * slope).astype(BF16)
            hidden_grad = hidden_grad + dot_nt(inner_grad, win[:, span])
    normed_one = normed_ref[...]
    small_ref[2:3, :] = column_sum(hidden_grad * normed_one)
    small_ref[3:4, :] = column_sum(hidden_grad)
    first_grad = norm_grad(hidden_grad, normed_one, reciprocal_one, vector(fg_ref))
    first_ref[...] = first_grad
    mixer_top = first_grad.astype(BF16)
    big_ref[adapt : 2 * adapt, :] = dot_tn(mixer_active, mixer_top).astype(BF16)
    small_ref[0:1, :] = column_sum(mixer_top.astype(F32))
    mixer_mid = (dot_nt(mixer_top, mu_ref[...]) * mixer_slope).astype(BF16)
    big_ref[0:adapt, :] = dot_tn(mixer_mid, attended_low).astype(BF16)
    mixer_mid_sum = column_sum(mixer_mid.astype(F32))
    attended_grad = (first_grad + dot(mixer_mid, md_ref[...])).astype(BF16)
    own_ref[...] = dot_nt(attended_grad, wo_ref[...]).astype(BF16)
    away_ref[...] = dot_nt(attended_grad, wo2_ref[...]).astype(BF16)
    lane = lax.broadcasted_iota(jnp.int32, (1, 128), 1)
    squares = jnp.where(lane == 0, mixer_square, jnp.where(lane == 1, dense_square, jnp.where(lane == 2, input_square, 0.0)))
    small_ref[6:7, :] = jnp.concatenate(
        [mixer_mid_sum, dense_mid_sum, squares, jnp.zeros((1, features - 2 * adapt - 128), F32)], 1
    )
    small_ref[7:8, :] = jnp.zeros((1, features), F32)
    tail = tail_of(small_ref[...])
    share = 2 * adapt
    for out_ref, which in ((mine_ref, half_ref[0]), (theirs_ref, 1 - half_ref[0])):
        out_ref[:share, :] = big_ref[aligned(which, share), :]
        out_ref[share:, :] = tail
    act_copy.wait()


def tail_of(vectors):
    high = vectors.astype(BF16)
    return jnp.concatenate([high, (vectors - high.astype(F32)).astype(BF16)], 0)


def vectors_of(tail):
    wide = tail.astype(F32)
    return wide[:8] + wide[8:]


def middle(half_index, x, keep, got, up, vectors, matrices):
    rows, features = x.shape
    width = keep.shape[1]
    adapt = matrices[2].shape[0]
    units = matrices[4].shape[1]
    packed = jax.ShapeDtypeStruct((2 * adapt + 16, features), BF16)
    return pl.pallas_call(
        middle_kernel,
        out_shape=(
            jax.ShapeDtypeStruct((rows, features), BF16),
            jax.ShapeDtypeStruct((rows, features), F32),
            jax.ShapeDtypeStruct((rows, width), BF16),
            jax.ShapeDtypeStruct((rows, width), BF16),
            packed,
            packed,
        ),
        in_specs=[SM] + [VM] * 12 + [HB] * 10,
        out_specs=(HB,) + (VM,) * 5,
        scratch_shapes=[pltpu.VMEM(m.shape, BF16) for m in matrices]
        + [
            pltpu.VMEM((rows, 2 * units), BF16),
            pltpu.VMEM((rows, features), F32),
            pltpu.VMEM((rows, features), F32),
            pltpu.VMEM((rows, features), BF16),
            pltpu.VMEM((4 * adapt, features), BF16),
            pltpu.VMEM((8, features), F32),
            pltpu.SemaphoreType.DMA((10,)),
            pltpu.SemaphoreType.DMA,
        ],
        compiler_params=pltpu.CompilerParams(vmem_limit_bytes=32 * MIB),
        cost_estimate=pl.CostEstimate(flops=2 * 10**10, bytes_accessed=16 * MIB, transcendentals=10**6),
        name="middle",
    )(half_index, x, keep, got, up, *vectors, *map(in_hbm, matrices))


def combine_kernel(held_ref, got_ref, out_ref):
    rows = held_ref.shape[0] - 16
    out_ref[:rows, :] = (held_ref[:rows, :].astype(F32) + got_ref[:rows, :].astype(F32)).astype(BF16)
    out_ref[rows:, :] = tail_of(vectors_of(held_ref[rows:, :]) + vectors_of(got_ref[rows:, :]))


def combine(held, got):
    return pl.pallas_call(
        combine_kernel,
        out_shape=jax.ShapeDtypeStruct(held.shape, BF16),
        in_specs=[VM] * 2,
        out_specs=VM,
        compiler_params=pltpu.CompilerParams(vmem_limit_bytes=4 * MIB),
        cost_estimate=pl.CostEstimate(flops=10**5, bytes_accessed=MIB, transcendentals=0),
        name="combine",
    )(held, got)


def finish_kernel(half_ref, held_ref, got_ref, md_ref, mdb_ref, mu_ref, mub_ref, dd_ref, ddb_ref, du_ref, dub_ref,
                  fg_ref, fs_ref, sg_ref, ss_ref, ratio_ref):
    adapt = md_ref.shape[0]

    def write(first_ref, second_ref):
        md_ref[...] = first_ref[:adapt, :].astype(F32)
        mu_ref[...] = first_ref[adapt : 2 * adapt, :].astype(F32)
        dd_ref[...] = second_ref[:adapt, :].astype(F32)
        du_ref[...] = second_ref[adapt : 2 * adapt, :].astype(F32)
        vectors = vectors_of(first_ref[2 * adapt :, :])
        for row, out_ref in enumerate((mub_ref, dub_ref, fg_ref, fs_ref, sg_ref, ss_ref)):
            out_ref[...] = vectors[row, :]
        last = vectors[6:7, :]
        mdb_ref[...] = last[0, :adapt]
        ddb_ref[...] = last[0, adapt : 2 * adapt]
        squares = last[:, 2 * adapt : 2 * adapt + 128]
        lane = lax.broadcasted_iota(jnp.int32, (1, 128), 1)
        base = jnp.sum(jnp.where(lane == 2, squares, 0.0), -1, keepdims=True)
        ratio_ref[...] = jnp.sqrt(squares / base)[0, :2]

    @pl.when(half_ref[0] == 0)
    def _():
        write(held_ref, got_ref)

    @pl.when(half_ref[0] != 0)
    def _():
        write(got_ref, held_ref)


def finish(half_index, held, got, adapt):
    features = held.shape[1]
    matrix = jax.ShapeDtypeStruct((adapt, features), F32)
    short, vector = jax.ShapeDtypeStruct((adapt,), F32), jax.ShapeDtypeStruct((features,), F32)
    return pl.pallas_call(
        finish_kernel,
        out_shape=(matrix, short, matrix, vector) * 2 + (vector,) * 4 + (jax.ShapeDtypeStruct((2,), F32),),
        in_specs=[SM, VM, VM],
        out_specs=(VM,) * 13,
        compiler_params=pltpu.CompilerParams(vmem_limit_bytes=4 * MIB),
        name="finish",
    )(half_index, held, got)


def swap_cores(value):
    return lax.ppermute(value, "mp", [(0, 1), (1, 0)])


def tie(*values):
    return lax.optimization_barrier(values)


def per_device(
    tokens, segment_ids, query_weight, key_weight, value_weight, output_weight, inner_weight, outer_weight,
    mixer_down, mixer_down_bias, mixer_up, mixer_up_bias, dense_down, dense_down_bias, dense_up, dense_up_bias,
    first_gain, first_shift, second_gain, second_shift, output_grad,
):
    half_index = lax.axis_index("mp").astype(jnp.int32).reshape(1)
    devices = lax.axis_size("dp")
    adapt = mixer_down.shape[1]
    other_tokens = swap_cores(tokens)
    kv, queries, across, turned, item, hide, rng = project(
        half_index, segment_ids, tokens, query_weight, key_weight, value_weight
    )
    kv, other_tokens, output_late, inner_late, outer_late = tie(
        kv, other_tokens, output_weight, inner_weight, outer_weight
    )
    other_output = swap_cores(output_late)
    other_inner = swap_cores(inner_late)
    other_outer = swap_cores(outer_late)
    kv, queries, keep, send, inverse, *shares = attention(
        half_index, rng, other_tokens, item, hide, query_weight, key_weight, value_weight, kv, queries, across, turned
    )
    got = swap_cores(send)
    vectors = (
        mixer_down_bias, mixer_up_bias, dense_down_bias, dense_up_bias, first_gain, first_shift, second_gain, second_shift,
    )
    matrices = (
        output_weight, other_output, mixer_down.T, mixer_up,
        inner_weight, other_inner, outer_weight, other_outer, dense_down.T, dense_up,
    )
    result, first_grad, own_grad, away_grad, mine, theirs = middle(
        half_index, tokens, keep, got, output_grad, vectors, matrices
    )
    got_grad = swap_cores(away_grad)
    packed = combine(mine, swap_cores(theirs))

    steps = []
    while 2 ** len(steps) < devices:
        steps.append(2 ** len(steps))
    steps.reverse()
    turn = len(steps) // 2
    pairs = len(shares)
    grads = []
    weights = (query_weight, key_weight, value_weight)
    for n, step in enumerate(steps):
        other_step = steps[(n + turn) % len(steps)]
        exchange = [(2 * i + c, 2 * (i ^ s) + c) for i in range(devices) for c, s in enumerate((step, other_step))]
        arriving = lax.ppermute(packed, ("dp", "mp"), exchange)
        if n < pairs:
            got_grad, packed = tie(got_grad, packed)
            parts = pair_grad(n, half_index, rng, kv, queries, keep, send, own_grad, got_grad, inverse, shares[n])
            arriving, *parts = tie(arriving, *parts)
            grads.append(parts)
        elif n == pairs:
            pieces = [grads[p][i] for i in range(3) for p in range(pairs)]
            away = swap_cores(input_call(away_kernel, half_index, (), pieces, weights, "away"))
            input_grad = input_call(home_kernel, half_index, (first_grad, away), pieces, weights, "home")
            arriving, input_grad = tie(arriving, input_grad)
        packed = combine(packed, arriving)
    md, mdb, mu, mub, dd, ddb, du, dub, *rest = finish(half_index, packed, swap_cores(packed), adapt)
    return (result, input_grad, md.T, mdb, mu, mub, dd.T, ddb, du, dub, *rest)


def solution(mesh):
    tokens = P(("dp", "mp"), None)
    columns, rows, whole = P(None, "mp"), P("mp", None), P()
    return jax.shard_map(
        per_device,
        mesh=mesh,
        in_specs=(tokens, P("dp", None), columns, columns, columns, rows, columns, rows) + (whole,) * 12 + (tokens,),
        out_specs=(tokens, tokens) + (whole,) * 13,
        check_vma=False,
    )
```

```python
import functools

import jax
import jax.numpy as jnp
from jax import lax
from jax.experimental import pallas as pl
from jax.experimental.pallas import tpu as pltpu
from jax.sharding import PartitionSpec as P

F32 = jnp.float32
BF16 = jnp.bfloat16
HEAD_DIM = 64
PAIR = 2 * HEAD_DIM
EPS = 1e-12
LOG2E = 1.4426950408889634
LN2 = 0.6931471805599453
ROOT_HALF = 0.7071067811865476
ROOT_TWO_PI = 0.3989422804014327
MASKED = -(2.0**100)
LARGEST = 2.0**100
SMALLEST = 2.0**-60
TURNED = 80
BLOCK = 256
STEP = 128
MIB = 1 << 20

VM = pl.BlockSpec(memory_space=pltpu.VMEM)
SM = pl.BlockSpec(memory_space=pltpu.SMEM)
HB = pl.BlockSpec(memory_space=pltpu.HBM)


def dot(left, right):
    return jnp.dot(left, right, preferred_element_type=F32)


def dot_nt(left, right):
    return lax.dot_general(left, right, (((1,), (1,)), ((), ())), preferred_element_type=F32)


def dot_tn(left, right):
    return lax.dot_general(left, right, (((0,), (0,)), ((), ())), preferred_element_type=F32)


def aligned(index, size):
    return pl.ds(pl.multiple_of(index * size, size), size)


def split_pair(pair):
    lane = lax.broadcasted_iota(jnp.int32, pair.shape, 1)
    zero = jnp.zeros_like(pair)
    return jnp.where(lane < HEAD_DIM, pair, zero), jnp.where(lane < HEAD_DIM, zero, pair)


def stack_heads(source, target, block):
    first, second = split_pair(source)
    for t in range(source.shape[0] // block):
        target[pl.ds(2 * t * block, block), :] = first[t * block : (t + 1) * block]
        target[pl.ds((2 * t + 1) * block, block), :] = second[t * block : (t + 1) * block]


def stack_heads_across(source, target, block):
    row = lax.broadcasted_iota(jnp.int32, source.shape, 0)
    zero = jnp.zeros_like(source)
    first = jnp.where(row < HEAD_DIM, source, zero)
    second = jnp.where(row < HEAD_DIM, zero, source)
    for t in range(source.shape[1] // block):
        target[:, 2 * t * block : (2 * t + 1) * block] = first[:, t * block : (t + 1) * block]
        target[:, (2 * t + 1) * block : (2 * t + 2) * block] = second[:, t * block : (t + 1) * block]


def in_hbm(value):
    return pltpu.with_memory_space_constraint(value, pltpu.HBM)


def start_all(sources, buffers, sems):
    copies = [pltpu.make_async_copy(src, dst, sems.at[i]) for i, (src, dst) in enumerate(zip(sources, buffers))]
    for copy in copies:
        copy.start()
    return copies


def write_projection(which, x, weights, copies, kv_ref, queries_ref, across_ref, turned_ref):
    rows, width = x.shape[0], weights[0].shape[1]
    pairs = width // PAIR
    if copies:
        copies[0].wait()
    queries = (dot(x, weights[0][...]) * (HEAD_DIM**-0.5 * LOG2E)).astype(BF16)
    for p in range(pairs):
        pair = queries[:, p * PAIR : (p + 1) * PAIR]
        stack_heads(pair, queries_ref.at[p, aligned(which, 2 * rows), :], BLOCK)
        stack_heads_across(pair.T, across_ref.at[p, :, aligned(which, 2 * rows)], BLOCK)
    if copies:
        copies[1].wait()
    kv_ref[aligned(which, rows), :width] = dot(x, weights[1][...]).astype(BF16)
    if copies:
        copies[2].wait()
    values = dot(x, weights[2][...]).astype(BF16)
    kv_ref[aligned(which, rows), width:] = values
    ones = jnp.ones((TURNED - HEAD_DIM, rows), BF16)
    for p in range(pairs):
        turned = values[:, p * PAIR : (p + 1) * PAIR].T
        for a in range(2):
            base = (2 * p + a) * TURNED
            turned_ref[base : base + HEAD_DIM, aligned(which, rows)] = turned[a * HEAD_DIM : (a + 1) * HEAD_DIM]
            turned_ref[base + HEAD_DIM : base + TURNED, aligned(which, rows)] = ones


def over_keys(low, high, visit):
    def whole(t, c):
        visit(pl.ds(pl.multiple_of(low * STEP + t * BLOCK, STEP), BLOCK), BLOCK)
        return c

    lax.fori_loop(0, (high - low) // 2, whole, 0)

    @pl.when((high - low) % 2 == 1)
    def _():
        visit(pl.ds(pl.multiple_of((high - 1) * STEP, STEP), STEP), STEP)


def is_shift(lane):
    return (lane == 63) | (lane == 95) | (lane == 127)


def project_kernel(
    seg_hbm, x_ref, wq_ref, wk_ref, wv_ref,
    kv_ref, queries_ref, across_ref, turned_ref, item_ref, hide_ref, rng_ref,
    seg_ref, x_buf, wq, wk, wv, sems,
):
    sources, buffers = (seg_hbm, x_ref, wq_ref, wk_ref, wv_ref), (seg_ref, x_buf, wq, wk, wv)
    seg_copy, *copies = start_all(sources, buffers, sems)
    count, block = kv_ref.shape[0], BLOCK
    seg_copy.wait()
    ids = seg_ref[...].astype(F32)
    position = lax.broadcasted_iota(jnp.int32, ids.shape, 1)
    for g in range(count // block):
        first, last = (
            jnp.sum(jnp.where(position == at, ids, 0.0), -1, keepdims=True) for at in (g * block, (g + 1) * block - 1)
        )
        rng_ref[0, g] = jnp.sum(jnp.where(ids < first, 1.0, 0.0)).astype(jnp.int32) // STEP
        rng_ref[1, g] = (jnp.sum(jnp.where(ids <= last, 1.0, 0.0)).astype(jnp.int32) + STEP - 1) // STEP
    lane = lax.broadcasted_iota(jnp.int32, (128, 128), 1)
    for t in range(count // 128):
        same = jnp.broadcast_to(ids[:, t * 128 : (t + 1) * 128], (128, 128)).T == lane.astype(F32)
        item_ref[t * 128 : (t + 1) * 128, :] = jnp.where(same | is_shift(lane), 1.0, 0.0).astype(BF16)
    row = lax.broadcasted_iota(jnp.int32, (128, block), 0)
    for t in range(count // block):
        same = row.astype(F32) == ids[:, t * block : (t + 1) * block]
        hide = jnp.where(same | is_shift(row), 0.0, MASKED).astype(BF16)
        for a in range(2):
            hide_ref[:, (2 * t + a) * block : (2 * t + a + 1) * block] = hide
    copies[0].wait()
    write_projection(lax.axis_index("mp"), x_buf[...], (wq, wk, wv), copies[1:], kv_ref, queries_ref, across_ref, turned_ref)


def project(seg, x, wq, wk, wv):
    rows, width = x.shape[0], wq.shape[1]
    count, pairs = 2 * rows, width // PAIR
    return pl.pallas_call(
        project_kernel,
        out_shape=(
            jax.ShapeDtypeStruct((count, 2 * width), BF16),
            jax.ShapeDtypeStruct((pairs, 2 * count, PAIR), BF16),
            jax.ShapeDtypeStruct((pairs, PAIR, 2 * count), BF16),
            jax.ShapeDtypeStruct((2 * pairs * TURNED, count), BF16),
            jax.ShapeDtypeStruct((count, 128), BF16),
            jax.ShapeDtypeStruct((128, 2 * count), BF16),
            jax.ShapeDtypeStruct((2, count // BLOCK), jnp.int32),
        ),
        in_specs=[HB] * 5,
        out_specs=(VM,) * 6 + (SM,),
        scratch_shapes=[pltpu.VMEM(v.shape, v.dtype) for v in (seg, x, wq, wk, wv)] + [pltpu.SemaphoreType.DMA((5,))],
        compiler_params=pltpu.CompilerParams(vmem_limit_bytes=16 * MIB),
        cost_estimate=pl.CostEstimate(flops=2 * rows * x.shape[1] * 3 * width, bytes_accessed=5 * MIB, transcendentals=0),
        name="project",
    )(*map(in_hbm, (seg, x, wq, wk, wv)))


def attention_kernel(
    rng_ref, x_ref, item_ref, hide_ref, wq_ref, wk_ref, wv_ref, kv_in, queries_in, across_in, turned_in,
    kv_ref, queries_ref, keep_ref, send_ref, inverse_ref, *rest,
):
    half = x_ref.shape[0]
    count, width = kv_ref.shape[0], wq_ref.shape[1]
    pairs, block = width // PAIR, BLOCK
    share_refs = rest[:pairs]
    across, turned, mix, shifted, peaks = rest[pairs:]
    here, there = lax.axis_index("mp"), 1 - lax.axis_index("mp")
    turned[:, aligned(here, half)] = turned_in[:, aligned(here, half)]
    across[:, :, aligned(here, 2 * half)] = across_in[:, :, aligned(here, 2 * half)]
    kv_ref[aligned(here, half), :] = kv_in[aligned(here, half), :]
    queries_ref[:, aligned(here, 2 * half), :] = queries_in[:, aligned(here, 2 * half), :]
    write_projection(there, x_ref[...], (wq_ref, wk_ref, wv_ref), (), kv_ref, queries_ref, across, turned)

    def scores(p, span, both, hide):
        keys = jnp.concatenate([kv_ref[span, p * PAIR : (p + 1) * PAIR], item_ref[span, :]], 1)
        return dot(keys, jnp.concatenate([across[p, :, both], hide], 0))

    def query_block(g, carry):
        rows, both = aligned(g, block), aligned(g, 2 * block)
        low, high = rng_ref[0, g], rng_ref[1, g]

        def mix_all(hide_of):
            mix[...] = jnp.zeros(mix.shape, F32)

            def visit(span, size):
                ahead = scores(0, span, both, hide_of(0))
                for p in range(pairs):
                    s = ahead
                    if p + 1 < pairs:
                        ahead = scores(p + 1, span, both, hide_of(p + 1))
                    e = jnp.exp2(s).astype(BF16)
                    share_refs[p][span, both] = e
                    for a in range(2):
                        head = slice((2 * p + a) * TURNED, (2 * p + a + 1) * TURNED)
                        mix[head, :] += dot(turned[head, span], e[:, a * block : (a + 1) * block])

            over_keys(low, high, visit)

        mix_all(lambda p: hide_ref[:, both])
        total_rows = [h * TURNED + HEAD_DIM for h in range(2 * pairs)]
        sums = jnp.concatenate([mix[r : r + 8, :] for r in total_rows], 0)
        fine = jnp.where((sums <= LARGEST) & (sums >= SMALLEST), 0.0, 1.0)

        @pl.when(jnp.max(fine) > 0.0)
        def _():
            peaks[...] = jnp.full(peaks.shape, MASKED, F32)

            def visit(span, size):
                for p in range(pairs):
                    s = scores(p, span, both, hide_ref[:, both])
                    peaks[p] = jnp.maximum(peaks[p], jnp.max(s, 0, keepdims=True))

            over_keys(low, high, visit)
            row = lax.broadcasted_iota(jnp.int32, (128, 2 * block), 0)
            hide = hide_ref[:, both].astype(F32)
            for p in range(pairs):
                peak = peaks[p]
                first = peak.astype(BF16).astype(F32)
                second = (peak - first).astype(BF16).astype(F32)
                third = peak - first - second
                parts = jnp.where(row < 64, first, jnp.where(row < 96, second, third))
                shifted[p] = jnp.where(is_shift(row), -parts, hide).astype(BF16)
            mix_all(lambda p: shifted[p])

        outs = []
        for p in range(pairs):
            scales = []
            for a in range(2):
                base = (2 * p + a) * TURNED
                scale = jnp.broadcast_to(1.0 / mix[base + HEAD_DIM : base + HEAD_DIM + 1, :], (HEAD_DIM, block))
                outs.append((mix[base : base + HEAD_DIM, :] * scale).astype(BF16))
                scales.append(scale)
            inverse_ref[rows, p * PAIR : (p + 1) * PAIR] = jnp.concatenate(scales, 0).T
        result = jnp.concatenate(outs, 0).T
        per_half = half // block

        @pl.when(g // per_half == here)
        def _():
            keep_ref[aligned(g % per_half, block), :] = result

        @pl.when(g // per_half != here)
        def _():
            send_ref[aligned(g % per_half, block), :] = result

        return carry

    lax.fori_loop(0, count // block, query_block, 0)


def attention(rng, x, item, hide, wq, wk, wv, kv, queries, across, turned):
    half, width = x.shape[0], wq.shape[1]
    count, pairs = 2 * half, width // PAIR
    like = lambda v: jax.ShapeDtypeStruct(v.shape, v.dtype)
    return pl.pallas_call(
        attention_kernel,
        out_shape=(
            like(kv),
            like(queries),
            jax.ShapeDtypeStruct((half, width), BF16),
            jax.ShapeDtypeStruct((half, width), BF16),
            jax.ShapeDtypeStruct((count, width), F32),
        )
        + (jax.ShapeDtypeStruct((count, 2 * count), BF16),) * pairs,
        in_specs=[SM] + [VM] * 10,
        out_specs=(VM,) * (5 + pairs),
        scratch_shapes=[
            pltpu.VMEM(across.shape, BF16),
            pltpu.VMEM(turned.shape, BF16),
            pltpu.VMEM((2 * pairs * TURNED, BLOCK), F32),
            pltpu.VMEM((pairs, 128, 2 * BLOCK), BF16),
            pltpu.VMEM((pairs, 1, 2 * BLOCK), F32),
        ],
        compiler_params=pltpu.CompilerParams(vmem_limit_bytes=12 * MIB),
        cost_estimate=pl.CostEstimate(flops=10**10, bytes_accessed=8 * MIB, transcendentals=10**6),
        name="attention",
    )(rng, x, item, hide, wq, wk, wv, kv, queries, across, turned)


def pair_grad_kernel(
    p, rng_ref, kv_ref, queries_ref, keep_ref, send_ref, own_ref, other_ref, inverse_ref, share_ref,
    dq_ref, dk_ref, dv_ref,
    grads, across, turned, delta, dq, dk, dv,
):
    half, width = keep_ref.shape
    count, block = kv_ref.shape[0], BLOCK
    cols = slice(p * PAIR, (p + 1) * PAIR)
    here, there = lax.axis_index("mp"), 1 - lax.axis_index("mp")
    row = lax.broadcasted_iota(jnp.int32, (8, PAIR), 0)
    column = lax.broadcasted_iota(jnp.int32, (8, PAIR), 1)
    pick = jnp.where(column // HEAD_DIM == row, 1.0, 0.0).astype(BF16)
    for which, mixed_ref, up_ref in ((here, keep_ref, own_ref), (there, send_ref, other_ref)):
        scaled = (up_ref[:, cols].astype(F32) * inverse_ref[aligned(which, half), cols]).astype(BF16)
        product = mixed_ref[:, cols].astype(F32) * scaled.astype(F32)
        high = product.astype(BF16)
        low = (product - high.astype(F32)).astype(BF16)
        delta[:, aligned(which, half)] = dot_nt(pick, high) + dot_nt(pick, low)
        stack_heads(scaled, grads.at[aligned(which, 2 * half), :], block)
        stack_heads_across(scaled.T, across.at[:, aligned(which, 2 * half)], block)
    turned[...] = kv_ref[:, cols].T
    dk[...] = jnp.zeros(dk.shape, F32)
    dv[...] = jnp.zeros(dv.shape, F32)

    def query_block(g, carry):
        rows, both = aligned(g, block), aligned(g, 2 * block)
        dq[...] = jnp.zeros(dq.shape, F32)
        level = jnp.concatenate([delta[0:1, rows], delta[1:2, rows]], 1)

        def visit(span, size):
            d = dot(kv_ref[span, width + p * PAIR : width + (p + 1) * PAIR], across[:, both])
            shares = share_ref[span, both]
            slopes = (shares.astype(F32) * (d - level)).astype(BF16)
            dv[span, :] += dot(shares, grads[both, :])
            dk[span, :] += dot(slopes, queries_ref[p, both, :])
            for a in range(2):
                head = slice(a * HEAD_DIM, (a + 1) * HEAD_DIM)
                dq[head, :] += dot(turned[head, span], slopes[:, a * block : (a + 1) * block])

        over_keys(rng_ref[0, g], rng_ref[1, g], visit)
        dq_ref[rows, :] = (dq[...] * HEAD_DIM**-0.5).astype(BF16).T
        return carry

    lax.fori_loop(0, count // block, query_block, 0)
    dk_ref[...] = (dk[...] * LN2).astype(BF16)
    dv_ref[...] = dv[...].astype(BF16)


def pair_grad(p, rng, kv, queries, keep, send, own, other, inverse, shares):
    count = kv.shape[0]
    return pl.pallas_call(
        functools.partial(pair_grad_kernel, p),
        out_shape=(jax.ShapeDtypeStruct((count, PAIR), BF16),) * 3,
        in_specs=[SM] + [VM] * 8,
        out_specs=(VM,) * 3,
        scratch_shapes=[
            pltpu.VMEM((2 * count, PAIR), BF16),
            pltpu.VMEM((PAIR, 2 * count), BF16),
            pltpu.VMEM((PAIR, count), BF16),
            pltpu.VMEM((8, count), F32),
            pltpu.VMEM((PAIR, BLOCK), F32),
            pltpu.VMEM((count, PAIR), F32),
            pltpu.VMEM((count, PAIR), F32),
        ],
        compiler_params=pltpu.CompilerParams(vmem_limit_bytes=12 * MIB),
        cost_estimate=pl.CostEstimate(flops=4 * 10**9, bytes_accessed=8 * MIB, transcendentals=0),
        name=f"pair_grad_{p}",
    )(rng, kv, queries, keep, send, own, other, inverse, shares)


def input_part(flip, pieces, weights, half):
    which = 1 - lax.axis_index("mp") if flip else lax.axis_index("mp")
    rows = aligned(which, half)
    left = jnp.concatenate([piece[rows, :] for piece in pieces], 1)
    right = jnp.concatenate([weight[...] for weight in weights], 1)
    return dot_nt(left, right)


def away_kernel(*refs):
    out_ref = refs[-1]
    out_ref[...] = input_part(True, refs[:-4], refs[-4:-1], out_ref.shape[0]).astype(BF16)


def home_kernel(first_ref, got_ref, *refs):
    *pieces, wq_ref, wk_ref, wv_ref, out_hbm, out_ref, sems = refs
    half = out_ref.shape[0]
    parts = 2
    size = half // parts
    right = jnp.concatenate([wq_ref[...], wk_ref[...], wv_ref[...]], 1)
    copies = []
    for t in range(parts):
        part = slice(t * size, (t + 1) * size)
        rows = aligned(lax.axis_index("mp") * parts + t, size)
        total = dot_nt(jnp.concatenate([piece[rows, :] for piece in pieces], 1), right)
        out_ref[part, :] = (total + first_ref[part, :] + got_ref[part, :].astype(F32)).astype(BF16)
        copies.append(pltpu.make_async_copy(out_ref.at[part, :], out_hbm.at[part, :], sems.at[t]))
        copies[-1].start()
    for copy in copies:
        copy.wait()


def input_call(kernel, extra, pieces, weights, name):
    half, features = pieces[0].shape[0] // 2, weights[0].shape[0]
    return pl.pallas_call(
        kernel,
        out_shape=jax.ShapeDtypeStruct((half, features), BF16),
        in_specs=[VM] * (len(extra) + len(pieces) + len(weights)),
        out_specs=HB if extra else VM,
        scratch_shapes=[pltpu.VMEM((half, features), BF16), pltpu.SemaphoreType.DMA((2,))] if extra else [],
        compiler_params=pltpu.CompilerParams(vmem_limit_bytes=16 * MIB),
        cost_estimate=pl.CostEstimate(flops=10**9, bytes_accessed=6 * MIB, transcendentals=0),
        name=name,
    )(*extra, *pieces, *weights)


def gelu_both(v):
    part = 0.5 + 0.5 * lax.erf(v * ROOT_HALF)
    return v * part, part + v * jnp.exp(-0.5 * v * v) * ROOT_TWO_PI


def norm(values, gain, shift):
    mean = jnp.mean(values, -1, keepdims=True)
    centred = values - mean
    reciprocal = lax.rsqrt(jnp.mean(centred * centred, -1, keepdims=True) + EPS)
    normed = centred * reciprocal
    return normed * gain + shift, normed, reciprocal


def norm_grad(upstream, normed, reciprocal, gain):
    scaled = upstream * gain
    return reciprocal * (
        scaled - jnp.mean(scaled, -1, keepdims=True) - normed * jnp.mean(scaled * normed, -1, keepdims=True)
    )


def column_sum(values):
    return jnp.sum(values, 0, keepdims=True)


def middle_kernel(
    x_ref, keep_ref, got_ref, up_ref,
    mdb_ref, mub_ref, ddb_ref, dub_ref, fg_ref, fs_ref, sg_ref, ss_ref,
    wo2_ref, w12_ref, w22_ref, wo_hbm, md_hbm, mu_hbm, w1_hbm, w2_hbm, dd_hbm, du_hbm,
    act_hbm, first_ref, own_ref, away_ref, mine_ref, theirs_ref,
    wo_ref, md_ref, mu_ref, w1_ref, w2_ref, dd_ref, du_ref,
    slope_ref, hidden_ref, normed_ref, act_ref, big_ref, small_ref, sems, act_sem,
):
    rows, features = x_ref.shape
    adapt = md_ref.shape[0]
    names = ("wo", "md", "mu", "w1", "w2", "dd", "du")
    waits = dict(
        zip(
            names,
            start_all(
                (wo_hbm, md_hbm, mu_hbm, w1_hbm, w2_hbm, dd_hbm, du_hbm),
                (wo_ref, md_ref, mu_ref, w1_ref, w2_ref, dd_ref, du_ref),
                sems,
            ),
        )
    )

    def vector(ref):
        return ref[...].astype(F32).reshape(1, -1)

    x = x_ref[...].astype(F32)
    waits["wo"].wait()
    attended = dot(keep_ref[...], wo_ref[...])
    attended = attended + dot(got_ref[...], wo2_ref[...])
    attended_low = attended.astype(BF16)
    waits["md"].wait()
    waits["mu"].wait()
    mixer_active, mixer_slope = gelu_both(dot_nt(attended_low, md_ref[...]) + vector(mdb_ref))
    mixer_active = mixer_active.astype(BF16)
    mixer_out = dot(mixer_active, mu_ref[...]) + vector(mub_ref)
    hidden, normed_one, reciprocal_one = norm(x + attended + mixer_out, vector(fg_ref), vector(fs_ref))
    normed_ref[...] = normed_one
    hidden_ref[...] = hidden
    mixer_square = jnp.sum(column_sum(mixer_out * mixer_out), -1, keepdims=True)
    input_square = jnp.sum(column_sum(x * x), -1, keepdims=True)
    hidden_low = hidden.astype(BF16)
    chunk = 512
    units = w1_ref.shape[1]
    sides = ((w1_ref, w2_ref, "w1", "w2"), (w12_ref, w22_ref, None, None))
    dense_in = jnp.zeros((rows, features), F32)
    for s, (win, wout, first, second) in enumerate(sides):
        for name in (first, second):
            if name:
                waits[name].wait()
        for c in range(units // chunk):
            span = slice(c * chunk, (c + 1) * chunk)
            value, slope = gelu_both(dot(hidden_low, win[:, span]))
            slope_ref[:, s * units + c * chunk : s * units + (c + 1) * chunk] = slope.astype(BF16)
            dense_in = dense_in + dot(value.astype(BF16), wout[span, :])
    dense_low = dense_in.astype(BF16)
    waits["dd"].wait()
    waits["du"].wait()
    dense_active, dense_slope = gelu_both(dot_nt(dense_low, dd_ref[...]) + vector(ddb_ref))
    dense_active = dense_active.astype(BF16)
    dense_out = dot(dense_active, du_ref[...]) + vector(dub_ref)
    second_gain = vector(sg_ref)
    result, normed_two, reciprocal_two = norm(hidden_ref[...] + dense_in + dense_out, second_gain, vector(ss_ref))
    act_ref[...] = result.astype(BF16)
    act_copy = pltpu.make_async_copy(act_ref, act_hbm, act_sem)
    act_copy.start()
    dense_square = jnp.sum(column_sum(dense_out * dense_out), -1, keepdims=True)

    upstream = up_ref[...].astype(F32)
    small_ref[4:5, :] = column_sum(upstream * normed_two)
    small_ref[5:6, :] = column_sum(upstream)
    second_grad = norm_grad(upstream, normed_two, reciprocal_two, second_gain)
    dense_top = second_grad.astype(BF16)
    big_ref[3 * adapt : 4 * adapt, :] = dot_tn(dense_active, dense_top).astype(BF16)
    small_ref[1:2, :] = column_sum(dense_top.astype(F32))
    dense_mid = (dot_nt(dense_top, du_ref[...]) * dense_slope).astype(BF16)
    big_ref[2 * adapt : 3 * adapt, :] = dot_tn(dense_mid, dense_low).astype(BF16)
    dense_mid_sum = column_sum(dense_mid.astype(F32))
    dense_in_grad = (second_grad + dot(dense_mid, dd_ref[...])).astype(BF16)
    hidden_grad = second_grad
    for s, (win, wout, _, _) in enumerate(sides):
        for c in range(units // chunk):
            span = slice(c * chunk, (c + 1) * chunk)
            slope = slope_ref[:, s * units + c * chunk : s * units + (c + 1) * chunk].astype(F32)
            inner_grad = (dot_nt(dense_in_grad, wout[span, :]) * slope).astype(BF16)
            hidden_grad = hidden_grad + dot_nt(inner_grad, win[:, span])
    normed_one = normed_ref[...]
    small_ref[2:3, :] = column_sum(hidden_grad * normed_one)
    small_ref[3:4, :] = column_sum(hidden_grad)
    first_grad = norm_grad(hidden_grad, normed_one, reciprocal_one, vector(fg_ref))
    first_ref[...] = first_grad
    mixer_top = first_grad.astype(BF16)
    big_ref[adapt : 2 * adapt, :] = dot_tn(mixer_active, mixer_top).astype(BF16)
    small_ref[0:1, :] = column_sum(mixer_top.astype(F32))
    mixer_mid = (dot_nt(mixer_top, mu_ref[...]) * mixer_slope).astype(BF16)
    big_ref[0:adapt, :] = dot_tn(mixer_mid, attended_low).astype(BF16)
    mixer_mid_sum = column_sum(mixer_mid.astype(F32))
    attended_grad = (first_grad + dot(mixer_mid, md_ref[...])).astype(BF16)
    own_ref[...] = dot_nt(attended_grad, wo_ref[...]).astype(BF16)
    away_ref[...] = dot_nt(attended_grad, wo2_ref[...]).astype(BF16)
    lane = lax.broadcasted_iota(jnp.int32, (1, 128), 1)
    squares = jnp.where(lane == 0, mixer_square, jnp.where(lane == 1, dense_square, jnp.where(lane == 2, input_square, 0.0)))
    small_ref[6:7, :] = jnp.concatenate(
        [mixer_mid_sum, dense_mid_sum, squares, jnp.zeros((1, features - 2 * adapt - 128), F32)], 1
    )
    small_ref[7:8, :] = jnp.zeros((1, features), F32)
    tail = tail_of(small_ref[...])
    share = 2 * adapt
    for out_ref, which in ((mine_ref, lax.axis_index("mp")), (theirs_ref, 1 - lax.axis_index("mp"))):
        out_ref[:share, :] = big_ref[aligned(which, share), :]
        out_ref[share:, :] = tail
    act_copy.wait()


def tail_of(vectors):
    high = vectors.astype(BF16)
    return jnp.concatenate([high, (vectors - high.astype(F32)).astype(BF16)], 0)


def vectors_of(tail):
    wide = tail.astype(F32)
    return wide[:8] + wide[8:]


def middle(x, keep, got, up, vectors, swapped, matrices):
    rows, features = x.shape
    width = keep.shape[1]
    adapt = matrices[1].shape[0]
    units = matrices[3].shape[1]
    packed = jax.ShapeDtypeStruct((2 * adapt + 16, features), BF16)
    return pl.pallas_call(
        middle_kernel,
        out_shape=(
            jax.ShapeDtypeStruct((rows, features), BF16),
            jax.ShapeDtypeStruct((rows, features), F32),
            jax.ShapeDtypeStruct((rows, width), BF16),
            jax.ShapeDtypeStruct((rows, width), BF16),
            packed,
            packed,
        ),
        in_specs=[VM] * 15 + [HB] * 7,
        out_specs=(HB,) + (VM,) * 5,
        scratch_shapes=[pltpu.VMEM(m.shape, BF16) for m in matrices]
        + [
            pltpu.VMEM((rows, 2 * units), BF16),
            pltpu.VMEM((rows, features), F32),
            pltpu.VMEM((rows, features), F32),
            pltpu.VMEM((rows, features), BF16),
            pltpu.VMEM((4 * adapt, features), BF16),
            pltpu.VMEM((8, features), F32),
            pltpu.SemaphoreType.DMA((7,)),
            pltpu.SemaphoreType.DMA,
        ],
        compiler_params=pltpu.CompilerParams(vmem_limit_bytes=26 * MIB),
        cost_estimate=pl.CostEstimate(flops=2 * 10**10, bytes_accessed=16 * MIB, transcendentals=10**6),
        name="middle",
    )(x, keep, got, up, *vectors, *swapped, *map(in_hbm, matrices))


def combine_kernel(held_ref, got_ref, out_ref):
    rows = held_ref.shape[0] - 16
    out_ref[:rows, :] = (held_ref[:rows, :].astype(F32) + got_ref[:rows, :].astype(F32)).astype(BF16)
    out_ref[rows:, :] = tail_of(vectors_of(held_ref[rows:, :]) + vectors_of(got_ref[rows:, :]))


def combine(held, got):
    return pl.pallas_call(
        combine_kernel,
        out_shape=jax.ShapeDtypeStruct(held.shape, BF16),
        in_specs=[VM] * 2,
        out_specs=VM,
        compiler_params=pltpu.CompilerParams(vmem_limit_bytes=4 * MIB),
        cost_estimate=pl.CostEstimate(flops=10**5, bytes_accessed=MIB, transcendentals=0),
        name="combine",
    )(held, got)


def finish_kernel(held_ref, got_ref, md_ref, mdb_ref, mu_ref, mub_ref, dd_ref, ddb_ref, du_ref, dub_ref,
                  fg_ref, fs_ref, sg_ref, ss_ref, ratio_ref):
    adapt = md_ref.shape[0]

    def write(first_ref, second_ref):
        md_ref[...] = first_ref[:adapt, :].astype(F32)
        mu_ref[...] = first_ref[adapt : 2 * adapt, :].astype(F32)
        dd_ref[...] = second_ref[:adapt, :].astype(F32)
        du_ref[...] = second_ref[adapt : 2 * adapt, :].astype(F32)
        vectors = vectors_of(first_ref[2 * adapt :, :])
        for row, out_ref in enumerate((mub_ref, dub_ref, fg_ref, fs_ref, sg_ref, ss_ref)):
            out_ref[...] = vectors[row, :]
        last = vectors[6:7, :]
        mdb_ref[...] = last[0, :adapt]
        ddb_ref[...] = last[0, adapt : 2 * adapt]
        squares = last[:, 2 * adapt : 2 * adapt + 128]
        lane = lax.broadcasted_iota(jnp.int32, (1, 128), 1)
        base = jnp.sum(jnp.where(lane == 2, squares, 0.0), -1, keepdims=True)
        ratio_ref[...] = jnp.sqrt(squares / base)[0, :2]

    @pl.when(lax.axis_index("mp") == 0)
    def _():
        write(held_ref, got_ref)

    @pl.when(lax.axis_index("mp") != 0)
    def _():
        write(got_ref, held_ref)


def finish(held, got, adapt):
    features = held.shape[1]
    matrix = jax.ShapeDtypeStruct((adapt, features), F32)
    short, vector = jax.ShapeDtypeStruct((adapt,), F32), jax.ShapeDtypeStruct((features,), F32)
    return pl.pallas_call(
        finish_kernel,
        out_shape=(matrix, short, matrix, vector) * 2 + (vector,) * 4 + (jax.ShapeDtypeStruct((2,), F32),),
        in_specs=[VM, VM],
        out_specs=(VM,) * 13,
        compiler_params=pltpu.CompilerParams(vmem_limit_bytes=4 * MIB),
        name="finish",
    )(held, got)


def swap_cores(value):
    return lax.ppermute(value, "mp", [(0, 1), (1, 0)])


def tie(*values):
    return lax.optimization_barrier(values)


def per_device(
    tokens, segment_ids, query_weight, key_weight, value_weight, output_weight, inner_weight, outer_weight,
    mixer_down, mixer_down_bias, mixer_up, mixer_up_bias, dense_down, dense_down_bias, dense_up, dense_up_bias,
    first_gain, first_shift, second_gain, second_shift, output_grad,
):
    devices = lax.axis_size("dp")
    adapt = mixer_down.shape[1]
    other_tokens = swap_cores(tokens)
    kv, queries, across, turned, item, hide, rng = project(
        segment_ids, tokens, query_weight, key_weight, value_weight
    )
    kv, other_tokens, output_late, inner_late, outer_late = tie(
        kv, other_tokens, output_weight, inner_weight, outer_weight
    )
    other_output = swap_cores(output_late)
    other_inner = swap_cores(inner_late)
    other_outer = swap_cores(outer_late)
    kv, queries, keep, send, inverse, *shares = attention(
        rng, other_tokens, item, hide, query_weight, key_weight, value_weight, kv, queries, across, turned
    )
    got = swap_cores(send)
    vectors = (
        mixer_down_bias, mixer_up_bias, dense_down_bias, dense_up_bias, first_gain, first_shift, second_gain, second_shift,
    )
    swapped = (other_output, other_inner, other_outer)
    matrices = (output_weight, mixer_down.T, mixer_up, inner_weight, outer_weight, dense_down.T, dense_up)
    result, first_grad, own_grad, away_grad, mine, theirs = middle(
        tokens, keep, got, output_grad, vectors, swapped, matrices
    )
    got_grad = swap_cores(away_grad)
    packed = combine(mine, swap_cores(theirs))

    steps = []
    while 2 ** len(steps) < devices:
        steps.append(2 ** len(steps))
    steps.reverse()
    turn = len(steps) // 2
    pairs = len(shares)
    grads = []
    weights = (query_weight, key_weight, value_weight)
    for n, step in enumerate(steps):
        other_step = steps[(n + turn) % len(steps)]
        exchange = [(2 * i + c, 2 * (i ^ s) + c) for i in range(devices) for c, s in enumerate((step, other_step))]
        arriving = lax.ppermute(packed, ("dp", "mp"), exchange)
        if n < pairs:
            got_grad, packed = tie(got_grad, packed)
            parts = pair_grad(n, rng, kv, queries, keep, send, own_grad, got_grad, inverse, shares[n])
            arriving, *parts = tie(arriving, *parts)
            grads.append(parts)
        elif n == pairs:
            pieces = [grads[p][i] for i in range(3) for p in range(pairs)]
            away = swap_cores(input_call(away_kernel, (), pieces, weights, "away"))
            input_grad = input_call(home_kernel, (first_grad, away), pieces, weights, "home")
            arriving, input_grad = tie(arriving, input_grad)
        packed = combine(packed, arriving)
    md, mdb, mu, mub, dd, ddb, du, dub, *rest = finish(packed, swap_cores(packed), adapt)
    return (result, input_grad, md.T, mdb, mu, mub, dd.T, ddb, du, dub, *rest)


def solution(mesh):
    tokens = P(("dp", "mp"), None)
    columns, rows, whole = P(None, "mp"), P("mp", None), P()
    return jax.shard_map(
        per_device,
        mesh=mesh,
        in_specs=(tokens, P("dp", None), columns, columns, columns, rows, columns, rows) + (whole,) * 12 + (tokens,),
        out_specs=(tokens, tokens) + (whole,) * 13,
        check_vma=False,
    )
```

```python
import functools

import jax
import jax.numpy as jnp
from jax import lax
from jax.experimental import pallas as pl
from jax.experimental.pallas import tpu as pltpu
from jax.sharding import PartitionSpec as P

F32 = jnp.float32
BF16 = jnp.bfloat16
HEAD_DIM = 64
PAIR = 2 * HEAD_DIM
EPS = 1e-12
LOG2E = 1.4426950408889634
LN2 = 0.6931471805599453
ROOT_HALF = 0.7071067811865476
ROOT_TWO_PI = 0.3989422804014327
MASKED = -(2.0**100)
LARGEST = 2.0**100
SMALLEST = 2.0**-60
TURNED = 80
BLOCK = 256
STEP = 128
MIB = 1 << 20

VM = pl.BlockSpec(memory_space=pltpu.VMEM)
SM = pl.BlockSpec(memory_space=pltpu.SMEM)
HB = pl.BlockSpec(memory_space=pltpu.HBM)


def dot(left, right):
    return jnp.dot(left, right, preferred_element_type=F32)


def dot_nt(left, right):
    return lax.dot_general(left, right, (((1,), (1,)), ((), ())), preferred_element_type=F32)


def dot_tn(left, right):
    return lax.dot_general(left, right, (((0,), (0,)), ((), ())), preferred_element_type=F32)


def aligned(index, size):
    return pl.ds(pl.multiple_of(index * size, size), size)


def split_pair(pair):
    lane = lax.broadcasted_iota(jnp.int32, pair.shape, 1)
    zero = jnp.zeros_like(pair)
    return jnp.where(lane < HEAD_DIM, pair, zero), jnp.where(lane < HEAD_DIM, zero, pair)


def stack_heads(source, target, block):
    first, second = split_pair(source)
    for t in range(source.shape[0] // block):
        target[pl.ds(2 * t * block, block), :] = first[t * block : (t + 1) * block]
        target[pl.ds((2 * t + 1) * block, block), :] = second[t * block : (t + 1) * block]


def stack_heads_across(source, target, block):
    row = lax.broadcasted_iota(jnp.int32, source.shape, 0)
    zero = jnp.zeros_like(source)
    first = jnp.where(row < HEAD_DIM, source, zero)
    second = jnp.where(row < HEAD_DIM, zero, source)
    for t in range(source.shape[1] // block):
        target[:, 2 * t * block : (2 * t + 1) * block] = first[:, t * block : (t + 1) * block]
        target[:, (2 * t + 1) * block : (2 * t + 2) * block] = second[:, t * block : (t + 1) * block]


def in_hbm(value):
    return pltpu.with_memory_space_constraint(value, pltpu.HBM)


def start_all(sources, buffers, sems):
    copies = [pltpu.make_async_copy(src, dst, sems.at[i]) for i, (src, dst) in enumerate(zip(sources, buffers))]
    for copy in copies:
        copy.start()
    return copies


def write_projection(which, x, weights, copies, kv_ref, queries_ref, across_ref, turned_ref):
    rows, width = x.shape[0], weights[0].shape[1]
    pairs = width // PAIR
    if copies:
        copies[0].wait()
    queries = (dot(x, weights[0][...]) * (HEAD_DIM**-0.5 * LOG2E)).astype(BF16)
    for p in range(pairs):
        pair = queries[:, p * PAIR : (p + 1) * PAIR]
        stack_heads(pair, queries_ref.at[p, aligned(which, 2 * rows), :], BLOCK)
        stack_heads_across(pair.T, across_ref.at[p, :, aligned(which, 2 * rows)], BLOCK)
    if copies:
        copies[1].wait()
    kv_ref[aligned(which, rows), :width] = dot(x, weights[1][...]).astype(BF16)
    if copies:
        copies[2].wait()
    values = dot(x, weights[2][...]).astype(BF16)
    kv_ref[aligned(which, rows), width:] = values
    ones = jnp.ones((TURNED - HEAD_DIM, rows), BF16)
    for p in range(pairs):
        turned = values[:, p * PAIR : (p + 1) * PAIR].T
        for a in range(2):
            base = (2 * p + a) * TURNED
            turned_ref[base : base + HEAD_DIM, aligned(which, rows)] = turned[a * HEAD_DIM : (a + 1) * HEAD_DIM]
            turned_ref[base + HEAD_DIM : base + TURNED, aligned(which, rows)] = ones


def over_keys(low, high, visit):
    def whole(t, c):
        visit(pl.ds(pl.multiple_of(low * STEP + t * BLOCK, STEP), BLOCK), BLOCK)
        return c

    lax.fori_loop(0, (high - low) // 2, whole, 0)

    @pl.when((high - low) % 2 == 1)
    def _():
        visit(pl.ds(pl.multiple_of((high - 1) * STEP, STEP), STEP), STEP)


def is_shift(lane):
    return (lane == 63) | (lane == 95) | (lane == 127)


def project_kernel(
    seg_hbm, x_ref, wq_ref, wk_ref, wv_ref,
    kv_ref, queries_ref, across_ref, turned_ref, item_ref, hide_ref, rng_ref,
    seg_ref, x_buf, wq, wk, wv, sems,
):
    sources, buffers = (seg_hbm, x_ref, wq_ref, wk_ref, wv_ref), (seg_ref, x_buf, wq, wk, wv)
    seg_copy, *copies = start_all(sources, buffers, sems)
    count, block = kv_ref.shape[0], BLOCK
    seg_copy.wait()
    ids = seg_ref[...].astype(F32)
    position = lax.broadcasted_iota(jnp.int32, ids.shape, 1)
    for g in range(count // block):
        first, last = (
            jnp.sum(jnp.where(position == at, ids, 0.0), -1, keepdims=True) for at in (g * block, (g + 1) * block - 1)
        )
        rng_ref[0, g] = jnp.sum(jnp.where(ids < first, 1.0, 0.0)).astype(jnp.int32) // STEP
        rng_ref[1, g] = (jnp.sum(jnp.where(ids <= last, 1.0, 0.0)).astype(jnp.int32) + STEP - 1) // STEP
    lane = lax.broadcasted_iota(jnp.int32, (128, 128), 1)
    for t in range(count // 128):
        same = jnp.broadcast_to(ids[:, t * 128 : (t + 1) * 128], (128, 128)).T == lane.astype(F32)
        item_ref[t * 128 : (t + 1) * 128, :] = jnp.where(same | is_shift(lane), 1.0, 0.0).astype(BF16)
    row = lax.broadcasted_iota(jnp.int32, (128, block), 0)
    for t in range(count // block):
        same = row.astype(F32) == ids[:, t * block : (t + 1) * block]
        hide = jnp.where(same | is_shift(row), 0.0, MASKED).astype(BF16)
        for a in range(2):
            hide_ref[:, (2 * t + a) * block : (2 * t + a + 1) * block] = hide
    copies[0].wait()
    write_projection(lax.axis_index("mp"), x_buf[...], (wq, wk, wv), copies[1:], kv_ref, queries_ref, across_ref, turned_ref)


def project(seg, x, wq, wk, wv):
    rows, width = x.shape[0], wq.shape[1]
    count, pairs = 2 * rows, width // PAIR
    return pl.pallas_call(
        project_kernel,
        out_shape=(
            jax.ShapeDtypeStruct((count, 2 * width), BF16),
            jax.ShapeDtypeStruct((pairs, 2 * count, PAIR), BF16),
            jax.ShapeDtypeStruct((pairs, PAIR, 2 * count), BF16),
            jax.ShapeDtypeStruct((2 * pairs * TURNED, count), BF16),
            jax.ShapeDtypeStruct((count, 128), BF16),
            jax.ShapeDtypeStruct((128, 2 * count), BF16),
            jax.ShapeDtypeStruct((2, count // BLOCK), jnp.int32),
        ),
        in_specs=[HB] * 5,
        out_specs=(VM,) * 6 + (SM,),
        scratch_shapes=[pltpu.VMEM(v.shape, v.dtype) for v in (seg, x, wq, wk, wv)] + [pltpu.SemaphoreType.DMA((5,))],
        compiler_params=pltpu.CompilerParams(vmem_limit_bytes=16 * MIB),
        cost_estimate=pl.CostEstimate(flops=2 * rows * x.shape[1] * 3 * width, bytes_accessed=5 * MIB, transcendentals=0),
        name="project",
    )(*map(in_hbm, (seg, x, wq, wk, wv)))


def attention_kernel(
    rng_ref, x_ref, item_ref, hide_ref, wq_ref, wk_ref, wv_ref, kv_in, queries_in, across_in, turned_in,
    kv_ref, queries_ref, keep_ref, send_ref, inverse_ref, *rest,
):
    half = x_ref.shape[0]
    count, width = kv_ref.shape[0], wq_ref.shape[1]
    pairs, block = width // PAIR, BLOCK
    share_refs = rest[:pairs]
    across, turned, mix, shifted, peaks = rest[pairs:]
    here, there = lax.axis_index("mp"), 1 - lax.axis_index("mp")
    turned[:, aligned(here, half)] = turned_in[:, aligned(here, half)]
    across[:, :, aligned(here, 2 * half)] = across_in[:, :, aligned(here, 2 * half)]
    kv_ref[aligned(here, half), :] = kv_in[aligned(here, half), :]
    queries_ref[:, aligned(here, 2 * half), :] = queries_in[:, aligned(here, 2 * half), :]
    write_projection(there, x_ref[...], (wq_ref, wk_ref, wv_ref), (), kv_ref, queries_ref, across, turned)

    def scores(p, span, both, hide):
        keys = jnp.concatenate([kv_ref[span, p * PAIR : (p + 1) * PAIR], item_ref[span, :]], 1)
        return dot(keys, jnp.concatenate([across[p, :, both], hide], 0))

    def query_block(g, carry):
        rows, both = aligned(g, block), aligned(g, 2 * block)
        low, high = rng_ref[0, g], rng_ref[1, g]

        def mix_all(hide_of):
            mix[...] = jnp.zeros(mix.shape, F32)

            def visit(span, size):
                ahead = scores(0, span, both, hide_of(0))
                for p in range(pairs):
                    s = ahead
                    if p + 1 < pairs:
                        ahead = scores(p + 1, span, both, hide_of(p + 1))
                    e = jnp.exp2(s).astype(BF16)
                    share_refs[p][span, both] = e
                    for a in range(2):
                        head = slice((2 * p + a) * TURNED, (2 * p + a + 1) * TURNED)
                        mix[head, :] += dot(turned[head, span], e[:, a * block : (a + 1) * block])

            over_keys(low, high, visit)

        mix_all(lambda p: hide_ref[:, both])
        total_rows = [h * TURNED + HEAD_DIM for h in range(2 * pairs)]
        sums = jnp.concatenate([mix[r : r + 8, :] for r in total_rows], 0)
        fine = jnp.where((sums <= LARGEST) & (sums >= SMALLEST), 0.0, 1.0)

        @pl.when(jnp.max(fine) > 0.0)
        def _():
            peaks[...] = jnp.full(peaks.shape, MASKED, F32)

            def visit(span, size):
                for p in range(pairs):
                    s = scores(p, span, both, hide_ref[:, both])
                    peaks[p] = jnp.maximum(peaks[p], jnp.max(s, 0, keepdims=True))

            over_keys(low, high, visit)
            row = lax.broadcasted_iota(jnp.int32, (128, 2 * block), 0)
            hide = hide_ref[:, both].astype(F32)
            for p in range(pairs):
                peak = peaks[p]
                first = peak.astype(BF16).astype(F32)
                second = (peak - first).astype(BF16).astype(F32)
                third = peak - first - second
                parts = jnp.where(row < 64, first, jnp.where(row < 96, second, third))
                shifted[p] = jnp.where(is_shift(row), -parts, hide).astype(BF16)
            mix_all(lambda p: shifted[p])

        outs = []
        for p in range(pairs):
            scales = []
            for a in range(2):
                base = (2 * p + a) * TURNED
                scale = jnp.broadcast_to(1.0 / mix[base + HEAD_DIM : base + HEAD_DIM + 1, :], (HEAD_DIM, block))
                outs.append((mix[base : base + HEAD_DIM, :] * scale).astype(BF16))
                scales.append(scale)
            inverse_ref[rows, p * PAIR : (p + 1) * PAIR] = jnp.concatenate(scales, 0).T
        result = jnp.concatenate(outs, 0).T
        per_half = half // block

        @pl.when(g // per_half == here)
        def _():
            keep_ref[aligned(g % per_half, block), :] = result

        @pl.when(g // per_half != here)
        def _():
            send_ref[aligned(g % per_half, block), :] = result

        return carry

    lax.fori_loop(0, count // block, query_block, 0)


def attention(rng, x, item, hide, wq, wk, wv, kv, queries, across, turned):
    half, width = x.shape[0], wq.shape[1]
    count, pairs = 2 * half, width // PAIR
    like = lambda v: jax.ShapeDtypeStruct(v.shape, v.dtype)
    return pl.pallas_call(
        attention_kernel,
        out_shape=(
            like(kv),
            like(queries),
            jax.ShapeDtypeStruct((half, width), BF16),
            jax.ShapeDtypeStruct((half, width), BF16),
            jax.ShapeDtypeStruct((count, width), F32),
        )
        + (jax.ShapeDtypeStruct((count, 2 * count), BF16),) * pairs,
        in_specs=[SM] + [VM] * 10,
        out_specs=(VM,) * (5 + pairs),
        scratch_shapes=[
            pltpu.VMEM(across.shape, BF16),
            pltpu.VMEM(turned.shape, BF16),
            pltpu.VMEM((2 * pairs * TURNED, BLOCK), F32),
            pltpu.VMEM((pairs, 128, 2 * BLOCK), BF16),
            pltpu.VMEM((pairs, 1, 2 * BLOCK), F32),
        ],
        compiler_params=pltpu.CompilerParams(vmem_limit_bytes=12 * MIB),
        cost_estimate=pl.CostEstimate(flops=10**10, bytes_accessed=8 * MIB, transcendentals=10**6),
        name="attention",
    )(rng, x, item, hide, wq, wk, wv, kv, queries, across, turned)


def pair_grad_kernel(
    p, rng_ref, kv_ref, queries_ref, keep_ref, send_ref, own_ref, other_ref, inverse_ref, share_ref,
    dq_ref, dk_ref, dv_ref,
    grads, across, turned, delta, dq, dk, dv,
):
    half, width = keep_ref.shape
    count, block = kv_ref.shape[0], BLOCK
    cols = slice(p * PAIR, (p + 1) * PAIR)
    here, there = lax.axis_index("mp"), 1 - lax.axis_index("mp")
    row = lax.broadcasted_iota(jnp.int32, (8, PAIR), 0)
    column = lax.broadcasted_iota(jnp.int32, (8, PAIR), 1)
    pick = jnp.where(column // HEAD_DIM == row, 1.0, 0.0).astype(BF16)
    for which, mixed_ref, up_ref in ((here, keep_ref, own_ref), (there, send_ref, other_ref)):
        scaled = (up_ref[:, cols].astype(F32) * inverse_ref[aligned(which, half), cols]).astype(BF16)
        product = mixed_ref[:, cols].astype(F32) * scaled.astype(F32)
        high = product.astype(BF16)
        low = (product - high.astype(F32)).astype(BF16)
        delta[:, aligned(which, half)] = dot_nt(pick, high) + dot_nt(pick, low)
        stack_heads(scaled, grads.at[aligned(which, 2 * half), :], block)
        stack_heads_across(scaled.T, across.at[:, aligned(which, 2 * half)], block)
    turned[...] = kv_ref[:, cols].T
    dk[...] = jnp.zeros(dk.shape, F32)
    dv[...] = jnp.zeros(dv.shape, F32)

    def query_block(g, carry):
        rows, both = aligned(g, block), aligned(g, 2 * block)
        dq[...] = jnp.zeros(dq.shape, F32)
        level = jnp.concatenate([delta[0:1, rows], delta[1:2, rows]], 1)

        def visit(span, size):
            d = dot(kv_ref[span, width + p * PAIR : width + (p + 1) * PAIR], across[:, both])
            shares = share_ref[span, both]
            slopes = (shares.astype(F32) * (d - level)).astype(BF16)
            dv[span, :] += dot(shares, grads[both, :])
            dk[span, :] += dot(slopes, queries_ref[p, both, :])
            for a in range(2):
                head = slice(a * HEAD_DIM, (a + 1) * HEAD_DIM)
                dq[head, :] += dot(turned[head, span], slopes[:, a * block : (a + 1) * block])

        over_keys(rng_ref[0, g], rng_ref[1, g], visit)
        dq_ref[rows, :] = (dq[...] * HEAD_DIM**-0.5).astype(BF16).T
        return carry

    lax.fori_loop(0, count // block, query_block, 0)
    dk_ref[...] = (dk[...] * LN2).astype(BF16)
    dv_ref[...] = dv[...].astype(BF16)


def pair_grad(p, rng, kv, queries, keep, send, own, other, inverse, shares):
    count = kv.shape[0]
    return pl.pallas_call(
        functools.partial(pair_grad_kernel, p),
        out_shape=(jax.ShapeDtypeStruct((count, PAIR), BF16),) * 3,
        in_specs=[SM] + [VM] * 8,
        out_specs=(VM,) * 3,
        scratch_shapes=[
            pltpu.VMEM((2 * count, PAIR), BF16),
            pltpu.VMEM((PAIR, 2 * count), BF16),
            pltpu.VMEM((PAIR, count), BF16),
            pltpu.VMEM((8, count), F32),
            pltpu.VMEM((PAIR, BLOCK), F32),
            pltpu.VMEM((count, PAIR), F32),
            pltpu.VMEM((count, PAIR), F32),
        ],
        compiler_params=pltpu.CompilerParams(vmem_limit_bytes=12 * MIB),
        cost_estimate=pl.CostEstimate(flops=4 * 10**9, bytes_accessed=8 * MIB, transcendentals=0),
        name=f"pair_grad_{p}",
    )(rng, kv, queries, keep, send, own, other, inverse, shares)


def input_part(flip, pieces, weights, half):
    which = 1 - lax.axis_index("mp") if flip else lax.axis_index("mp")
    rows = aligned(which, half)
    left = jnp.concatenate([piece[rows, :] for piece in pieces], 1)
    right = jnp.concatenate([weight[...] for weight in weights], 1)
    return dot_nt(left, right)


def away_kernel(*refs):
    out_ref = refs[-1]
    out_ref[...] = input_part(True, refs[:-4], refs[-4:-1], out_ref.shape[0]).astype(BF16)


def home_kernel(first_ref, got_ref, *refs):
    *pieces, wq_ref, wk_ref, wv_ref, out_hbm, out_ref, sems = refs
    half = out_ref.shape[0]
    parts = 2
    size = half // parts
    right = jnp.concatenate([wq_ref[...], wk_ref[...], wv_ref[...]], 1)
    copies = []
    for t in range(parts):
        part = slice(t * size, (t + 1) * size)
        rows = aligned(lax.axis_index("mp") * parts + t, size)
        total = dot_nt(jnp.concatenate([piece[rows, :] for piece in pieces], 1), right)
        out_ref[part, :] = (total + first_ref[part, :] + got_ref[part, :].astype(F32)).astype(BF16)
        copies.append(pltpu.make_async_copy(out_ref.at[part, :], out_hbm.at[part, :], sems.at[t]))
        copies[-1].start()
    for copy in copies:
        copy.wait()


def input_call(kernel, extra, pieces, weights, name):
    half, features = pieces[0].shape[0] // 2, weights[0].shape[0]
    return pl.pallas_call(
        kernel,
        out_shape=jax.ShapeDtypeStruct((half, features), BF16),
        in_specs=[VM] * (len(extra) + len(pieces) + len(weights)),
        out_specs=HB if extra else VM,
        scratch_shapes=[pltpu.VMEM((half, features), BF16), pltpu.SemaphoreType.DMA((2,))] if extra else [],
        compiler_params=pltpu.CompilerParams(vmem_limit_bytes=16 * MIB),
        cost_estimate=pl.CostEstimate(flops=10**9, bytes_accessed=6 * MIB, transcendentals=0),
        name=name,
    )(*extra, *pieces, *weights)


def gelu_both(v):
    part = 0.5 + 0.5 * lax.erf(v * ROOT_HALF)
    return v * part, part + v * jnp.exp(-0.5 * v * v) * ROOT_TWO_PI


def norm(values, gain, shift):
    mean = jnp.mean(values, -1, keepdims=True)
    centred = values - mean
    reciprocal = lax.rsqrt(jnp.mean(centred * centred, -1, keepdims=True) + EPS)
    normed = centred * reciprocal
    return normed * gain + shift, normed, reciprocal


def norm_grad(upstream, normed, reciprocal, gain):
    scaled = upstream * gain
    return reciprocal * (
        scaled - jnp.mean(scaled, -1, keepdims=True) - normed * jnp.mean(scaled * normed, -1, keepdims=True)
    )


def column_sum(values):
    return jnp.sum(values, 0, keepdims=True)


def eight_rows(values):
    return jnp.sum(values.reshape(-1, 8, values.shape[1]), 0)


def interleave(first, second):
    done = 0
    for i, step in enumerate(first):
        step()
        while done < len(second) and (done + 1) * len(first) <= (i + 1) * len(second):
            second[done]()
            done += 1
    for step in second[done:]:
        step()


def middle_kernel(
    x_ref, keep_ref, got_ref, up_ref,
    mdb_ref, mub_ref, ddb_ref, dub_ref, fg_ref, fs_ref, sg_ref, ss_ref,
    wo2_ref, w12_ref, w22_ref, wo_hbm, md_hbm, mu_hbm, w1_hbm, w2_hbm, dd_hbm, du_hbm,
    act_hbm, first_ref, own_ref, away_ref, mine_ref, theirs_ref,
    wo_ref, md_ref, mu_ref, w1_ref, w2_ref, dd_ref, du_ref,
    slope_ref, wide_ref, out_ref, hidden_ref, normed_ref, low_ref, hidden_low_ref, act_ref, top_ref,
    big_ref, small_ref, sems, act_sem,
):
    rows, features = x_ref.shape
    adapt = md_ref.shape[0]
    names = ("wo", "md", "mu", "w1", "w2", "dd", "du")
    waits = dict(
        zip(
            names,
            start_all(
                (wo_hbm, md_hbm, mu_hbm, w1_hbm, w2_hbm, dd_hbm, du_hbm),
                (wo_ref, md_ref, mu_ref, w1_ref, w2_ref, dd_ref, du_ref),
                sems,
            ),
        )
    )
    waited = set()

    def need(*wanted):
        for name in wanted:
            if name not in waited:
                waited.add(name)
                waits[name].wait()

    def vector(ref):
        return ref[...].astype(F32).reshape(1, -1)

    units = w1_ref.shape[1]
    chunk, piece_rows = 512, 64
    sides = ((w1_ref, w2_ref, ("w1", "w2")), (w12_ref, w22_ref, ()))
    pieces = [(side, slice(c * chunk, (c + 1) * chunk)) for side in sides for c in range(units // chunk)]
    kept = {}
    sums = {}

    def add(name, value):
        sums[name] = sums[name] + value if name in sums else value

    def parts(half):
        return [slice(r, r + piece_rows) for r in range(half.start, half.stop, piece_rows)]

    def attend(half):
        def first():
            need("wo")
            attended = dot(keep_ref[half, :], wo_ref[...]) + dot(got_ref[half, :], wo2_ref[...])
            wide_ref[half, :] = attended
            low_ref[half, :] = attended.astype(BF16)

        def second():
            need("md", "mu")
            active, slope = gelu_both(dot_nt(low_ref[half, :], md_ref[...]) + vector(mdb_ref))
            kept["mixer", half.start] = (active.astype(BF16), slope)

        def third():
            out_ref[half, :] = dot(kept["mixer", half.start][0], mu_ref[...]) + vector(mub_ref)

        return [first, second, third]

    def norm_one(half):
        def one(part):
            x, mixer_out = x_ref[part, :].astype(F32), out_ref[part, :]
            add("mixer_square", eight_rows(mixer_out * mixer_out))
            add("input_square", eight_rows(x * x))
            hidden, normed, reciprocal = norm(x + wide_ref[part, :] + mixer_out, vector(fg_ref), vector(fs_ref))
            normed_ref[part, :] = normed
            hidden_ref[part, :] = hidden
            hidden_low_ref[part, :] = hidden.astype(BF16)
            kept["reciprocal", part.start] = reciprocal

        return [functools.partial(one, part) for part in parts(half)]

    def feed_forward(half):
        state = {}

        def start():
            need("w1", "w2")
            side, span = pieces[0]
            state["ahead"] = dot(hidden_low_ref[half, :], side[0][:, span])

        def one(n):
            side, span = pieces[n]
            inner = state["ahead"]
            if n + 1 < len(pieces):
                after, after_span = pieces[n + 1]
                state["ahead"] = dot(hidden_low_ref[half, :], after[0][:, after_span])
            value, slope = gelu_both(inner)
            slope_ref[half, n * chunk : (n + 1) * chunk] = slope.astype(BF16)
            state["value"] = value.astype(BF16)

        def two(n):
            side, span = pieces[n]
            total = dot(state["value"], side[1][span, :])
            state["total"] = state["total"] + total if n else total
            if n + 1 == len(pieces):
                wide_ref[half, :] = state["total"]

        steps = [start]
        for n in range(len(pieces)):
            steps += [functools.partial(one, n), functools.partial(two, n)]
        return steps

    def dense(half):
        def first():
            need("dd", "du")
            dense_low = wide_ref[half, :].astype(BF16)
            active, slope = gelu_both(dot_nt(dense_low, dd_ref[...]) + vector(ddb_ref))
            kept["dense", half.start] = (active.astype(BF16), slope, dense_low)

        def second():
            out_ref[half, :] = dot(kept["dense", half.start][0], du_ref[...]) + vector(dub_ref)

        return [first, second]

    def norm_two(half):
        def one(part):
            dense_out = out_ref[part, :]
            add("dense_square", eight_rows(dense_out * dense_out))
            gain = vector(sg_ref)
            result, normed, reciprocal = norm(hidden_ref[part, :] + wide_ref[part, :] + dense_out, gain, vector(ss_ref))
            act_ref[part, :] = result.astype(BF16)
            upstream = up_ref[part, :].astype(F32)
            add(4, eight_rows(upstream * normed))
            add(5, eight_rows(upstream))
            second_grad = norm_grad(upstream, normed, reciprocal, gain)
            hidden_ref[part, :] = second_grad
            top = second_grad.astype(BF16)
            top_ref[part, :] = top
            add(1, eight_rows(top.astype(F32)))

        return [functools.partial(one, part) for part in parts(half)]

    def dense_back(half):
        def first():
            active, slope, dense_low = kept["dense", half.start]
            top = top_ref[half, :]
            add("dense_up", dot_tn(active, top))
            mid = (dot_nt(top, du_ref[...]) * slope).astype(BF16)
            kept["dense_mid", half.start] = mid
            add("dense_mid", eight_rows(mid.astype(F32)))

        def second():
            mid = kept["dense_mid", half.start]
            add("dense_down", dot_tn(mid, kept["dense", half.start][2]))
            hidden_low_ref[half, :] = (hidden_ref[half, :] + dot(mid, dd_ref[...])).astype(BF16)

        return [first, second]

    def feed_back(half):
        state = {}

        def start():
            side, span = pieces[0]
            state["ahead"] = dot_nt(hidden_low_ref[half, :], side[1][span, :])

        def one(n):
            back = state["ahead"]
            if n + 1 < len(pieces):
                after, after_span = pieces[n + 1]
                state["ahead"] = dot_nt(hidden_low_ref[half, :], after[1][after_span, :])
            slope = slope_ref[half, n * chunk : (n + 1) * chunk].astype(F32)
            state["value"] = (back * slope).astype(BF16)

        def two(n):
            side, span = pieces[n]
            total = dot_nt(state["value"], side[0][:, span])
            state["total"] = state["total"] + total if n else total
            if n + 1 == len(pieces):
                hidden_ref[half, :] = hidden_ref[half, :] + state["total"]

        steps = [start]
        for n in range(len(pieces)):
            steps += [functools.partial(one, n), functools.partial(two, n)]
        return steps

    def norm_one_back(half):
        def one(part):
            hidden_grad, normed = hidden_ref[part, :], normed_ref[part, :]
            add(2, eight_rows(hidden_grad * normed))
            add(3, eight_rows(hidden_grad))
            first_grad = norm_grad(hidden_grad, normed, kept["reciprocal", part.start], vector(fg_ref))
            first_ref[part, :] = first_grad
            top = first_grad.astype(BF16)
            top_ref[part, :] = top
            add(0, eight_rows(top.astype(F32)))

        return [functools.partial(one, part) for part in parts(half)]

    def attend_back(half):
        def first():
            active, slope = kept["mixer", half.start]
            top = top_ref[half, :]
            add("mixer_up", dot_tn(active, top))
            mid = (dot_nt(top, mu_ref[...]) * slope).astype(BF16)
            kept["mixer_mid", half.start] = mid
            add("mixer_mid", eight_rows(mid.astype(F32)))

        def second():
            mid = kept["mixer_mid", half.start]
            add("mixer_down", dot_tn(mid, low_ref[half, :]))
            kept["attended", half.start] = (first_ref[half, :] + dot(mid, md_ref[...])).astype(BF16)

        def third():
            own_ref[half, :] = dot_nt(kept["attended", half.start], wo_ref[...]).astype(BF16)

        def fourth():
            away_ref[half, :] = dot_nt(kept["attended", half.start], wo2_ref[...]).astype(BF16)

        return [first, second, third, fourth]

    def send_result(half, index):
        copy = pltpu.make_async_copy(act_ref.at[half, :], act_hbm.at[half, :], act_sem.at[index])
        copy.start()
        return copy

    one, two = slice(0, rows // 2), slice(rows // 2, rows)
    interleave(attend(one), [])
    interleave(norm_one(one), attend(two))
    interleave(feed_forward(one), norm_one(two))
    interleave(feed_forward(two), dense(one) + norm_two(one) + dense_back(one))
    copies = [send_result(one, 0)]
    interleave(feed_back(one), dense(two) + norm_two(two) + dense_back(two))
    copies.append(send_result(two, 1))
    interleave(feed_back(two), norm_one_back(one) + attend_back(one))
    interleave(norm_one_back(two), [])
    interleave(attend_back(two), [])

    for n, name in enumerate(("mixer_down", "mixer_up", "dense_down", "dense_up")):
        big_ref[n * adapt : (n + 1) * adapt, :] = sums[name].astype(BF16)
    for row in range(6):
        small_ref[row : row + 1, :] = column_sum(sums[row])
    lane = lax.broadcasted_iota(jnp.int32, (1, 128), 1)
    squares = jnp.zeros((1, 128), F32)
    for n, name in enumerate(("mixer_square", "dense_square", "input_square")):
        squares = jnp.where(lane == n, jnp.sum(column_sum(sums[name]), -1, keepdims=True), squares)
    small_ref[6:7, :] = jnp.concatenate(
        [column_sum(sums["mixer_mid"]), column_sum(sums["dense_mid"]), squares, jnp.zeros((1, features - 2 * adapt - 128), F32)], 1
    )
    small_ref[7:8, :] = jnp.zeros((1, features), F32)
    tail = tail_of(small_ref[...])
    share = 2 * adapt
    for pack_ref, which in ((mine_ref, lax.axis_index("mp")), (theirs_ref, 1 - lax.axis_index("mp"))):
        pack_ref[:share, :] = big_ref[aligned(which, share), :]
        pack_ref[share:, :] = tail
    for copy in copies:
        copy.wait()


def tail_of(vectors):
    high = vectors.astype(BF16)
    return jnp.concatenate([high, (vectors - high.astype(F32)).astype(BF16)], 0)


def vectors_of(tail):
    wide = tail.astype(F32)
    return wide[:8] + wide[8:]


def middle(x, keep, got, up, vectors, swapped, matrices):
    rows, features = x.shape
    width = keep.shape[1]
    adapt = matrices[1].shape[0]
    units = matrices[3].shape[1]
    packed = jax.ShapeDtypeStruct((2 * adapt + 16, features), BF16)
    return pl.pallas_call(
        middle_kernel,
        out_shape=(
            jax.ShapeDtypeStruct((rows, features), BF16),
            jax.ShapeDtypeStruct((rows, features), F32),
            jax.ShapeDtypeStruct((rows, width), BF16),
            jax.ShapeDtypeStruct((rows, width), BF16),
            packed,
            packed,
        ),
        in_specs=[VM] * 15 + [HB] * 7,
        out_specs=(HB,) + (VM,) * 5,
        scratch_shapes=[pltpu.VMEM(m.shape, BF16) for m in matrices]
        + [pltpu.VMEM((rows, 2 * units), BF16)]
        + [pltpu.VMEM((rows, features), F32)] * 4
        + [pltpu.VMEM((rows, features), BF16)] * 4
        + [
            pltpu.VMEM((4 * adapt, features), BF16),
            pltpu.VMEM((8, features), F32),
            pltpu.SemaphoreType.DMA((7,)),
            pltpu.SemaphoreType.DMA((2,)),
        ],
        compiler_params=pltpu.CompilerParams(vmem_limit_bytes=28 * MIB),
        cost_estimate=pl.CostEstimate(flops=2 * 10**10, bytes_accessed=16 * MIB, transcendentals=10**6),
        name="middle",
    )(x, keep, got, up, *vectors, *swapped, *map(in_hbm, matrices))


def combine_kernel(held_ref, got_ref, out_ref):
    rows = held_ref.shape[0] - 16
    out_ref[:rows, :] = (held_ref[:rows, :].astype(F32) + got_ref[:rows, :].astype(F32)).astype(BF16)
    out_ref[rows:, :] = tail_of(vectors_of(held_ref[rows:, :]) + vectors_of(got_ref[rows:, :]))


def combine(held, got):
    return pl.pallas_call(
        combine_kernel,
        out_shape=jax.ShapeDtypeStruct(held.shape, BF16),
        in_specs=[VM] * 2,
        out_specs=VM,
        compiler_params=pltpu.CompilerParams(vmem_limit_bytes=4 * MIB),
        cost_estimate=pl.CostEstimate(flops=10**5, bytes_accessed=MIB, transcendentals=0),
        name="combine",
    )(held, got)


def finish_kernel(held_ref, got_ref, md_ref, mdb_ref, mu_ref, mub_ref, dd_ref, ddb_ref, du_ref, dub_ref,
                  fg_ref, fs_ref, sg_ref, ss_ref, ratio_ref):
    adapt = md_ref.shape[0]

    def write(first_ref, second_ref):
        md_ref[...] = first_ref[:adapt, :].astype(F32)
        mu_ref[...] = first_ref[adapt : 2 * adapt, :].astype(F32)
        dd_ref[...] = second_ref[:adapt, :].astype(F32)
        du_ref[...] = second_ref[adapt : 2 * adapt, :].astype(F32)
        vectors = vectors_of(first_ref[2 * adapt :, :])
        for row, out_ref in enumerate((mub_ref, dub_ref, fg_ref, fs_ref, sg_ref, ss_ref)):
            out_ref[...] = vectors[row, :]
        last = vectors[6:7, :]
        mdb_ref[...] = last[0, :adapt]
        ddb_ref[...] = last[0, adapt : 2 * adapt]
        squares = last[:, 2 * adapt : 2 * adapt + 128]
        lane = lax.broadcasted_iota(jnp.int32, (1, 128), 1)
        base = jnp.sum(jnp.where(lane == 2, squares, 0.0), -1, keepdims=True)
        ratio_ref[...] = jnp.sqrt(squares / base)[0, :2]

    @pl.when(lax.axis_index("mp") == 0)
    def _():
        write(held_ref, got_ref)

    @pl.when(lax.axis_index("mp") != 0)
    def _():
        write(got_ref, held_ref)


def finish(held, got, adapt):
    features = held.shape[1]
    matrix = jax.ShapeDtypeStruct((adapt, features), F32)
    short, vector = jax.ShapeDtypeStruct((adapt,), F32), jax.ShapeDtypeStruct((features,), F32)
    return pl.pallas_call(
        finish_kernel,
        out_shape=(matrix, short, matrix, vector) * 2 + (vector,) * 4 + (jax.ShapeDtypeStruct((2,), F32),),
        in_specs=[VM, VM],
        out_specs=(VM,) * 13,
        compiler_params=pltpu.CompilerParams(vmem_limit_bytes=4 * MIB),
        name="finish",
    )(held, got)


def swap_cores(value):
    return lax.ppermute(value, "mp", [(0, 1), (1, 0)])


def tie(*values):
    return lax.optimization_barrier(values)


def per_device(
    tokens, segment_ids, query_weight, key_weight, value_weight, output_weight, inner_weight, outer_weight,
    mixer_down, mixer_down_bias, mixer_up, mixer_up_bias, dense_down, dense_down_bias, dense_up, dense_up_bias,
    first_gain, first_shift, second_gain, second_shift, output_grad,
):
    devices = lax.axis_size("dp")
    adapt = mixer_down.shape[1]
    other_tokens = swap_cores(tokens)
    kv, queries, across, turned, item, hide, rng = project(
        segment_ids, tokens, query_weight, key_weight, value_weight
    )
    kv, other_tokens, output_late, inner_late, outer_late = tie(
        kv, other_tokens, output_weight, inner_weight, outer_weight
    )
    other_output = swap_cores(output_late)
    other_inner = swap_cores(inner_late)
    other_outer = swap_cores(outer_late)
    kv, queries, keep, send, inverse, *shares = attention(
        rng, other_tokens, item, hide, query_weight, key_weight, value_weight, kv, queries, across, turned
    )
    got = swap_cores(send)
    vectors = (
        mixer_down_bias, mixer_up_bias, dense_down_bias, dense_up_bias, first_gain, first_shift, second_gain, second_shift,
    )
    swapped = (other_output, other_inner, other_outer)
    matrices = (output_weight, mixer_down.T, mixer_up, inner_weight, outer_weight, dense_down.T, dense_up)
    result, first_grad, own_grad, away_grad, mine, theirs = middle(
        tokens, keep, got, output_grad, vectors, swapped, matrices
    )
    got_grad = swap_cores(away_grad)
    packed = combine(mine, swap_cores(theirs))

    steps = []
    while 2 ** len(steps) < devices:
        steps.append(2 ** len(steps))
    steps.reverse()
    turn = len(steps) // 2
    pairs = len(shares)
    grads = []
    weights = (query_weight, key_weight, value_weight)
    for n, step in enumerate(steps):
        other_step = steps[(n + turn) % len(steps)]
        exchange = [(2 * i + c, 2 * (i ^ s) + c) for i in range(devices) for c, s in enumerate((step, other_step))]
        arriving = lax.ppermute(packed, ("dp", "mp"), exchange)
        if n < pairs:
            got_grad, packed = tie(got_grad, packed)
            parts = pair_grad(n, rng, kv, queries, keep, send, own_grad, got_grad, inverse, shares[n])
            arriving, *parts = tie(arriving, *parts)
            grads.append(parts)
        elif n == pairs:
            pieces = [grads[p][i] for i in range(3) for p in range(pairs)]
            away = swap_cores(input_call(away_kernel, (), pieces, weights, "away"))
            input_grad = input_call(home_kernel, (first_grad, away), pieces, weights, "home")
            arriving, input_grad = tie(arriving, input_grad)
        packed = combine(packed, arriving)
    md, mdb, mu, mub, dd, ddb, du, dub, *rest = finish(packed, swap_cores(packed), adapt)
    return (result, input_grad, md.T, mdb, mu, mub, dd.T, ddb, du, dub, *rest)


def solution(mesh):
    tokens = P(("dp", "mp"), None)
    columns, rows, whole = P(None, "mp"), P("mp", None), P()
    return jax.shard_map(
        per_device,
        mesh=mesh,
        in_specs=(tokens, P("dp", None), columns, columns, columns, rows, columns, rows) + (whole,) * 12 + (tokens,),
        out_specs=(tokens, tokens) + (whole,) * 13,
        check_vma=False,
    )
```

```python
import functools

import jax
import jax.numpy as jnp
from jax import lax
from jax.experimental import pallas as pl
from jax.experimental.pallas import tpu as pltpu
from jax.sharding import PartitionSpec as P

F32 = jnp.float32
BF16 = jnp.bfloat16
HEAD_DIM = 64
PAIR = 2 * HEAD_DIM
EPS = 1e-12
LOG2E = 1.4426950408889634
LN2 = 0.6931471805599453
ROOT_HALF = 0.7071067811865476
ROOT_TWO_PI = 0.3989422804014327
MASKED = -(2.0**100)
LARGEST = 2.0**100
SMALLEST = 2.0**-60
TURNED = 80
BLOCK = 256
STEP = 128
MIB = 1 << 20
SHORT = pl.CostEstimate(flops=10**4, bytes_accessed=10**3, transcendentals=0)

VM = pl.BlockSpec(memory_space=pltpu.VMEM)
SM = pl.BlockSpec(memory_space=pltpu.SMEM)
HB = pl.BlockSpec(memory_space=pltpu.HBM)


def dot(left, right):
    return jnp.dot(left, right, preferred_element_type=F32)


def dot_nt(left, right):
    return lax.dot_general(left, right, (((1,), (1,)), ((), ())), preferred_element_type=F32)


def dot_tn(left, right):
    return lax.dot_general(left, right, (((0,), (0,)), ((), ())), preferred_element_type=F32)


def aligned(index, size):
    return pl.ds(pl.multiple_of(index * size, size), size)


def split_pair(pair):
    lane = lax.broadcasted_iota(jnp.int32, pair.shape, 1)
    zero = jnp.zeros_like(pair)
    return jnp.where(lane < HEAD_DIM, pair, zero), jnp.where(lane < HEAD_DIM, zero, pair)


def stack_heads(source, target, block):
    first, second = split_pair(source)
    for t in range(source.shape[0] // block):
        target[pl.ds(2 * t * block, block), :] = first[t * block : (t + 1) * block]
        target[pl.ds((2 * t + 1) * block, block), :] = second[t * block : (t + 1) * block]


def stack_heads_across(source, target, block):
    row = lax.broadcasted_iota(jnp.int32, source.shape, 0)
    zero = jnp.zeros_like(source)
    first = jnp.where(row < HEAD_DIM, source, zero)
    second = jnp.where(row < HEAD_DIM, zero, source)
    for t in range(source.shape[1] // block):
        target[:, 2 * t * block : (2 * t + 1) * block] = first[:, t * block : (t + 1) * block]
        target[:, (2 * t + 1) * block : (2 * t + 2) * block] = second[:, t * block : (t + 1) * block]


def in_hbm(value):
    return pltpu.with_memory_space_constraint(value, pltpu.HBM)


def start_all(sources, buffers, sems):
    copies = [pltpu.make_async_copy(src, dst, sems.at[i]) for i, (src, dst) in enumerate(zip(sources, buffers))]
    for copy in copies:
        copy.start()
    return copies


def write_projection(which, x, weights, copies, kv_ref, queries_ref, across_ref, turned_ref, between=None):
    rows, width = x.shape[0], weights[0].shape[1]
    pairs = width // PAIR
    if copies:
        copies[0].wait()
    queries = (dot(x, weights[0][...]) * (HEAD_DIM**-0.5 * LOG2E)).astype(BF16)
    if between is not None:
        between()
    for p in range(pairs):
        pair = queries[:, p * PAIR : (p + 1) * PAIR]
        stack_heads(pair, queries_ref.at[p, aligned(which, 2 * rows), :], BLOCK)
        stack_heads_across(pair.T, across_ref.at[p, :, aligned(which, 2 * rows)], BLOCK)
    if copies:
        copies[1].wait()
    kv_ref[aligned(which, rows), :width] = dot(x, weights[1][...]).astype(BF16)
    if copies:
        copies[2].wait()
    values = dot(x, weights[2][...]).astype(BF16)
    kv_ref[aligned(which, rows), width:] = values
    ones = jnp.ones((TURNED - HEAD_DIM, rows), BF16)
    for p in range(pairs):
        turned = values[:, p * PAIR : (p + 1) * PAIR].T
        for a in range(2):
            base = (2 * p + a) * TURNED
            turned_ref[base : base + HEAD_DIM, aligned(which, rows)] = turned[a * HEAD_DIM : (a + 1) * HEAD_DIM]
            turned_ref[base + HEAD_DIM : base + TURNED, aligned(which, rows)] = ones


def over_keys(low, high, visit):
    def whole(t, c):
        visit(pl.ds(pl.multiple_of(low * STEP + t * BLOCK, STEP), BLOCK), BLOCK)
        return c

    lax.fori_loop(0, (high - low) // 2, whole, 0)

    @pl.when((high - low) % 2 == 1)
    def _():
        visit(pl.ds(pl.multiple_of((high - 1) * STEP, STEP), STEP), STEP)


def is_shift(lane):
    return (lane == 63) | (lane == 95) | (lane == 127)


def project_kernel(
    seg_hbm, x_ref, wq_ref, wk_ref, wv_ref,
    kv_ref, queries_ref, across_ref, turned_ref, item_ref, hide_ref, rng_ref,
    seg_ref, x_buf, wq, wk, wv, sems,
):
    sources, buffers = (seg_hbm, x_ref, wq_ref, wk_ref, wv_ref), (seg_ref, x_buf, wq, wk, wv)
    seg_copy, *copies = start_all(sources, buffers, sems)
    count, block = kv_ref.shape[0], BLOCK

    def items():
        ids = seg_ref[...].astype(F32)
        position = lax.broadcasted_iota(jnp.int32, ids.shape, 1)
        for g in range(count // block):
            first, last = (
                jnp.sum(jnp.where(position == at, ids, 0.0), -1, keepdims=True) for at in (g * block, (g + 1) * block - 1)
            )
            rng_ref[0, g] = jnp.sum(jnp.where(ids < first, 1.0, 0.0)).astype(jnp.int32) // STEP
            rng_ref[1, g] = (jnp.sum(jnp.where(ids <= last, 1.0, 0.0)).astype(jnp.int32) + STEP - 1) // STEP
        lane = lax.broadcasted_iota(jnp.int32, (128, 128), 1)
        for t in range(count // 128):
            same = jnp.broadcast_to(ids[:, t * 128 : (t + 1) * 128], (128, 128)).T == lane.astype(F32)
            item_ref[t * 128 : (t + 1) * 128, :] = jnp.where(same | is_shift(lane), 1.0, 0.0).astype(BF16)
        row = lax.broadcasted_iota(jnp.int32, (128, block), 0)
        for t in range(count // block):
            same = row.astype(F32) == ids[:, t * block : (t + 1) * block]
            hide = jnp.where(same | is_shift(row), 0.0, MASKED).astype(BF16)
            for a in range(2):
                hide_ref[:, (2 * t + a) * block : (2 * t + a + 1) * block] = hide

    seg_copy.wait()
    copies[0].wait()
    write_projection(
        lax.axis_index("mp"), x_buf[...], (wq, wk, wv), copies[1:], kv_ref, queries_ref, across_ref, turned_ref, items
    )


def project(seg, x, wq, wk, wv):
    rows, width = x.shape[0], wq.shape[1]
    count, pairs = 2 * rows, width // PAIR
    return pl.pallas_call(
        project_kernel,
        out_shape=(
            jax.ShapeDtypeStruct((count, 2 * width), BF16),
            jax.ShapeDtypeStruct((pairs, 2 * count, PAIR), BF16),
            jax.ShapeDtypeStruct((pairs, PAIR, 2 * count), BF16),
            jax.ShapeDtypeStruct((2 * pairs * TURNED, count), BF16),
            jax.ShapeDtypeStruct((count, 128), BF16),
            jax.ShapeDtypeStruct((128, 2 * count), BF16),
            jax.ShapeDtypeStruct((2, count // BLOCK), jnp.int32),
        ),
        in_specs=[HB] * 5,
        out_specs=(VM,) * 6 + (SM,),
        scratch_shapes=[pltpu.VMEM(v.shape, v.dtype) for v in (seg, x, wq, wk, wv)] + [pltpu.SemaphoreType.DMA((5,))],
        compiler_params=pltpu.CompilerParams(vmem_limit_bytes=16 * MIB),
        cost_estimate=pl.CostEstimate(flops=2 * rows * x.shape[1] * 3 * width, bytes_accessed=5 * MIB, transcendentals=0),
        name="project",
    )(*map(in_hbm, (seg, x, wq, wk, wv)))


def attention_kernel(
    rng_ref, x_ref, item_ref, hide_ref, wq_ref, wk_ref, wv_ref, kv_in, queries_in, across_in, turned_in,
    kv_ref, queries_ref, keep_ref, send_ref, inverse_ref, *rest,
):
    half = x_ref.shape[0]
    count, width = kv_ref.shape[0], wq_ref.shape[1]
    pairs, block = width // PAIR, BLOCK
    share_refs = rest[:pairs]
    across, turned, mix, shifted, peaks = rest[pairs:]
    here, there = lax.axis_index("mp"), 1 - lax.axis_index("mp")
    turned[:, aligned(here, half)] = turned_in[:, aligned(here, half)]
    across[:, :, aligned(here, 2 * half)] = across_in[:, :, aligned(here, 2 * half)]
    kv_ref[aligned(here, half), :] = kv_in[aligned(here, half), :]
    queries_ref[:, aligned(here, 2 * half), :] = queries_in[:, aligned(here, 2 * half), :]
    write_projection(there, x_ref[...], (wq_ref, wk_ref, wv_ref), (), kv_ref, queries_ref, across, turned)

    def scores(p, span, both, hide):
        keys = jnp.concatenate([kv_ref[span, p * PAIR : (p + 1) * PAIR], item_ref[span, :]], 1)
        return dot(keys, jnp.concatenate([across[p, :, both], hide], 0))

    def query_block(g, carry):
        rows, both = aligned(g, block), aligned(g, 2 * block)
        low, high = rng_ref[0, g], rng_ref[1, g]

        def mix_all(hide_of):
            mix[...] = jnp.zeros(mix.shape, F32)

            def visit(span, size):
                ahead = scores(0, span, both, hide_of(0))
                for p in range(pairs):
                    s = ahead
                    if p + 1 < pairs:
                        ahead = scores(p + 1, span, both, hide_of(p + 1))
                    e = jnp.exp2(s).astype(BF16)
                    share_refs[p][span, both] = e
                    for a in range(2):
                        head = slice((2 * p + a) * TURNED, (2 * p + a + 1) * TURNED)
                        mix[head, :] += dot(turned[head, span], e[:, a * block : (a + 1) * block])

            over_keys(low, high, visit)

        mix_all(lambda p: hide_ref[:, both])
        total_rows = [h * TURNED + HEAD_DIM for h in range(2 * pairs)]
        sums = jnp.concatenate([mix[r : r + 8, :] for r in total_rows], 0)
        fine = jnp.where((sums <= LARGEST) & (sums >= SMALLEST), 0.0, 1.0)

        @pl.when(jnp.max(fine) > 0.0)
        def _():
            peaks[...] = jnp.full(peaks.shape, MASKED, F32)

            def visit(span, size):
                for p in range(pairs):
                    s = scores(p, span, both, hide_ref[:, both])
                    peaks[p] = jnp.maximum(peaks[p], jnp.max(s, 0, keepdims=True))

            over_keys(low, high, visit)
            row = lax.broadcasted_iota(jnp.int32, (128, 2 * block), 0)
            hide = hide_ref[:, both].astype(F32)
            for p in range(pairs):
                peak = peaks[p]
                first = peak.astype(BF16).astype(F32)
                second = (peak - first).astype(BF16).astype(F32)
                third = peak - first - second
                parts = jnp.where(row < 64, first, jnp.where(row < 96, second, third))
                shifted[p] = jnp.where(is_shift(row), -parts, hide).astype(BF16)
            mix_all(lambda p: shifted[p])

        outs = []
        for p in range(pairs):
            scales = []
            for a in range(2):
                base = (2 * p + a) * TURNED
                scale = jnp.broadcast_to(1.0 / mix[base + HEAD_DIM : base + HEAD_DIM + 1, :], (HEAD_DIM, block))
                outs.append((mix[base : base + HEAD_DIM, :] * scale).astype(BF16))
                scales.append(scale)
            inverse_ref[rows, p * PAIR : (p + 1) * PAIR] = jnp.concatenate(scales, 0).T
        result = jnp.concatenate(outs, 0).T
        per_half = half // block

        @pl.when(g // per_half == here)
        def _():
            keep_ref[aligned(g % per_half, block), :] = result

        @pl.when(g // per_half != here)
        def _():
            send_ref[aligned(g % per_half, block), :] = result

        return carry

    lax.fori_loop(0, count // block, query_block, 0)


def attention(rng, x, item, hide, wq, wk, wv, kv, queries, across, turned):
    half, width = x.shape[0], wq.shape[1]
    count, pairs = 2 * half, width // PAIR
    like = lambda v: jax.ShapeDtypeStruct(v.shape, v.dtype)
    return pl.pallas_call(
        attention_kernel,
        out_shape=(
            like(kv),
            like(queries),
            jax.ShapeDtypeStruct((half, width), BF16),
            jax.ShapeDtypeStruct((half, width), BF16),
            jax.ShapeDtypeStruct((count, width), F32),
        )
        + (jax.ShapeDtypeStruct((count, 2 * count), BF16),) * pairs,
        in_specs=[SM] + [VM] * 10,
        out_specs=(VM,) * (5 + pairs),
        scratch_shapes=[
            pltpu.VMEM(across.shape, BF16),
            pltpu.VMEM(turned.shape, BF16),
            pltpu.VMEM((2 * pairs * TURNED, BLOCK), F32),
            pltpu.VMEM((pairs, 128, 2 * BLOCK), BF16),
            pltpu.VMEM((pairs, 1, 2 * BLOCK), F32),
        ],
        compiler_params=pltpu.CompilerParams(vmem_limit_bytes=12 * MIB),
        cost_estimate=pl.CostEstimate(flops=10**10, bytes_accessed=8 * MIB, transcendentals=10**6),
        name="attention",
    )(rng, x, item, hide, wq, wk, wv, kv, queries, across, turned)


def pair_grad_kernel(
    p, rng_ref, kv_ref, queries_ref, keep_ref, send_ref, own_ref, other_ref, inverse_ref, share_ref,
    home_ref, away_ref,
    grads, across, turned, delta, dq, dk, dv,
):
    half, width = keep_ref.shape
    count, block = kv_ref.shape[0], BLOCK
    cols = slice(p * PAIR, (p + 1) * PAIR)
    here, there = lax.axis_index("mp"), 1 - lax.axis_index("mp")
    row = lax.broadcasted_iota(jnp.int32, (8, PAIR), 0)
    column = lax.broadcasted_iota(jnp.int32, (8, PAIR), 1)
    pick = jnp.where(column // HEAD_DIM == row, 1.0, 0.0).astype(BF16)
    for which, mixed_ref, up_ref in ((here, keep_ref, own_ref), (there, send_ref, other_ref)):
        scaled = (up_ref[:, cols].astype(F32) * inverse_ref[aligned(which, half), cols]).astype(BF16)
        product = mixed_ref[:, cols].astype(F32) * scaled.astype(F32)
        high = product.astype(BF16)
        low = (product - high.astype(F32)).astype(BF16)
        delta[:, aligned(which, half)] = dot_nt(pick, high) + dot_nt(pick, low)
        stack_heads(scaled, grads.at[aligned(which, 2 * half), :], block)
        stack_heads_across(scaled.T, across.at[:, aligned(which, 2 * half)], block)
    turned[...] = kv_ref[:, cols].T
    dk[...] = jnp.zeros(dk.shape, F32)
    dv[...] = jnp.zeros(dv.shape, F32)

    def query_block(g, carry):
        rows, both = aligned(g, block), aligned(g, 2 * block)
        dq[...] = jnp.zeros(dq.shape, F32)
        level = jnp.concatenate([delta[0:1, rows], delta[1:2, rows]], 1)

        def visit(span, size):
            d = dot(kv_ref[span, width + p * PAIR : width + (p + 1) * PAIR], across[:, both])
            shares = share_ref[span, both]
            slopes = (shares.astype(F32) * (d - level)).astype(BF16)
            dv[span, :] += dot(shares, grads[both, :])
            dk[span, :] += dot(slopes, queries_ref[p, both, :])
            for a in range(2):
                head = slice(a * HEAD_DIM, (a + 1) * HEAD_DIM)
                dq[head, :] += dot(turned[head, span], slopes[:, a * block : (a + 1) * block])

        over_keys(rng_ref[0, g], rng_ref[1, g], visit)
        result = (dq[...] * HEAD_DIM**-0.5).astype(BF16).T
        per_half = half // block

        @pl.when(g // per_half == here)
        def _():
            home_ref[aligned(g % per_half, block), :PAIR] = result

        @pl.when(g // per_half != here)
        def _():
            away_ref[aligned(g % per_half, block), :PAIR] = result

        return carry

    lax.fori_loop(0, count // block, query_block, 0)
    for which, out_ref in ((here, home_ref), (there, away_ref)):
        rows = aligned(which, half)
        out_ref[:, PAIR : 2 * PAIR] = (dk[rows, :] * LN2).astype(BF16)
        out_ref[:, 2 * PAIR :] = dv[rows, :].astype(BF16)


def pair_grad(p, rng, kv, queries, keep, send, own, other, inverse, shares):
    count = kv.shape[0]
    return pl.pallas_call(
        functools.partial(pair_grad_kernel, p),
        out_shape=(jax.ShapeDtypeStruct((count // 2, 3 * PAIR), BF16),) * 2,
        in_specs=[SM] + [VM] * 8,
        out_specs=(VM,) * 2,
        scratch_shapes=[
            pltpu.VMEM((2 * count, PAIR), BF16),
            pltpu.VMEM((PAIR, 2 * count), BF16),
            pltpu.VMEM((PAIR, count), BF16),
            pltpu.VMEM((8, count), F32),
            pltpu.VMEM((PAIR, BLOCK), F32),
            pltpu.VMEM((count, PAIR), F32),
            pltpu.VMEM((count, PAIR), F32),
        ],
        compiler_params=pltpu.CompilerParams(vmem_limit_bytes=12 * MIB),
        cost_estimate=pl.CostEstimate(flops=4 * 10**9, bytes_accessed=8 * MIB, transcendentals=0),
        name=f"pair_grad_{p}",
    )(rng, kv, queries, keep, send, own, other, inverse, shares)


def input_kernel(pairs, first_ref, *refs):
    *refs, out_hbm, out_ref, sems = refs
    pieces, weights = refs[: 2 * pairs], refs[2 * pairs :]
    spans = [slice(p * PAIR, (p + 1) * PAIR) for p in range(pairs)]
    right = jnp.concatenate(
        [weight[:, span] for side in (weights[:3], weights[3:]) for span in spans for weight in side], 1
    )
    size = out_ref.shape[0] // 2
    copies = []
    for t in range(2):
        part = slice(t * size, (t + 1) * size)
        left = jnp.concatenate([piece[part, :] for piece in pieces], 1)
        out_ref[part, :] = (dot_nt(left, right) + first_ref[part, :]).astype(BF16)
        copies.append(pltpu.make_async_copy(out_ref.at[part, :], out_hbm.at[part, :], sems.at[t]))
        copies[-1].start()
    for copy in copies:
        copy.wait()


def input_gradient(first_grad, pieces, weights):
    return pl.pallas_call(
        functools.partial(input_kernel, len(pieces) // 2),
        out_shape=jax.ShapeDtypeStruct(first_grad.shape, BF16),
        in_specs=[VM] * (1 + len(pieces) + len(weights)),
        out_specs=HB,
        scratch_shapes=[pltpu.VMEM(first_grad.shape, BF16), pltpu.SemaphoreType.DMA((2,))],
        compiler_params=pltpu.CompilerParams(vmem_limit_bytes=16 * MIB),
        cost_estimate=pl.CostEstimate(flops=2 * 10**9, bytes_accessed=8 * MIB, transcendentals=0),
        name="input_gradient",
    )(first_grad, *pieces, *weights)


def gelu_both(v):
    part = 0.5 + 0.5 * lax.erf(v * ROOT_HALF)
    return v * part, part + v * jnp.exp(-0.5 * v * v) * ROOT_TWO_PI


def norm(values, gain, shift):
    mean = jnp.mean(values, -1, keepdims=True)
    centred = values - mean
    reciprocal = lax.rsqrt(jnp.mean(centred * centred, -1, keepdims=True) + EPS)
    normed = centred * reciprocal
    return normed * gain + shift, normed, reciprocal


def norm_grad(upstream, normed, reciprocal, gain):
    scaled = upstream * gain
    return reciprocal * (
        scaled - jnp.mean(scaled, -1, keepdims=True) - normed * jnp.mean(scaled * normed, -1, keepdims=True)
    )


def column_sum(values):
    return jnp.sum(values, 0, keepdims=True)


def eight_rows(values):
    return jnp.sum(values.reshape(-1, 8, values.shape[1]), 0)


def interleave(first, second):
    done = 0
    for i, step in enumerate(first):
        step()
        while done < len(second) and (done + 1) * len(first) <= (i + 1) * len(second):
            second[done]()
            done += 1
    for step in second[done:]:
        step()


def middle_kernel(
    x_ref, keep_ref, got_ref, up_ref,
    mdb_ref, mub_ref, ddb_ref, dub_ref, fg_ref, fs_ref, sg_ref, ss_ref,
    wo2_ref, w12_ref, w22_ref, wo_hbm, md_hbm, mu_hbm, w1_hbm, w2_hbm, dd_hbm, du_hbm,
    act_hbm, first_ref, attended_ref, mine_ref, theirs_ref,
    wo_ref, md_ref, mu_ref, w1_ref, w2_ref, dd_ref, du_ref,
    slope_ref, wide_ref, out_ref, hidden_ref, normed_ref, low_ref, hidden_low_ref, act_ref, top_ref,
    big_ref, small_ref, sems, act_sem,
):
    rows, features = x_ref.shape
    adapt = md_ref.shape[0]
    names = ("wo", "md", "mu", "w1", "w2", "dd", "du")
    waits = dict(
        zip(
            names,
            start_all(
                (wo_hbm, md_hbm, mu_hbm, w1_hbm, w2_hbm, dd_hbm, du_hbm),
                (wo_ref, md_ref, mu_ref, w1_ref, w2_ref, dd_ref, du_ref),
                sems,
            ),
        )
    )
    waited = set()

    def need(*wanted):
        for name in wanted:
            if name not in waited:
                waited.add(name)
                waits[name].wait()

    def vector(ref):
        return ref[...].astype(F32).reshape(1, -1)

    units = w1_ref.shape[1]
    chunk, piece_rows = 512, 64
    sides = ((w1_ref, w2_ref, ("w1", "w2")), (w12_ref, w22_ref, ()))
    pieces = [(side, slice(c * chunk, (c + 1) * chunk)) for side in sides for c in range(units // chunk)]
    kept = {}
    sums = {}

    def add(name, value):
        sums[name] = sums[name] + value if name in sums else value

    def parts(half):
        return [slice(r, r + piece_rows) for r in range(half.start, half.stop, piece_rows)]

    def attend(half):
        def first():
            need("wo")
            attended = dot(keep_ref[half, :], wo_ref[...]) + dot(got_ref[half, :], wo2_ref[...])
            wide_ref[half, :] = attended
            low_ref[half, :] = attended.astype(BF16)

        def second():
            need("md", "mu")
            active, slope = gelu_both(dot_nt(low_ref[half, :], md_ref[...]) + vector(mdb_ref))
            kept["mixer", half.start] = (active.astype(BF16), slope)

        def third():
            out_ref[half, :] = dot(kept["mixer", half.start][0], mu_ref[...]) + vector(mub_ref)

        return [first, second, third]

    def norm_one(half):
        def one(part):
            x, mixer_out = x_ref[part, :].astype(F32), out_ref[part, :]
            add("mixer_square", eight_rows(mixer_out * mixer_out))
            add("input_square", eight_rows(x * x))
            hidden, normed, reciprocal = norm(x + wide_ref[part, :] + mixer_out, vector(fg_ref), vector(fs_ref))
            normed_ref[part, :] = normed
            hidden_ref[part, :] = hidden
            hidden_low_ref[part, :] = hidden.astype(BF16)
            kept["reciprocal", part.start] = reciprocal

        return [functools.partial(one, part) for part in parts(half)]

    def feed_forward(half):
        state = {}

        def start():
            need("w1", "w2")
            side, span = pieces[0]
            state["ahead"] = dot(hidden_low_ref[half, :], side[0][:, span])

        def one(n):
            side, span = pieces[n]
            inner = state["ahead"]
            if n + 1 < len(pieces):
                after, after_span = pieces[n + 1]
                state["ahead"] = dot(hidden_low_ref[half, :], after[0][:, after_span])
            value, slope = gelu_both(inner)
            slope_ref[half, n * chunk : (n + 1) * chunk] = slope.astype(BF16)
            state["value"] = value.astype(BF16)

        def two(n):
            side, span = pieces[n]
            total = dot(state["value"], side[1][span, :])
            state["total"] = state["total"] + total if n else total
            if n + 1 == len(pieces):
                wide_ref[half, :] = state["total"]

        steps = [start]
        for n in range(len(pieces)):
            steps += [functools.partial(one, n), functools.partial(two, n)]
        return steps

    def dense(half):
        def first():
            need("dd", "du")
            dense_low = wide_ref[half, :].astype(BF16)
            active, slope = gelu_both(dot_nt(dense_low, dd_ref[...]) + vector(ddb_ref))
            kept["dense", half.start] = (active.astype(BF16), slope, dense_low)

        def second():
            out_ref[half, :] = dot(kept["dense", half.start][0], du_ref[...]) + vector(dub_ref)

        return [first, second]

    def norm_two(half):
        def one(part):
            dense_out = out_ref[part, :]
            add("dense_square", eight_rows(dense_out * dense_out))
            gain = vector(sg_ref)
            result, normed, reciprocal = norm(hidden_ref[part, :] + wide_ref[part, :] + dense_out, gain, vector(ss_ref))
            act_ref[part, :] = result.astype(BF16)
            upstream = up_ref[part, :].astype(F32)
            add(4, eight_rows(upstream * normed))
            add(5, eight_rows(upstream))
            second_grad = norm_grad(upstream, normed, reciprocal, gain)
            hidden_ref[part, :] = second_grad
            top = second_grad.astype(BF16)
            top_ref[part, :] = top
            add(1, eight_rows(top.astype(F32)))

        return [functools.partial(one, part) for part in parts(half)]

    def dense_back(half):
        def first():
            active, slope, dense_low = kept["dense", half.start]
            top = top_ref[half, :]
            add("dense_up", dot_tn(active, top))
            mid = (dot_nt(top, du_ref[...]) * slope).astype(BF16)
            kept["dense_mid", half.start] = mid
            add("dense_mid", eight_rows(mid.astype(F32)))

        def second():
            mid = kept["dense_mid", half.start]
            add("dense_down", dot_tn(mid, kept["dense", half.start][2]))
            hidden_low_ref[half, :] = (hidden_ref[half, :] + dot(mid, dd_ref[...])).astype(BF16)

        return [first, second]

    def feed_back(half):
        state = {}

        def start():
            side, span = pieces[0]
            state["ahead"] = dot_nt(hidden_low_ref[half, :], side[1][span, :])

        def one(n):
            back = state["ahead"]
            if n + 1 < len(pieces):
                after, after_span = pieces[n + 1]
                state["ahead"] = dot_nt(hidden_low_ref[half, :], after[1][after_span, :])
            slope = slope_ref[half, n * chunk : (n + 1) * chunk].astype(F32)
            state["value"] = (back * slope).astype(BF16)

        def two(n):
            side, span = pieces[n]
            total = dot_nt(state["value"], side[0][:, span])
            state["total"] = state["total"] + total if n else total
            if n + 1 == len(pieces):
                hidden_ref[half, :] = hidden_ref[half, :] + state["total"]

        steps = [start]
        for n in range(len(pieces)):
            steps += [functools.partial(one, n), functools.partial(two, n)]
        return steps

    def norm_one_back(half):
        def one(part):
            hidden_grad, normed = hidden_ref[part, :], normed_ref[part, :]
            add(2, eight_rows(hidden_grad * normed))
            add(3, eight_rows(hidden_grad))
            first_grad = norm_grad(hidden_grad, normed, kept["reciprocal", part.start], vector(fg_ref))
            first_ref[part, :] = first_grad
            top = first_grad.astype(BF16)
            top_ref[part, :] = top
            add(0, eight_rows(top.astype(F32)))

        return [functools.partial(one, part) for part in parts(half)]

    def attend_back(half):
        def first():
            active, slope = kept["mixer", half.start]
            top = top_ref[half, :]
            add("mixer_up", dot_tn(active, top))
            mid = (dot_nt(top, mu_ref[...]) * slope).astype(BF16)
            kept["mixer_mid", half.start] = mid
            add("mixer_mid", eight_rows(mid.astype(F32)))

        def second():
            mid = kept["mixer_mid", half.start]
            add("mixer_down", dot_tn(mid, low_ref[half, :]))
            attended_ref[half, :] = (first_ref[half, :] + dot(mid, md_ref[...])).astype(BF16)

        return [first, second]

    def send_result(half, index):
        copy = pltpu.make_async_copy(act_ref.at[half, :], act_hbm.at[half, :], act_sem.at[index])
        copy.start()
        return copy

    one, two = slice(0, rows // 2), slice(rows // 2, rows)
    interleave(attend(one), [])
    interleave(norm_one(one), attend(two))
    interleave(feed_forward(one), norm_one(two))
    interleave(feed_forward(two), dense(one) + norm_two(one) + dense_back(one))
    copies = [send_result(one, 0)]
    interleave(feed_back(one), dense(two) + norm_two(two) + dense_back(two))
    copies.append(send_result(two, 1))
    interleave(feed_back(two), norm_one_back(one) + attend_back(one))
    interleave(norm_one_back(two), [])
    interleave(attend_back(two), [])

    for n, name in enumerate(("mixer_down", "mixer_up", "dense_down", "dense_up")):
        big_ref[n * adapt : (n + 1) * adapt, :] = sums[name].astype(BF16)
    for row in range(6):
        small_ref[row : row + 1, :] = column_sum(sums[row])
    lane = lax.broadcasted_iota(jnp.int32, (1, 128), 1)
    squares = jnp.zeros((1, 128), F32)
    for n, name in enumerate(("mixer_square", "dense_square", "input_square")):
        squares = jnp.where(lane == n, jnp.sum(column_sum(sums[name]), -1, keepdims=True), squares)
    small_ref[6:7, :] = jnp.concatenate(
        [column_sum(sums["mixer_mid"]), column_sum(sums["dense_mid"]), squares, jnp.zeros((1, features - 2 * adapt - 128), F32)], 1
    )
    small_ref[7:8, :] = jnp.zeros((1, features), F32)
    tail = tail_of(small_ref[...])
    share = 2 * adapt
    for pack_ref, which in ((mine_ref, lax.axis_index("mp")), (theirs_ref, 1 - lax.axis_index("mp"))):
        pack_ref[:share, :] = big_ref[aligned(which, share), :]
        pack_ref[share:, :] = tail
    for copy in copies:
        copy.wait()


def tail_of(vectors):
    high = vectors.astype(BF16)
    return jnp.concatenate([high, (vectors - high.astype(F32)).astype(BF16)], 0)


def vectors_of(tail):
    wide = tail.astype(F32)
    return wide[:8] + wide[8:]


def middle(x, keep, got, up, vectors, swapped, matrices):
    rows, features = x.shape
    adapt = matrices[1].shape[0]
    units = matrices[3].shape[1]
    packed = jax.ShapeDtypeStruct((2 * adapt + 16, features), BF16)
    return pl.pallas_call(
        middle_kernel,
        out_shape=(
            jax.ShapeDtypeStruct((rows, features), BF16),
            jax.ShapeDtypeStruct((rows, features), F32),
            jax.ShapeDtypeStruct((rows, features), BF16),
            packed,
            packed,
        ),
        in_specs=[VM] * 15 + [HB] * 7,
        out_specs=(HB,) + (VM,) * 4,
        scratch_shapes=[pltpu.VMEM(m.shape, BF16) for m in matrices]
        + [pltpu.VMEM((rows, 2 * units), BF16)]
        + [pltpu.VMEM((rows, features), F32)] * 4
        + [pltpu.VMEM((rows, features), BF16)] * 4
        + [
            pltpu.VMEM((4 * adapt, features), BF16),
            pltpu.VMEM((8, features), F32),
            pltpu.SemaphoreType.DMA((7,)),
            pltpu.SemaphoreType.DMA((2,)),
        ],
        compiler_params=pltpu.CompilerParams(vmem_limit_bytes=25 * MIB),
        cost_estimate=pl.CostEstimate(flops=2 * 10**10, bytes_accessed=16 * MIB, transcendentals=10**6),
        name="middle",
    )(x, keep, got, up, *vectors, *swapped, *map(in_hbm, matrices))


def spread_kernel(attended_ref, wo_ref, wo2_ref, own_ref, away_ref):
    attended = attended_ref[...]
    away_ref[...] = dot_nt(attended, wo2_ref[...]).astype(BF16)
    own_ref[...] = dot_nt(attended, wo_ref[...]).astype(BF16)


def spread(attended, wo, wo2):
    rows, width = attended.shape[0], wo.shape[0]
    return pl.pallas_call(
        spread_kernel,
        out_shape=(jax.ShapeDtypeStruct((rows, width), BF16),) * 2,
        in_specs=[VM] * 3,
        out_specs=(VM,) * 2,
        compiler_params=pltpu.CompilerParams(vmem_limit_bytes=8 * MIB),
        cost_estimate=SHORT,
        name="spread",
    )(attended, wo, wo2)


def combine_kernel(held_ref, got_ref, out_ref):
    rows = held_ref.shape[0] - 16
    out_ref[:rows, :] = (held_ref[:rows, :].astype(F32) + got_ref[:rows, :].astype(F32)).astype(BF16)
    out_ref[rows:, :] = tail_of(vectors_of(held_ref[rows:, :]) + vectors_of(got_ref[rows:, :]))


def combine(held, got):
    return pl.pallas_call(
        combine_kernel,
        out_shape=jax.ShapeDtypeStruct(held.shape, BF16),
        in_specs=[VM] * 2,
        out_specs=VM,
        compiler_params=pltpu.CompilerParams(vmem_limit_bytes=4 * MIB),
        cost_estimate=pl.CostEstimate(flops=10**5, bytes_accessed=MIB, transcendentals=0),
        name="combine",
    )(held, got)


def finish_kernel(held_ref, got_ref, md_ref, mdb_ref, mu_ref, mub_ref, dd_ref, ddb_ref, du_ref, dub_ref,
                  fg_ref, fs_ref, sg_ref, ss_ref, ratio_ref):
    adapt = md_ref.shape[0]

    def write(first_ref, second_ref):
        md_ref[...] = first_ref[:adapt, :].astype(F32)
        mu_ref[...] = first_ref[adapt : 2 * adapt, :].astype(F32)
        dd_ref[...] = second_ref[:adapt, :].astype(F32)
        du_ref[...] = second_ref[adapt : 2 * adapt, :].astype(F32)
        vectors = vectors_of(first_ref[2 * adapt :, :])
        for row, out_ref in enumerate((mub_ref, dub_ref, fg_ref, fs_ref, sg_ref, ss_ref)):
            out_ref[...] = vectors[row, :]
        last = vectors[6:7, :]
        mdb_ref[...] = last[0, :adapt]
        ddb_ref[...] = last[0, adapt : 2 * adapt]
        squares = last[:, 2 * adapt : 2 * adapt + 128]
        lane = lax.broadcasted_iota(jnp.int32, (1, 128), 1)
        base = jnp.sum(jnp.where(lane == 2, squares, 0.0), -1, keepdims=True)
        ratio_ref[...] = jnp.sqrt(squares / base)[0, :2]

    @pl.when(lax.axis_index("mp") == 0)
    def _():
        write(held_ref, got_ref)

    @pl.when(lax.axis_index("mp") != 0)
    def _():
        write(got_ref, held_ref)


def finish(held, got, adapt):
    features = held.shape[1]
    matrix = jax.ShapeDtypeStruct((adapt, features), F32)
    short, vector = jax.ShapeDtypeStruct((adapt,), F32), jax.ShapeDtypeStruct((features,), F32)
    return pl.pallas_call(
        finish_kernel,
        out_shape=(matrix, short, matrix, vector) * 2 + (vector,) * 4 + (jax.ShapeDtypeStruct((2,), F32),),
        in_specs=[VM, VM],
        out_specs=(VM,) * 13,
        compiler_params=pltpu.CompilerParams(vmem_limit_bytes=4 * MIB),
        name="finish",
    )(held, got)


def swap_cores(value):
    return lax.ppermute(value, "mp", [(0, 1), (1, 0)])


def tie(*values):
    return lax.optimization_barrier(values)


def per_device(
    tokens, segment_ids, query_weight, key_weight, value_weight, output_weight, inner_weight, outer_weight,
    mixer_down, mixer_down_bias, mixer_up, mixer_up_bias, dense_down, dense_down_bias, dense_up, dense_up_bias,
    first_gain, first_shift, second_gain, second_shift, output_grad,
):
    devices = lax.axis_size("dp")
    adapt = mixer_down.shape[1]
    other_tokens = swap_cores(tokens)
    kv, queries, across, turned, item, hide, rng = project(
        segment_ids, tokens, query_weight, key_weight, value_weight
    )
    kv, other_tokens, output_late, inner_late, outer_late = tie(
        kv, other_tokens, output_weight, inner_weight, outer_weight
    )
    other_output = swap_cores(output_late)
    other_inner = swap_cores(inner_late)
    other_outer = swap_cores(outer_late)
    kv, queries, keep, send, inverse, *shares = attention(
        rng, other_tokens, item, hide, query_weight, key_weight, value_weight, kv, queries, across, turned
    )
    got = swap_cores(send)
    vectors = (
        mixer_down_bias, mixer_up_bias, dense_down_bias, dense_up_bias, first_gain, first_shift, second_gain, second_shift,
    )
    swapped = (other_output, other_inner, other_outer)
    matrices = (output_weight, mixer_down.T, mixer_up, inner_weight, outer_weight, dense_down.T, dense_up)
    got, *late = tie(got, query_weight, key_weight, value_weight)
    late = [swap_cores(weight) for weight in late]
    result, first_grad, attended, mine, theirs = middle(
        tokens, keep, got, output_grad, vectors, swapped, matrices
    )
    theirs, *late = tie(theirs, *late)
    weights = (query_weight, key_weight, value_weight, *late)
    arriving = swap_cores(theirs)
    own_grad, away_grad = spread(attended, output_weight, other_output)
    arriving, own_grad = tie(arriving, own_grad)
    packed = combine(mine, arriving)
    away_grad, packed = tie(away_grad, packed)
    got_grad = swap_cores(away_grad)

    steps = []
    while 2 ** len(steps) < devices:
        steps.append(2 ** len(steps))
    steps.reverse()
    turn = len(steps) // 2
    pairs = len(shares)
    home, away = [], []
    input_grad = None
    for n in range(max(len(steps), pairs + 1)):
        arriving = None
        if n < len(steps):
            both = (steps[n], steps[(n + turn) % len(steps)])
            exchange = [(2 * i + c, 2 * (i ^ s) + c) for i in range(devices) for c, s in enumerate(both)]
            arriving = lax.ppermute(packed, ("dp", "mp"), exchange)
        work = None
        if n < pairs:
            got_grad, packed = tie(got_grad, packed)
            work = pair_grad(n, rng, kv, queries, keep, send, own_grad, got_grad, inverse, shares[n])
        elif n == pairs:
            away[-1], packed = tie(away[-1], packed)
            work = (input_gradient(first_grad, home + away, weights),)
        if work is not None and arriving is not None:
            early = away[-1:] if n < pairs else []
            arriving, *work = tie(arriving, *work, *early)
            if early:
                away[-1] = work.pop()
        if n < pairs:
            home.append(work[0])
            away.append(swap_cores(work[1]))
        elif n == pairs:
            input_grad = work[0]
        if arriving is not None:
            packed = combine(packed, arriving)
    last = swap_cores(packed)
    md, mdb, mu, mub, dd, ddb, du, dub, *rest = finish(packed, last, adapt)
    return (result, input_grad, md.T, mdb, mu, mub, dd.T, ddb, du, dub, *rest)


def solution(mesh):
    tokens = P(("dp", "mp"), None)
    columns, rows, whole = P(None, "mp"), P("mp", None), P()
    return jax.shard_map(
        per_device,
        mesh=mesh,
        in_specs=(tokens, P("dp", None), columns, columns, columns, rows, columns, rows) + (whole,) * 12 + (tokens,),
        out_specs=(tokens, tokens) + (whole,) * 13,
        check_vma=False,
    )
```

```python
import functools

import jax
import jax.numpy as jnp
from jax import lax
from jax.experimental import pallas as pl
from jax.experimental.pallas import tpu as pltpu
from jax.sharding import PartitionSpec as P

F32 = jnp.float32
BF16 = jnp.bfloat16
HEAD_DIM = 64
PAIR = 2 * HEAD_DIM
EPS = 1e-12
LOG2E = 1.4426950408889634
LN2 = 0.6931471805599453
ROOT_HALF = 0.7071067811865476
ROOT_TWO_PI = 0.3989422804014327
MASKED = -(2.0**100)
LARGEST = 2.0**100
SMALLEST = 2.0**-60
TURNED = 80
BLOCK = 256
STEP = 128
MIB = 1 << 20

VM = pl.BlockSpec(memory_space=pltpu.VMEM)
SM = pl.BlockSpec(memory_space=pltpu.SMEM)
HB = pl.BlockSpec(memory_space=pltpu.HBM)


def dot(left, right):
    return jnp.dot(left, right, preferred_element_type=F32)


def dot_nt(left, right):
    return lax.dot_general(left, right, (((1,), (1,)), ((), ())), preferred_element_type=F32)


def dot_tn(left, right):
    return lax.dot_general(left, right, (((0,), (0,)), ((), ())), preferred_element_type=F32)


def aligned(index, size):
    return pl.ds(pl.multiple_of(index * size, size), size)


def split_pair(pair):
    lane = lax.broadcasted_iota(jnp.int32, pair.shape, 1)
    zero = jnp.zeros_like(pair)
    return jnp.where(lane < HEAD_DIM, pair, zero), jnp.where(lane < HEAD_DIM, zero, pair)


def stack_heads(source, target, block):
    first, second = split_pair(source)
    for t in range(source.shape[0] // block):
        target[pl.ds(2 * t * block, block), :] = first[t * block : (t + 1) * block]
        target[pl.ds((2 * t + 1) * block, block), :] = second[t * block : (t + 1) * block]


def stack_heads_across(source, target, block):
    row = lax.broadcasted_iota(jnp.int32, source.shape, 0)
    zero = jnp.zeros_like(source)
    first = jnp.where(row < HEAD_DIM, source, zero)
    second = jnp.where(row < HEAD_DIM, zero, source)
    for t in range(source.shape[1] // block):
        target[:, 2 * t * block : (2 * t + 1) * block] = first[:, t * block : (t + 1) * block]
        target[:, (2 * t + 1) * block : (2 * t + 2) * block] = second[:, t * block : (t + 1) * block]


def in_hbm(value):
    return pltpu.with_memory_space_constraint(value, pltpu.HBM)


def start_all(sources, buffers, sems):
    copies = [pltpu.make_async_copy(src, dst, sems.at[i]) for i, (src, dst) in enumerate(zip(sources, buffers))]
    for copy in copies:
        copy.start()
    return copies


def write_projection(which, x, weights, copies, kv_ref, queries_ref, across_ref, turned_ref, between=None):
    rows, width = x.shape[0], weights[0].shape[1]
    pairs = width // PAIR
    if copies:
        copies[0].wait()
    queries = (dot(x, weights[0][...]) * (HEAD_DIM**-0.5 * LOG2E)).astype(BF16)
    if between is not None:
        between()
    for p in range(pairs):
        pair = queries[:, p * PAIR : (p + 1) * PAIR]
        stack_heads(pair, queries_ref.at[p, aligned(which, 2 * rows), :], BLOCK)
        stack_heads_across(pair.T, across_ref.at[p, :, aligned(which, 2 * rows)], BLOCK)
    if copies:
        copies[1].wait()
    kv_ref[aligned(which, rows), :width] = dot(x, weights[1][...]).astype(BF16)
    if copies:
        copies[2].wait()
    values = dot(x, weights[2][...]).astype(BF16)
    kv_ref[aligned(which, rows), width:] = values
    ones = jnp.ones((TURNED - HEAD_DIM, rows), BF16)
    for p in range(pairs):
        turned = values[:, p * PAIR : (p + 1) * PAIR].T
        for a in range(2):
            base = (2 * p + a) * TURNED
            turned_ref[base : base + HEAD_DIM, aligned(which, rows)] = turned[a * HEAD_DIM : (a + 1) * HEAD_DIM]
            turned_ref[base + HEAD_DIM : base + TURNED, aligned(which, rows)] = ones


def over_keys(low, high, visit):
    def whole(t, c):
        visit(pl.ds(pl.multiple_of(low * STEP + t * BLOCK, STEP), BLOCK), BLOCK)
        return c

    lax.fori_loop(0, (high - low) // 2, whole, 0)

    @pl.when((high - low) % 2 == 1)
    def _():
        visit(pl.ds(pl.multiple_of((high - 1) * STEP, STEP), STEP), STEP)


def is_shift(lane):
    return (lane == 63) | (lane == 95) | (lane == 127)


def project_kernel(
    seg_hbm, x_ref, wq_ref, wk_ref, wv_ref,
    kv_ref, queries_ref, across_ref, turned_ref, item_ref, hide_ref, rng_ref,
    seg_ref, x_buf, wq, wk, wv, sems,
):
    sources, buffers = (seg_hbm, x_ref, wq_ref, wk_ref, wv_ref), (seg_ref, x_buf, wq, wk, wv)
    seg_copy, *copies = start_all(sources, buffers, sems)
    count, block = kv_ref.shape[0], BLOCK

    def items():
        ids = seg_ref[...].astype(F32)
        position = lax.broadcasted_iota(jnp.int32, ids.shape, 1)
        for g in range(count // block):
            first, last = (
                jnp.sum(jnp.where(position == at, ids, 0.0), -1, keepdims=True) for at in (g * block, (g + 1) * block - 1)
            )
            rng_ref[0, g] = jnp.sum(jnp.where(ids < first, 1.0, 0.0)).astype(jnp.int32) // STEP
            rng_ref[1, g] = (jnp.sum(jnp.where(ids <= last, 1.0, 0.0)).astype(jnp.int32) + STEP - 1) // STEP
        lane = lax.broadcasted_iota(jnp.int32, (128, 128), 1)
        for t in range(count // 128):
            same = jnp.broadcast_to(ids[:, t * 128 : (t + 1) * 128], (128, 128)).T == lane.astype(F32)
            item_ref[t * 128 : (t + 1) * 128, :] = jnp.where(same | is_shift(lane), 1.0, 0.0).astype(BF16)
        row = lax.broadcasted_iota(jnp.int32, (128, block), 0)
        for t in range(count // block):
            same = row.astype(F32) == ids[:, t * block : (t + 1) * block]
            hide = jnp.where(same | is_shift(row), 0.0, MASKED).astype(BF16)
            for a in range(2):
                hide_ref[:, (2 * t + a) * block : (2 * t + a + 1) * block] = hide

    seg_copy.wait()
    copies[0].wait()
    write_projection(
        lax.axis_index("mp"), x_buf[...], (wq, wk, wv), copies[1:], kv_ref, queries_ref, across_ref, turned_ref, items
    )


def project(seg, x, wq, wk, wv):
    rows, width = x.shape[0], wq.shape[1]
    count, pairs = 2 * rows, width // PAIR
    return pl.pallas_call(
        project_kernel,
        out_shape=(
            jax.ShapeDtypeStruct((count, 2 * width), BF16),
            jax.ShapeDtypeStruct((pairs, 2 * count, PAIR), BF16),
            jax.ShapeDtypeStruct((pairs, PAIR, 2 * count), BF16),
            jax.ShapeDtypeStruct((2 * pairs * TURNED, count), BF16),
            jax.ShapeDtypeStruct((count, 128), BF16),
            jax.ShapeDtypeStruct((128, 2 * count), BF16),
            jax.ShapeDtypeStruct((2, count // BLOCK), jnp.int32),
        ),
        in_specs=[HB] * 5,
        out_specs=(VM,) * 6 + (SM,),
        scratch_shapes=[pltpu.VMEM(v.shape, v.dtype) for v in (seg, x, wq, wk, wv)] + [pltpu.SemaphoreType.DMA((5,))],
        compiler_params=pltpu.CompilerParams(vmem_limit_bytes=16 * MIB),
        cost_estimate=pl.CostEstimate(flops=2 * rows * x.shape[1] * 3 * width, bytes_accessed=5 * MIB, transcendentals=0),
        name="project",
    )(*map(in_hbm, (seg, x, wq, wk, wv)))


def attend_queries(which, rng_ref, item_ref, hide_ref, kv_ref, across, turned, out_ref, inverse_ref, share_refs, mix, shifted, peaks):
    pairs, block = len(share_refs), BLOCK
    per_half = out_ref.shape[0] // block

    def scores(p, span, both, hide):
        keys = jnp.concatenate([kv_ref[span, p * PAIR : (p + 1) * PAIR], item_ref[span, :]], 1)
        return dot(keys, jnp.concatenate([across[p, :, both], hide], 0))

    def query_block(i, carry):
        g = which * per_half + i
        both, here = aligned(g, 2 * block), aligned(i, 2 * block)
        low, high = rng_ref[0, g], rng_ref[1, g]

        def mix_all(hide_of):
            mix[...] = jnp.zeros(mix.shape, F32)

            def visit(span, size):
                ahead = scores(0, span, both, hide_of(0))
                for p in range(pairs):
                    s = ahead
                    if p + 1 < pairs:
                        ahead = scores(p + 1, span, both, hide_of(p + 1))
                    e = jnp.exp2(s).astype(BF16)
                    share_refs[p][span, here] = e
                    for a in range(2):
                        head = slice((2 * p + a) * TURNED, (2 * p + a + 1) * TURNED)
                        mix[head, :] += dot(turned[head, span], e[:, a * block : (a + 1) * block])

            over_keys(low, high, visit)

        mix_all(lambda p: hide_ref[:, both])
        total_rows = [h * TURNED + HEAD_DIM for h in range(2 * pairs)]
        sums = jnp.concatenate([mix[r : r + 8, :] for r in total_rows], 0)
        fine = jnp.where((sums <= LARGEST) & (sums >= SMALLEST), 0.0, 1.0)

        @pl.when(jnp.max(fine) > 0.0)
        def _():
            peaks[...] = jnp.full(peaks.shape, MASKED, F32)

            def visit(span, size):
                for p in range(pairs):
                    s = scores(p, span, both, hide_ref[:, both])
                    peaks[p] = jnp.maximum(peaks[p], jnp.max(s, 0, keepdims=True))

            over_keys(low, high, visit)
            row = lax.broadcasted_iota(jnp.int32, (128, 2 * block), 0)
            hide = hide_ref[:, both].astype(F32)
            for p in range(pairs):
                peak = peaks[p]
                first = peak.astype(BF16).astype(F32)
                second = (peak - first).astype(BF16).astype(F32)
                third = peak - first - second
                parts = jnp.where(row < 64, first, jnp.where(row < 96, second, third))
                shifted[p] = jnp.where(is_shift(row), -parts, hide).astype(BF16)
            mix_all(lambda p: shifted[p])

        rows = aligned(i, block)
        outs = []
        for p in range(pairs):
            scales = []
            for a in range(2):
                base = (2 * p + a) * TURNED
                scale = jnp.broadcast_to(1.0 / mix[base + HEAD_DIM : base + HEAD_DIM + 1, :], (HEAD_DIM, block))
                outs.append((mix[base : base + HEAD_DIM, :] * scale).astype(BF16))
                scales.append(scale)
            inverse_ref[rows, p * PAIR : (p + 1) * PAIR] = jnp.concatenate(scales, 0).T
        out_ref[rows, :] = jnp.concatenate(outs, 0).T
        return carry

    lax.fori_loop(0, per_half, query_block, 0)


def attention_kernel(
    rng_ref, x_ref, item_ref, hide_ref, wq_ref, wk_ref, wv_ref, kv_in, queries_in, across_in, turned_in,
    kv_ref, queries_ref, across, turned, out_ref, inverse_ref, *rest,
):
    half = x_ref.shape[0]
    *share_refs, mix, shifted, peaks = rest
    here, there = lax.axis_index("mp"), 1 - lax.axis_index("mp")
    turned[:, aligned(here, half)] = turned_in[:, aligned(here, half)]
    across[:, :, aligned(here, 2 * half)] = across_in[:, :, aligned(here, 2 * half)]
    kv_ref[aligned(here, half), :] = kv_in[aligned(here, half), :]
    queries_ref[:, aligned(here, 2 * half), :] = queries_in[:, aligned(here, 2 * half), :]
    write_projection(there, x_ref[...], (wq_ref, wk_ref, wv_ref), (), kv_ref, queries_ref, across, turned)
    attend_queries(there, rng_ref, item_ref, hide_ref, kv_ref, across, turned, out_ref, inverse_ref, share_refs, mix, shifted, peaks)


def own_attention_kernel(rng_ref, item_ref, hide_ref, kv_ref, across, turned, out_ref, inverse_ref, *rest):
    *share_refs, mix, shifted, peaks = rest
    here = lax.axis_index("mp")
    attend_queries(here, rng_ref, item_ref, hide_ref, kv_ref, across, turned, out_ref, inverse_ref, share_refs, mix, shifted, peaks)


def attention_call(kernel, name, kept, half, operands):
    kv = operands[7] if kept else operands[3]
    count, width = kv.shape[0], kv.shape[1] // 2
    pairs = width // PAIR
    return pl.pallas_call(
        kernel,
        out_shape=tuple(jax.ShapeDtypeStruct(v.shape, v.dtype) for v in kept)
        + (jax.ShapeDtypeStruct((half, width), BF16), jax.ShapeDtypeStruct((half, width), F32))
        + (jax.ShapeDtypeStruct((count, 2 * half), BF16),) * pairs,
        in_specs=[SM] + [VM] * (len(operands) - 1),
        out_specs=(VM,) * (len(kept) + 2 + pairs),
        scratch_shapes=[
            pltpu.VMEM((2 * pairs * TURNED, BLOCK), F32),
            pltpu.VMEM((pairs, 128, 2 * BLOCK), BF16),
            pltpu.VMEM((pairs, 1, 2 * BLOCK), F32),
        ],
        compiler_params=pltpu.CompilerParams(vmem_limit_bytes=10 * MIB),
        cost_estimate=pl.CostEstimate(flops=5 * 10**9, bytes_accessed=8 * MIB, transcendentals=10**6),
        name=name,
    )(*operands)


def pair_grad_kernel(
    p, rng_ref, kv_ref, queries_ref, keep_ref, send_ref, own_ref, other_ref, inverse_ref, inverse2_ref, share_ref, share2_ref,
    dq_ref, dk_ref, dv_ref,
    grads, across, turned, delta, dq, dk, dv,
):
    half, width = keep_ref.shape
    count, block = kv_ref.shape[0], BLOCK
    cols = slice(p * PAIR, (p + 1) * PAIR)
    here, there = lax.axis_index("mp"), 1 - lax.axis_index("mp")
    row = lax.broadcasted_iota(jnp.int32, (8, PAIR), 0)
    column = lax.broadcasted_iota(jnp.int32, (8, PAIR), 1)
    pick = jnp.where(column // HEAD_DIM == row, 1.0, 0.0).astype(BF16)
    sides = ((here, keep_ref, own_ref, inverse_ref), (there, send_ref, other_ref, inverse2_ref))
    for which, mixed_ref, up_ref, scale_ref in sides:
        scaled = (up_ref[:, cols].astype(F32) * scale_ref[:, cols]).astype(BF16)
        product = mixed_ref[:, cols].astype(F32) * scaled.astype(F32)
        high = product.astype(BF16)
        low = (product - high.astype(F32)).astype(BF16)
        delta[:, aligned(which, half)] = dot_nt(pick, high) + dot_nt(pick, low)
        stack_heads(scaled, grads.at[aligned(which, 2 * half), :], block)
        stack_heads_across(scaled.T, across.at[:, aligned(which, 2 * half)], block)
    turned[...] = kv_ref[:, cols].T
    dk[...] = jnp.zeros(dk.shape, F32)
    dv[...] = jnp.zeros(dv.shape, F32)

    def query_block(which, shares_ref, i, carry):
        g = which * (half // block) + i
        rows, both = aligned(g, block), aligned(g, 2 * block)
        dq[...] = jnp.zeros(dq.shape, F32)
        level = jnp.concatenate([delta[0:1, rows], delta[1:2, rows]], 1)

        def visit(span, size):
            d = dot(kv_ref[span, width + p * PAIR : width + (p + 1) * PAIR], across[:, both])
            shares = shares_ref[span, aligned(i, 2 * block)]
            slopes = (shares.astype(F32) * (d - level)).astype(BF16)
            dv[span, :] += dot(shares, grads[both, :])
            dk[span, :] += dot(slopes, queries_ref[p, both, :])
            for a in range(2):
                head = slice(a * HEAD_DIM, (a + 1) * HEAD_DIM)
                dq[head, :] += dot(turned[head, span], slopes[:, a * block : (a + 1) * block])

        over_keys(rng_ref[0, g], rng_ref[1, g], visit)
        dq_ref[rows, :] = (dq[...] * HEAD_DIM**-0.5).astype(BF16).T
        return carry

    for which, shares_ref in ((here, share_ref), (there, share2_ref)):
        lax.fori_loop(0, half // block, functools.partial(query_block, which, shares_ref), 0)
    dk_ref[...] = (dk[...] * LN2).astype(BF16)
    dv_ref[...] = dv[...].astype(BF16)


def pair_grad(p, rng, kv, queries, keep, send, own, other, *per_half):
    count = kv.shape[0]
    return pl.pallas_call(
        functools.partial(pair_grad_kernel, p),
        out_shape=(jax.ShapeDtypeStruct((count, PAIR), BF16),) * 3,
        in_specs=[SM] + [VM] * 10,
        out_specs=(VM,) * 3,
        scratch_shapes=[
            pltpu.VMEM((2 * count, PAIR), BF16),
            pltpu.VMEM((PAIR, 2 * count), BF16),
            pltpu.VMEM((PAIR, count), BF16),
            pltpu.VMEM((8, count), F32),
            pltpu.VMEM((PAIR, BLOCK), F32),
            pltpu.VMEM((count, PAIR), F32),
            pltpu.VMEM((count, PAIR), F32),
        ],
        compiler_params=pltpu.CompilerParams(vmem_limit_bytes=12 * MIB),
        cost_estimate=pl.CostEstimate(flops=4 * 10**9, bytes_accessed=8 * MIB, transcendentals=0),
        name=f"pair_grad_{p}",
    )(rng, kv, queries, keep, send, own, other, *per_half)


def input_part(flip, pieces, weights, half):
    which = 1 - lax.axis_index("mp") if flip else lax.axis_index("mp")
    rows = aligned(which, half)
    left = jnp.concatenate([piece[rows, :] for piece in pieces], 1)
    right = jnp.concatenate([weight[...] for weight in weights], 1)
    return dot_nt(left, right)


def away_kernel(*refs):
    out_ref = refs[-1]
    out_ref[...] = input_part(True, refs[:-4], refs[-4:-1], out_ref.shape[0]).astype(BF16)


def home_kernel(first_ref, got_ref, *refs):
    *pieces, wq_ref, wk_ref, wv_ref, out_hbm, out_ref, sems = refs
    half = out_ref.shape[0]
    parts = 2
    size = half // parts
    right = jnp.concatenate([wq_ref[...], wk_ref[...], wv_ref[...]], 1)
    copies = []
    for t in range(parts):
        part = slice(t * size, (t + 1) * size)
        rows = aligned(lax.axis_index("mp") * parts + t, size)
        total = dot_nt(jnp.concatenate([piece[rows, :] for piece in pieces], 1), right)
        out_ref[part, :] = (total + first_ref[part, :] + got_ref[part, :].astype(F32)).astype(BF16)
        copies.append(pltpu.make_async_copy(out_ref.at[part, :], out_hbm.at[part, :], sems.at[t]))
        copies[-1].start()
    for copy in copies:
        copy.wait()


def input_call(kernel, extra, pieces, weights, name):
    half, features = pieces[0].shape[0] // 2, weights[0].shape[0]
    return pl.pallas_call(
        kernel,
        out_shape=jax.ShapeDtypeStruct((half, features), BF16),
        in_specs=[VM] * (len(extra) + len(pieces) + len(weights)),
        out_specs=HB if extra else VM,
        scratch_shapes=[pltpu.VMEM((half, features), BF16), pltpu.SemaphoreType.DMA((2,))] if extra else [],
        compiler_params=pltpu.CompilerParams(vmem_limit_bytes=16 * MIB),
        cost_estimate=pl.CostEstimate(flops=10**9, bytes_accessed=6 * MIB, transcendentals=0),
        name=name,
    )(*extra, *pieces, *weights)


def gelu_both(v):
    part = 0.5 + 0.5 * lax.erf(v * ROOT_HALF)
    return v * part, part + v * jnp.exp(-0.5 * v * v) * ROOT_TWO_PI


def norm(values, gain, shift):
    mean = jnp.mean(values, -1, keepdims=True)
    centred = values - mean
    reciprocal = lax.rsqrt(jnp.mean(centred * centred, -1, keepdims=True) + EPS)
    normed = centred * reciprocal
    return normed * gain + shift, normed, reciprocal


def norm_grad(upstream, normed, reciprocal, gain):
    scaled = upstream * gain
    return reciprocal * (
        scaled - jnp.mean(scaled, -1, keepdims=True) - normed * jnp.mean(scaled * normed, -1, keepdims=True)
    )


def column_sum(values):
    return jnp.sum(values, 0, keepdims=True)


def eight_rows(values):
    return jnp.sum(values.reshape(-1, 8, values.shape[1]), 0)


def interleave(first, second):
    done = 0
    for i, step in enumerate(first):
        step()
        while done < len(second) and (done + 1) * len(first) <= (i + 1) * len(second):
            second[done]()
            done += 1
    for step in second[done:]:
        step()


def middle_kernel(
    x_ref, keep_ref, got_ref, up_ref,
    mdb_ref, mub_ref, ddb_ref, dub_ref, fg_ref, fs_ref, sg_ref, ss_ref,
    wo2_ref, w12_ref, w22_ref, wo_hbm, md_hbm, mu_hbm, w1_hbm, w2_hbm, dd_hbm, du_hbm,
    act_hbm, first_ref, attended_ref, mine_ref, theirs_ref,
    wo_ref, md_ref, mu_ref, w1_ref, w2_ref, dd_ref, du_ref,
    slope_ref, wide_ref, out_ref, hidden_ref, normed_ref, low_ref, hidden_low_ref, act_ref, top_ref,
    big_ref, small_ref, sems, act_sem,
):
    rows, features = x_ref.shape
    adapt = md_ref.shape[0]
    names = ("wo", "md", "mu", "w1", "w2", "dd", "du")
    waits = dict(
        zip(
            names,
            start_all(
                (wo_hbm, md_hbm, mu_hbm, w1_hbm, w2_hbm, dd_hbm, du_hbm),
                (wo_ref, md_ref, mu_ref, w1_ref, w2_ref, dd_ref, du_ref),
                sems,
            ),
        )
    )
    waited = set()

    def need(*wanted):
        for name in wanted:
            if name not in waited:
                waited.add(name)
                waits[name].wait()

    def vector(ref):
        return ref[...].astype(F32).reshape(1, -1)

    units = w1_ref.shape[1]
    chunk, piece_rows = 512, 64
    sides = ((w1_ref, w2_ref, ("w1", "w2")), (w12_ref, w22_ref, ()))
    pieces = [(side, slice(c * chunk, (c + 1) * chunk)) for side in sides for c in range(units // chunk)]
    kept = {}
    sums = {}

    def add(name, value):
        sums[name] = sums[name] + value if name in sums else value

    def parts(half):
        return [slice(r, r + piece_rows) for r in range(half.start, half.stop, piece_rows)]

    def attend(half):
        def first():
            need("wo")
            attended = dot(keep_ref[half, :], wo_ref[...]) + dot(got_ref[half, :], wo2_ref[...])
            wide_ref[half, :] = attended
            low_ref[half, :] = attended.astype(BF16)

        def second():
            need("md", "mu")
            active, slope = gelu_both(dot_nt(low_ref[half, :], md_ref[...]) + vector(mdb_ref))
            kept["mixer", half.start] = (active.astype(BF16), slope)

        def third():
            out_ref[half, :] = dot(kept["mixer", half.start][0], mu_ref[...]) + vector(mub_ref)

        return [first, second, third]

    def norm_one(half):
        def one(part):
            x, mixer_out = x_ref[part, :].astype(F32), out_ref[part, :]
            add("mixer_square", eight_rows(mixer_out * mixer_out))
            add("input_square", eight_rows(x * x))
            hidden, normed, reciprocal = norm(x + wide_ref[part, :] + mixer_out, vector(fg_ref), vector(fs_ref))
            normed_ref[part, :] = normed
            hidden_ref[part, :] = hidden
            hidden_low_ref[part, :] = hidden.astype(BF16)
            kept["reciprocal", part.start] = reciprocal

        return [functools.partial(one, part) for part in parts(half)]

    def feed_forward(half):
        state = {}

        def start():
            need("w1", "w2")
            side, span = pieces[0]
            state["ahead"] = dot(hidden_low_ref[half, :], side[0][:, span])

        def one(n):
            side, span = pieces[n]
            inner = state["ahead"]
            if n + 1 < len(pieces):
                after, after_span = pieces[n + 1]
                state["ahead"] = dot(hidden_low_ref[half, :], after[0][:, after_span])
            value, slope = gelu_both(inner)
            slope_ref[half, n * chunk : (n + 1) * chunk] = slope.astype(BF16)
            state["value"] = value.astype(BF16)

        def two(n):
            side, span = pieces[n]
            total = dot(state["value"], side[1][span, :])
            state["total"] = state["total"] + total if n else total
            if n + 1 == len(pieces):
                wide_ref[half, :] = state["total"]

        steps = [start]
        for n in range(len(pieces)):
            steps += [functools.partial(one, n), functools.partial(two, n)]
        return steps

    def dense(half):
        def first():
            need("dd", "du")
            dense_low = wide_ref[half, :].astype(BF16)
            active, slope = gelu_both(dot_nt(dense_low, dd_ref[...]) + vector(ddb_ref))
            kept["dense", half.start] = (active.astype(BF16), slope, dense_low)

        def second():
            out_ref[half, :] = dot(kept["dense", half.start][0], du_ref[...]) + vector(dub_ref)

        return [first, second]

    def norm_two(half):
        def one(part):
            dense_out = out_ref[part, :]
            add("dense_square", eight_rows(dense_out * dense_out))
            gain = vector(sg_ref)
            result, normed, reciprocal = norm(hidden_ref[part, :] + wide_ref[part, :] + dense_out, gain, vector(ss_ref))
            act_ref[part, :] = result.astype(BF16)
            upstream = up_ref[part, :].astype(F32)
            add(4, eight_rows(upstream * normed))
            add(5, eight_rows(upstream))
            second_grad = norm_grad(upstream, normed, reciprocal, gain)
            hidden_ref[part, :] = second_grad
            top = second_grad.astype(BF16)
            top_ref[part, :] = top
            add(1, eight_rows(top.astype(F32)))

        return [functools.partial(one, part) for part in parts(half)]

    def dense_back(half):
        def first():
            active, slope, dense_low = kept["dense", half.start]
            top = top_ref[half, :]
            add("dense_up", dot_tn(active, top))
            mid = (dot_nt(top, du_ref[...]) * slope).astype(BF16)
            kept["dense_mid", half.start] = mid
            add("dense_mid", eight_rows(mid.astype(F32)))

        def second():
            mid = kept["dense_mid", half.start]
            add("dense_down", dot_tn(mid, kept["dense", half.start][2]))
            hidden_low_ref[half, :] = (hidden_ref[half, :] + dot(mid, dd_ref[...])).astype(BF16)

        return [first, second]

    def feed_back(half):
        state = {}

        def start():
            side, span = pieces[0]
            state["ahead"] = dot_nt(hidden_low_ref[half, :], side[1][span, :])

        def one(n):
            back = state["ahead"]
            if n + 1 < len(pieces):
                after, after_span = pieces[n + 1]
                state["ahead"] = dot_nt(hidden_low_ref[half, :], after[1][after_span, :])
            slope = slope_ref[half, n * chunk : (n + 1) * chunk].astype(F32)
            state["value"] = (back * slope).astype(BF16)

        def two(n):
            side, span = pieces[n]
            total = dot_nt(state["value"], side[0][:, span])
            state["total"] = state["total"] + total if n else total
            if n + 1 == len(pieces):
                hidden_ref[half, :] = hidden_ref[half, :] + state["total"]

        steps = [start]
        for n in range(len(pieces)):
            steps += [functools.partial(one, n), functools.partial(two, n)]
        return steps

    def norm_one_back(half):
        def one(part):
            hidden_grad, normed = hidden_ref[part, :], normed_ref[part, :]
            add(2, eight_rows(hidden_grad * normed))
            add(3, eight_rows(hidden_grad))
            first_grad = norm_grad(hidden_grad, normed, kept["reciprocal", part.start], vector(fg_ref))
            first_ref[part, :] = first_grad
            top = first_grad.astype(BF16)
            top_ref[part, :] = top
            add(0, eight_rows(top.astype(F32)))

        return [functools.partial(one, part) for part in parts(half)]

    def attend_back(half):
        def first():
            active, slope = kept["mixer", half.start]
            top = top_ref[half, :]
            add("mixer_up", dot_tn(active, top))
            mid = (dot_nt(top, mu_ref[...]) * slope).astype(BF16)
            kept["mixer_mid", half.start] = mid
            add("mixer_mid", eight_rows(mid.astype(F32)))

        def second():
            mid = kept["mixer_mid", half.start]
            add("mixer_down", dot_tn(mid, low_ref[half, :]))
            attended_ref[half, :] = (first_ref[half, :] + dot(mid, md_ref[...])).astype(BF16)

        return [first, second]

    def send_result(half, index):
        copy = pltpu.make_async_copy(act_ref.at[half, :], act_hbm.at[half, :], act_sem.at[index])
        copy.start()
        return copy

    one, two = slice(0, rows // 2), slice(rows // 2, rows)
    interleave(attend(one), [])
    interleave(norm_one(one), attend(two))
    interleave(feed_forward(one), norm_one(two))
    interleave(feed_forward(two), dense(one) + norm_two(one) + dense_back(one))
    copies = [send_result(one, 0)]
    interleave(feed_back(one), dense(two) + norm_two(two) + dense_back(two))
    copies.append(send_result(two, 1))
    interleave(feed_back(two), norm_one_back(one) + attend_back(one))
    interleave(norm_one_back(two), [])
    interleave(attend_back(two), [])

    for n, name in enumerate(("mixer_down", "mixer_up", "dense_down", "dense_up")):
        big_ref[n * adapt : (n + 1) * adapt, :] = sums[name].astype(BF16)
    for row in range(6):
        small_ref[row : row + 1, :] = column_sum(sums[row])
    lane = lax.broadcasted_iota(jnp.int32, (1, 128), 1)
    squares = jnp.zeros((1, 128), F32)
    for n, name in enumerate(("mixer_square", "dense_square", "input_square")):
        squares = jnp.where(lane == n, jnp.sum(column_sum(sums[name]), -1, keepdims=True), squares)
    small_ref[6:7, :] = jnp.concatenate(
        [column_sum(sums["mixer_mid"]), column_sum(sums["dense_mid"]), squares, jnp.zeros((1, features - 2 * adapt - 128), F32)], 1
    )
    small_ref[7:8, :] = jnp.zeros((1, features), F32)
    tail = tail_of(small_ref[...])
    share = 2 * adapt
    for pack_ref, which in ((mine_ref, lax.axis_index("mp")), (theirs_ref, 1 - lax.axis_index("mp"))):
        pack_ref[:share, :] = big_ref[aligned(which, share), :]
        pack_ref[share:, :] = tail
    for copy in copies:
        copy.wait()


def tail_of(vectors):
    high = vectors.astype(BF16)
    return jnp.concatenate([high, (vectors - high.astype(F32)).astype(BF16)], 0)


def vectors_of(tail):
    wide = tail.astype(F32)
    return wide[:8] + wide[8:]


def middle(x, keep, got, up, vectors, swapped, matrices):
    rows, features = x.shape
    adapt = matrices[1].shape[0]
    units = matrices[3].shape[1]
    packed = jax.ShapeDtypeStruct((2 * adapt + 16, features), BF16)
    return pl.pallas_call(
        middle_kernel,
        out_shape=(
            jax.ShapeDtypeStruct((rows, features), BF16),
            jax.ShapeDtypeStruct((rows, features), F32),
            jax.ShapeDtypeStruct((rows, features), BF16),
            packed,
            packed,
        ),
        in_specs=[VM] * 15 + [HB] * 7,
        out_specs=(HB,) + (VM,) * 4,
        scratch_shapes=[pltpu.VMEM(m.shape, BF16) for m in matrices]
        + [pltpu.VMEM((rows, 2 * units), BF16)]
        + [pltpu.VMEM((rows, features), F32)] * 4
        + [pltpu.VMEM((rows, features), BF16)] * 4
        + [
            pltpu.VMEM((4 * adapt, features), BF16),
            pltpu.VMEM((8, features), F32),
            pltpu.SemaphoreType.DMA((7,)),
            pltpu.SemaphoreType.DMA((2,)),
        ],
        compiler_params=pltpu.CompilerParams(vmem_limit_bytes=25 * MIB),
        cost_estimate=pl.CostEstimate(flops=2 * 10**10, bytes_accessed=16 * MIB, transcendentals=10**6),
        name="middle",
    )(x, keep, got, up, *vectors, *swapped, *map(in_hbm, matrices))


def spread_kernel(attended_ref, wo_ref, wo2_ref, own_ref, away_ref):
    attended = attended_ref[...]
    away_ref[...] = dot_nt(attended, wo2_ref[...]).astype(BF16)
    own_ref[...] = dot_nt(attended, wo_ref[...]).astype(BF16)


def spread(attended, wo, wo2):
    rows, width = attended.shape[0], wo.shape[0]
    return pl.pallas_call(
        spread_kernel,
        out_shape=(jax.ShapeDtypeStruct((rows, width), BF16),) * 2,
        in_specs=[VM] * 3,
        out_specs=(VM,) * 2,
        compiler_params=pltpu.CompilerParams(vmem_limit_bytes=8 * MIB),
        cost_estimate=pl.CostEstimate(flops=4 * rows * attended.shape[1] * width, bytes_accessed=3 * MIB, transcendentals=0),
        name="spread",
    )(attended, wo, wo2)


def combine_kernel(held_ref, got_ref, out_ref):
    rows = held_ref.shape[0] - 16
    out_ref[:rows, :] = (held_ref[:rows, :].astype(F32) + got_ref[:rows, :].astype(F32)).astype(BF16)
    out_ref[rows:, :] = tail_of(vectors_of(held_ref[rows:, :]) + vectors_of(got_ref[rows:, :]))


def combine(held, got):
    return pl.pallas_call(
        combine_kernel,
        out_shape=jax.ShapeDtypeStruct(held.shape, BF16),
        in_specs=[VM] * 2,
        out_specs=VM,
        compiler_params=pltpu.CompilerParams(vmem_limit_bytes=4 * MIB),
        cost_estimate=pl.CostEstimate(flops=10**5, bytes_accessed=MIB, transcendentals=0),
        name="combine",
    )(held, got)


def finish_kernel(held_ref, got_ref, md_ref, mdb_ref, mu_ref, mub_ref, dd_ref, ddb_ref, du_ref, dub_ref,
                  fg_ref, fs_ref, sg_ref, ss_ref, ratio_ref):
    adapt = md_ref.shape[0]

    def write(first_ref, second_ref):
        md_ref[...] = first_ref[:adapt, :].astype(F32)
        mu_ref[...] = first_ref[adapt : 2 * adapt, :].astype(F32)
        dd_ref[...] = second_ref[:adapt, :].astype(F32)
        du_ref[...] = second_ref[adapt : 2 * adapt, :].astype(F32)
        vectors = vectors_of(first_ref[2 * adapt :, :])
        for row, out_ref in enumerate((mub_ref, dub_ref, fg_ref, fs_ref, sg_ref, ss_ref)):
            out_ref[...] = vectors[row, :]
        last = vectors[6:7, :]
        mdb_ref[...] = last[0, :adapt]
        ddb_ref[...] = last[0, adapt : 2 * adapt]
        squares = last[:, 2 * adapt : 2 * adapt + 128]
        lane = lax.broadcasted_iota(jnp.int32, (1, 128), 1)
        base = jnp.sum(jnp.where(lane == 2, squares, 0.0), -1, keepdims=True)
        ratio_ref[...] = jnp.sqrt(squares / base)[0, :2]

    @pl.when(lax.axis_index("mp") == 0)
    def _():
        write(held_ref, got_ref)

    @pl.when(lax.axis_index("mp") != 0)
    def _():
        write(got_ref, held_ref)


def finish(held, got, adapt):
    features = held.shape[1]
    matrix = jax.ShapeDtypeStruct((adapt, features), F32)
    short, vector = jax.ShapeDtypeStruct((adapt,), F32), jax.ShapeDtypeStruct((features,), F32)
    return pl.pallas_call(
        finish_kernel,
        out_shape=(matrix, short, matrix, vector) * 2 + (vector,) * 4 + (jax.ShapeDtypeStruct((2,), F32),),
        in_specs=[VM, VM],
        out_specs=(VM,) * 13,
        compiler_params=pltpu.CompilerParams(vmem_limit_bytes=4 * MIB),
        name="finish",
    )(held, got)


def swap_cores(value):
    return lax.ppermute(value, "mp", [(0, 1), (1, 0)])


def tie(*values):
    return lax.optimization_barrier(values)


def per_device(
    tokens, segment_ids, query_weight, key_weight, value_weight, output_weight, inner_weight, outer_weight,
    mixer_down, mixer_down_bias, mixer_up, mixer_up_bias, dense_down, dense_down_bias, dense_up, dense_up_bias,
    first_gain, first_shift, second_gain, second_shift, output_grad,
):
    devices = lax.axis_size("dp")
    adapt = mixer_down.shape[1]
    other_tokens = swap_cores(tokens)
    kv, queries, across, turned, item, hide, rng = project(
        segment_ids, tokens, query_weight, key_weight, value_weight
    )
    kv, other_tokens, output_late, inner_late, outer_late = tie(
        kv, other_tokens, output_weight, inner_weight, outer_weight
    )
    other_output = swap_cores(output_late)
    other_inner = swap_cores(inner_late)
    other_outer = swap_cores(outer_late)
    half = tokens.shape[0]
    written = (kv, queries, across, turned)
    kv, queries, across, turned, send, inverse2, *shares2 = attention_call(
        attention_kernel, "attention", written, half,
        (rng, other_tokens, item, hide, query_weight, key_weight, value_weight, *written),
    )
    got = swap_cores(send)
    keep, inverse, *shares = attention_call(
        own_attention_kernel, "own_attention", (), half, (rng, item, hide, kv, across, turned)
    )
    got, keep = tie(got, keep)
    vectors = (
        mixer_down_bias, mixer_up_bias, dense_down_bias, dense_up_bias, first_gain, first_shift, second_gain, second_shift,
    )
    swapped = (other_output, other_inner, other_outer)
    matrices = (output_weight, mixer_down.T, mixer_up, inner_weight, outer_weight, dense_down.T, dense_up)
    result, first_grad, attended, mine, theirs = middle(
        tokens, keep, got, output_grad, vectors, swapped, matrices
    )
    arriving = swap_cores(theirs)
    own_grad, away_grad = spread(attended, output_weight, other_output)
    arriving, own_grad = tie(arriving, own_grad)
    packed = combine(mine, arriving)
    away_grad, packed = tie(away_grad, packed)
    got_grad = swap_cores(away_grad)

    steps = []
    while 2 ** len(steps) < devices:
        steps.append(2 ** len(steps))
    steps.reverse()
    turn = len(steps) // 2
    pairs = len(shares)
    grads = []
    weights = (query_weight, key_weight, value_weight)
    for n, step in enumerate(steps):
        other_step = steps[(n + turn) % len(steps)]
        exchange = [(2 * i + c, 2 * (i ^ s) + c) for i in range(devices) for c, s in enumerate((step, other_step))]
        arriving = lax.ppermute(packed, ("dp", "mp"), exchange)
        if n < pairs:
            got_grad, packed = tie(got_grad, packed)
            parts = pair_grad(n, rng, kv, queries, keep, send, own_grad, got_grad, inverse, inverse2, shares[n], shares2[n])
            arriving, *parts = tie(arriving, *parts)
            grads.append(parts)
        elif n == pairs:
            pieces = [grads[p][i] for i in range(3) for p in range(pairs)]
            away = swap_cores(input_call(away_kernel, (), pieces, weights, "away"))
            input_grad = input_call(home_kernel, (first_grad, away), pieces, weights, "home")
            arriving, input_grad = tie(arriving, input_grad)
        packed = combine(packed, arriving)
    md, mdb, mu, mub, dd, ddb, du, dub, *rest = finish(packed, swap_cores(packed), adapt)
    return (result, input_grad, md.T, mdb, mu, mub, dd.T, ddb, du, dub, *rest)


def solution(mesh):
    tokens = P(("dp", "mp"), None)
    columns, rows, whole = P(None, "mp"), P("mp", None), P()
    return jax.shard_map(
        per_device,
        mesh=mesh,
        in_specs=(tokens, P("dp", None), columns, columns, columns, rows, columns, rows) + (whole,) * 12 + (tokens,),
        out_specs=(tokens, tokens) + (whole,) * 13,
        check_vma=False,
    )
```

```python
import functools

import jax
import jax.numpy as jnp
from jax import lax
from jax.experimental import pallas as pl
from jax.experimental.pallas import tpu as pltpu
from jax.sharding import PartitionSpec as P

F32 = jnp.float32
BF16 = jnp.bfloat16
HEAD_DIM = 64
PAIR = 2 * HEAD_DIM
EPS = 1e-12
LOG2E = 1.4426950408889634
LN2 = 0.6931471805599453
ROOT_HALF = 0.7071067811865476
ROOT_TWO_PI = 0.3989422804014327
MASKED = -(2.0**100)
LARGEST = 2.0**100
SMALLEST = 2.0**-60
TURNED = 80
BLOCK = 256
STEP = 128
MIB = 1 << 20

VM = pl.BlockSpec(memory_space=pltpu.VMEM)
SM = pl.BlockSpec(memory_space=pltpu.SMEM)
HB = pl.BlockSpec(memory_space=pltpu.HBM)


def dot(left, right):
    return jnp.dot(left, right, preferred_element_type=F32)


def dot_nt(left, right):
    return lax.dot_general(left, right, (((1,), (1,)), ((), ())), preferred_element_type=F32)


def dot_tn(left, right):
    return lax.dot_general(left, right, (((0,), (0,)), ((), ())), preferred_element_type=F32)


def aligned(index, size):
    return pl.ds(pl.multiple_of(index * size, size), size)


def split_pair(pair):
    lane = lax.broadcasted_iota(jnp.int32, pair.shape, 1)
    zero = jnp.zeros_like(pair)
    return jnp.where(lane < HEAD_DIM, pair, zero), jnp.where(lane < HEAD_DIM, zero, pair)


def stack_heads(source, target, block):
    first, second = split_pair(source)
    for t in range(source.shape[0] // block):
        target[pl.ds(2 * t * block, block), :] = first[t * block : (t + 1) * block]
        target[pl.ds((2 * t + 1) * block, block), :] = second[t * block : (t + 1) * block]


def stack_heads_across(source, target, block):
    row = lax.broadcasted_iota(jnp.int32, source.shape, 0)
    zero = jnp.zeros_like(source)
    first = jnp.where(row < HEAD_DIM, source, zero)
    second = jnp.where(row < HEAD_DIM, zero, source)
    for t in range(source.shape[1] // block):
        target[:, 2 * t * block : (2 * t + 1) * block] = first[:, t * block : (t + 1) * block]
        target[:, (2 * t + 1) * block : (2 * t + 2) * block] = second[:, t * block : (t + 1) * block]


def in_hbm(value):
    return pltpu.with_memory_space_constraint(value, pltpu.HBM)


def start_all(sources, buffers, sems):
    copies = [pltpu.make_async_copy(src, dst, sems.at[i]) for i, (src, dst) in enumerate(zip(sources, buffers))]
    for copy in copies:
        copy.start()
    return copies


def write_projection(which, x, weights, copies, kv_ref, queries_ref, across_ref, turned_ref, between=None):
    rows, width = x.shape[0], weights[0].shape[1]
    pairs = width // PAIR
    if copies:
        copies[0].wait()
    queries = (dot(x, weights[0][...]) * (HEAD_DIM**-0.5 * LOG2E)).astype(BF16)
    if between is not None:
        between()
    for p in range(pairs):
        pair = queries[:, p * PAIR : (p + 1) * PAIR]
        stack_heads(pair, queries_ref.at[p, aligned(which, 2 * rows), :], BLOCK)
        stack_heads_across(pair.T, across_ref.at[p, :, aligned(which, 2 * rows)], BLOCK)
    if copies:
        copies[1].wait()
    kv_ref[aligned(which, rows), :width] = dot(x, weights[1][...]).astype(BF16)
    if copies:
        copies[2].wait()
    values = dot(x, weights[2][...]).astype(BF16)
    kv_ref[aligned(which, rows), width:] = values
    ones = jnp.ones((TURNED - HEAD_DIM, rows), BF16)
    for p in range(pairs):
        turned = values[:, p * PAIR : (p + 1) * PAIR].T
        for a in range(2):
            base = (2 * p + a) * TURNED
            turned_ref[base : base + HEAD_DIM, aligned(which, rows)] = turned[a * HEAD_DIM : (a + 1) * HEAD_DIM]
            turned_ref[base + HEAD_DIM : base + TURNED, aligned(which, rows)] = ones


def over_keys(low, high, visit):
    odd = (high - low) % 2

    def whole(t, c):
        visit(pl.ds(pl.multiple_of(low * STEP + t * BLOCK, STEP), BLOCK), BLOCK)
        return c

    lax.fori_loop(0, (high - low) // 2 - odd, whole, 0)

    @pl.when(odd == 1)
    def _():
        size = BLOCK + STEP
        visit(pl.ds(pl.multiple_of(high * STEP - size, STEP), size), size)


def is_shift(lane):
    return (lane == 63) | (lane == 95) | (lane == 127)


def project_kernel(
    seg_hbm, x_ref, wq_ref, wk_ref, wv_ref,
    kv_ref, queries_ref, across_ref, turned_ref, item_ref, hide_ref, rng_ref,
    seg_ref, x_buf, wq, wk, wv, sems,
):
    sources, buffers = (seg_hbm, x_ref, wq_ref, wk_ref, wv_ref), (seg_ref, x_buf, wq, wk, wv)
    seg_copy, *copies = start_all(sources, buffers, sems)
    count, block = kv_ref.shape[0], BLOCK

    def items():
        ids = seg_ref[...].astype(F32)
        position = lax.broadcasted_iota(jnp.int32, ids.shape, 1)
        for g in range(count // block):
            first, last = (
                jnp.sum(jnp.where(position == at, ids, 0.0), -1, keepdims=True) for at in (g * block, (g + 1) * block - 1)
            )
            rng_ref[0, g] = jnp.sum(jnp.where(ids < first, 1.0, 0.0)).astype(jnp.int32) // STEP
            rng_ref[1, g] = (jnp.sum(jnp.where(ids <= last, 1.0, 0.0)).astype(jnp.int32) + STEP - 1) // STEP
        lane = lax.broadcasted_iota(jnp.int32, (128, 128), 1)
        for t in range(count // 128):
            same = jnp.broadcast_to(ids[:, t * 128 : (t + 1) * 128], (128, 128)).T == lane.astype(F32)
            item_ref[t * 128 : (t + 1) * 128, :] = jnp.where(same | is_shift(lane), 1.0, 0.0).astype(BF16)
        row = lax.broadcasted_iota(jnp.int32, (128, block), 0)
        for t in range(count // block):
            same = row.astype(F32) == ids[:, t * block : (t + 1) * block]
            hide = jnp.where(same | is_shift(row), 0.0, MASKED).astype(BF16)
            for a in range(2):
                hide_ref[:, (2 * t + a) * block : (2 * t + a + 1) * block] = hide

    seg_copy.wait()
    copies[0].wait()
    write_projection(
        lax.axis_index("mp"), x_buf[...], (wq, wk, wv), copies[1:], kv_ref, queries_ref, across_ref, turned_ref, items
    )


def project(seg, x, wq, wk, wv):
    rows, width = x.shape[0], wq.shape[1]
    count, pairs = 2 * rows, width // PAIR
    return pl.pallas_call(
        project_kernel,
        out_shape=(
            jax.ShapeDtypeStruct((count, 2 * width), BF16),
            jax.ShapeDtypeStruct((pairs, 2 * count, PAIR), BF16),
            jax.ShapeDtypeStruct((pairs, PAIR, 2 * count), BF16),
            jax.ShapeDtypeStruct((2 * pairs * TURNED, count), BF16),
            jax.ShapeDtypeStruct((count, 128), BF16),
            jax.ShapeDtypeStruct((128, 2 * count), BF16),
            jax.ShapeDtypeStruct((2, count // BLOCK), jnp.int32),
        ),
        in_specs=[HB] * 5,
        out_specs=(VM,) * 6 + (SM,),
        scratch_shapes=[pltpu.VMEM(v.shape, v.dtype) for v in (seg, x, wq, wk, wv)] + [pltpu.SemaphoreType.DMA((5,))],
        compiler_params=pltpu.CompilerParams(vmem_limit_bytes=16 * MIB),
        cost_estimate=pl.CostEstimate(flops=2 * rows * x.shape[1] * 3 * width, bytes_accessed=5 * MIB, transcendentals=0),
        name="project",
    )(*map(in_hbm, (seg, x, wq, wk, wv)))


def attend_queries(which, rng_ref, item_ref, hide_ref, kv_ref, across, turned, out_ref, inverse_ref, share_refs, mix, shifted, peaks):
    pairs, block = len(share_refs), BLOCK
    per_half = out_ref.shape[0] // block

    def scores(p, span, both, hide):
        keys = jnp.concatenate([kv_ref[span, p * PAIR : (p + 1) * PAIR], item_ref[span, :]], 1)
        return dot(keys, jnp.concatenate([across[p, :, both], hide], 0))

    def query_block(i, carry):
        g = which * per_half + i
        both, here = aligned(g, 2 * block), aligned(i, 2 * block)
        low, high = rng_ref[0, g], rng_ref[1, g]

        def mix_all(hide_of):
            mix[...] = jnp.zeros(mix.shape, F32)

            def visit(span, size):
                ahead = scores(0, span, both, hide_of(0))
                for p in range(pairs):
                    s = ahead
                    if p + 1 < pairs:
                        ahead = scores(p + 1, span, both, hide_of(p + 1))
                    e = jnp.exp2(s).astype(BF16)
                    share_refs[p][span, here] = e
                    for a in range(2):
                        head = slice((2 * p + a) * TURNED, (2 * p + a + 1) * TURNED)
                        mix[head, :] += dot(turned[head, span], e[:, a * block : (a + 1) * block])

            over_keys(low, high, visit)

        mix_all(lambda p: hide_ref[:, both])
        total_rows = [h * TURNED + HEAD_DIM for h in range(2 * pairs)]
        sums = jnp.concatenate([mix[r : r + 8, :] for r in total_rows], 0)
        fine = jnp.where((sums <= LARGEST) & (sums >= SMALLEST), 0.0, 1.0)

        @pl.when(jnp.max(fine) > 0.0)
        def _():
            peaks[...] = jnp.full(peaks.shape, MASKED, F32)

            def visit(span, size):
                for p in range(pairs):
                    s = scores(p, span, both, hide_ref[:, both])
                    peaks[p] = jnp.maximum(peaks[p], jnp.max(s, 0, keepdims=True))

            over_keys(low, high, visit)
            row = lax.broadcasted_iota(jnp.int32, (128, 2 * block), 0)
            hide = hide_ref[:, both].astype(F32)
            for p in range(pairs):
                peak = peaks[p]
                first = peak.astype(BF16).astype(F32)
                second = (peak - first).astype(BF16).astype(F32)
                third = peak - first - second
                parts = jnp.where(row < 64, first, jnp.where(row < 96, second, third))
                shifted[p] = jnp.where(is_shift(row), -parts, hide).astype(BF16)
            mix_all(lambda p: shifted[p])

        rows = aligned(i, block)
        outs = []
        for p in range(pairs):
            scales = []
            for a in range(2):
                base = (2 * p + a) * TURNED
                scale = jnp.broadcast_to(1.0 / mix[base + HEAD_DIM : base + HEAD_DIM + 1, :], (HEAD_DIM, block))
                outs.append((mix[base : base + HEAD_DIM, :] * scale).astype(BF16))
                scales.append(scale)
            inverse_ref[rows, p * PAIR : (p + 1) * PAIR] = jnp.concatenate(scales, 0).T
        out_ref[rows, :] = jnp.concatenate(outs, 0).T
        return carry

    lax.fori_loop(0, per_half, query_block, 0)


def attention_kernel(
    rng_ref, x_ref, item_ref, hide_ref, wq_ref, wk_ref, wv_ref, kv_in, queries_in, across_in, turned_in,
    kv_ref, queries_ref, across, turned, out_ref, inverse_ref, *rest,
):
    half = x_ref.shape[0]
    *share_refs, mix, shifted, peaks = rest
    here, there = lax.axis_index("mp"), 1 - lax.axis_index("mp")
    turned[:, aligned(here, half)] = turned_in[:, aligned(here, half)]
    across[:, :, aligned(here, 2 * half)] = across_in[:, :, aligned(here, 2 * half)]
    kv_ref[aligned(here, half), :] = kv_in[aligned(here, half), :]
    queries_ref[:, aligned(here, 2 * half), :] = queries_in[:, aligned(here, 2 * half), :]
    write_projection(there, x_ref[...], (wq_ref, wk_ref, wv_ref), (), kv_ref, queries_ref, across, turned)
    attend_queries(there, rng_ref, item_ref, hide_ref, kv_ref, across, turned, out_ref, inverse_ref, share_refs, mix, shifted, peaks)


def own_attention_kernel(rng_ref, item_ref, hide_ref, kv_ref, across, turned, out_ref, inverse_ref, *rest):
    *share_refs, mix, shifted, peaks = rest
    here = lax.axis_index("mp")
    attend_queries(here, rng_ref, item_ref, hide_ref, kv_ref, across, turned, out_ref, inverse_ref, share_refs, mix, shifted, peaks)


def attention_call(kernel, name, kept, half, operands):
    kv = operands[7] if kept else operands[3]
    count, width = kv.shape[0], kv.shape[1] // 2
    pairs = width // PAIR
    return pl.pallas_call(
        kernel,
        out_shape=tuple(jax.ShapeDtypeStruct(v.shape, v.dtype) for v in kept)
        + (jax.ShapeDtypeStruct((half, width), BF16), jax.ShapeDtypeStruct((half, width), F32))
        + (jax.ShapeDtypeStruct((count, 2 * half), BF16),) * pairs,
        in_specs=[SM] + [VM] * (len(operands) - 1),
        out_specs=(VM,) * (len(kept) + 2 + pairs),
        scratch_shapes=[
            pltpu.VMEM((2 * pairs * TURNED, BLOCK), F32),
            pltpu.VMEM((pairs, 128, 2 * BLOCK), BF16),
            pltpu.VMEM((pairs, 1, 2 * BLOCK), F32),
        ],
        compiler_params=pltpu.CompilerParams(vmem_limit_bytes=10 * MIB),
        cost_estimate=pl.CostEstimate(flops=5 * 10**9, bytes_accessed=8 * MIB, transcendentals=10**6),
        name=name,
    )(*operands)


def pair_grad_kernel(
    p, rng_ref, kv_ref, queries_ref, keep_ref, send_ref, own_ref, other_ref, inverse_ref, inverse2_ref, share_ref, share2_ref,
    dq_ref, dk_ref, dv_ref,
    grads, across, turned, delta, dq, dk, dv,
):
    half, width = keep_ref.shape
    count, block = kv_ref.shape[0], BLOCK
    cols = slice(p * PAIR, (p + 1) * PAIR)
    here, there = lax.axis_index("mp"), 1 - lax.axis_index("mp")
    row = lax.broadcasted_iota(jnp.int32, (8, PAIR), 0)
    column = lax.broadcasted_iota(jnp.int32, (8, PAIR), 1)
    pick = jnp.where(column // HEAD_DIM == row, 1.0, 0.0).astype(BF16)
    sides = ((here, keep_ref, own_ref, inverse_ref), (there, send_ref, other_ref, inverse2_ref))
    for which, mixed_ref, up_ref, scale_ref in sides:
        scaled = (up_ref[:, cols].astype(F32) * scale_ref[:, cols]).astype(BF16)
        product = mixed_ref[:, cols].astype(F32) * scaled.astype(F32)
        high = product.astype(BF16)
        low = (product - high.astype(F32)).astype(BF16)
        delta[:, aligned(which, half)] = dot_nt(pick, high) + dot_nt(pick, low)
        stack_heads(scaled, grads.at[aligned(which, 2 * half), :], block)
        stack_heads_across(scaled.T, across.at[:, aligned(which, 2 * half)], block)
    turned[...] = kv_ref[:, cols].T
    dk[...] = jnp.zeros(dk.shape, F32)
    dv[...] = jnp.zeros(dv.shape, F32)

    def query_block(which, shares_ref, i, carry):
        g = which * (half // block) + i
        rows, both = aligned(g, block), aligned(g, 2 * block)
        dq[...] = jnp.zeros(dq.shape, F32)
        level = jnp.concatenate([delta[0:1, rows], delta[1:2, rows]], 1)

        def visit(span, size):
            d = dot(kv_ref[span, width + p * PAIR : width + (p + 1) * PAIR], across[:, both])
            shares = shares_ref[span, aligned(i, 2 * block)]
            slopes = (shares.astype(F32) * (d - level)).astype(BF16)
            dv[span, :] += dot(shares, grads[both, :])
            dk[span, :] += dot(slopes, queries_ref[p, both, :])
            for a in range(2):
                head = slice(a * HEAD_DIM, (a + 1) * HEAD_DIM)
                dq[head, :] += dot(turned[head, span], slopes[:, a * block : (a + 1) * block])

        over_keys(rng_ref[0, g], rng_ref[1, g], visit)
        dq_ref[rows, :] = (dq[...] * HEAD_DIM**-0.5).astype(BF16).T
        return carry

    for which, shares_ref in ((here, share_ref), (there, share2_ref)):
        lax.fori_loop(0, half // block, functools.partial(query_block, which, shares_ref), 0)
    dk_ref[...] = (dk[...] * LN2).astype(BF16)
    dv_ref[...] = dv[...].astype(BF16)


def pair_grad(p, rng, kv, queries, keep, send, own, other, *per_half):
    count = kv.shape[0]
    return pl.pallas_call(
        functools.partial(pair_grad_kernel, p),
        out_shape=(jax.ShapeDtypeStruct((count, PAIR), BF16),) * 3,
        in_specs=[SM] + [VM] * 10,
        out_specs=(VM,) * 3,
        scratch_shapes=[
            pltpu.VMEM((2 * count, PAIR), BF16),
            pltpu.VMEM((PAIR, 2 * count), BF16),
            pltpu.VMEM((PAIR, count), BF16),
            pltpu.VMEM((8, count), F32),
            pltpu.VMEM((PAIR, BLOCK), F32),
            pltpu.VMEM((count, PAIR), F32),
            pltpu.VMEM((count, PAIR), F32),
        ],
        compiler_params=pltpu.CompilerParams(vmem_limit_bytes=12 * MIB),
        cost_estimate=pl.CostEstimate(flops=4 * 10**9, bytes_accessed=8 * MIB, transcendentals=0),
        name=f"pair_grad_{p}",
    )(rng, kv, queries, keep, send, own, other, *per_half)


def input_part(flip, pieces, weights, half):
    which = 1 - lax.axis_index("mp") if flip else lax.axis_index("mp")
    rows = aligned(which, half)
    left = jnp.concatenate([piece[rows, :] for piece in pieces], 1)
    right = jnp.concatenate([weight[...] for weight in weights], 1)
    return dot_nt(left, right)


def away_kernel(*refs):
    out_ref = refs[-1]
    out_ref[...] = input_part(True, refs[:-4], refs[-4:-1], out_ref.shape[0]).astype(BF16)


def home_kernel(first_ref, got_ref, *refs):
    *pieces, wq_ref, wk_ref, wv_ref, out_hbm, out_ref, sems = refs
    half = out_ref.shape[0]
    parts = 2
    size = half // parts
    right = jnp.concatenate([wq_ref[...], wk_ref[...], wv_ref[...]], 1)
    copies = []
    for t in range(parts):
        part = slice(t * size, (t + 1) * size)
        rows = aligned(lax.axis_index("mp") * parts + t, size)
        total = dot_nt(jnp.concatenate([piece[rows, :] for piece in pieces], 1), right)
        out_ref[part, :] = (total + first_ref[part, :] + got_ref[part, :].astype(F32)).astype(BF16)
        copies.append(pltpu.make_async_copy(out_ref.at[part, :], out_hbm.at[part, :], sems.at[t]))
        copies[-1].start()
    for copy in copies:
        copy.wait()


def input_call(kernel, extra, pieces, weights, name):
    half, features = pieces[0].shape[0] // 2, weights[0].shape[0]
    return pl.pallas_call(
        kernel,
        out_shape=jax.ShapeDtypeStruct((half, features), BF16),
        in_specs=[VM] * (len(extra) + len(pieces) + len(weights)),
        out_specs=HB if extra else VM,
        scratch_shapes=[pltpu.VMEM((half, features), BF16), pltpu.SemaphoreType.DMA((2,))] if extra else [],
        compiler_params=pltpu.CompilerParams(vmem_limit_bytes=16 * MIB),
        cost_estimate=pl.CostEstimate(flops=10**9, bytes_accessed=6 * MIB, transcendentals=0),
        name=name,
    )(*extra, *pieces, *weights)


def gelu_both(v):
    part = 0.5 + 0.5 * lax.erf(v * ROOT_HALF)
    return v * part, part + v * jnp.exp(-0.5 * v * v) * ROOT_TWO_PI


def norm(values, gain, shift):
    mean = jnp.mean(values, -1, keepdims=True)
    centred = values - mean
    reciprocal = lax.rsqrt(jnp.mean(centred * centred, -1, keepdims=True) + EPS)
    normed = centred * reciprocal
    return normed * gain + shift, normed, reciprocal


def norm_grad(upstream, normed, reciprocal, gain):
    scaled = upstream * gain
    return reciprocal * (
        scaled - jnp.mean(scaled, -1, keepdims=True) - normed * jnp.mean(scaled * normed, -1, keepdims=True)
    )


def column_sum(values):
    return jnp.sum(values, 0, keepdims=True)


def eight_rows(values):
    return jnp.sum(values.reshape(-1, 8, values.shape[1]), 0)


def interleave(first, second):
    done = 0
    for i, step in enumerate(first):
        step()
        while done < len(second) and (done + 1) * len(first) <= (i + 1) * len(second):
            second[done]()
            done += 1
    for step in second[done:]:
        step()


def middle_kernel(
    x_ref, keep_ref, got_ref, up_ref,
    mdb_ref, mub_ref, ddb_ref, dub_ref, fg_ref, fs_ref, sg_ref, ss_ref,
    wo_ref, wo2_ref, w12_ref, w22_ref, md_hbm, mu_hbm, w1_hbm, w2_hbm, dd_hbm, du_hbm,
    act_hbm, first_ref, attended_ref, mine_ref, theirs_ref,
    md_ref, mu_ref, w1_ref, w2_ref, dd_ref, du_ref,
    slope_ref, wide_ref, out_ref, hidden_ref, normed_ref, low_ref, hidden_low_ref, act_ref, top_ref,
    big_ref, small_ref, sems, act_sem,
):
    rows, features = x_ref.shape
    adapt = md_ref.shape[0]
    names = ("md", "mu", "w1", "w2", "dd", "du")
    waits = dict(
        zip(
            names,
            start_all(
                (md_hbm, mu_hbm, w1_hbm, w2_hbm, dd_hbm, du_hbm),
                (md_ref, mu_ref, w1_ref, w2_ref, dd_ref, du_ref),
                sems,
            ),
        )
    )
    waited = set()

    def need(*wanted):
        for name in wanted:
            if name not in waited:
                waited.add(name)
                waits[name].wait()

    def vector(ref):
        return ref[...].astype(F32).reshape(1, -1)

    units = w1_ref.shape[1]
    chunk, piece_rows = 512, 64
    sides = ((w1_ref, w2_ref, ("w1", "w2")), (w12_ref, w22_ref, ()))
    pieces = [(side, slice(c * chunk, (c + 1) * chunk)) for side in sides for c in range(units // chunk)]
    kept = {}
    sums = {}

    def add(name, value):
        sums[name] = sums[name] + value if name in sums else value

    def parts(half):
        return [slice(r, r + piece_rows) for r in range(half.start, half.stop, piece_rows)]

    def attend(half):
        def first():
            attended = dot(keep_ref[half, :], wo_ref[...]) + dot(got_ref[half, :], wo2_ref[...])
            wide_ref[half, :] = attended
            low_ref[half, :] = attended.astype(BF16)

        def second():
            need("md", "mu")
            active, slope = gelu_both(dot_nt(low_ref[half, :], md_ref[...]) + vector(mdb_ref))
            kept["mixer", half.start] = (active.astype(BF16), slope)

        def third():
            out_ref[half, :] = dot(kept["mixer", half.start][0], mu_ref[...]) + vector(mub_ref)

        return [first, second, third]

    def norm_one(half):
        def one(part):
            x, mixer_out = x_ref[part, :].astype(F32), out_ref[part, :]
            add("mixer_square", eight_rows(mixer_out * mixer_out))
            add("input_square", eight_rows(x * x))
            hidden, normed, reciprocal = norm(x + wide_ref[part, :] + mixer_out, vector(fg_ref), vector(fs_ref))
            normed_ref[part, :] = normed
            hidden_ref[part, :] = hidden
            hidden_low_ref[part, :] = hidden.astype(BF16)
            kept["reciprocal", part.start] = reciprocal

        return [functools.partial(one, part) for part in parts(half)]

    def feed_forward(half):
        state = {}

        def start():
            need("w1", "w2")
            side, span = pieces[0]
            state["ahead"] = dot(hidden_low_ref[half, :], side[0][:, span])

        def one(n):
            side, span = pieces[n]
            inner = state["ahead"]
            if n + 1 < len(pieces):
                after, after_span = pieces[n + 1]
                state["ahead"] = dot(hidden_low_ref[half, :], after[0][:, after_span])
            value, slope = gelu_both(inner)
            slope_ref[half, n * chunk : (n + 1) * chunk] = slope.astype(BF16)
            state["value"] = value.astype(BF16)

        def two(n):
            side, span = pieces[n]
            total = dot(state["value"], side[1][span, :])
            state["total"] = state["total"] + total if n else total
            if n + 1 == len(pieces):
                wide_ref[half, :] = state["total"]

        steps = [start]
        for n in range(len(pieces)):
            steps += [functools.partial(one, n), functools.partial(two, n)]
        return steps

    def dense(half):
        def first():
            need("dd", "du")
            dense_low = wide_ref[half, :].astype(BF16)
            active, slope = gelu_both(dot_nt(dense_low, dd_ref[...]) + vector(ddb_ref))
            kept["dense", half.start] = (active.astype(BF16), slope, dense_low)

        def second():
            out_ref[half, :] = dot(kept["dense", half.start][0], du_ref[...]) + vector(dub_ref)

        return [first, second]

    def norm_two(half):
        def one(part):
            dense_out = out_ref[part, :]
            add("dense_square", eight_rows(dense_out * dense_out))
            gain = vector(sg_ref)
            result, normed, reciprocal = norm(hidden_ref[part, :] + wide_ref[part, :] + dense_out, gain, vector(ss_ref))
            act_ref[part, :] = result.astype(BF16)
            upstream = up_ref[part, :].astype(F32)
            add(4, eight_rows(upstream * normed))
            add(5, eight_rows(upstream))
            second_grad = norm_grad(upstream, normed, reciprocal, gain)
            hidden_ref[part, :] = second_grad
            top = second_grad.astype(BF16)
            top_ref[part, :] = top
            add(1, eight_rows(top.astype(F32)))

        return [functools.partial(one, part) for part in parts(half)]

    def dense_back(half):
        def first():
            active, slope, dense_low = kept["dense", half.start]
            top = top_ref[half, :]
            add("dense_up", dot_tn(active, top))
            mid = (dot_nt(top, du_ref[...]) * slope).astype(BF16)
            kept["dense_mid", half.start] = mid
            add("dense_mid", eight_rows(mid.astype(F32)))

        def second():
            mid = kept["dense_mid", half.start]
            add("dense_down", dot_tn(mid, kept["dense", half.start][2]))
            hidden_low_ref[half, :] = (hidden_ref[half, :] + dot(mid, dd_ref[...])).astype(BF16)

        return [first, second]

    def feed_back(half):
        state = {}

        def start():
            side, span = pieces[0]
            state["ahead"] = dot_nt(hidden_low_ref[half, :], side[1][span, :])

        def one(n):
            back = state["ahead"]
            if n + 1 < len(pieces):
                after, after_span = pieces[n + 1]
                state["ahead"] = dot_nt(hidden_low_ref[half, :], after[1][after_span, :])
            slope = slope_ref[half, n * chunk : (n + 1) * chunk].astype(F32)
            state["value"] = (back * slope).astype(BF16)

        def two(n):
            side, span = pieces[n]
            total = dot_nt(state["value"], side[0][:, span])
            state["total"] = state["total"] + total if n else total
            if n + 1 == len(pieces):
                hidden_ref[half, :] = hidden_ref[half, :] + state["total"]

        steps = [start]
        for n in range(len(pieces)):
            steps += [functools.partial(one, n), functools.partial(two, n)]
        return steps

    def norm_one_back(half):
        def one(part):
            hidden_grad, normed = hidden_ref[part, :], normed_ref[part, :]
            add(2, eight_rows(hidden_grad * normed))
            add(3, eight_rows(hidden_grad))
            first_grad = norm_grad(hidden_grad, normed, kept["reciprocal", part.start], vector(fg_ref))
            first_ref[part, :] = first_grad
            top = first_grad.astype(BF16)
            top_ref[part, :] = top
            add(0, eight_rows(top.astype(F32)))

        return [functools.partial(one, part) for part in parts(half)]

    def attend_back(half):
        def first():
            active, slope = kept["mixer", half.start]
            top = top_ref[half, :]
            add("mixer_up", dot_tn(active, top))
            mid = (dot_nt(top, mu_ref[...]) * slope).astype(BF16)
            kept["mixer_mid", half.start] = mid
            add("mixer_mid", eight_rows(mid.astype(F32)))

        def second():
            mid = kept["mixer_mid", half.start]
            add("mixer_down", dot_tn(mid, low_ref[half, :]))
            attended_ref[half, :] = (first_ref[half, :] + dot(mid, md_ref[...])).astype(BF16)

        return [first, second]

    def send_result(half, index):
        copy = pltpu.make_async_copy(act_ref.at[half, :], act_hbm.at[half, :], act_sem.at[index])
        copy.start()
        return copy

    one, two = slice(0, rows // 2), slice(rows // 2, rows)
    interleave(attend(one), [])
    interleave(norm_one(one), attend(two))
    interleave(feed_forward(one), norm_one(two))
    interleave(feed_forward(two), dense(one) + norm_two(one) + dense_back(one))
    copies = [send_result(one, 0)]
    interleave(feed_back(one), dense(two) + norm_two(two) + dense_back(two))
    copies.append(send_result(two, 1))
    interleave(feed_back(two), norm_one_back(one) + attend_back(one))
    interleave(norm_one_back(two), [])
    interleave(attend_back(two), [])

    for n, name in enumerate(("mixer_down", "mixer_up", "dense_down", "dense_up")):
        big_ref[n * adapt : (n + 1) * adapt, :] = sums[name].astype(BF16)
    for row in range(6):
        small_ref[row : row + 1, :] = column_sum(sums[row])
    lane = lax.broadcasted_iota(jnp.int32, (1, 128), 1)
    squares = jnp.zeros((1, 128), F32)
    for n, name in enumerate(("mixer_square", "dense_square", "input_square")):
        squares = jnp.where(lane == n, jnp.sum(column_sum(sums[name]), -1, keepdims=True), squares)
    small_ref[6:7, :] = jnp.concatenate(
        [column_sum(sums["mixer_mid"]), column_sum(sums["dense_mid"]), squares, jnp.zeros((1, features - 2 * adapt - 128), F32)], 1
    )
    small_ref[7:8, :] = jnp.zeros((1, features), F32)
    tail = tail_of(small_ref[...])
    share = 2 * adapt
    for pack_ref, which in ((mine_ref, lax.axis_index("mp")), (theirs_ref, 1 - lax.axis_index("mp"))):
        pack_ref[:share, :] = big_ref[aligned(which, share), :]
        pack_ref[share:, :] = tail
    for copy in copies:
        copy.wait()


def tail_of(vectors):
    high = vectors.astype(BF16)
    return jnp.concatenate([high, (vectors - high.astype(F32)).astype(BF16)], 0)


def vectors_of(tail):
    wide = tail.astype(F32)
    return wide[:8] + wide[8:]


def middle(x, keep, got, up, vectors, swapped, matrices):
    rows, features = x.shape
    adapt = matrices[0].shape[0]
    units = matrices[2].shape[1]
    packed = jax.ShapeDtypeStruct((2 * adapt + 16, features), BF16)
    return pl.pallas_call(
        middle_kernel,
        out_shape=(
            jax.ShapeDtypeStruct((rows, features), BF16),
            jax.ShapeDtypeStruct((rows, features), F32),
            jax.ShapeDtypeStruct((rows, features), BF16),
            packed,
            packed,
        ),
        in_specs=[VM] * 16 + [HB] * 6,
        out_specs=(HB,) + (VM,) * 4,
        scratch_shapes=[pltpu.VMEM(m.shape, BF16) for m in matrices]
        + [pltpu.VMEM((rows, 2 * units), BF16)]
        + [pltpu.VMEM((rows, features), F32)] * 4
        + [pltpu.VMEM((rows, features), BF16)] * 4
        + [
            pltpu.VMEM((4 * adapt, features), BF16),
            pltpu.VMEM((8, features), F32),
            pltpu.SemaphoreType.DMA((6,)),
            pltpu.SemaphoreType.DMA((2,)),
        ],
        compiler_params=pltpu.CompilerParams(vmem_limit_bytes=25 * MIB),
        cost_estimate=pl.CostEstimate(flops=2 * 10**10, bytes_accessed=16 * MIB, transcendentals=10**6),
        name="middle",
    )(x, keep, got, up, *vectors, *swapped, *map(in_hbm, matrices))


def spread_kernel(attended_ref, wo_ref, wo2_ref, own_ref, away_ref):
    attended = attended_ref[...]
    away_ref[...] = dot_nt(attended, wo2_ref[...]).astype(BF16)
    own_ref[...] = dot_nt(attended, wo_ref[...]).astype(BF16)


def spread(attended, wo, wo2):
    rows, width = attended.shape[0], wo.shape[0]
    return pl.pallas_call(
        spread_kernel,
        out_shape=(jax.ShapeDtypeStruct((rows, width), BF16),) * 2,
        in_specs=[VM] * 3,
        out_specs=(VM,) * 2,
        compiler_params=pltpu.CompilerParams(vmem_limit_bytes=8 * MIB),
        cost_estimate=pl.CostEstimate(flops=4 * rows * attended.shape[1] * width, bytes_accessed=3 * MIB, transcendentals=0),
        name="spread",
    )(attended, wo, wo2)


def combine_kernel(held_ref, got_ref, out_ref):
    rows = held_ref.shape[0] - 16
    out_ref[:rows, :] = (held_ref[:rows, :].astype(F32) + got_ref[:rows, :].astype(F32)).astype(BF16)
    out_ref[rows:, :] = tail_of(vectors_of(held_ref[rows:, :]) + vectors_of(got_ref[rows:, :]))


def combine(held, got):
    return pl.pallas_call(
        combine_kernel,
        out_shape=jax.ShapeDtypeStruct(held.shape, BF16),
        in_specs=[VM] * 2,
        out_specs=VM,
        compiler_params=pltpu.CompilerParams(vmem_limit_bytes=4 * MIB),
        cost_estimate=pl.CostEstimate(flops=10**5, bytes_accessed=MIB, transcendentals=0),
        name="combine",
    )(held, got)


def finish_kernel(held_ref, got_ref, md_ref, mdb_ref, mu_ref, mub_ref, dd_ref, ddb_ref, du_ref, dub_ref,
                  fg_ref, fs_ref, sg_ref, ss_ref, ratio_ref):
    adapt = md_ref.shape[0]

    def write(first_ref, second_ref):
        md_ref[...] = first_ref[:adapt, :].astype(F32)
        mu_ref[...] = first_ref[adapt : 2 * adapt, :].astype(F32)
        dd_ref[...] = second_ref[:adapt, :].astype(F32)
        du_ref[...] = second_ref[adapt : 2 * adapt, :].astype(F32)
        vectors = vectors_of(first_ref[2 * adapt :, :])
        for row, out_ref in enumerate((mub_ref, dub_ref, fg_ref, fs_ref, sg_ref, ss_ref)):
            out_ref[...] = vectors[row, :]
        last = vectors[6:7, :]
        mdb_ref[...] = last[0, :adapt]
        ddb_ref[...] = last[0, adapt : 2 * adapt]
        squares = last[:, 2 * adapt : 2 * adapt + 128]
        lane = lax.broadcasted_iota(jnp.int32, (1, 128), 1)
        base = jnp.sum(jnp.where(lane == 2, squares, 0.0), -1, keepdims=True)
        ratio_ref[...] = jnp.sqrt(squares / base)[0, :2]

    @pl.when(lax.axis_index("mp") == 0)
    def _():
        write(held_ref, got_ref)

    @pl.when(lax.axis_index("mp") != 0)
    def _():
        write(got_ref, held_ref)


def finish(held, got, adapt):
    features = held.shape[1]
    matrix = jax.ShapeDtypeStruct((adapt, features), F32)
    short, vector = jax.ShapeDtypeStruct((adapt,), F32), jax.ShapeDtypeStruct((features,), F32)
    return pl.pallas_call(
        finish_kernel,
        out_shape=(matrix, short, matrix, vector) * 2 + (vector,) * 4 + (jax.ShapeDtypeStruct((2,), F32),),
        in_specs=[VM, VM],
        out_specs=(VM,) * 13,
        compiler_params=pltpu.CompilerParams(vmem_limit_bytes=4 * MIB),
        name="finish",
    )(held, got)


def swap_cores(value):
    return lax.ppermute(value, "mp", [(0, 1), (1, 0)])


def tie(*values):
    return lax.optimization_barrier(values)


def per_device(
    tokens, segment_ids, query_weight, key_weight, value_weight, output_weight, inner_weight, outer_weight,
    mixer_down, mixer_down_bias, mixer_up, mixer_up_bias, dense_down, dense_down_bias, dense_up, dense_up_bias,
    first_gain, first_shift, second_gain, second_shift, output_grad,
):
    devices = lax.axis_size("dp")
    adapt = mixer_down.shape[1]
    other_tokens = swap_cores(tokens)
    kv, queries, across, turned, item, hide, rng = project(
        segment_ids, tokens, query_weight, key_weight, value_weight
    )
    kv, other_tokens, output_late, inner_late, outer_late = tie(
        kv, other_tokens, output_weight, inner_weight, outer_weight
    )
    other_output = swap_cores(output_late)
    other_inner = swap_cores(inner_late)
    other_outer = swap_cores(outer_late)
    half = tokens.shape[0]
    written = (kv, queries, across, turned)
    kv, queries, across, turned, send, inverse2, *shares2 = attention_call(
        attention_kernel, "attention", written, half,
        (rng, other_tokens, item, hide, query_weight, key_weight, value_weight, *written),
    )
    got = swap_cores(send)
    keep, inverse, *shares = attention_call(
        own_attention_kernel, "own_attention", (), half, (rng, item, hide, kv, across, turned)
    )
    got, keep = tie(got, keep)
    vectors = (
        mixer_down_bias, mixer_up_bias, dense_down_bias, dense_up_bias, first_gain, first_shift, second_gain, second_shift,
    )
    swapped = (output_weight, other_output, other_inner, other_outer)
    matrices = (mixer_down.T, mixer_up, inner_weight, outer_weight, dense_down.T, dense_up)
    result, first_grad, attended, mine, theirs = middle(
        tokens, keep, got, output_grad, vectors, swapped, matrices
    )
    arriving = swap_cores(theirs)
    own_grad, away_grad = spread(attended, output_weight, other_output)
    arriving, own_grad = tie(arriving, own_grad)
    packed = combine(mine, arriving)
    away_grad, packed = tie(away_grad, packed)
    got_grad = swap_cores(away_grad)

    steps = []
    while 2 ** len(steps) < devices:
        steps.append(2 ** len(steps))
    steps.reverse()
    turn = len(steps) // 2
    pairs = len(shares)
    grads = []
    weights = (query_weight, key_weight, value_weight)
    for n, step in enumerate(steps):
        other_step = steps[(n + turn) % len(steps)]
        exchange = [(2 * i + c, 2 * (i ^ s) + c) for i in range(devices) for c, s in enumerate((step, other_step))]
        arriving = lax.ppermute(packed, ("dp", "mp"), exchange)
        if n < pairs:
            got_grad, packed = tie(got_grad, packed)
            parts = pair_grad(n, rng, kv, queries, keep, send, own_grad, got_grad, inverse, inverse2, shares[n], shares2[n])
            arriving, *parts = tie(arriving, *parts)
            grads.append(parts)
        elif n == pairs:
            pieces = [grads[p][i] for i in range(3) for p in range(pairs)]
            away = swap_cores(input_call(away_kernel, (), pieces, weights, "away"))
            input_grad = input_call(home_kernel, (first_grad, away), pieces, weights, "home")
            arriving, input_grad = tie(arriving, input_grad)
        packed = combine(packed, arriving)
    md, mdb, mu, mub, dd, ddb, du, dub, *rest = finish(packed, swap_cores(packed), adapt)
    return (result, input_grad, md.T, mdb, mu, mub, dd.T, ddb, du, dub, *rest)


def solution(mesh):
    tokens = P(("dp", "mp"), None)
    columns, rows, whole = P(None, "mp"), P("mp", None), P()
    return jax.shard_map(
        per_device,
        mesh=mesh,
        in_specs=(tokens, P("dp", None), columns, columns, columns, rows, columns, rows) + (whole,) * 12 + (tokens,),
        out_specs=(tokens, tokens) + (whole,) * 13,
        check_vma=False,
    )
```

```python
import functools

import jax
import jax.numpy as jnp
from jax import lax
from jax.experimental import pallas as pl
from jax.experimental.pallas import tpu as pltpu
from jax.sharding import PartitionSpec as P

F32 = jnp.float32
BF16 = jnp.bfloat16
HEAD_DIM = 64
PAIR = 2 * HEAD_DIM
EPS = 1e-12
LOG2E = 1.4426950408889634
LN2 = 0.6931471805599453
ROOT_HALF = 0.7071067811865476
ROOT_TWO_PI = 0.3989422804014327
MASKED = -(2.0**100)
LARGEST = 2.0**100
SMALLEST = 2.0**-60
TURNED = 80
BLOCK = 256
STEP = 128
MIB = 1 << 20

VM = pl.BlockSpec(memory_space=pltpu.VMEM)
SM = pl.BlockSpec(memory_space=pltpu.SMEM)
HB = pl.BlockSpec(memory_space=pltpu.HBM)


def dot(left, right):
    return jnp.dot(left, right, preferred_element_type=F32)


def dot_nt(left, right):
    return lax.dot_general(left, right, (((1,), (1,)), ((), ())), preferred_element_type=F32)


def dot_tn(left, right):
    return lax.dot_general(left, right, (((0,), (0,)), ((), ())), preferred_element_type=F32)


def aligned(index, size):
    return pl.ds(pl.multiple_of(index * size, size), size)


def split_pair(pair):
    lane = lax.broadcasted_iota(jnp.int32, pair.shape, 1)
    zero = jnp.zeros_like(pair)
    return jnp.where(lane < HEAD_DIM, pair, zero), jnp.where(lane < HEAD_DIM, zero, pair)


def stack_heads(source, target, block):
    first, second = split_pair(source)
    for t in range(source.shape[0] // block):
        target[pl.ds(2 * t * block, block), :] = first[t * block : (t + 1) * block]
        target[pl.ds((2 * t + 1) * block, block), :] = second[t * block : (t + 1) * block]


def stack_heads_across(source, target, block):
    row = lax.broadcasted_iota(jnp.int32, source.shape, 0)
    zero = jnp.zeros_like(source)
    first = jnp.where(row < HEAD_DIM, source, zero)
    second = jnp.where(row < HEAD_DIM, zero, source)
    for t in range(source.shape[1] // block):
        target[:, 2 * t * block : (2 * t + 1) * block] = first[:, t * block : (t + 1) * block]
        target[:, (2 * t + 1) * block : (2 * t + 2) * block] = second[:, t * block : (t + 1) * block]


def in_hbm(value):
    return pltpu.with_memory_space_constraint(value, pltpu.HBM)


def start_all(sources, buffers, sems):
    copies = [pltpu.make_async_copy(src, dst, sems.at[i]) for i, (src, dst) in enumerate(zip(sources, buffers))]
    for copy in copies:
        copy.start()
    return copies


def write_projection(which, x, weights, copies, kv_ref, queries_ref, across_ref, turned_ref, between=None):
    rows, width = x.shape[0], weights[0].shape[1]
    pairs = width // PAIR
    if copies:
        copies[0].wait()
    queries = (dot(x, weights[0][...]) * (HEAD_DIM**-0.5 * LOG2E)).astype(BF16)
    if between is not None:
        between()
    for p in range(pairs):
        pair = queries[:, p * PAIR : (p + 1) * PAIR]
        stack_heads(pair, queries_ref.at[p, aligned(which, 2 * rows), :], BLOCK)
        stack_heads_across(pair.T, across_ref.at[p, :, aligned(which, 2 * rows)], BLOCK)
    if copies:
        copies[1].wait()
    kv_ref[aligned(which, rows), :width] = dot(x, weights[1][...]).astype(BF16)
    if copies:
        copies[2].wait()
    values = dot(x, weights[2][...]).astype(BF16)
    kv_ref[aligned(which, rows), width:] = values
    ones = jnp.ones((TURNED - HEAD_DIM, rows), BF16)
    for p in range(pairs):
        turned = values[:, p * PAIR : (p + 1) * PAIR].T
        for a in range(2):
            base = (2 * p + a) * TURNED
            turned_ref[base : base + HEAD_DIM, aligned(which, rows)] = turned[a * HEAD_DIM : (a + 1) * HEAD_DIM]
            turned_ref[base + HEAD_DIM : base + TURNED, aligned(which, rows)] = ones


def over_keys(low, high, visit):
    odd = (high - low) % 2

    def whole(t, c):
        visit(pl.ds(pl.multiple_of(low * STEP + t * BLOCK, STEP), BLOCK), BLOCK)
        return c

    lax.fori_loop(0, (high - low) // 2 - odd, whole, 0)

    @pl.when(odd == 1)
    def _():
        size = BLOCK + STEP
        visit(pl.ds(pl.multiple_of(high * STEP - size, STEP), size), size)


def is_shift(lane):
    return (lane == 63) | (lane == 95) | (lane == 127)


def project_kernel(
    seg_hbm, x_ref, wq_ref, wk_ref, wv_ref,
    kv_ref, queries_ref, across_ref, turned_ref, item_ref, hide_ref, rng_ref,
    seg_ref, x_buf, wq, wk, wv, sems,
):
    sources, buffers = (seg_hbm, x_ref, wq_ref, wk_ref, wv_ref), (seg_ref, x_buf, wq, wk, wv)
    seg_copy, *copies = start_all(sources, buffers, sems)
    count, block = kv_ref.shape[0], BLOCK

    def items():
        ids = seg_ref[...].astype(F32)
        position = lax.broadcasted_iota(jnp.int32, ids.shape, 1)
        for g in range(count // block):
            first, last = (
                jnp.sum(jnp.where(position == at, ids, 0.0), -1, keepdims=True) for at in (g * block, (g + 1) * block - 1)
            )
            rng_ref[0, g] = jnp.sum(jnp.where(ids < first, 1.0, 0.0)).astype(jnp.int32) // STEP
            rng_ref[1, g] = (jnp.sum(jnp.where(ids <= last, 1.0, 0.0)).astype(jnp.int32) + STEP - 1) // STEP
        lane = lax.broadcasted_iota(jnp.int32, (128, 128), 1)
        for t in range(count // 128):
            same = jnp.broadcast_to(ids[:, t * 128 : (t + 1) * 128], (128, 128)).T == lane.astype(F32)
            item_ref[t * 128 : (t + 1) * 128, :] = jnp.where(same | is_shift(lane), 1.0, 0.0).astype(BF16)
        row = lax.broadcasted_iota(jnp.int32, (128, block), 0)
        for t in range(count // block):
            same = row.astype(F32) == ids[:, t * block : (t + 1) * block]
            hide = jnp.where(same | is_shift(row), 0.0, MASKED).astype(BF16)
            for a in range(2):
                hide_ref[:, (2 * t + a) * block : (2 * t + a + 1) * block] = hide

    seg_copy.wait()
    copies[0].wait()
    write_projection(
        lax.axis_index("mp"), x_buf[...], (wq, wk, wv), copies[1:], kv_ref, queries_ref, across_ref, turned_ref, items
    )


def project(seg, x, wq, wk, wv):
    rows, width = x.shape[0], wq.shape[1]
    count, pairs = 2 * rows, width // PAIR
    return pl.pallas_call(
        project_kernel,
        out_shape=(
            jax.ShapeDtypeStruct((count, 2 * width), BF16),
            jax.ShapeDtypeStruct((pairs, 2 * count, PAIR), BF16),
            jax.ShapeDtypeStruct((pairs, PAIR, 2 * count), BF16),
            jax.ShapeDtypeStruct((2 * pairs * TURNED, count), BF16),
            jax.ShapeDtypeStruct((count, 128), BF16),
            jax.ShapeDtypeStruct((128, 2 * count), BF16),
            jax.ShapeDtypeStruct((2, count // BLOCK), jnp.int32),
        ),
        in_specs=[HB] * 5,
        out_specs=(VM,) * 6 + (SM,),
        scratch_shapes=[pltpu.VMEM(v.shape, v.dtype) for v in (seg, x, wq, wk, wv)] + [pltpu.SemaphoreType.DMA((5,))],
        compiler_params=pltpu.CompilerParams(vmem_limit_bytes=16 * MIB),
        cost_estimate=pl.CostEstimate(flops=2 * rows * x.shape[1] * 3 * width, bytes_accessed=5 * MIB, transcendentals=0),
        name="project",
    )(*map(in_hbm, (seg, x, wq, wk, wv)))


def attend_queries(which, rng_ref, item_ref, hide_ref, kv_ref, across, turned, out_ref, inverse_ref, share_refs, mix, shifted, peaks):
    pairs, block = len(share_refs), BLOCK
    per_half = out_ref.shape[0] // block

    def scores(p, span, both, hide):
        keys = jnp.concatenate([kv_ref[span, p * PAIR : (p + 1) * PAIR], item_ref[span, :]], 1)
        return dot(keys, jnp.concatenate([across[p, :, both], hide], 0))

    def query_block(i, carry):
        g = which * per_half + i
        both, here = aligned(g, 2 * block), aligned(i, 2 * block)
        low, high = rng_ref[0, g], rng_ref[1, g]

        def mix_all(hide_of):
            mix[...] = jnp.zeros(mix.shape, F32)

            def visit(span, size):
                ahead = scores(0, span, both, hide_of(0))
                for p in range(pairs):
                    s = ahead
                    if p + 1 < pairs:
                        ahead = scores(p + 1, span, both, hide_of(p + 1))
                    e = jnp.exp2(s).astype(BF16)
                    share_refs[p][span, here] = e
                    for a in range(2):
                        head = slice((2 * p + a) * TURNED, (2 * p + a + 1) * TURNED)
                        mix[head, :] += dot(turned[head, span], e[:, a * block : (a + 1) * block])

            over_keys(low, high, visit)

        mix_all(lambda p: hide_ref[:, both])
        total_rows = [h * TURNED + HEAD_DIM for h in range(2 * pairs)]
        sums = jnp.concatenate([mix[r : r + 8, :] for r in total_rows], 0)
        fine = jnp.where((sums <= LARGEST) & (sums >= SMALLEST), 0.0, 1.0)

        @pl.when(jnp.max(fine) > 0.0)
        def _():
            peaks[...] = jnp.full(peaks.shape, MASKED, F32)

            def visit(span, size):
                for p in range(pairs):
                    s = scores(p, span, both, hide_ref[:, both])
                    peaks[p] = jnp.maximum(peaks[p], jnp.max(s, 0, keepdims=True))

            over_keys(low, high, visit)
            row = lax.broadcasted_iota(jnp.int32, (128, 2 * block), 0)
            hide = hide_ref[:, both].astype(F32)
            for p in range(pairs):
                peak = peaks[p]
                first = peak.astype(BF16).astype(F32)
                second = (peak - first).astype(BF16).astype(F32)
                third = peak - first - second
                parts = jnp.where(row < 64, first, jnp.where(row < 96, second, third))
                shifted[p] = jnp.where(is_shift(row), -parts, hide).astype(BF16)
            mix_all(lambda p: shifted[p])

        rows = aligned(i, block)
        outs = []
        for p in range(pairs):
            scales = []
            for a in range(2):
                base = (2 * p + a) * TURNED
                scale = jnp.broadcast_to(1.0 / mix[base + HEAD_DIM : base + HEAD_DIM + 1, :], (HEAD_DIM, block))
                outs.append((mix[base : base + HEAD_DIM, :] * scale).astype(BF16))
                scales.append(scale)
            inverse_ref[rows, p * PAIR : (p + 1) * PAIR] = jnp.concatenate(scales, 0).T
        out_ref[rows, :] = jnp.concatenate(outs, 0).T
        return carry

    lax.fori_loop(0, per_half, query_block, 0)


def attention_kernel(
    rng_ref, x_ref, item_ref, hide_ref, wq_ref, wk_ref, wv_ref, kv_in, queries_in, across_in, turned_in,
    kv_ref, queries_ref, across, turned, out_ref, inverse_ref, *rest,
):
    half = x_ref.shape[0]
    *share_refs, mix, shifted, peaks = rest
    here, there = lax.axis_index("mp"), 1 - lax.axis_index("mp")
    turned[:, aligned(here, half)] = turned_in[:, aligned(here, half)]
    across[:, :, aligned(here, 2 * half)] = across_in[:, :, aligned(here, 2 * half)]
    kv_ref[aligned(here, half), :] = kv_in[aligned(here, half), :]
    queries_ref[:, aligned(here, 2 * half), :] = queries_in[:, aligned(here, 2 * half), :]
    write_projection(there, x_ref[...], (wq_ref, wk_ref, wv_ref), (), kv_ref, queries_ref, across, turned)
    attend_queries(there, rng_ref, item_ref, hide_ref, kv_ref, across, turned, out_ref, inverse_ref, share_refs, mix, shifted, peaks)


def own_attention_kernel(rng_ref, item_ref, hide_ref, kv_ref, across, turned, out_ref, inverse_ref, *rest):
    *share_refs, mix, shifted, peaks = rest
    here = lax.axis_index("mp")
    attend_queries(here, rng_ref, item_ref, hide_ref, kv_ref, across, turned, out_ref, inverse_ref, share_refs, mix, shifted, peaks)


def attention_call(kernel, name, kept, half, operands):
    kv = operands[7] if kept else operands[3]
    count, width = kv.shape[0], kv.shape[1] // 2
    pairs = width // PAIR
    return pl.pallas_call(
        kernel,
        out_shape=tuple(jax.ShapeDtypeStruct(v.shape, v.dtype) for v in kept)
        + (jax.ShapeDtypeStruct((half, width), BF16), jax.ShapeDtypeStruct((half, width), F32))
        + (jax.ShapeDtypeStruct((count, 2 * half), BF16),) * pairs,
        in_specs=[SM] + [VM] * (len(operands) - 1),
        out_specs=(VM,) * (len(kept) + 2 + pairs),
        scratch_shapes=[
            pltpu.VMEM((2 * pairs * TURNED, BLOCK), F32),
            pltpu.VMEM((pairs, 128, 2 * BLOCK), BF16),
            pltpu.VMEM((pairs, 1, 2 * BLOCK), F32),
        ],
        compiler_params=pltpu.CompilerParams(vmem_limit_bytes=10 * MIB),
        cost_estimate=pl.CostEstimate(flops=5 * 10**9, bytes_accessed=8 * MIB, transcendentals=10**6),
        name=name,
    )(*operands)


def pair_grad_kernel(
    p, rng_ref, kv_ref, queries_ref, keep_ref, send_ref, own_ref, other_ref, inverse_ref, inverse2_ref, share_ref, share2_ref,
    dq_ref, dk_ref, dv_ref,
    grads, across, turned, delta, dq, dk, dv,
):
    half, width = keep_ref.shape
    count, block = kv_ref.shape[0], BLOCK
    cols = slice(p * PAIR, (p + 1) * PAIR)
    here, there = lax.axis_index("mp"), 1 - lax.axis_index("mp")
    row = lax.broadcasted_iota(jnp.int32, (8, PAIR), 0)
    column = lax.broadcasted_iota(jnp.int32, (8, PAIR), 1)
    pick = jnp.where(column // HEAD_DIM == row, 1.0, 0.0).astype(BF16)
    sides = ((here, keep_ref, own_ref, inverse_ref), (there, send_ref, other_ref, inverse2_ref))
    for which, mixed_ref, up_ref, scale_ref in sides:
        scaled = (up_ref[:, cols].astype(F32) * scale_ref[:, cols]).astype(BF16)
        product = mixed_ref[:, cols].astype(F32) * scaled.astype(F32)
        high = product.astype(BF16)
        low = (product - high.astype(F32)).astype(BF16)
        delta[:, aligned(which, half)] = dot_nt(pick, high) + dot_nt(pick, low)
        stack_heads(scaled, grads.at[aligned(which, 2 * half), :], block)
        stack_heads_across(scaled.T, across.at[:, aligned(which, 2 * half)], block)
    turned[...] = kv_ref[:, cols].T
    dk[...] = jnp.zeros(dk.shape, F32)
    dv[...] = jnp.zeros(dv.shape, F32)

    def query_block(which, shares_ref, i, carry):
        g = which * (half // block) + i
        rows, both = aligned(g, block), aligned(g, 2 * block)
        dq[...] = jnp.zeros(dq.shape, F32)
        level = jnp.concatenate([delta[0:1, rows], delta[1:2, rows]], 1)

        def visit(span, size):
            d = dot(kv_ref[span, width + p * PAIR : width + (p + 1) * PAIR], across[:, both])
            shares = shares_ref[span, aligned(i, 2 * block)]
            slopes = (shares.astype(F32) * (d - level)).astype(BF16)
            dv[span, :] += dot(shares, grads[both, :])
            dk[span, :] += dot(slopes, queries_ref[p, both, :])
            for a in range(2):
                head = slice(a * HEAD_DIM, (a + 1) * HEAD_DIM)
                dq[head, :] += dot(turned[head, span], slopes[:, a * block : (a + 1) * block])

        over_keys(rng_ref[0, g], rng_ref[1, g], visit)
        dq_ref[rows, :] = (dq[...] * HEAD_DIM**-0.5).astype(BF16).T
        return carry

    for which, shares_ref in ((here, share_ref), (there, share2_ref)):
        lax.fori_loop(0, half // block, functools.partial(query_block, which, shares_ref), 0)
    dk_ref[...] = (dk[...] * LN2).astype(BF16)
    dv_ref[...] = dv[...].astype(BF16)


def pair_grad(p, rng, kv, queries, keep, send, own, other, *per_half):
    count = kv.shape[0]
    return pl.pallas_call(
        functools.partial(pair_grad_kernel, p),
        out_shape=(jax.ShapeDtypeStruct((count, PAIR), BF16),) * 3,
        in_specs=[SM] + [VM] * 10,
        out_specs=(VM,) * 3,
        scratch_shapes=[
            pltpu.VMEM((2 * count, PAIR), BF16),
            pltpu.VMEM((PAIR, 2 * count), BF16),
            pltpu.VMEM((PAIR, count), BF16),
            pltpu.VMEM((8, count), F32),
            pltpu.VMEM((PAIR, BLOCK), F32),
            pltpu.VMEM((count, PAIR), F32),
            pltpu.VMEM((count, PAIR), F32),
        ],
        compiler_params=pltpu.CompilerParams(vmem_limit_bytes=12 * MIB),
        cost_estimate=pl.CostEstimate(flops=4 * 10**9, bytes_accessed=8 * MIB, transcendentals=0),
        name=f"pair_grad_{p}",
    )(rng, kv, queries, keep, send, own, other, *per_half)


def input_kernel(first_ref, *refs):
    *pieces, wq_ref, wk_ref, wv_ref, away_ref, home_ref = refs
    half = home_ref.shape[0]
    right = jnp.concatenate([wq_ref[...], wk_ref[...], wv_ref[...]], 1)

    def part(which):
        rows = aligned(which, half)
        return dot_nt(jnp.concatenate([piece[rows, :] for piece in pieces], 1), right)

    away_ref[...] = part(1 - lax.axis_index("mp")).astype(BF16)
    home_ref[...] = part(lax.axis_index("mp")) + first_ref[...]


def input_parts(first_grad, pieces, weights):
    half, features = first_grad.shape
    return pl.pallas_call(
        input_kernel,
        out_shape=(jax.ShapeDtypeStruct((half, features), BF16), jax.ShapeDtypeStruct((half, features), F32)),
        in_specs=[VM] * (1 + len(pieces) + len(weights)),
        out_specs=(VM,) * 2,
        compiler_params=pltpu.CompilerParams(vmem_limit_bytes=16 * MIB),
        cost_estimate=pl.CostEstimate(flops=2 * 10**9, bytes_accessed=8 * MIB, transcendentals=0),
        name="input_parts",
    )(first_grad, *pieces, *weights)


def gelu_both(v):
    part = 0.5 + 0.5 * lax.erf(v * ROOT_HALF)
    return v * part, part + v * jnp.exp(-0.5 * v * v) * ROOT_TWO_PI


def norm(values, gain, shift):
    mean = jnp.mean(values, -1, keepdims=True)
    centred = values - mean
    reciprocal = lax.rsqrt(jnp.mean(centred * centred, -1, keepdims=True) + EPS)
    normed = centred * reciprocal
    return normed * gain + shift, normed, reciprocal


def norm_grad(upstream, normed, reciprocal, gain):
    scaled = upstream * gain
    return reciprocal * (
        scaled - jnp.mean(scaled, -1, keepdims=True) - normed * jnp.mean(scaled * normed, -1, keepdims=True)
    )


def column_sum(values):
    return jnp.sum(values, 0, keepdims=True)


def eight_rows(values):
    return jnp.sum(values.reshape(-1, 8, values.shape[1]), 0)


def interleave(first, second):
    done = 0
    for i, step in enumerate(first):
        step()
        while done < len(second) and (done + 1) * len(first) <= (i + 1) * len(second):
            second[done]()
            done += 1
    for step in second[done:]:
        step()


def middle_kernel(
    x_ref, keep_ref, got_ref, up_ref,
    mdb_ref, mub_ref, ddb_ref, dub_ref, fg_ref, fs_ref, sg_ref, ss_ref,
    wo_ref, wo2_ref, w12_ref, w22_ref, md_hbm, mu_hbm, w1_hbm, w2_hbm, dd_hbm, du_hbm,
    act_hbm, first_ref, attended_ref, mine_ref, theirs_ref,
    md_ref, mu_ref, w1_ref, w2_ref, dd_ref, du_ref,
    slope_ref, wide_ref, out_ref, hidden_ref, normed_ref, low_ref, hidden_low_ref, act_ref, top_ref,
    big_ref, small_ref, sems, act_sem,
):
    rows, features = x_ref.shape
    adapt = md_ref.shape[0]
    names = ("md", "mu", "w1", "w2", "dd", "du")
    waits = dict(
        zip(
            names,
            start_all(
                (md_hbm, mu_hbm, w1_hbm, w2_hbm, dd_hbm, du_hbm),
                (md_ref, mu_ref, w1_ref, w2_ref, dd_ref, du_ref),
                sems,
            ),
        )
    )
    waited = set()

    def need(*wanted):
        for name in wanted:
            if name not in waited:
                waited.add(name)
                waits[name].wait()

    def vector(ref):
        return ref[...].astype(F32).reshape(1, -1)

    units = w1_ref.shape[1]
    chunk, piece_rows = 512, 64
    sides = ((w1_ref, w2_ref, ("w1", "w2")), (w12_ref, w22_ref, ()))
    pieces = [(side, slice(c * chunk, (c + 1) * chunk)) for side in sides for c in range(units // chunk)]
    kept = {}
    sums = {}

    def add(name, value):
        sums[name] = sums[name] + value if name in sums else value

    def parts(half):
        return [slice(r, r + piece_rows) for r in range(half.start, half.stop, piece_rows)]

    def attend(half):
        def first():
            attended = dot(keep_ref[half, :], wo_ref[...]) + dot(got_ref[half, :], wo2_ref[...])
            wide_ref[half, :] = attended
            low_ref[half, :] = attended.astype(BF16)

        def second():
            need("md", "mu")
            active, slope = gelu_both(dot_nt(low_ref[half, :], md_ref[...]) + vector(mdb_ref))
            kept["mixer", half.start] = (active.astype(BF16), slope)

        def third():
            out_ref[half, :] = dot(kept["mixer", half.start][0], mu_ref[...]) + vector(mub_ref)

        return [first, second, third]

    def norm_one(half):
        def one(part):
            x, mixer_out = x_ref[part, :].astype(F32), out_ref[part, :]
            add("mixer_square", eight_rows(mixer_out * mixer_out))
            add("input_square", eight_rows(x * x))
            hidden, normed, reciprocal = norm(x + wide_ref[part, :] + mixer_out, vector(fg_ref), vector(fs_ref))
            normed_ref[part, :] = normed
            hidden_ref[part, :] = hidden
            hidden_low_ref[part, :] = hidden.astype(BF16)
            kept["reciprocal", part.start] = reciprocal

        return [functools.partial(one, part) for part in parts(half)]

    def feed_forward(half):
        state = {}

        def start():
            need("w1", "w2")
            side, span = pieces[0]
            state["ahead"] = dot(hidden_low_ref[half, :], side[0][:, span])

        def one(n):
            side, span = pieces[n]
            inner = state["ahead"]
            if n + 1 < len(pieces):
                after, after_span = pieces[n + 1]
                state["ahead"] = dot(hidden_low_ref[half, :], after[0][:, after_span])
            value, slope = gelu_both(inner)
            slope_ref[half, n * chunk : (n + 1) * chunk] = slope.astype(BF16)
            state["value"] = value.astype(BF16)

        def two(n):
            side, span = pieces[n]
            total = dot(state["value"], side[1][span, :])
            state["total"] = state["total"] + total if n else total
            if n + 1 == len(pieces):
                wide_ref[half, :] = state["total"]

        steps = [start]
        for n in range(len(pieces)):
            steps += [functools.partial(one, n), functools.partial(two, n)]
        return steps

    def dense(half):
        def first():
            need("dd", "du")
            dense_low = wide_ref[half, :].astype(BF16)
            active, slope = gelu_both(dot_nt(dense_low, dd_ref[...]) + vector(ddb_ref))
            kept["dense", half.start] = (active.astype(BF16), slope, dense_low)

        def second():
            out_ref[half, :] = dot(kept["dense", half.start][0], du_ref[...]) + vector(dub_ref)

        return [first, second]

    def norm_two(half):
        def one(part):
            dense_out = out_ref[part, :]
            add("dense_square", eight_rows(dense_out * dense_out))
            gain = vector(sg_ref)
            result, normed, reciprocal = norm(hidden_ref[part, :] + wide_ref[part, :] + dense_out, gain, vector(ss_ref))
            act_ref[part, :] = result.astype(BF16)
            upstream = up_ref[part, :].astype(F32)
            add(4, eight_rows(upstream * normed))
            add(5, eight_rows(upstream))
            second_grad = norm_grad(upstream, normed, reciprocal, gain)
            hidden_ref[part, :] = second_grad
            top = second_grad.astype(BF16)
            top_ref[part, :] = top
            add(1, eight_rows(top.astype(F32)))

        return [functools.partial(one, part) for part in parts(half)]

    def dense_back(half):
        def first():
            active, slope, dense_low = kept["dense", half.start]
            top = top_ref[half, :]
            add("dense_up", dot_tn(active, top))
            mid = (dot_nt(top, du_ref[...]) * slope).astype(BF16)
            kept["dense_mid", half.start] = mid
            add("dense_mid", eight_rows(mid.astype(F32)))

        def second():
            mid = kept["dense_mid", half.start]
            add("dense_down", dot_tn(mid, kept["dense", half.start][2]))
            hidden_low_ref[half, :] = (hidden_ref[half, :] + dot(mid, dd_ref[...])).astype(BF16)

        return [first, second]

    def feed_back(half):
        state = {}

        def start():
            side, span = pieces[0]
            state["ahead"] = dot_nt(hidden_low_ref[half, :], side[1][span, :])

        def one(n):
            back = state["ahead"]
            if n + 1 < len(pieces):
                after, after_span = pieces[n + 1]
                state["ahead"] = dot_nt(hidden_low_ref[half, :], after[1][after_span, :])
            slope = slope_ref[half, n * chunk : (n + 1) * chunk].astype(F32)
            state["value"] = (back * slope).astype(BF16)

        def two(n):
            side, span = pieces[n]
            total = dot_nt(state["value"], side[0][:, span])
            state["total"] = state["total"] + total if n else total
            if n + 1 == len(pieces):
                hidden_ref[half, :] = hidden_ref[half, :] + state["total"]

        steps = [start]
        for n in range(len(pieces)):
            steps += [functools.partial(one, n), functools.partial(two, n)]
        return steps

    def norm_one_back(half):
        def one(part):
            hidden_grad, normed = hidden_ref[part, :], normed_ref[part, :]
            add(2, eight_rows(hidden_grad * normed))
            add(3, eight_rows(hidden_grad))
            first_grad = norm_grad(hidden_grad, normed, kept["reciprocal", part.start], vector(fg_ref))
            first_ref[part, :] = first_grad
            top = first_grad.astype(BF16)
            top_ref[part, :] = top
            add(0, eight_rows(top.astype(F32)))

        return [functools.partial(one, part) for part in parts(half)]

    def attend_back(half):
        def first():
            active, slope = kept["mixer", half.start]
            top = top_ref[half, :]
            add("mixer_up", dot_tn(active, top))
            mid = (dot_nt(top, mu_ref[...]) * slope).astype(BF16)
            kept["mixer_mid", half.start] = mid
            add("mixer_mid", eight_rows(mid.astype(F32)))

        def second():
            mid = kept["mixer_mid", half.start]
            add("mixer_down", dot_tn(mid, low_ref[half, :]))
            attended_ref[half, :] = (first_ref[half, :] + dot(mid, md_ref[...])).astype(BF16)

        return [first, second]

    def send_result(half, index):
        copy = pltpu.make_async_copy(act_ref.at[half, :], act_hbm.at[half, :], act_sem.at[index])
        copy.start()
        return copy

    one, two = slice(0, rows // 2), slice(rows // 2, rows)
    interleave(attend(one), [])
    interleave(norm_one(one), attend(two))
    interleave(feed_forward(one), norm_one(two))
    interleave(feed_forward(two), dense(one) + norm_two(one) + dense_back(one))
    copies = [send_result(one, 0)]
    interleave(feed_back(one), dense(two) + norm_two(two) + dense_back(two))
    copies.append(send_result(two, 1))
    interleave(feed_back(two), norm_one_back(one) + attend_back(one))
    interleave(norm_one_back(two), [])
    interleave(attend_back(two), [])

    for n, name in enumerate(("mixer_down", "mixer_up", "dense_down", "dense_up")):
        big_ref[n * adapt : (n + 1) * adapt, :] = sums[name].astype(BF16)
    for row in range(6):
        small_ref[row : row + 1, :] = column_sum(sums[row])
    lane = lax.broadcasted_iota(jnp.int32, (1, 128), 1)
    squares = jnp.zeros((1, 128), F32)
    for n, name in enumerate(("mixer_square", "dense_square", "input_square")):
        squares = jnp.where(lane == n, jnp.sum(column_sum(sums[name]), -1, keepdims=True), squares)
    small_ref[6:7, :] = jnp.concatenate(
        [column_sum(sums["mixer_mid"]), column_sum(sums["dense_mid"]), squares, jnp.zeros((1, features - 2 * adapt - 128), F32)], 1
    )
    small_ref[7:8, :] = jnp.zeros((1, features), F32)
    tail = tail_of(small_ref[...])
    share = 2 * adapt
    for pack_ref, which in ((mine_ref, lax.axis_index("mp")), (theirs_ref, 1 - lax.axis_index("mp"))):
        pack_ref[:share, :] = big_ref[aligned(which, share), :]
        pack_ref[share:, :] = tail
    for copy in copies:
        copy.wait()


def tail_of(vectors):
    high = vectors.astype(BF16)
    return jnp.concatenate([high, (vectors - high.astype(F32)).astype(BF16)], 0)


def vectors_of(tail):
    wide = tail.astype(F32)
    return wide[:8] + wide[8:]


def middle(x, keep, got, up, vectors, swapped, matrices):
    rows, features = x.shape
    adapt = matrices[0].shape[0]
    units = matrices[2].shape[1]
    packed = jax.ShapeDtypeStruct((2 * adapt + 16, features), BF16)
    return pl.pallas_call(
        middle_kernel,
        out_shape=(
            jax.ShapeDtypeStruct((rows, features), BF16),
            jax.ShapeDtypeStruct((rows, features), F32),
            jax.ShapeDtypeStruct((rows, features), BF16),
            packed,
            packed,
        ),
        in_specs=[VM] * 16 + [HB] * 6,
        out_specs=(HB,) + (VM,) * 4,
        scratch_shapes=[pltpu.VMEM(m.shape, BF16) for m in matrices]
        + [pltpu.VMEM((rows, 2 * units), BF16)]
        + [pltpu.VMEM((rows, features), F32)] * 4
        + [pltpu.VMEM((rows, features), BF16)] * 4
        + [
            pltpu.VMEM((4 * adapt, features), BF16),
            pltpu.VMEM((8, features), F32),
            pltpu.SemaphoreType.DMA((6,)),
            pltpu.SemaphoreType.DMA((2,)),
        ],
        compiler_params=pltpu.CompilerParams(vmem_limit_bytes=25 * MIB),
        cost_estimate=pl.CostEstimate(flops=2 * 10**10, bytes_accessed=16 * MIB, transcendentals=10**6),
        name="middle",
    )(x, keep, got, up, *vectors, *swapped, *map(in_hbm, matrices))


def spread_kernel(attended_ref, wo_ref, wo2_ref, own_ref, away_ref):
    attended = attended_ref[...]
    away_ref[...] = dot_nt(attended, wo2_ref[...]).astype(BF16)
    own_ref[...] = dot_nt(attended, wo_ref[...]).astype(BF16)


def spread(attended, wo, wo2):
    rows, width = attended.shape[0], wo.shape[0]
    return pl.pallas_call(
        spread_kernel,
        out_shape=(jax.ShapeDtypeStruct((rows, width), BF16),) * 2,
        in_specs=[VM] * 3,
        out_specs=(VM,) * 2,
        compiler_params=pltpu.CompilerParams(vmem_limit_bytes=8 * MIB),
        cost_estimate=pl.CostEstimate(flops=4 * rows * attended.shape[1] * width, bytes_accessed=3 * MIB, transcendentals=0),
        name="spread",
    )(attended, wo, wo2)


def combine_kernel(held_ref, got_ref, out_ref):
    rows = held_ref.shape[0] - 16
    out_ref[:rows, :] = (held_ref[:rows, :].astype(F32) + got_ref[:rows, :].astype(F32)).astype(BF16)
    out_ref[rows:, :] = tail_of(vectors_of(held_ref[rows:, :]) + vectors_of(got_ref[rows:, :]))


def combine(held, got):
    return pl.pallas_call(
        combine_kernel,
        out_shape=jax.ShapeDtypeStruct(held.shape, BF16),
        in_specs=[VM] * 2,
        out_specs=VM,
        compiler_params=pltpu.CompilerParams(vmem_limit_bytes=4 * MIB),
        cost_estimate=pl.CostEstimate(flops=10**5, bytes_accessed=MIB, transcendentals=0),
        name="combine",
    )(held, got)


def finish_kernel(
    held_ref, got_ref, home_ref, away_ref,
    input_hbm, md_ref, mdb_ref, mu_ref, mub_ref, dd_ref, ddb_ref, du_ref, dub_ref, fg_ref, fs_ref, sg_ref, ss_ref, ratio_ref,
    input_ref, sems,
):
    adapt = md_ref.shape[0]
    size = input_ref.shape[0] // 2
    copies = []
    for t in range(2):
        part = slice(t * size, (t + 1) * size)
        input_ref[part, :] = (home_ref[part, :] + away_ref[part, :].astype(F32)).astype(BF16)
        copies.append(pltpu.make_async_copy(input_ref.at[part, :], input_hbm.at[part, :], sems.at[t]))
        copies[-1].start()

    def write(first_ref, second_ref):
        md_ref[...] = first_ref[:adapt, :].astype(F32)
        mu_ref[...] = first_ref[adapt : 2 * adapt, :].astype(F32)
        dd_ref[...] = second_ref[:adapt, :].astype(F32)
        du_ref[...] = second_ref[adapt : 2 * adapt, :].astype(F32)
        vectors = vectors_of(first_ref[2 * adapt :, :])
        for row, out_ref in enumerate((mub_ref, dub_ref, fg_ref, fs_ref, sg_ref, ss_ref)):
            out_ref[...] = vectors[row, :]
        last = vectors[6:7, :]
        mdb_ref[...] = last[0, :adapt]
        ddb_ref[...] = last[0, adapt : 2 * adapt]
        squares = last[:, 2 * adapt : 2 * adapt + 128]
        lane = lax.broadcasted_iota(jnp.int32, (1, 128), 1)
        base = jnp.sum(jnp.where(lane == 2, squares, 0.0), -1, keepdims=True)
        ratio_ref[...] = jnp.sqrt(squares / base)[0, :2]

    @pl.when(lax.axis_index("mp") == 0)
    def _():
        write(held_ref, got_ref)

    @pl.when(lax.axis_index("mp") != 0)
    def _():
        write(got_ref, held_ref)

    for copy in copies:
        copy.wait()


def finish(held, got, home, away, adapt):
    features = held.shape[1]
    matrix = jax.ShapeDtypeStruct((adapt, features), F32)
    short, vector = jax.ShapeDtypeStruct((adapt,), F32), jax.ShapeDtypeStruct((features,), F32)
    return pl.pallas_call(
        finish_kernel,
        out_shape=(jax.ShapeDtypeStruct(away.shape, BF16),)
        + (matrix, short, matrix, vector) * 2
        + (vector,) * 4
        + (jax.ShapeDtypeStruct((2,), F32),),
        in_specs=[VM] * 4,
        out_specs=(HB,) + (VM,) * 13,
        scratch_shapes=[pltpu.VMEM(away.shape, BF16), pltpu.SemaphoreType.DMA((2,))],
        compiler_params=pltpu.CompilerParams(vmem_limit_bytes=8 * MIB),
        name="finish",
    )(held, got, home, away)


def swap_cores(value):
    return lax.ppermute(value, "mp", [(0, 1), (1, 0)])


def tie(*values):
    return lax.optimization_barrier(values)


def per_device(
    tokens, segment_ids, query_weight, key_weight, value_weight, output_weight, inner_weight, outer_weight,
    mixer_down, mixer_down_bias, mixer_up, mixer_up_bias, dense_down, dense_down_bias, dense_up, dense_up_bias,
    first_gain, first_shift, second_gain, second_shift, output_grad,
):
    devices = lax.axis_size("dp")
    adapt = mixer_down.shape[1]
    other_tokens = swap_cores(tokens)
    kv, queries, across, turned, item, hide, rng = project(
        segment_ids, tokens, query_weight, key_weight, value_weight
    )
    kv, other_tokens, output_late, inner_late, outer_late = tie(
        kv, other_tokens, output_weight, inner_weight, outer_weight
    )
    other_output = swap_cores(output_late)
    other_inner = swap_cores(inner_late)
    other_outer = swap_cores(outer_late)
    half = tokens.shape[0]
    written = (kv, queries, across, turned)
    kv, queries, across, turned, send, inverse2, *shares2 = attention_call(
        attention_kernel, "attention", written, half,
        (rng, other_tokens, item, hide, query_weight, key_weight, value_weight, *written),
    )
    got = swap_cores(send)
    keep, inverse, *shares = attention_call(
        own_attention_kernel, "own_attention", (), half, (rng, item, hide, kv, across, turned)
    )
    got, keep = tie(got, keep)
    vectors = (
        mixer_down_bias, mixer_up_bias, dense_down_bias, dense_up_bias, first_gain, first_shift, second_gain, second_shift,
    )
    swapped = (output_weight, other_output, other_inner, other_outer)
    matrices = (mixer_down.T, mixer_up, inner_weight, outer_weight, dense_down.T, dense_up)
    result, first_grad, attended, mine, theirs = middle(
        tokens, keep, got, output_grad, vectors, swapped, matrices
    )
    arriving = swap_cores(theirs)
    own_grad, away_grad = spread(attended, output_weight, other_output)
    arriving, own_grad = tie(arriving, own_grad)
    packed = combine(mine, arriving)
    away_grad, packed = tie(away_grad, packed)
    got_grad = swap_cores(away_grad)

    steps = []
    while 2 ** len(steps) < devices:
        steps.append(2 ** len(steps))
    steps.reverse()
    turn = len(steps) // 2
    pairs = len(shares)
    grads = []
    weights = (query_weight, key_weight, value_weight)
    for n, step in enumerate(steps):
        other_step = steps[(n + turn) % len(steps)]
        exchange = [(2 * i + c, 2 * (i ^ s) + c) for i in range(devices) for c, s in enumerate((step, other_step))]
        arriving = lax.ppermute(packed, ("dp", "mp"), exchange)
        if n < pairs:
            got_grad, packed = tie(got_grad, packed)
            parts = pair_grad(n, rng, kv, queries, keep, send, own_grad, got_grad, inverse, inverse2, shares[n], shares2[n])
            arriving, *parts = tie(arriving, *parts)
            grads.append(parts)
        elif n == pairs:
            pieces = [grads[p][i] for i in range(3) for p in range(pairs)]
            pieces[0], packed = tie(pieces[0], packed)
            away, home = input_parts(first_grad, pieces, weights)
            arriving, away, home = tie(arriving, away, home)
        packed = combine(packed, arriving)
    input_grad, md, mdb, mu, mub, dd, ddb, du, dub, *rest = finish(packed, swap_cores(packed), home, swap_cores(away), adapt)
    return (result, input_grad, md.T, mdb, mu, mub, dd.T, ddb, du, dub, *rest)


def solution(mesh):
    tokens = P(("dp", "mp"), None)
    columns, rows, whole = P(None, "mp"), P("mp", None), P()
    return jax.shard_map(
        per_device,
        mesh=mesh,
        in_specs=(tokens, P("dp", None), columns, columns, columns, rows, columns, rows) + (whole,) * 12 + (tokens,),
        out_specs=(tokens, tokens) + (whole,) * 13,
        check_vma=False,
    )
```

```python
import functools

import jax
import jax.numpy as jnp
from jax import lax
from jax.experimental import pallas as pl
from jax.experimental.pallas import tpu as pltpu
from jax.sharding import PartitionSpec as P

F32 = jnp.float32
BF16 = jnp.bfloat16
HEAD_DIM = 64
PAIR = 2 * HEAD_DIM
EPS = 1e-12
LOG2E = 1.4426950408889634
LN2 = 0.6931471805599453
ROOT_HALF = 0.7071067811865476
ROOT_TWO_PI = 0.3989422804014327
MASKED = -(2.0**100)
LARGEST = 2.0**100
SMALLEST = 2.0**-60
TURNED = 80
BLOCK = 256
STEP = 128
MIB = 1 << 20

VM = pl.BlockSpec(memory_space=pltpu.VMEM)
SM = pl.BlockSpec(memory_space=pltpu.SMEM)
HB = pl.BlockSpec(memory_space=pltpu.HBM)


def dot(left, right):
    return jnp.dot(left, right, preferred_element_type=F32)


def dot_nt(left, right):
    return lax.dot_general(left, right, (((1,), (1,)), ((), ())), preferred_element_type=F32)


def dot_tn(left, right):
    return lax.dot_general(left, right, (((0,), (0,)), ((), ())), preferred_element_type=F32)


def aligned(index, size):
    return pl.ds(pl.multiple_of(index * size, size), size)


def split_pair(pair):
    lane = lax.broadcasted_iota(jnp.int32, pair.shape, 1)
    zero = jnp.zeros_like(pair)
    return jnp.where(lane < HEAD_DIM, pair, zero), jnp.where(lane < HEAD_DIM, zero, pair)


def stack_heads(source, target, block):
    first, second = split_pair(source)
    for t in range(source.shape[0] // block):
        target[pl.ds(2 * t * block, block), :] = first[t * block : (t + 1) * block]
        target[pl.ds((2 * t + 1) * block, block), :] = second[t * block : (t + 1) * block]


def stack_heads_across(source, target, block):
    row = lax.broadcasted_iota(jnp.int32, source.shape, 0)
    zero = jnp.zeros_like(source)
    first = jnp.where(row < HEAD_DIM, source, zero)
    second = jnp.where(row < HEAD_DIM, zero, source)
    for t in range(source.shape[1] // block):
        target[:, 2 * t * block : (2 * t + 1) * block] = first[:, t * block : (t + 1) * block]
        target[:, (2 * t + 1) * block : (2 * t + 2) * block] = second[:, t * block : (t + 1) * block]


def in_hbm(value):
    return pltpu.with_memory_space_constraint(value, pltpu.HBM)


def start_all(sources, buffers, sems):
    copies = [pltpu.make_async_copy(src, dst, sems.at[i]) for i, (src, dst) in enumerate(zip(sources, buffers))]
    for copy in copies:
        copy.start()
    return copies


def write_projection(which, x, weights, copies, kv_ref, queries_ref, across_ref, turned_ref, between=None):
    rows, width = x.shape[0], weights[0].shape[1]
    pairs = width // PAIR
    if copies:
        copies[0].wait()
    queries = (dot(x, weights[0][...]) * (HEAD_DIM**-0.5 * LOG2E)).astype(BF16)
    if between is not None:
        between()
    for p in range(pairs):
        pair = queries[:, p * PAIR : (p + 1) * PAIR]
        stack_heads(pair, queries_ref.at[p, aligned(which, 2 * rows), :], BLOCK)
        stack_heads_across(pair.T, across_ref.at[p, :, aligned(which, 2 * rows)], BLOCK)
    if copies:
        copies[1].wait()
    kv_ref[aligned(which, rows), :width] = dot(x, weights[1][...]).astype(BF16)
    if copies:
        copies[2].wait()
    values = dot(x, weights[2][...]).astype(BF16)
    kv_ref[aligned(which, rows), width:] = values
    ones = jnp.ones((TURNED - HEAD_DIM, rows), BF16)
    for p in range(pairs):
        turned = values[:, p * PAIR : (p + 1) * PAIR].T
        for a in range(2):
            base = (2 * p + a) * TURNED
            turned_ref[base : base + HEAD_DIM, aligned(which, rows)] = turned[a * HEAD_DIM : (a + 1) * HEAD_DIM]
            turned_ref[base + HEAD_DIM : base + TURNED, aligned(which, rows)] = ones


def over_keys(low, high, visit):
    odd = (high - low) % 2

    def whole(t, c):
        visit(pl.ds(pl.multiple_of(low * STEP + t * BLOCK, STEP), BLOCK), BLOCK)
        return c

    lax.fori_loop(0, (high - low) // 2 - odd, whole, 0)

    @pl.when(odd == 1)
    def _():
        size = BLOCK + STEP
        visit(pl.ds(pl.multiple_of(high * STEP - size, STEP), size), size)


def over_keys_coarse(low, high, visit):
    steps = high - low
    doubles = jnp.where(steps % 4 == 0, steps // 4, (steps - 2) // 4)

    def double(t, c):
        visit(pl.ds(pl.multiple_of(low * STEP + t * 2 * BLOCK, STEP), 2 * BLOCK), 2 * BLOCK)
        return c

    lax.fori_loop(0, doubles, double, 0)
    start = low + 4 * doubles
    left = high - start

    @pl.when((left == 2) | (left == 5))
    def _():
        visit(pl.ds(pl.multiple_of(start * STEP, STEP), BLOCK), BLOCK)

    @pl.when((left == 3) | (left == 5))
    def _():
        size = BLOCK + STEP
        visit(pl.ds(pl.multiple_of(high * STEP - size, STEP), size), size)


def over_keys_fine(low, high, visit):
    def one(t, c):
        visit(pl.ds(pl.multiple_of((low + t) * STEP, STEP), STEP), STEP)
        return c

    lax.fori_loop(0, high - low, one, 0)


def is_shift(lane):
    return (lane == 63) | (lane == 95) | (lane == 127)


def project_kernel(
    seg_hbm, x_ref, wq_ref, wk_ref, wv_ref,
    kv_ref, queries_ref, across_ref, turned_ref, item_ref, hide_ref, rng_ref,
    seg_ref, x_buf, wq, wk, wv, sems,
):
    sources, buffers = (seg_hbm, x_ref, wq_ref, wk_ref, wv_ref), (seg_ref, x_buf, wq, wk, wv)
    seg_copy, *copies = start_all(sources, buffers, sems)
    count, block = kv_ref.shape[0], BLOCK

    def items():
        ids = seg_ref[...].astype(F32)
        position = lax.broadcasted_iota(jnp.int32, ids.shape, 1)
        for g in range(count // block):
            first, last = (
                jnp.sum(jnp.where(position == at, ids, 0.0), -1, keepdims=True) for at in (g * block, (g + 1) * block - 1)
            )
            rng_ref[0, g] = jnp.sum(jnp.where(ids < first, 1.0, 0.0)).astype(jnp.int32) // STEP
            rng_ref[1, g] = (jnp.sum(jnp.where(ids <= last, 1.0, 0.0)).astype(jnp.int32) + STEP - 1) // STEP
        lane = lax.broadcasted_iota(jnp.int32, (128, 128), 1)
        for t in range(count // 128):
            same = jnp.broadcast_to(ids[:, t * 128 : (t + 1) * 128], (128, 128)).T == lane.astype(F32)
            item_ref[t * 128 : (t + 1) * 128, :] = jnp.where(same | is_shift(lane), 1.0, 0.0).astype(BF16)
        row = lax.broadcasted_iota(jnp.int32, (128, block), 0)
        for t in range(count // block):
            same = row.astype(F32) == ids[:, t * block : (t + 1) * block]
            hide = jnp.where(same | is_shift(row), 0.0, MASKED).astype(BF16)
            for a in range(2):
                hide_ref[:, (2 * t + a) * block : (2 * t + a + 1) * block] = hide

    seg_copy.wait()
    copies[0].wait()
    write_projection(
        lax.axis_index("mp"), x_buf[...], (wq, wk, wv), copies[1:], kv_ref, queries_ref, across_ref, turned_ref, items
    )


def project(seg, x, wq, wk, wv):
    rows, width = x.shape[0], wq.shape[1]
    count, pairs = 2 * rows, width // PAIR
    return pl.pallas_call(
        project_kernel,
        out_shape=(
            jax.ShapeDtypeStruct((count, 2 * width), BF16),
            jax.ShapeDtypeStruct((pairs, 2 * count, PAIR), BF16),
            jax.ShapeDtypeStruct((pairs, PAIR, 2 * count), BF16),
            jax.ShapeDtypeStruct((2 * pairs * TURNED, count), BF16),
            jax.ShapeDtypeStruct((count, 128), BF16),
            jax.ShapeDtypeStruct((128, 2 * count), BF16),
            jax.ShapeDtypeStruct((2, count // BLOCK), jnp.int32),
        ),
        in_specs=[HB] * 5,
        out_specs=(VM,) * 6 + (SM,),
        scratch_shapes=[pltpu.VMEM(v.shape, v.dtype) for v in (seg, x, wq, wk, wv)] + [pltpu.SemaphoreType.DMA((5,))],
        compiler_params=pltpu.CompilerParams(vmem_limit_bytes=16 * MIB),
        cost_estimate=pl.CostEstimate(flops=2 * rows * x.shape[1] * 3 * width, bytes_accessed=5 * MIB, transcendentals=0),
        name="project",
    )(*map(in_hbm, (seg, x, wq, wk, wv)))


def attend_queries(which, rng_ref, item_ref, hide_ref, kv_ref, across, turned, out_ref, inverse_ref, share_refs, mix, shifted, peaks):
    pairs, block = len(share_refs), BLOCK
    per_half = out_ref.shape[0] // block

    def scores(p, span, both, hide):
        keys = jnp.concatenate([kv_ref[span, p * PAIR : (p + 1) * PAIR], item_ref[span, :]], 1)
        return dot(keys, jnp.concatenate([across[p, :, both], hide], 0))

    def query_block(i, carry):
        g = which * per_half + i
        both, here = aligned(g, 2 * block), aligned(i, 2 * block)
        low, high = rng_ref[0, g], rng_ref[1, g]

        def mix_all(hide_of, walk):
            mix[...] = jnp.zeros(mix.shape, F32)

            def visit(span, size):
                ahead = scores(0, span, both, hide_of(0))
                for p in range(pairs):
                    s = ahead
                    if p + 1 < pairs:
                        ahead = scores(p + 1, span, both, hide_of(p + 1))
                    e = jnp.exp2(s).astype(BF16)
                    share_refs[p][span, here] = e
                    for a in range(2):
                        head = slice((2 * p + a) * TURNED, (2 * p + a + 1) * TURNED)
                        mix[head, :] += dot(turned[head, span], e[:, a * block : (a + 1) * block])

            walk(low, high, visit)

        mix_all(lambda p: hide_ref[:, both], over_keys_coarse)
        total_rows = [h * TURNED + HEAD_DIM for h in range(2 * pairs)]
        sums = jnp.concatenate([mix[r : r + 8, :] for r in total_rows], 0)
        fine = jnp.where((sums <= LARGEST) & (sums >= SMALLEST), 0.0, 1.0)

        @pl.when(jnp.max(fine) > 0.0)
        def _():
            peaks[...] = jnp.full(peaks.shape, MASKED, F32)

            def visit(span, size):
                for p in range(pairs):
                    s = scores(p, span, both, hide_ref[:, both])
                    peaks[p] = jnp.maximum(peaks[p], jnp.max(s, 0, keepdims=True))

            over_keys_fine(low, high, visit)
            row = lax.broadcasted_iota(jnp.int32, (128, 2 * block), 0)
            hide = hide_ref[:, both].astype(F32)
            for p in range(pairs):
                peak = peaks[p]
                first = peak.astype(BF16).astype(F32)
                second = (peak - first).astype(BF16).astype(F32)
                third = peak - first - second
                parts = jnp.where(row < 64, first, jnp.where(row < 96, second, third))
                shifted[p] = jnp.where(is_shift(row), -parts, hide).astype(BF16)
            mix_all(lambda p: shifted[p], over_keys_fine)

        rows = aligned(i, block)
        outs = []
        for p in range(pairs):
            scales = []
            for a in range(2):
                base = (2 * p + a) * TURNED
                scale = jnp.broadcast_to(1.0 / mix[base + HEAD_DIM : base + HEAD_DIM + 1, :], (HEAD_DIM, block))
                outs.append((mix[base : base + HEAD_DIM, :] * scale).astype(BF16))
                scales.append(scale)
            inverse_ref[rows, p * PAIR : (p + 1) * PAIR] = jnp.concatenate(scales, 0).T
        out_ref[rows, :] = jnp.concatenate(outs, 0).T
        return carry

    lax.fori_loop(0, per_half, query_block, 0)


def attention_kernel(
    rng_ref, x_ref, item_ref, hide_ref, wq_ref, wk_ref, wv_ref, kv_in, queries_in, across_in, turned_in,
    kv_ref, queries_ref, across, turned, out_ref, inverse_ref, *rest,
):
    half = x_ref.shape[0]
    *share_refs, mix, shifted, peaks = rest
    here, there = lax.axis_index("mp"), 1 - lax.axis_index("mp")
    turned[:, aligned(here, half)] = turned_in[:, aligned(here, half)]
    across[:, :, aligned(here, 2 * half)] = across_in[:, :, aligned(here, 2 * half)]
    kv_ref[aligned(here, half), :] = kv_in[aligned(here, half), :]
    queries_ref[:, aligned(here, 2 * half), :] = queries_in[:, aligned(here, 2 * half), :]
    write_projection(there, x_ref[...], (wq_ref, wk_ref, wv_ref), (), kv_ref, queries_ref, across, turned)
    attend_queries(there, rng_ref, item_ref, hide_ref, kv_ref, across, turned, out_ref, inverse_ref, share_refs, mix, shifted, peaks)


def own_attention_kernel(rng_ref, item_ref, hide_ref, kv_ref, across, turned, out_ref, inverse_ref, *rest):
    *share_refs, mix, shifted, peaks = rest
    here = lax.axis_index("mp")
    attend_queries(here, rng_ref, item_ref, hide_ref, kv_ref, across, turned, out_ref, inverse_ref, share_refs, mix, shifted, peaks)


def attention_call(kernel, name, kept, half, operands):
    kv = operands[7] if kept else operands[3]
    count, width = kv.shape[0], kv.shape[1] // 2
    pairs = width // PAIR
    return pl.pallas_call(
        kernel,
        out_shape=tuple(jax.ShapeDtypeStruct(v.shape, v.dtype) for v in kept)
        + (jax.ShapeDtypeStruct((half, width), BF16), jax.ShapeDtypeStruct((half, width), F32))
        + (jax.ShapeDtypeStruct((count, 2 * half), BF16),) * pairs,
        in_specs=[SM] + [VM] * (len(operands) - 1),
        out_specs=(VM,) * (len(kept) + 2 + pairs),
        scratch_shapes=[
            pltpu.VMEM((2 * pairs * TURNED, BLOCK), F32),
            pltpu.VMEM((pairs, 128, 2 * BLOCK), BF16),
            pltpu.VMEM((pairs, 1, 2 * BLOCK), F32),
        ],
        compiler_params=pltpu.CompilerParams(vmem_limit_bytes=10 * MIB),
        cost_estimate=pl.CostEstimate(flops=5 * 10**9, bytes_accessed=8 * MIB, transcendentals=10**6),
        name=name,
    )(*operands)


def pair_grad_kernel(
    p, rng_ref, kv_ref, queries_ref, keep_ref, send_ref, own_ref, other_ref, inverse_ref, inverse2_ref, share_ref, share2_ref,
    dq_ref, dk_ref, dv_ref,
    grads, across, turned, delta, dq, dk, dv,
):
    half, width = keep_ref.shape
    count, block = kv_ref.shape[0], BLOCK
    cols = slice(p * PAIR, (p + 1) * PAIR)
    here, there = lax.axis_index("mp"), 1 - lax.axis_index("mp")
    row = lax.broadcasted_iota(jnp.int32, (8, PAIR), 0)
    column = lax.broadcasted_iota(jnp.int32, (8, PAIR), 1)
    pick = jnp.where(column // HEAD_DIM == row, 1.0, 0.0).astype(BF16)
    sides = ((here, keep_ref, own_ref, inverse_ref), (there, send_ref, other_ref, inverse2_ref))
    for which, mixed_ref, up_ref, scale_ref in sides:
        scaled = (up_ref[:, cols].astype(F32) * scale_ref[:, cols]).astype(BF16)
        product = mixed_ref[:, cols].astype(F32) * scaled.astype(F32)
        high = product.astype(BF16)
        low = (product - high.astype(F32)).astype(BF16)
        delta[:, aligned(which, half)] = dot_nt(pick, high) + dot_nt(pick, low)
        stack_heads(scaled, grads.at[aligned(which, 2 * half), :], block)
        stack_heads_across(scaled.T, across.at[:, aligned(which, 2 * half)], block)
    turned[...] = kv_ref[:, cols].T
    dk[...] = jnp.zeros(dk.shape, F32)
    dv[...] = jnp.zeros(dv.shape, F32)

    def query_block(which, shares_ref, i, carry):
        g = which * (half // block) + i
        rows, both = aligned(g, block), aligned(g, 2 * block)
        dq[...] = jnp.zeros(dq.shape, F32)
        level = jnp.concatenate([delta[0:1, rows], delta[1:2, rows]], 1)

        def visit(span, size):
            d = dot(kv_ref[span, width + p * PAIR : width + (p + 1) * PAIR], across[:, both])
            shares = shares_ref[span, aligned(i, 2 * block)]
            slopes = (shares.astype(F32) * (d - level)).astype(BF16)
            dv[span, :] += dot(shares, grads[both, :])
            dk[span, :] += dot(slopes, queries_ref[p, both, :])
            for a in range(2):
                head = slice(a * HEAD_DIM, (a + 1) * HEAD_DIM)
                dq[head, :] += dot(turned[head, span], slopes[:, a * block : (a + 1) * block])

        over_keys(rng_ref[0, g], rng_ref[1, g], visit)
        dq_ref[rows, :] = (dq[...] * HEAD_DIM**-0.5).astype(BF16).T
        return carry

    for which, shares_ref in ((here, share_ref), (there, share2_ref)):
        lax.fori_loop(0, half // block, functools.partial(query_block, which, shares_ref), 0)
    dk_ref[...] = (dk[...] * LN2).astype(BF16)
    dv_ref[...] = dv[...].astype(BF16)


def pair_grad(p, rng, kv, queries, keep, send, own, other, *per_half):
    count = kv.shape[0]
    return pl.pallas_call(
        functools.partial(pair_grad_kernel, p),
        out_shape=(jax.ShapeDtypeStruct((count, PAIR), BF16),) * 3,
        in_specs=[SM] + [VM] * 10,
        out_specs=(VM,) * 3,
        scratch_shapes=[
            pltpu.VMEM((2 * count, PAIR), BF16),
            pltpu.VMEM((PAIR, 2 * count), BF16),
            pltpu.VMEM((PAIR, count), BF16),
            pltpu.VMEM((8, count), F32),
            pltpu.VMEM((PAIR, BLOCK), F32),
            pltpu.VMEM((count, PAIR), F32),
            pltpu.VMEM((count, PAIR), F32),
        ],
        compiler_params=pltpu.CompilerParams(vmem_limit_bytes=12 * MIB),
        cost_estimate=pl.CostEstimate(flops=4 * 10**9, bytes_accessed=8 * MIB, transcendentals=0),
        name=f"pair_grad_{p}",
    )(rng, kv, queries, keep, send, own, other, *per_half)


def input_kernel(first_ref, *refs):
    *pieces, wq_ref, wk_ref, wv_ref, away_ref, home_ref = refs
    half = home_ref.shape[0]
    right = jnp.concatenate([wq_ref[...], wk_ref[...], wv_ref[...]], 1)

    def part(which):
        rows = aligned(which, half)
        return dot_nt(jnp.concatenate([piece[rows, :] for piece in pieces], 1), right)

    away_ref[...] = part(1 - lax.axis_index("mp")).astype(BF16)
    home_ref[...] = part(lax.axis_index("mp")) + first_ref[...]


def input_parts(first_grad, pieces, weights):
    half, features = first_grad.shape
    return pl.pallas_call(
        input_kernel,
        out_shape=(jax.ShapeDtypeStruct((half, features), BF16), jax.ShapeDtypeStruct((half, features), F32)),
        in_specs=[VM] * (1 + len(pieces) + len(weights)),
        out_specs=(VM,) * 2,
        compiler_params=pltpu.CompilerParams(vmem_limit_bytes=16 * MIB),
        cost_estimate=pl.CostEstimate(flops=2 * 10**9, bytes_accessed=8 * MIB, transcendentals=0),
        name="input_parts",
    )(first_grad, *pieces, *weights)


def gelu_both(v):
    part = 0.5 + 0.5 * lax.erf(v * ROOT_HALF)
    return v * part, part + v * jnp.exp(-0.5 * v * v) * ROOT_TWO_PI


def norm(values, gain, shift):
    mean = jnp.mean(values, -1, keepdims=True)
    centred = values - mean
    reciprocal = lax.rsqrt(jnp.mean(centred * centred, -1, keepdims=True) + EPS)
    normed = centred * reciprocal
    return normed * gain + shift, normed, reciprocal


def norm_grad(upstream, normed, reciprocal, gain):
    scaled = upstream * gain
    return reciprocal * (
        scaled - jnp.mean(scaled, -1, keepdims=True) - normed * jnp.mean(scaled * normed, -1, keepdims=True)
    )


def column_sum(values):
    return jnp.sum(values, 0, keepdims=True)


def eight_rows(values):
    return jnp.sum(values.reshape(-1, 8, values.shape[1]), 0)


def interleave(first, second):
    done = 0
    for i, step in enumerate(first):
        step()
        while done < len(second) and (done + 1) * len(first) <= (i + 1) * len(second):
            second[done]()
            done += 1
    for step in second[done:]:
        step()


def middle_kernel(
    x_ref, keep_ref, got_ref, up_ref,
    mdb_ref, mub_ref, ddb_ref, dub_ref, fg_ref, fs_ref, sg_ref, ss_ref,
    wo_ref, wo2_ref, w12_ref, w22_ref, md_hbm, mu_hbm, w1_hbm, w2_hbm, dd_hbm, du_hbm,
    act_hbm, first_ref, attended_ref, mine_ref, theirs_ref,
    md_ref, mu_ref, w1_ref, w2_ref, dd_ref, du_ref,
    slope_ref, wide_ref, out_ref, hidden_ref, normed_ref, low_ref, hidden_low_ref, act_ref, top_ref,
    big_ref, small_ref, sems, act_sem,
):
    rows, features = x_ref.shape
    adapt = md_ref.shape[0]
    names = ("md", "mu", "w1", "w2", "dd", "du")
    waits = dict(
        zip(
            names,
            start_all(
                (md_hbm, mu_hbm, w1_hbm, w2_hbm, dd_hbm, du_hbm),
                (md_ref, mu_ref, w1_ref, w2_ref, dd_ref, du_ref),
                sems,
            ),
        )
    )
    waited = set()

    def need(*wanted):
        for name in wanted:
            if name not in waited:
                waited.add(name)
                waits[name].wait()

    def vector(ref):
        return ref[...].astype(F32).reshape(1, -1)

    units = w1_ref.shape[1]
    chunk, piece_rows = 512, 64
    sides = ((w1_ref, w2_ref, ("w1", "w2")), (w12_ref, w22_ref, ()))
    pieces = [(side, slice(c * chunk, (c + 1) * chunk)) for side in sides for c in range(units // chunk)]
    kept = {}
    sums = {}

    def add(name, value):
        sums[name] = sums[name] + value if name in sums else value

    def parts(half):
        return [slice(r, r + piece_rows) for r in range(half.start, half.stop, piece_rows)]

    def attend(half):
        def first():
            attended = dot(keep_ref[half, :], wo_ref[...]) + dot(got_ref[half, :], wo2_ref[...])
            wide_ref[half, :] = attended
            low_ref[half, :] = attended.astype(BF16)

        def second():
            need("md", "mu")
            active, slope = gelu_both(dot_nt(low_ref[half, :], md_ref[...]) + vector(mdb_ref))
            kept["mixer", half.start] = (active.astype(BF16), slope)

        def third():
            out_ref[half, :] = dot(kept["mixer", half.start][0], mu_ref[...]) + vector(mub_ref)

        return [first, second, third]

    def norm_one(half):
        def one(part):
            x, mixer_out = x_ref[part, :].astype(F32), out_ref[part, :]
            add("mixer_square", eight_rows(mixer_out * mixer_out))
            add("input_square", eight_rows(x * x))
            hidden, normed, reciprocal = norm(x + wide_ref[part, :] + mixer_out, vector(fg_ref), vector(fs_ref))
            normed_ref[part, :] = normed
            hidden_ref[part, :] = hidden
            hidden_low_ref[part, :] = hidden.astype(BF16)
            kept["reciprocal", part.start] = reciprocal

        return [functools.partial(one, part) for part in parts(half)]

    def feed_forward(half):
        state = {}

        def start():
            need("w1", "w2")
            side, span = pieces[0]
            state["ahead"] = dot(hidden_low_ref[half, :], side[0][:, span])

        def one(n):
            side, span = pieces[n]
            inner = state["ahead"]
            if n + 1 < len(pieces):
                after, after_span = pieces[n + 1]
                state["ahead"] = dot(hidden_low_ref[half, :], after[0][:, after_span])
            value, slope = gelu_both(inner)
            slope_ref[half, n * chunk : (n + 1) * chunk] = slope.astype(BF16)
            state["value"] = value.astype(BF16)

        def two(n):
            side, span = pieces[n]
            total = dot(state["value"], side[1][span, :])
            state["total"] = state["total"] + total if n else total
            if n + 1 == len(pieces):
                wide_ref[half, :] = state["total"]

        steps = [start]
        for n in range(len(pieces)):
            steps += [functools.partial(one, n), functools.partial(two, n)]
        return steps

    def dense(half):
        def first():
            need("dd", "du")
            dense_low = wide_ref[half, :].astype(BF16)
            active, slope = gelu_both(dot_nt(dense_low, dd_ref[...]) + vector(ddb_ref))
            kept["dense", half.start] = (active.astype(BF16), slope, dense_low)

        def second():
            out_ref[half, :] = dot(kept["dense", half.start][0], du_ref[...]) + vector(dub_ref)

        return [first, second]

    def norm_two(half):
        def one(part):
            dense_out = out_ref[part, :]
            add("dense_square", eight_rows(dense_out * dense_out))
            gain = vector(sg_ref)
            result, normed, reciprocal = norm(hidden_ref[part, :] + wide_ref[part, :] + dense_out, gain, vector(ss_ref))
            act_ref[part, :] = result.astype(BF16)
            upstream = up_ref[part, :].astype(F32)
            add(4, eight_rows(upstream * normed))
            add(5, eight_rows(upstream))
            second_grad = norm_grad(upstream, normed, reciprocal, gain)
            hidden_ref[part, :] = second_grad
            top = second_grad.astype(BF16)
            top_ref[part, :] = top
            add(1, eight_rows(top.astype(F32)))

        return [functools.partial(one, part) for part in parts(half)]

    def dense_back(half):
        def first():
            active, slope, dense_low = kept["dense", half.start]
            top = top_ref[half, :]
            add("dense_up", dot_tn(active, top))
            mid = (dot_nt(top, du_ref[...]) * slope).astype(BF16)
            kept["dense_mid", half.start] = mid
            add("dense_mid", eight_rows(mid.astype(F32)))

        def second():
            mid = kept["dense_mid", half.start]
            add("dense_down", dot_tn(mid, kept["dense", half.start][2]))
            hidden_low_ref[half, :] = (hidden_ref[half, :] + dot(mid, dd_ref[...])).astype(BF16)

        return [first, second]

    def feed_back(half):
        state = {}

        def start():
            side, span = pieces[0]
            state["ahead"] = dot_nt(hidden_low_ref[half, :], side[1][span, :])

        def one(n):
            back = state["ahead"]
            if n + 1 < len(pieces):
                after, after_span = pieces[n + 1]
                state["ahead"] = dot_nt(hidden_low_ref[half, :], after[1][after_span, :])
            slope = slope_ref[half, n * chunk : (n + 1) * chunk].astype(F32)
            state["value"] = (back * slope).astype(BF16)

        def two(n):
            side, span = pieces[n]
            total = dot_nt(state["value"], side[0][:, span])
            state["total"] = state["total"] + total if n else total
            if n + 1 == len(pieces):
                hidden_ref[half, :] = hidden_ref[half, :] + state["total"]

        steps = [start]
        for n in range(len(pieces)):
            steps += [functools.partial(one, n), functools.partial(two, n)]
        return steps

    def norm_one_back(half):
        def one(part):
            hidden_grad, normed = hidden_ref[part, :], normed_ref[part, :]
            add(2, eight_rows(hidden_grad * normed))
            add(3, eight_rows(hidden_grad))
            first_grad = norm_grad(hidden_grad, normed, kept["reciprocal", part.start], vector(fg_ref))
            first_ref[part, :] = first_grad
            top = first_grad.astype(BF16)
            top_ref[part, :] = top
            add(0, eight_rows(top.astype(F32)))

        return [functools.partial(one, part) for part in parts(half)]

    def attend_back(half):
        def first():
            active, slope = kept["mixer", half.start]
            top = top_ref[half, :]
            add("mixer_up", dot_tn(active, top))
            mid = (dot_nt(top, mu_ref[...]) * slope).astype(BF16)
            kept["mixer_mid", half.start] = mid
            add("mixer_mid", eight_rows(mid.astype(F32)))

        def second():
            mid = kept["mixer_mid", half.start]
            add("mixer_down", dot_tn(mid, low_ref[half, :]))
            attended_ref[half, :] = (first_ref[half, :] + dot(mid, md_ref[...])).astype(BF16)

        return [first, second]

    def send_result(half, index):
        copy = pltpu.make_async_copy(act_ref.at[half, :], act_hbm.at[half, :], act_sem.at[index])
        copy.start()
        return copy

    one, two = slice(0, rows // 2), slice(rows // 2, rows)
    interleave(attend(one), [])
    interleave(norm_one(one), attend(two))
    interleave(feed_forward(one), norm_one(two))
    interleave(feed_forward(two), dense(one) + norm_two(one) + dense_back(one))
    copies = [send_result(one, 0)]
    interleave(feed_back(one), dense(two) + norm_two(two) + dense_back(two))
    copies.append(send_result(two, 1))
    interleave(feed_back(two), norm_one_back(one) + attend_back(one))
    interleave(norm_one_back(two), [])
    interleave(attend_back(two), [])

    for n, name in enumerate(("mixer_down", "mixer_up", "dense_down", "dense_up")):
        big_ref[n * adapt : (n + 1) * adapt, :] = sums[name].astype(BF16)
    for row in range(6):
        small_ref[row : row + 1, :] = column_sum(sums[row])
    lane = lax.broadcasted_iota(jnp.int32, (1, 128), 1)
    squares = jnp.zeros((1, 128), F32)
    for n, name in enumerate(("mixer_square", "dense_square", "input_square")):
        squares = jnp.where(lane == n, jnp.sum(column_sum(sums[name]), -1, keepdims=True), squares)
    small_ref[6:7, :] = jnp.concatenate(
        [column_sum(sums["mixer_mid"]), column_sum(sums["dense_mid"]), squares, jnp.zeros((1, features - 2 * adapt - 128), F32)], 1
    )
    small_ref[7:8, :] = jnp.zeros((1, features), F32)
    tail = tail_of(small_ref[...])
    share = 2 * adapt
    for pack_ref, which in ((mine_ref, lax.axis_index("mp")), (theirs_ref, 1 - lax.axis_index("mp"))):
        pack_ref[:share, :] = big_ref[aligned(which, share), :]
        pack_ref[share:, :] = tail
    for copy in copies:
        copy.wait()


def tail_of(vectors):
    high = vectors.astype(BF16)
    return jnp.concatenate([high, (vectors - high.astype(F32)).astype(BF16)], 0)


def vectors_of(tail):
    wide = tail.astype(F32)
    return wide[:8] + wide[8:]


def middle(x, keep, got, up, vectors, swapped, matrices):
    rows, features = x.shape
    adapt = matrices[0].shape[0]
    units = matrices[2].shape[1]
    packed = jax.ShapeDtypeStruct((2 * adapt + 16, features), BF16)
    return pl.pallas_call(
        middle_kernel,
        out_shape=(
            jax.ShapeDtypeStruct((rows, features), BF16),
            jax.ShapeDtypeStruct((rows, features), F32),
            jax.ShapeDtypeStruct((rows, features), BF16),
            packed,
            packed,
        ),
        in_specs=[VM] * 16 + [HB] * 6,
        out_specs=(HB,) + (VM,) * 4,
        scratch_shapes=[pltpu.VMEM(m.shape, BF16) for m in matrices]
        + [pltpu.VMEM((rows, 2 * units), BF16)]
        + [pltpu.VMEM((rows, features), F32)] * 4
        + [pltpu.VMEM((rows, features), BF16)] * 4
        + [
            pltpu.VMEM((4 * adapt, features), BF16),
            pltpu.VMEM((8, features), F32),
            pltpu.SemaphoreType.DMA((6,)),
            pltpu.SemaphoreType.DMA((2,)),
        ],
        compiler_params=pltpu.CompilerParams(vmem_limit_bytes=25 * MIB),
        cost_estimate=pl.CostEstimate(flops=2 * 10**10, bytes_accessed=16 * MIB, transcendentals=10**6),
        name="middle",
    )(x, keep, got, up, *vectors, *swapped, *map(in_hbm, matrices))


def spread_kernel(attended_ref, wo_ref, wo2_ref, own_ref, away_ref):
    attended = attended_ref[...]
    away_ref[...] = dot_nt(attended, wo2_ref[...]).astype(BF16)
    own_ref[...] = dot_nt(attended, wo_ref[...]).astype(BF16)


def spread(attended, wo, wo2):
    rows, width = attended.shape[0], wo.shape[0]
    return pl.pallas_call(
        spread_kernel,
        out_shape=(jax.ShapeDtypeStruct((rows, width), BF16),) * 2,
        in_specs=[VM] * 3,
        out_specs=(VM,) * 2,
        compiler_params=pltpu.CompilerParams(vmem_limit_bytes=8 * MIB),
        cost_estimate=pl.CostEstimate(flops=4 * rows * attended.shape[1] * width, bytes_accessed=3 * MIB, transcendentals=0),
        name="spread",
    )(attended, wo, wo2)


def combine_kernel(held_ref, got_ref, out_ref):
    rows = held_ref.shape[0] - 16
    out_ref[:rows, :] = (held_ref[:rows, :].astype(F32) + got_ref[:rows, :].astype(F32)).astype(BF16)
    out_ref[rows:, :] = tail_of(vectors_of(held_ref[rows:, :]) + vectors_of(got_ref[rows:, :]))


def combine(held, got):
    return pl.pallas_call(
        combine_kernel,
        out_shape=jax.ShapeDtypeStruct(held.shape, BF16),
        in_specs=[VM] * 2,
        out_specs=VM,
        compiler_params=pltpu.CompilerParams(vmem_limit_bytes=4 * MIB),
        cost_estimate=pl.CostEstimate(flops=10**5, bytes_accessed=MIB, transcendentals=0),
        name="combine",
    )(held, got)


def finish_kernel(
    held_ref, got_ref, home_ref, away_ref,
    input_hbm, md_ref, mdb_ref, mu_ref, mub_ref, dd_ref, ddb_ref, du_ref, dub_ref, fg_ref, fs_ref, sg_ref, ss_ref, ratio_ref,
    input_ref, sems,
):
    adapt = md_ref.shape[0]
    size = input_ref.shape[0] // 2
    copies = []
    for t in range(2):
        part = slice(t * size, (t + 1) * size)
        input_ref[part, :] = (home_ref[part, :] + away_ref[part, :].astype(F32)).astype(BF16)
        copies.append(pltpu.make_async_copy(input_ref.at[part, :], input_hbm.at[part, :], sems.at[t]))
        copies[-1].start()

    def write(first_ref, second_ref):
        md_ref[...] = first_ref[:adapt, :].astype(F32)
        mu_ref[...] = first_ref[adapt : 2 * adapt, :].astype(F32)
        dd_ref[...] = second_ref[:adapt, :].astype(F32)
        du_ref[...] = second_ref[adapt : 2 * adapt, :].astype(F32)
        vectors = vectors_of(first_ref[2 * adapt :, :])
        for row, out_ref in enumerate((mub_ref, dub_ref, fg_ref, fs_ref, sg_ref, ss_ref)):
            out_ref[...] = vectors[row, :]
        last = vectors[6:7, :]
        mdb_ref[...] = last[0, :adapt]
        ddb_ref[...] = last[0, adapt : 2 * adapt]
        squares = last[:, 2 * adapt : 2 * adapt + 128]
        lane = lax.broadcasted_iota(jnp.int32, (1, 128), 1)
        base = jnp.sum(jnp.where(lane == 2, squares, 0.0), -1, keepdims=True)
        ratio_ref[...] = jnp.sqrt(squares / base)[0, :2]

    @pl.when(lax.axis_index("mp") == 0)
    def _():
        write(held_ref, got_ref)

    @pl.when(lax.axis_index("mp") != 0)
    def _():
        write(got_ref, held_ref)

    for copy in copies:
        copy.wait()


def finish(held, got, home, away, adapt):
    features = held.shape[1]
    matrix = jax.ShapeDtypeStruct((adapt, features), F32)
    short, vector = jax.ShapeDtypeStruct((adapt,), F32), jax.ShapeDtypeStruct((features,), F32)
    return pl.pallas_call(
        finish_kernel,
        out_shape=(jax.ShapeDtypeStruct(away.shape, BF16),)
        + (matrix, short, matrix, vector) * 2
        + (vector,) * 4
        + (jax.ShapeDtypeStruct((2,), F32),),
        in_specs=[VM] * 4,
        out_specs=(HB,) + (VM,) * 13,
        scratch_shapes=[pltpu.VMEM(away.shape, BF16), pltpu.SemaphoreType.DMA((2,))],
        compiler_params=pltpu.CompilerParams(vmem_limit_bytes=8 * MIB),
        name="finish",
    )(held, got, home, away)


def swap_cores(value):
    return lax.ppermute(value, "mp", [(0, 1), (1, 0)])


def tie(*values):
    return lax.optimization_barrier(values)


def per_device(
    tokens, segment_ids, query_weight, key_weight, value_weight, output_weight, inner_weight, outer_weight,
    mixer_down, mixer_down_bias, mixer_up, mixer_up_bias, dense_down, dense_down_bias, dense_up, dense_up_bias,
    first_gain, first_shift, second_gain, second_shift, output_grad,
):
    devices = lax.axis_size("dp")
    adapt = mixer_down.shape[1]
    other_tokens = swap_cores(tokens)
    kv, queries, across, turned, item, hide, rng = project(
        segment_ids, tokens, query_weight, key_weight, value_weight
    )
    kv, other_tokens, output_late, inner_late, outer_late = tie(
        kv, other_tokens, output_weight, inner_weight, outer_weight
    )
    other_output = swap_cores(output_late)
    other_inner = swap_cores(inner_late)
    other_outer = swap_cores(outer_late)
    half = tokens.shape[0]
    written = (kv, queries, across, turned)
    kv, queries, across, turned, send, inverse2, *shares2 = attention_call(
        attention_kernel, "attention", written, half,
        (rng, other_tokens, item, hide, query_weight, key_weight, value_weight, *written),
    )
    got = swap_cores(send)
    keep, inverse, *shares = attention_call(
        own_attention_kernel, "own_attention", (), half, (rng, item, hide, kv, across, turned)
    )
    got, keep = tie(got, keep)
    vectors = (
        mixer_down_bias, mixer_up_bias, dense_down_bias, dense_up_bias, first_gain, first_shift, second_gain, second_shift,
    )
    swapped = (output_weight, other_output, other_inner, other_outer)
    matrices = (mixer_down.T, mixer_up, inner_weight, outer_weight, dense_down.T, dense_up)
    result, first_grad, attended, mine, theirs = middle(
        tokens, keep, got, output_grad, vectors, swapped, matrices
    )
    arriving = swap_cores(theirs)
    own_grad, away_grad = spread(attended, output_weight, other_output)
    arriving, own_grad = tie(arriving, own_grad)
    packed = combine(mine, arriving)
    away_grad, packed = tie(away_grad, packed)
    got_grad = swap_cores(away_grad)

    steps = []
    while 2 ** len(steps) < devices:
        steps.append(2 ** len(steps))
    steps.reverse()
    turn = len(steps) // 2
    pairs = len(shares)
    grads = []
    weights = (query_weight, key_weight, value_weight)
    for n, step in enumerate(steps):
        other_step = steps[(n + turn) % len(steps)]
        exchange = [(2 * i + c, 2 * (i ^ s) + c) for i in range(devices) for c, s in enumerate((step, other_step))]
        arriving = lax.ppermute(packed, ("dp", "mp"), exchange)
        if n < pairs:
            got_grad, packed = tie(got_grad, packed)
            parts = pair_grad(n, rng, kv, queries, keep, send, own_grad, got_grad, inverse, inverse2, shares[n], shares2[n])
            arriving, *parts = tie(arriving, *parts)
            grads.append(parts)
        elif n == pairs:
            pieces = [grads[p][i] for i in range(3) for p in range(pairs)]
            pieces[0], packed = tie(pieces[0], packed)
            away, home = input_parts(first_grad, pieces, weights)
            arriving, away, home = tie(arriving, away, home)
        packed = combine(packed, arriving)
    input_grad, md, mdb, mu, mub, dd, ddb, du, dub, *rest = finish(packed, swap_cores(packed), home, swap_cores(away), adapt)
    return (result, input_grad, md.T, mdb, mu, mub, dd.T, ddb, du, dub, *rest)


def solution(mesh):
    tokens = P(("dp", "mp"), None)
    columns, rows, whole = P(None, "mp"), P("mp", None), P()
    return jax.shard_map(
        per_device,
        mesh=mesh,
        in_specs=(tokens, P("dp", None), columns, columns, columns, rows, columns, rows) + (whole,) * 12 + (tokens,),
        out_specs=(tokens, tokens) + (whole,) * 13,
        check_vma=False,
    )
```

```python
import functools

import jax
import jax.numpy as jnp
from jax import lax
from jax.experimental import pallas as pl
from jax.experimental.pallas import tpu as pltpu
from jax.sharding import PartitionSpec as P

F32 = jnp.float32
BF16 = jnp.bfloat16
HEAD_DIM = 64
PAIR = 2 * HEAD_DIM
EPS = 1e-12
LOG2E = 1.4426950408889634
LN2 = 0.6931471805599453
ROOT_HALF = 0.7071067811865476
ROOT_TWO_PI = 0.3989422804014327
MASKED = -(2.0**100)
LARGEST = 2.0**100
SMALLEST = 2.0**-60
TURNED = 80
BLOCK = 256
STEP = 128
MIB = 1 << 20

VM = pl.BlockSpec(memory_space=pltpu.VMEM)
SM = pl.BlockSpec(memory_space=pltpu.SMEM)
HB = pl.BlockSpec(memory_space=pltpu.HBM)


def dot(left, right):
    return jnp.dot(left, right, preferred_element_type=F32)


def dot_nt(left, right):
    return lax.dot_general(left, right, (((1,), (1,)), ((), ())), preferred_element_type=F32)


def dot_tn(left, right):
    return lax.dot_general(left, right, (((0,), (0,)), ((), ())), preferred_element_type=F32)


def aligned(index, size):
    return pl.ds(pl.multiple_of(index * size, size), size)


def split_pair(pair):
    lane = lax.broadcasted_iota(jnp.int32, pair.shape, 1)
    zero = jnp.zeros_like(pair)
    return jnp.where(lane < HEAD_DIM, pair, zero), jnp.where(lane < HEAD_DIM, zero, pair)


def stack_heads(source, target, block):
    first, second = split_pair(source)
    for t in range(source.shape[0] // block):
        target[pl.ds(2 * t * block, block), :] = first[t * block : (t + 1) * block]
        target[pl.ds((2 * t + 1) * block, block), :] = second[t * block : (t + 1) * block]


def stack_heads_across(source, target, block):
    row = lax.broadcasted_iota(jnp.int32, source.shape, 0)
    zero = jnp.zeros_like(source)
    first = jnp.where(row < HEAD_DIM, source, zero)
    second = jnp.where(row < HEAD_DIM, zero, source)
    for t in range(source.shape[1] // block):
        target[:, 2 * t * block : (2 * t + 1) * block] = first[:, t * block : (t + 1) * block]
        target[:, (2 * t + 1) * block : (2 * t + 2) * block] = second[:, t * block : (t + 1) * block]


def in_hbm(value):
    return pltpu.with_memory_space_constraint(value, pltpu.HBM)


def start_all(sources, buffers, sems):
    copies = [pltpu.make_async_copy(src, dst, sems.at[i]) for i, (src, dst) in enumerate(zip(sources, buffers))]
    for copy in copies:
        copy.start()
    return copies


def write_projection(which, x, weights, copies, kv_ref, queries_ref, across_ref, turned_ref, between=None):
    rows, width = x.shape[0], weights[0].shape[1]
    pairs = width // PAIR
    if copies:
        copies[0].wait()
    queries = (dot(x, weights[0][...]) * (HEAD_DIM**-0.5 * LOG2E)).astype(BF16)
    if between is not None:
        between()
    for p in range(pairs):
        pair = queries[:, p * PAIR : (p + 1) * PAIR]
        stack_heads(pair, queries_ref.at[p, aligned(which, 2 * rows), :], BLOCK)
        stack_heads_across(pair.T, across_ref.at[p, :, aligned(which, 2 * rows)], BLOCK)
    if copies:
        copies[1].wait()
    kv_ref[aligned(which, rows), :width] = dot(x, weights[1][...]).astype(BF16)
    if copies:
        copies[2].wait()
    values = dot(x, weights[2][...]).astype(BF16)
    kv_ref[aligned(which, rows), width:] = values
    ones = jnp.ones((TURNED - HEAD_DIM, rows), BF16)
    for p in range(pairs):
        turned = values[:, p * PAIR : (p + 1) * PAIR].T
        for a in range(2):
            base = (2 * p + a) * TURNED
            turned_ref[base : base + HEAD_DIM, aligned(which, rows)] = turned[a * HEAD_DIM : (a + 1) * HEAD_DIM]
            turned_ref[base + HEAD_DIM : base + TURNED, aligned(which, rows)] = ones


def over_keys_coarse(low, high, visit):
    steps = high - low
    doubles = jnp.where(steps % 4 == 0, steps // 4, (steps - 2) // 4)

    def double(t, c):
        visit(pl.ds(pl.multiple_of(low * STEP + t * 2 * BLOCK, STEP), 2 * BLOCK), 2 * BLOCK)
        return c

    lax.fori_loop(0, doubles, double, 0)
    start = low + 4 * doubles
    left = high - start

    @pl.when((left == 2) | (left == 5))
    def _():
        visit(pl.ds(pl.multiple_of(start * STEP, STEP), BLOCK), BLOCK)

    @pl.when((left == 3) | (left == 5))
    def _():
        size = BLOCK + STEP
        visit(pl.ds(pl.multiple_of(high * STEP - size, STEP), size), size)


def over_keys_fine(low, high, visit):
    def one(t, c):
        visit(pl.ds(pl.multiple_of((low + t) * STEP, STEP), STEP), STEP)
        return c

    lax.fori_loop(0, high - low, one, 0)


def is_shift(lane):
    return (lane == 63) | (lane == 95) | (lane == 127)


def project_kernel(
    seg_hbm, x_ref, wq_ref, wk_ref, wv_ref,
    kv_ref, queries_ref, across_ref, turned_ref, item_ref, hide_ref, rng_ref,
    seg_ref, x_buf, wq, wk, wv, sems,
):
    sources, buffers = (seg_hbm, x_ref, wq_ref, wk_ref, wv_ref), (seg_ref, x_buf, wq, wk, wv)
    seg_copy, *copies = start_all(sources, buffers, sems)
    count, block = kv_ref.shape[0], BLOCK

    def items():
        ids = seg_ref[...].astype(F32)
        position = lax.broadcasted_iota(jnp.int32, ids.shape, 1)
        for g in range(count // block):
            first, last = (
                jnp.sum(jnp.where(position == at, ids, 0.0), -1, keepdims=True) for at in (g * block, (g + 1) * block - 1)
            )
            rng_ref[0, g] = jnp.sum(jnp.where(ids < first, 1.0, 0.0)).astype(jnp.int32) // STEP
            rng_ref[1, g] = (jnp.sum(jnp.where(ids <= last, 1.0, 0.0)).astype(jnp.int32) + STEP - 1) // STEP
        lane = lax.broadcasted_iota(jnp.int32, (128, 128), 1)
        for t in range(count // 128):
            same = jnp.broadcast_to(ids[:, t * 128 : (t + 1) * 128], (128, 128)).T == lane.astype(F32)
            item_ref[t * 128 : (t + 1) * 128, :] = jnp.where(same | is_shift(lane), 1.0, 0.0).astype(BF16)
        row = lax.broadcasted_iota(jnp.int32, (128, block), 0)
        for t in range(count // block):
            same = row.astype(F32) == ids[:, t * block : (t + 1) * block]
            hide = jnp.where(same | is_shift(row), 0.0, MASKED).astype(BF16)
            for a in range(2):
                hide_ref[:, (2 * t + a) * block : (2 * t + a + 1) * block] = hide

    seg_copy.wait()
    copies[0].wait()
    write_projection(
        lax.axis_index("mp"), x_buf[...], (wq, wk, wv), copies[1:], kv_ref, queries_ref, across_ref, turned_ref, items
    )


def project(seg, x, wq, wk, wv):
    rows, width = x.shape[0], wq.shape[1]
    count, pairs = 2 * rows, width // PAIR
    return pl.pallas_call(
        project_kernel,
        out_shape=(
            jax.ShapeDtypeStruct((count, 2 * width), BF16),
            jax.ShapeDtypeStruct((pairs, 2 * count, PAIR), BF16),
            jax.ShapeDtypeStruct((pairs, PAIR, 2 * count), BF16),
            jax.ShapeDtypeStruct((2 * pairs * TURNED, count), BF16),
            jax.ShapeDtypeStruct((count, 128), BF16),
            jax.ShapeDtypeStruct((128, 2 * count), BF16),
            jax.ShapeDtypeStruct((2, count // BLOCK), jnp.int32),
        ),
        in_specs=[HB] * 5,
        out_specs=(VM,) * 6 + (SM,),
        scratch_shapes=[pltpu.VMEM(v.shape, v.dtype) for v in (seg, x, wq, wk, wv)] + [pltpu.SemaphoreType.DMA((5,))],
        compiler_params=pltpu.CompilerParams(vmem_limit_bytes=16 * MIB),
        cost_estimate=pl.CostEstimate(flops=2 * rows * x.shape[1] * 3 * width, bytes_accessed=5 * MIB, transcendentals=0),
        name="project",
    )(*map(in_hbm, (seg, x, wq, wk, wv)))


def attend_queries(which, rng_ref, item_ref, hide_ref, kv_ref, across, turned, out_ref, inverse_ref, share_refs, mix, shifted, peaks):
    pairs, block = len(share_refs), BLOCK
    per_half = out_ref.shape[0] // block

    def scores(p, span, both, hide):
        keys = jnp.concatenate([kv_ref[span, p * PAIR : (p + 1) * PAIR], item_ref[span, :]], 1)
        return dot(keys, jnp.concatenate([across[p, :, both], hide], 0))

    def query_block(i, carry):
        g = which * per_half + i
        both, here = aligned(g, 2 * block), aligned(i, 2 * block)
        low, high = rng_ref[0, g], rng_ref[1, g]

        def mix_all(hide_of, walk):
            mix[...] = jnp.zeros(mix.shape, F32)

            def visit(span, size):
                ahead = scores(0, span, both, hide_of(0))
                for p in range(pairs):
                    s = ahead
                    if p + 1 < pairs:
                        ahead = scores(p + 1, span, both, hide_of(p + 1))
                    e = jnp.exp2(s).astype(BF16)
                    share_refs[p][span, here] = e
                    for a in range(2):
                        head = slice((2 * p + a) * TURNED, (2 * p + a + 1) * TURNED)
                        mix[head, :] += dot(turned[head, span], e[:, a * block : (a + 1) * block])

            walk(low, high, visit)

        mix_all(lambda p: hide_ref[:, both], over_keys_coarse)
        total_rows = [h * TURNED + HEAD_DIM for h in range(2 * pairs)]
        sums = jnp.concatenate([mix[r : r + 8, :] for r in total_rows], 0)
        fine = jnp.where((sums <= LARGEST) & (sums >= SMALLEST), 0.0, 1.0)

        @pl.when(jnp.max(fine) > 0.0)
        def _():
            peaks[...] = jnp.full(peaks.shape, MASKED, F32)

            def visit(span, size):
                for p in range(pairs):
                    s = scores(p, span, both, hide_ref[:, both])
                    peaks[p] = jnp.maximum(peaks[p], jnp.max(s, 0, keepdims=True))

            over_keys_fine(low, high, visit)
            row = lax.broadcasted_iota(jnp.int32, (128, 2 * block), 0)
            hide = hide_ref[:, both].astype(F32)
            for p in range(pairs):
                peak = peaks[p]
                first = peak.astype(BF16).astype(F32)
                second = (peak - first).astype(BF16).astype(F32)
                third = peak - first - second
                parts = jnp.where(row < 64, first, jnp.where(row < 96, second, third))
                shifted[p] = jnp.where(is_shift(row), -parts, hide).astype(BF16)
            mix_all(lambda p: shifted[p], over_keys_fine)

        rows = aligned(i, block)
        outs = []
        for p in range(pairs):
            scales = []
            for a in range(2):
                base = (2 * p + a) * TURNED
                scale = jnp.broadcast_to(1.0 / mix[base + HEAD_DIM : base + HEAD_DIM + 1, :], (HEAD_DIM, block))
                outs.append((mix[base : base + HEAD_DIM, :] * scale).astype(BF16))
                scales.append(scale)
            inverse_ref[rows, p * PAIR : (p + 1) * PAIR] = jnp.concatenate(scales, 0).T
        out_ref[rows, :] = jnp.concatenate(outs, 0).T
        return carry

    lax.fori_loop(0, per_half, query_block, 0)


def attention_kernel(
    rng_ref, x_ref, item_ref, hide_ref, wq_ref, wk_ref, wv_ref, kv_in, queries_in, across_in, turned_in,
    kv_ref, queries_ref, across, turned, out_ref, inverse_ref, *rest,
):
    half = x_ref.shape[0]
    *share_refs, mix, shifted, peaks = rest
    here, there = lax.axis_index("mp"), 1 - lax.axis_index("mp")
    turned[:, aligned(here, half)] = turned_in[:, aligned(here, half)]
    across[:, :, aligned(here, 2 * half)] = across_in[:, :, aligned(here, 2 * half)]
    kv_ref[aligned(here, half), :] = kv_in[aligned(here, half), :]
    queries_ref[:, aligned(here, 2 * half), :] = queries_in[:, aligned(here, 2 * half), :]
    write_projection(there, x_ref[...], (wq_ref, wk_ref, wv_ref), (), kv_ref, queries_ref, across, turned)
    attend_queries(there, rng_ref, item_ref, hide_ref, kv_ref, across, turned, out_ref, inverse_ref, share_refs, mix, shifted, peaks)


def own_attention_kernel(rng_ref, item_ref, hide_ref, kv_ref, across, turned, out_ref, inverse_ref, *rest):
    *share_refs, mix, shifted, peaks = rest
    here = lax.axis_index("mp")
    attend_queries(here, rng_ref, item_ref, hide_ref, kv_ref, across, turned, out_ref, inverse_ref, share_refs, mix, shifted, peaks)


def attention_call(kernel, name, kept, half, operands):
    kv = operands[7] if kept else operands[3]
    count, width = kv.shape[0], kv.shape[1] // 2
    pairs = width // PAIR
    return pl.pallas_call(
        kernel,
        out_shape=tuple(jax.ShapeDtypeStruct(v.shape, v.dtype) for v in kept)
        + (jax.ShapeDtypeStruct((half, width), BF16), jax.ShapeDtypeStruct((half, width), F32))
        + (jax.ShapeDtypeStruct((count, 2 * half), BF16),) * pairs,
        in_specs=[SM] + [VM] * (len(operands) - 1),
        out_specs=(VM,) * (len(kept) + 2 + pairs),
        scratch_shapes=[
            pltpu.VMEM((2 * pairs * TURNED, BLOCK), F32),
            pltpu.VMEM((pairs, 128, 2 * BLOCK), BF16),
            pltpu.VMEM((pairs, 1, 2 * BLOCK), F32),
        ],
        compiler_params=pltpu.CompilerParams(vmem_limit_bytes=10 * MIB),
        cost_estimate=pl.CostEstimate(flops=5 * 10**9, bytes_accessed=8 * MIB, transcendentals=10**6),
        name=name,
    )(*operands)


def pair_grad_kernel(
    p, rng_ref, kv_ref, queries_ref, keep_ref, send_ref, own_ref, other_ref, inverse_ref, inverse2_ref, share_ref, share2_ref,
    dq_ref, dk_ref, dv_ref,
    grads, across, turned, delta, dq, dk, dv,
):
    half, width = keep_ref.shape
    count, block = kv_ref.shape[0], BLOCK
    cols = slice(p * PAIR, (p + 1) * PAIR)
    here, there = lax.axis_index("mp"), 1 - lax.axis_index("mp")
    row = lax.broadcasted_iota(jnp.int32, (8, PAIR), 0)
    column = lax.broadcasted_iota(jnp.int32, (8, PAIR), 1)
    pick = jnp.where(column // HEAD_DIM == row, 1.0, 0.0).astype(BF16)
    sides = ((here, keep_ref, own_ref, inverse_ref), (there, send_ref, other_ref, inverse2_ref))
    for which, mixed_ref, up_ref, scale_ref in sides:
        scaled = (up_ref[:, cols].astype(F32) * scale_ref[:, cols]).astype(BF16)
        product = mixed_ref[:, cols].astype(F32) * scaled.astype(F32)
        high = product.astype(BF16)
        low = (product - high.astype(F32)).astype(BF16)
        delta[:, aligned(which, half)] = dot_nt(pick, high) + dot_nt(pick, low)
        stack_heads(scaled, grads.at[aligned(which, 2 * half), :], block)
        stack_heads_across(scaled.T, across.at[:, aligned(which, 2 * half)], block)
    turned[...] = kv_ref[:, cols].T
    dk[...] = jnp.zeros(dk.shape, F32)
    dv[...] = jnp.zeros(dv.shape, F32)

    def query_block(which, shares_ref, i, carry):
        g = which * (half // block) + i
        rows, both = aligned(g, block), aligned(g, 2 * block)
        dq[...] = jnp.zeros(dq.shape, F32)
        level = jnp.concatenate([delta[0:1, rows], delta[1:2, rows]], 1)

        def visit(span, size):
            d = dot(kv_ref[span, width + p * PAIR : width + (p + 1) * PAIR], across[:, both])
            shares = shares_ref[span, aligned(i, 2 * block)]
            slopes = (shares.astype(F32) * (d - level)).astype(BF16)
            dv[span, :] += dot(shares, grads[both, :])
            dk[span, :] += dot(slopes, queries_ref[p, both, :])
            for a in range(2):
                head = slice(a * HEAD_DIM, (a + 1) * HEAD_DIM)
                dq[head, :] += dot(turned[head, span], slopes[:, a * block : (a + 1) * block])

        over_keys_coarse(rng_ref[0, g], rng_ref[1, g], visit)
        dq_ref[rows, :] = (dq[...] * HEAD_DIM**-0.5).astype(BF16).T
        return carry

    for which, shares_ref in ((here, share_ref), (there, share2_ref)):
        lax.fori_loop(0, half // block, functools.partial(query_block, which, shares_ref), 0)
    dk_ref[...] = (dk[...] * LN2).astype(BF16)
    dv_ref[...] = dv[...].astype(BF16)


def pair_grad(p, rng, kv, queries, keep, send, own, other, *per_half):
    count = kv.shape[0]
    return pl.pallas_call(
        functools.partial(pair_grad_kernel, p),
        out_shape=(jax.ShapeDtypeStruct((count, PAIR), BF16),) * 3,
        in_specs=[SM] + [VM] * 10,
        out_specs=(VM,) * 3,
        scratch_shapes=[
            pltpu.VMEM((2 * count, PAIR), BF16),
            pltpu.VMEM((PAIR, 2 * count), BF16),
            pltpu.VMEM((PAIR, count), BF16),
            pltpu.VMEM((8, count), F32),
            pltpu.VMEM((PAIR, BLOCK), F32),
            pltpu.VMEM((count, PAIR), F32),
            pltpu.VMEM((count, PAIR), F32),
        ],
        compiler_params=pltpu.CompilerParams(vmem_limit_bytes=12 * MIB),
        cost_estimate=pl.CostEstimate(flops=4 * 10**9, bytes_accessed=8 * MIB, transcendentals=0),
        name=f"pair_grad_{p}",
    )(rng, kv, queries, keep, send, own, other, *per_half)


def input_kernel(first_ref, *refs):
    *pieces, wq_ref, wk_ref, wv_ref, away_ref, home_ref = refs
    half = home_ref.shape[0]
    right = jnp.concatenate([wq_ref[...], wk_ref[...], wv_ref[...]], 1)

    def part(which):
        rows = aligned(which, half)
        return dot_nt(jnp.concatenate([piece[rows, :] for piece in pieces], 1), right)

    away_ref[...] = part(1 - lax.axis_index("mp")).astype(BF16)
    home_ref[...] = part(lax.axis_index("mp")) + first_ref[...]


def input_parts(first_grad, pieces, weights):
    half, features = first_grad.shape
    return pl.pallas_call(
        input_kernel,
        out_shape=(jax.ShapeDtypeStruct((half, features), BF16), jax.ShapeDtypeStruct((half, features), F32)),
        in_specs=[VM] * (1 + len(pieces) + len(weights)),
        out_specs=(VM,) * 2,
        compiler_params=pltpu.CompilerParams(vmem_limit_bytes=16 * MIB),
        cost_estimate=pl.CostEstimate(flops=2 * 10**9, bytes_accessed=8 * MIB, transcendentals=0),
        name="input_parts",
    )(first_grad, *pieces, *weights)


def gelu_both(v):
    part = 0.5 + 0.5 * lax.erf(v * ROOT_HALF)
    return v * part, part + v * jnp.exp(-0.5 * v * v) * ROOT_TWO_PI


def norm(values, gain, shift):
    mean = jnp.mean(values, -1, keepdims=True)
    centred = values - mean
    reciprocal = lax.rsqrt(jnp.mean(centred * centred, -1, keepdims=True) + EPS)
    normed = centred * reciprocal
    return normed * gain + shift, normed, reciprocal


def norm_grad(upstream, normed, reciprocal, gain):
    scaled = upstream * gain
    return reciprocal * (
        scaled - jnp.mean(scaled, -1, keepdims=True) - normed * jnp.mean(scaled * normed, -1, keepdims=True)
    )


def column_sum(values):
    return jnp.sum(values, 0, keepdims=True)


def eight_rows(values):
    return jnp.sum(values.reshape(-1, 8, values.shape[1]), 0)


def interleave(first, second):
    done = 0
    for i, step in enumerate(first):
        step()
        while done < len(second) and (done + 1) * len(first) <= (i + 1) * len(second):
            second[done]()
            done += 1
    for step in second[done:]:
        step()


def middle_kernel(
    x_ref, keep_ref, got_ref, up_ref,
    mdb_ref, mub_ref, ddb_ref, dub_ref, fg_ref, fs_ref, sg_ref, ss_ref,
    wo_ref, wo2_ref, w12_ref, w22_ref, md_hbm, mu_hbm, w1_hbm, w2_hbm, dd_hbm, du_hbm,
    act_hbm, first_ref, attended_ref, mine_ref, theirs_ref,
    md_ref, mu_ref, w1_ref, w2_ref, dd_ref, du_ref,
    slope_ref, wide_ref, out_ref, hidden_ref, normed_ref, low_ref, hidden_low_ref, act_ref, top_ref,
    big_ref, small_ref, sems, act_sem,
):
    rows, features = x_ref.shape
    adapt = md_ref.shape[0]
    names = ("md", "mu", "w1", "w2", "dd", "du")
    waits = dict(
        zip(
            names,
            start_all(
                (md_hbm, mu_hbm, w1_hbm, w2_hbm, dd_hbm, du_hbm),
                (md_ref, mu_ref, w1_ref, w2_ref, dd_ref, du_ref),
                sems,
            ),
        )
    )
    waited = set()

    def need(*wanted):
        for name in wanted:
            if name not in waited:
                waited.add(name)
                waits[name].wait()

    def vector(ref):
        return ref[...].astype(F32).reshape(1, -1)

    units = w1_ref.shape[1]
    chunk, piece_rows = 512, 64
    sides = ((w1_ref, w2_ref, ("w1", "w2")), (w12_ref, w22_ref, ()))
    pieces = [(side, slice(c * chunk, (c + 1) * chunk)) for side in sides for c in range(units // chunk)]
    kept = {}
    sums = {}

    def add(name, value):
        sums[name] = sums[name] + value if name in sums else value

    def parts(half):
        return [slice(r, r + piece_rows) for r in range(half.start, half.stop, piece_rows)]

    def attend(half):
        def first():
            attended = dot(keep_ref[half, :], wo_ref[...]) + dot(got_ref[half, :], wo2_ref[...])
            wide_ref[half, :] = attended
            low_ref[half, :] = attended.astype(BF16)

        def second():
            need("md", "mu")
            active, slope = gelu_both(dot_nt(low_ref[half, :], md_ref[...]) + vector(mdb_ref))
            kept["mixer", half.start] = (active.astype(BF16), slope)

        def third():
            out_ref[half, :] = dot(kept["mixer", half.start][0], mu_ref[...]) + vector(mub_ref)

        return [first, second, third]

    def norm_one(half):
        def one(part):
            x, mixer_out = x_ref[part, :].astype(F32), out_ref[part, :]
            add("mixer_square", eight_rows(mixer_out * mixer_out))
            add("input_square", eight_rows(x * x))
            hidden, normed, reciprocal = norm(x + wide_ref[part, :] + mixer_out, vector(fg_ref), vector(fs_ref))
            normed_ref[part, :] = normed
            hidden_ref[part, :] = hidden
            hidden_low_ref[part, :] = hidden.astype(BF16)
            kept["reciprocal", part.start] = reciprocal

        return [functools.partial(one, part) for part in parts(half)]

    def feed_forward(half):
        state = {}

        def start():
            need("w1", "w2")
            side, span = pieces[0]
            state["ahead"] = dot(hidden_low_ref[half, :], side[0][:, span])

        def one(n):
            side, span = pieces[n]
            inner = state["ahead"]
            if n + 1 < len(pieces):
                after, after_span = pieces[n + 1]
                state["ahead"] = dot(hidden_low_ref[half, :], after[0][:, after_span])
            value, slope = gelu_both(inner)
            slope_ref[half, n * chunk : (n + 1) * chunk] = slope.astype(BF16)
            state["value"] = value.astype(BF16)

        def two(n):
            side, span = pieces[n]
            total = dot(state["value"], side[1][span, :])
            state["total"] = state["total"] + total if n else total
            if n + 1 == len(pieces):
                wide_ref[half, :] = state["total"]

        steps = [start]
        for n in range(len(pieces)):
            steps += [functools.partial(one, n), functools.partial(two, n)]
        return steps

    def dense(half):
        def first():
            need("dd", "du")
            dense_low = wide_ref[half, :].astype(BF16)
            active, slope = gelu_both(dot_nt(dense_low, dd_ref[...]) + vector(ddb_ref))
            kept["dense", half.start] = (active.astype(BF16), slope, dense_low)

        def second():
            out_ref[half, :] = dot(kept["dense", half.start][0], du_ref[...]) + vector(dub_ref)

        return [first, second]

    def norm_two(half):
        def one(part):
            dense_out = out_ref[part, :]
            add("dense_square", eight_rows(dense_out * dense_out))
            gain = vector(sg_ref)
            result, normed, reciprocal = norm(hidden_ref[part, :] + wide_ref[part, :] + dense_out, gain, vector(ss_ref))
            act_ref[part, :] = result.astype(BF16)
            upstream = up_ref[part, :].astype(F32)
            add(4, eight_rows(upstream * normed))
            add(5, eight_rows(upstream))
            second_grad = norm_grad(upstream, normed, reciprocal, gain)
            hidden_ref[part, :] = second_grad
            top = second_grad.astype(BF16)
            top_ref[part, :] = top
            add(1, eight_rows(top.astype(F32)))

        return [functools.partial(one, part) for part in parts(half)]

    def dense_back(half):
        def first():
            active, slope, dense_low = kept["dense", half.start]
            top = top_ref[half, :]
            add("dense_up", dot_tn(active, top))
            mid = (dot_nt(top, du_ref[...]) * slope).astype(BF16)
            kept["dense_mid", half.start] = mid
            add("dense_mid", eight_rows(mid.astype(F32)))

        def second():
            mid = kept["dense_mid", half.start]
            add("dense_down", dot_tn(mid, kept["dense", half.start][2]))
            hidden_low_ref[half, :] = (hidden_ref[half, :] + dot(mid, dd_ref[...])).astype(BF16)

        return [first, second]

    def feed_back(half):
        state = {}

        def start():
            side, span = pieces[0]
            state["ahead"] = dot_nt(hidden_low_ref[half, :], side[1][span, :])

        def one(n):
            back = state["ahead"]
            if n + 1 < len(pieces):
                after, after_span = pieces[n + 1]
                state["ahead"] = dot_nt(hidden_low_ref[half, :], after[1][after_span, :])
            slope = slope_ref[half, n * chunk : (n + 1) * chunk].astype(F32)
            state["value"] = (back * slope).astype(BF16)

        def two(n):
            side, span = pieces[n]
            total = dot_nt(state["value"], side[0][:, span])
            state["total"] = state["total"] + total if n else total
            if n + 1 == len(pieces):
                hidden_ref[half, :] = hidden_ref[half, :] + state["total"]

        steps = [start]
        for n in range(len(pieces)):
            steps += [functools.partial(one, n), functools.partial(two, n)]
        return steps

    def norm_one_back(half):
        def one(part):
            hidden_grad, normed = hidden_ref[part, :], normed_ref[part, :]
            add(2, eight_rows(hidden_grad * normed))
            add(3, eight_rows(hidden_grad))
            first_grad = norm_grad(hidden_grad, normed, kept["reciprocal", part.start], vector(fg_ref))
            first_ref[part, :] = first_grad
            top = first_grad.astype(BF16)
            top_ref[part, :] = top
            add(0, eight_rows(top.astype(F32)))

        return [functools.partial(one, part) for part in parts(half)]

    def attend_back(half):
        def first():
            active, slope = kept["mixer", half.start]
            top = top_ref[half, :]
            add("mixer_up", dot_tn(active, top))
            mid = (dot_nt(top, mu_ref[...]) * slope).astype(BF16)
            kept["mixer_mid", half.start] = mid
            add("mixer_mid", eight_rows(mid.astype(F32)))

        def second():
            mid = kept["mixer_mid", half.start]
            add("mixer_down", dot_tn(mid, low_ref[half, :]))
            attended_ref[half, :] = (first_ref[half, :] + dot(mid, md_ref[...])).astype(BF16)

        return [first, second]

    def send_result(half, index):
        copy = pltpu.make_async_copy(act_ref.at[half, :], act_hbm.at[half, :], act_sem.at[index])
        copy.start()
        return copy

    one, two = slice(0, rows // 2), slice(rows // 2, rows)
    interleave(attend(one), [])
    interleave(norm_one(one), attend(two))
    interleave(feed_forward(one), norm_one(two))
    interleave(feed_forward(two), dense(one) + norm_two(one) + dense_back(one))
    copies = [send_result(one, 0)]
    interleave(feed_back(one), dense(two) + norm_two(two) + dense_back(two))
    copies.append(send_result(two, 1))
    interleave(feed_back(two), norm_one_back(one) + attend_back(one))
    interleave(norm_one_back(two), [])
    interleave(attend_back(two), [])

    for n, name in enumerate(("mixer_down", "mixer_up", "dense_down", "dense_up")):
        big_ref[n * adapt : (n + 1) * adapt, :] = sums[name].astype(BF16)
    for row in range(6):
        small_ref[row : row + 1, :] = column_sum(sums[row])
    lane = lax.broadcasted_iota(jnp.int32, (1, 128), 1)
    squares = jnp.zeros((1, 128), F32)
    for n, name in enumerate(("mixer_square", "dense_square", "input_square")):
        squares = jnp.where(lane == n, jnp.sum(column_sum(sums[name]), -1, keepdims=True), squares)
    small_ref[6:7, :] = jnp.concatenate(
        [column_sum(sums["mixer_mid"]), column_sum(sums["dense_mid"]), squares, jnp.zeros((1, features - 2 * adapt - 128), F32)], 1
    )
    small_ref[7:8, :] = jnp.zeros((1, features), F32)
    tail = tail_of(small_ref[...])
    share = 2 * adapt
    for pack_ref, which in ((mine_ref, lax.axis_index("mp")), (theirs_ref, 1 - lax.axis_index("mp"))):
        pack_ref[:share, :] = big_ref[aligned(which, share), :]
        pack_ref[share:, :] = tail
    for copy in copies:
        copy.wait()


def tail_of(vectors):
    high = vectors.astype(BF16)
    return jnp.concatenate([high, (vectors - high.astype(F32)).astype(BF16)], 0)


def vectors_of(tail):
    wide = tail.astype(F32)
    return wide[:8] + wide[8:]


def middle(x, keep, got, up, vectors, swapped, matrices):
    rows, features = x.shape
    adapt = matrices[0].shape[0]
    units = matrices[2].shape[1]
    packed = jax.ShapeDtypeStruct((2 * adapt + 16, features), BF16)
    return pl.pallas_call(
        middle_kernel,
        out_shape=(
            jax.ShapeDtypeStruct((rows, features), BF16),
            jax.ShapeDtypeStruct((rows, features), F32),
            jax.ShapeDtypeStruct((rows, features), BF16),
            packed,
            packed,
        ),
        in_specs=[VM] * 16 + [HB] * 6,
        out_specs=(HB,) + (VM,) * 4,
        scratch_shapes=[pltpu.VMEM(m.shape, BF16) for m in matrices]
        + [pltpu.VMEM((rows, 2 * units), BF16)]
        + [pltpu.VMEM((rows, features), F32)] * 4
        + [pltpu.VMEM((rows, features), BF16)] * 4
        + [
            pltpu.VMEM((4 * adapt, features), BF16),
            pltpu.VMEM((8, features), F32),
            pltpu.SemaphoreType.DMA((6,)),
            pltpu.SemaphoreType.DMA((2,)),
        ],
        compiler_params=pltpu.CompilerParams(vmem_limit_bytes=25 * MIB),
        cost_estimate=pl.CostEstimate(flops=2 * 10**10, bytes_accessed=16 * MIB, transcendentals=10**6),
        name="middle",
    )(x, keep, got, up, *vectors, *swapped, *map(in_hbm, matrices))


def spread_kernel(attended_ref, wo_ref, wo2_ref, own_ref, away_ref):
    attended = attended_ref[...]
    away_ref[...] = dot_nt(attended, wo2_ref[...]).astype(BF16)
    own_ref[...] = dot_nt(attended, wo_ref[...]).astype(BF16)


def spread(attended, wo, wo2):
    rows, width = attended.shape[0], wo.shape[0]
    return pl.pallas_call(
        spread_kernel,
        out_shape=(jax.ShapeDtypeStruct((rows, width), BF16),) * 2,
        in_specs=[VM] * 3,
        out_specs=(VM,) * 2,
        compiler_params=pltpu.CompilerParams(vmem_limit_bytes=8 * MIB),
        cost_estimate=pl.CostEstimate(flops=4 * rows * attended.shape[1] * width, bytes_accessed=3 * MIB, transcendentals=0),
        name="spread",
    )(attended, wo, wo2)


def combine_kernel(held_ref, got_ref, out_ref):
    rows = held_ref.shape[0] - 16
    out_ref[:rows, :] = (held_ref[:rows, :].astype(F32) + got_ref[:rows, :].astype(F32)).astype(BF16)
    out_ref[rows:, :] = tail_of(vectors_of(held_ref[rows:, :]) + vectors_of(got_ref[rows:, :]))


def combine(held, got):
    return pl.pallas_call(
        combine_kernel,
        out_shape=jax.ShapeDtypeStruct(held.shape, BF16),
        in_specs=[VM] * 2,
        out_specs=VM,
        compiler_params=pltpu.CompilerParams(vmem_limit_bytes=4 * MIB),
        cost_estimate=pl.CostEstimate(flops=10**5, bytes_accessed=MIB, transcendentals=0),
        name="combine",
    )(held, got)


def finish_kernel(
    held_ref, got_ref, home_ref, away_ref,
    input_hbm, md_ref, mdb_ref, mu_ref, mub_ref, dd_ref, ddb_ref, du_ref, dub_ref, fg_ref, fs_ref, sg_ref, ss_ref, ratio_ref,
    input_ref, sems,
):
    adapt = md_ref.shape[0]
    size = input_ref.shape[0] // 2
    copies = []
    for t in range(2):
        part = slice(t * size, (t + 1) * size)
        input_ref[part, :] = (home_ref[part, :] + away_ref[part, :].astype(F32)).astype(BF16)
        copies.append(pltpu.make_async_copy(input_ref.at[part, :], input_hbm.at[part, :], sems.at[t]))
        copies[-1].start()

    def write(first_ref, second_ref):
        md_ref[...] = first_ref[:adapt, :].astype(F32)
        mu_ref[...] = first_ref[adapt : 2 * adapt, :].astype(F32)
        dd_ref[...] = second_ref[:adapt, :].astype(F32)
        du_ref[...] = second_ref[adapt : 2 * adapt, :].astype(F32)
        vectors = vectors_of(first_ref[2 * adapt :, :])
        for row, out_ref in enumerate((mub_ref, dub_ref, fg_ref, fs_ref, sg_ref, ss_ref)):
            out_ref[...] = vectors[row, :]
        last = vectors[6:7, :]
        mdb_ref[...] = last[0, :adapt]
        ddb_ref[...] = last[0, adapt : 2 * adapt]
        squares = last[:, 2 * adapt : 2 * adapt + 128]
        lane = lax.broadcasted_iota(jnp.int32, (1, 128), 1)
        base = jnp.sum(jnp.where(lane == 2, squares, 0.0), -1, keepdims=True)
        ratio_ref[...] = jnp.sqrt(squares / base)[0, :2]

    @pl.when(lax.axis_index("mp") == 0)
    def _():
        write(held_ref, got_ref)

    @pl.when(lax.axis_index("mp") != 0)
    def _():
        write(got_ref, held_ref)

    for copy in copies:
        copy.wait()


def finish(held, got, home, away, adapt):
    features = held.shape[1]
    matrix = jax.ShapeDtypeStruct((adapt, features), F32)
    short, vector = jax.ShapeDtypeStruct((adapt,), F32), jax.ShapeDtypeStruct((features,), F32)
    return pl.pallas_call(
        finish_kernel,
        out_shape=(jax.ShapeDtypeStruct(away.shape, BF16),)
        + (matrix, short, matrix, vector) * 2
        + (vector,) * 4
        + (jax.ShapeDtypeStruct((2,), F32),),
        in_specs=[VM] * 4,
        out_specs=(HB,) + (VM,) * 13,
        scratch_shapes=[pltpu.VMEM(away.shape, BF16), pltpu.SemaphoreType.DMA((2,))],
        compiler_params=pltpu.CompilerParams(vmem_limit_bytes=8 * MIB),
        name="finish",
    )(held, got, home, away)


def swap_cores(value):
    return lax.ppermute(value, "mp", [(0, 1), (1, 0)])


def tie(*values):
    return lax.optimization_barrier(values)


def per_device(
    tokens, segment_ids, query_weight, key_weight, value_weight, output_weight, inner_weight, outer_weight,
    mixer_down, mixer_down_bias, mixer_up, mixer_up_bias, dense_down, dense_down_bias, dense_up, dense_up_bias,
    first_gain, first_shift, second_gain, second_shift, output_grad,
):
    devices = lax.axis_size("dp")
    adapt = mixer_down.shape[1]
    other_tokens = swap_cores(tokens)
    kv, queries, across, turned, item, hide, rng = project(
        segment_ids, tokens, query_weight, key_weight, value_weight
    )
    kv, other_tokens, output_late, inner_late, outer_late = tie(
        kv, other_tokens, output_weight, inner_weight, outer_weight
    )
    other_output = swap_cores(output_late)
    other_inner = swap_cores(inner_late)
    other_outer = swap_cores(outer_late)
    half = tokens.shape[0]
    written = (kv, queries, across, turned)
    kv, queries, across, turned, send, inverse2, *shares2 = attention_call(
        attention_kernel, "attention", written, half,
        (rng, other_tokens, item, hide, query_weight, key_weight, value_weight, *written),
    )
    got = swap_cores(send)
    keep, inverse, *shares = attention_call(
        own_attention_kernel, "own_attention", (), half, (rng, item, hide, kv, across, turned)
    )
    got, keep = tie(got, keep)
    vectors = (
        mixer_down_bias, mixer_up_bias, dense_down_bias, dense_up_bias, first_gain, first_shift, second_gain, second_shift,
    )
    swapped = (output_weight, other_output, other_inner, other_outer)
    matrices = (mixer_down.T, mixer_up, inner_weight, outer_weight, dense_down.T, dense_up)
    result, first_grad, attended, mine, theirs = middle(
        tokens, keep, got, output_grad, vectors, swapped, matrices
    )
    arriving = swap_cores(theirs)
    own_grad, away_grad = spread(attended, output_weight, other_output)
    arriving, own_grad = tie(arriving, own_grad)
    packed = combine(mine, arriving)
    away_grad, packed = tie(away_grad, packed)
    got_grad = swap_cores(away_grad)

    steps = []
    while 2 ** len(steps) < devices:
        steps.append(2 ** len(steps))
    steps.reverse()
    turn = len(steps) // 2
    pairs = len(shares)
    grads = []
    weights = (query_weight, key_weight, value_weight)
    for n, step in enumerate(steps):
        other_step = steps[(n + turn) % len(steps)]
        exchange = [(2 * i + c, 2 * (i ^ s) + c) for i in range(devices) for c, s in enumerate((step, other_step))]
        arriving = lax.ppermute(packed, ("dp", "mp"), exchange)
        if n < pairs:
            got_grad, packed = tie(got_grad, packed)
            parts = pair_grad(n, rng, kv, queries, keep, send, own_grad, got_grad, inverse, inverse2, shares[n], shares2[n])
            arriving, *parts = tie(arriving, *parts)
            grads.append(parts)
        elif n == pairs:
            pieces = [grads[p][i] for i in range(3) for p in range(pairs)]
            pieces[0], packed = tie(pieces[0], packed)
            away, home = input_parts(first_grad, pieces, weights)
            arriving, away, home = tie(arriving, away, home)
        packed = combine(packed, arriving)
    input_grad, md, mdb, mu, mub, dd, ddb, du, dub, *rest = finish(packed, swap_cores(packed), home, swap_cores(away), adapt)
    return (result, input_grad, md.T, mdb, mu, mub, dd.T, ddb, du, dub, *rest)


def solution(mesh):
    tokens = P(("dp", "mp"), None)
    columns, rows, whole = P(None, "mp"), P("mp", None), P()
    return jax.shard_map(
        per_device,
        mesh=mesh,
        in_specs=(tokens, P("dp", None), columns, columns, columns, rows, columns, rows) + (whole,) * 12 + (tokens,),
        out_specs=(tokens, tokens) + (whole,) * 13,
        check_vma=False,
    )
```
